32 devices in a mesh: row: 4 (over y, x), col: 8 (over z, core).
Axes of the slice: x: 2, y: 2, z: 4, core: 2. Of those that a mesh axis runs over, the one named last changes fastest.
Arguments:
- block_in: bfloat16 [8, 2048, 1024], P('col', 'row'), may hold values from -6 to 6
- cotangent: bfloat16 [8, 2048, 1024], P('col', 'row'), may hold values from -6 to 6
- seq_lengths: int32 [8, 12], P('col'), may hold values from 1 to 256, as said below
- seq_order: int32 [8, 12], P('col'), may hold values from 0 to 11, as said below
- expert_ids: int32 [8, 2048, 8], P('col'), may hold values from 0 to 31, as said below
- places: int32 [8, 2048, 8], P('col'), may hold values from 0 to 2047, as said below
- attn_gain: float32 [1024], replicated, may hold values from 0.5 to 1.5
- w_qkv: bfloat16 [1024, 2048], P('col', 'row'), may hold values from -0.59765625 to 0.59765625
- w_out: bfloat16 [1024, 1024], P('col', 'row'), may hold values from -1.796875 to 1.796875
- moe_gain: float32 [1024], replicated, may hold values from 0.5 to 1.5
- w_router: bfloat16 [1024, 32], P('col'), may hold values from -0.099609375 to 0.099609375
- w_gate: bfloat16 [1024, 32, 512], P('col', 'row'), may hold values from -0.1875 to 0.1875
- w_up: bfloat16 [1024, 32, 512], P('col', 'row'), may hold values from -0.1875 to 0.1875
- w_down: bfloat16 [1024, 32, 512], P('col', 'row'), may hold values from -3.59375 to 3.59375
Outputs:
- block_out: bfloat16 [8, 2048, 1024], P('col', 'row')
- input_grad: float32 [8, 2048, 1024], P('col', 'row')
- attn_gain_grad: float32 [1024], replicated
- qkv_grad: float32 [1024, 2048], P('col', 'row')
- out_grad: float32 [1024, 1024], P('col', 'row')
- moe_gain_grad: float32 [1024], replicated
- router_grad: float32 [1024, 32], P('col')
- gate_grad: float32 [1024, 32, 512], P('col', 'row')
- up_grad: float32 [1024, 32, 512], P('col', 'row')
- down_grad: float32 [1024, 32, 512], P('col', 'row')
The draws below stay inside these ranges and needn't reach their ends.
Inputs may be any that keep to these rules, and one draw needn't show every extreme that they name: `seq_lengths`: the sequences of dealt slots r*3 to (r+1)*3 - 1 of a group add up to 512 tokens, and one of them has 256. `seq_order`: each row is a permutation of the group's 12 sequences. `expert_ids`: each token names 8 different experts; in each group one expert is named by every token. `places`: a pair's place is the number of earlier pairs of its group, tokens in dealt order and a token's 8 choices in order, that name the same expert.
All inputs are finite; a program needn't handle non-finite values.
Results may differ from the reference program's by a relative error of at most 0.012.
The reference program's roundings to bfloat16 on the way count: a program that leaves them out, or rounds other values in their place, can miss the bound.
Values may be sent and summed in bfloat16 or wider, within the bound.
A program may use at most 256 MiB of HBM per device.

```python
import jax
import jax.numpy as jnp
from jax import lax

D = 1024
HEAD_WIDTH = 64
QUERY_HEADS = 16
KEY_VALUE_HEADS = 8
EXPERT_COUNT = 32
FE = 512
TOPK = 8
DEVICE_TOKENS = 512
SEQ_DEV = 3
SEQS = 12
GROUP_TOKENS = 2048
GROUPS = 8
SEQ_LONG = 256
CAP = 512
QKV = 2048


def route_table(key):
    expert_demand = jax.random.randint(jax.random.fold_in(key, 7), (GROUPS, 1, EXPERT_COUNT), 0, 2 ** 20)
    random_noise_bits = jax.random.randint(jax.random.fold_in(key, 8), (GROUPS, GROUP_TOKENS, EXPERT_COUNT), 0, 2 ** 20)
    preferred_expert = jax.random.randint(jax.random.fold_in(key, 9), (GROUPS, 1, 1), 0, EXPERT_COUNT)
    expert_columns = jnp.arange(EXPERT_COUNT, dtype=jnp.int32)
    extra_logit = jnp.where(expert_columns[None, None, :] == preferred_expert, 2 ** 21, 0).astype(jnp.int32)
    attention_logits = (expert_demand + random_noise_bits + extra_logit) * EXPERT_COUNT + expert_columns
    return lax.top_k(attention_logits, TOPK)[1].astype(jnp.int32)


def deal_tables(key):
    row_count = SEQS // SEQ_DEV
    remainder = DEVICE_TOKENS - SEQ_LONG
    long_slot = jax.random.randint(jax.random.fold_in(key, 11), (GROUPS, row_count, 1), 0, SEQ_DEV)
    first_cut = jax.random.randint(jax.random.fold_in(key, 12), (GROUPS, row_count, 1), 1, remainder)
    slot_ids = jnp.arange(SEQ_DEV, dtype=jnp.int32)[None, None, :]
    slot_rank = slot_ids - (slot_ids > long_slot).astype(jnp.int32)
    dealt_len = jnp.where(slot_ids == long_slot, SEQ_LONG, jnp.where(slot_rank == 0, first_cut, remainder - first_cut))
    dealt_len = dealt_len.reshape(GROUPS, SEQS).astype(jnp.int32)
    shuffle_bits = jax.random.randint(jax.random.fold_in(key, 13), (GROUPS, SEQS), 0, 2 ** 20) * SEQS + jnp.arange(SEQS, dtype=jnp.int32)[None, :]
    seq_perm = jnp.argsort(shuffle_bits, axis=1).astype(jnp.int32)
    inverse = jnp.argsort(seq_perm, axis=1).astype(jnp.int32)
    given_len = jnp.take_along_axis(dealt_len, inverse, axis=1).astype(jnp.int32)
    return (given_len, seq_perm)


def draw_seq_lengths(key, part):
    return deal_tables(key)[0]


def draw_seq_order(key, part):
    return deal_tables(key)[1]


def draw_expert_ids(key, part):
    return route_table(key)


def draw_places(key, part):
    chosen = route_table(key)
    flat_ids = chosen.reshape(GROUPS, GROUP_TOKENS * TOPK)
    matches = (flat_ids[:, :, None] == jnp.arange(EXPERT_COUNT, dtype=jnp.int32)).astype(jnp.int32)
    earlier = jnp.cumsum(matches, axis=1) - matches
    return jnp.sum(earlier * matches, axis=2).astype(jnp.int32).reshape(GROUPS, GROUP_TOKENS, TOPK)


def steps_of(own_key, dims, shards, least, largest):
    gain, own = 1.0, jax.random.fold_in(own_key, 6)
    for dim, blocks in shards:
        heights = jnp.exp(jax.random.uniform(jax.random.fold_in(own, dim), (blocks,), jnp.float32, least / len(shards), largest / len(shards)))
        gain = gain * jnp.repeat(heights, dims[dim] // blocks).reshape([-1 if axis == dim else 1 for axis in range(len(dims))])
    return gain


def gaussian(key, dims, width, limit, split=(), kind=jnp.bfloat16):
    values = jax.random.normal(key, dims, jnp.float32) * width
    if len(split) > 0:
        values = steps_of(key, dims, split, -0.22, 0.18) * values
    return jnp.clip(values, min=-limit, max=limit).astype(kind)


def setup_inputs(seed: int = 0) -> dict:
    key_of = jax.random.split(jax.random.key(seed), 15)
    block_in = gaussian(key_of[0], (GROUPS, GROUP_TOKENS, D), 1.0, 6.0, ((0, 8), (1, 4)))
    cotangent = gaussian(key_of[1], (GROUPS, GROUP_TOKENS, D), 1.0, 6.0, ((0, 8), (1, 4)))
    seq_lengths = draw_seq_lengths(jax.random.fold_in(key_of[14], 71), 0)
    seq_order = draw_seq_order(jax.random.fold_in(key_of[14], 71), 0)
    expert_ids = draw_expert_ids(jax.random.fold_in(key_of[14], 71), 0)
    places = draw_places(jax.random.fold_in(key_of[14], 71), 0)
    attn_gain = jnp.clip(1.0 + 0.1 * jax.random.normal(key_of[6], (D,), jnp.float32), 0.5, 1.5)
    w_qkv = gaussian(key_of[7], (D, QKV), 0.1, 0.59765625, ((0, 8), (1, 4)))
    w_out = gaussian(key_of[8], (D, QUERY_HEADS * HEAD_WIDTH), 0.3, 1.796875, ((0, 8), (1, 4)))
    moe_gain = jnp.clip(1.0 + 0.1 * jax.random.normal(key_of[9], (D,), jnp.float32), 0.5, 1.5)
    w_router = gaussian(key_of[10], (D, EXPERT_COUNT), 0.016, 0.099609375, ((0, 8),))
    w_gate = gaussian(key_of[11], (D, EXPERT_COUNT, FE), D ** -0.5, 0.1875, ((0, 8), (1, 4)))
    w_up = gaussian(key_of[12], (D, EXPERT_COUNT, FE), D ** -0.5, 0.1875, ((0, 8), (1, 4)))
    w_down = gaussian(key_of[13], (D, EXPERT_COUNT, FE), 0.6, 3.59375, ((0, 8), (1, 4)))
    return dict(block_in=block_in, cotangent=cotangent, seq_lengths=seq_lengths, seq_order=seq_order, expert_ids=expert_ids, places=places, attn_gain=attn_gain, w_qkv=w_qkv, w_out=w_out, moe_gain=moe_gain, w_router=w_router, w_gate=w_gate, w_up=w_up, w_down=w_down)


EPSILON = 1e-06
RESIDUAL_SCALE = 0.22
SCORE_SCALE = 0.015625
ROPE_BASE = 10000.0
MASKED = -1e+30
HIGHEST = lax.Precision.HIGHEST

@jax.custom_vjp
def low(v):
    return lax.optimization_barrier(v.astype(jnp.bfloat16)).astype(jnp.float32)

@jax.custom_vjp
def reduced_backward(v):
    return v

def low_keep(v):
    return (low(v), None)

def low_pass(kept, grad):
    return (grad,)

def back_keep(v):
    return (v, None)

def back_low(kept, grad):
    return (low(grad),)
low.defvjp(low_keep, low_pass)
reduced_backward.defvjp(back_keep, back_low)

def matrix_product(left, right):
    return jnp.dot(left, right, precision=HIGHEST, preferred_element_type=jnp.float32)

def norm_rows(values, gain_vec):
    return values * lax.rsqrt(lax.optimization_barrier(jnp.mean(values * values, axis=-1, keepdims=True)) + EPSILON) * gain_vec

def dealt_tables(lengths, seq_perm, group_tokens):
    seq_ids = jnp.arange(lengths.shape[0], dtype=jnp.int32)
    picked = seq_perm[:, None] == seq_ids[None, :]
    dealt_len = lax.optimization_barrier(jnp.sum(jnp.where(picked, lengths[None, :], 0), axis=1)).astype(jnp.int32)
    before = seq_ids[None, :] < seq_perm[:, None]
    source_base = lax.optimization_barrier(jnp.sum(jnp.where(before, lengths[None, :], 0), axis=1)).astype(jnp.int32)
    seq_ends = jnp.cumsum(dealt_len).astype(jnp.int32)
    positions = jnp.arange(group_tokens, dtype=jnp.int32)
    past_end = positions[:, None] >= seq_ends[None, :]
    seq_starts = lax.optimization_barrier(jnp.sum(jnp.where(past_end, dealt_len[None, :], 0), axis=1)).astype(jnp.int32)
    slot_of = lax.optimization_barrier(jnp.sum(past_end.astype(jnp.int32), axis=1)).astype(jnp.int32)
    offset = (positions - seq_starts).astype(jnp.int32)
    source_rows = (lax.optimization_barrier(jnp.sum(jnp.where(slot_of[:, None] == seq_ids[None, :], source_base[None, :], 0), axis=1)) + offset).astype(jnp.int32)
    return (offset, seq_starts, source_rows, positions)

def angles(offset):
    frequency = ROPE_BASE ** (-jnp.arange(HEAD_WIDTH // 2, dtype=jnp.float32) * 2.0 / HEAD_WIDTH)
    turned = offset.astype(jnp.float32)[:, None] * frequency[None, :]
    return (jnp.cos(turned), jnp.sin(turned))

def rotate(values, cosine, sine_table):
    half_size = values.shape[-1] // 2
    first_half = values[..., :half_size]
    second_half = values[..., half_size:]
    return jnp.concatenate([first_half * cosine - second_half * sine_table, second_half * cosine + first_half * sine_table], axis=-1)

def attend_one_block(pieces):
    query_block, key_block, value_block, starts_block = pieces
    local_pos = jnp.arange(DEVICE_TOKENS, dtype=jnp.int32)
    raw_scores = reduced_backward(jnp.einsum('qgjd,kgd->gjqk', query_block, key_block, precision=HIGHEST))
    allowed = (local_pos[None, :] <= local_pos[:, None]) & (local_pos[None, :] >= starts_block[:, None])
    attention_logits = jnp.where(allowed, raw_scores * SCORE_SCALE, MASKED)
    prob_rows = low(jax.nn.softmax(attention_logits, axis=-1))
    mixed_block = low(reduced_backward(jnp.einsum('gjqk,kgd->qgjd', prob_rows, value_block, precision=HIGHEST)))
    return mixed_block.reshape(DEVICE_TOKENS, QUERY_HEADS * HEAD_WIDTH)

def group_forward(group_in, lengths, seq_perm, chosen_ids, pair_places, gain_attn, query_key_value_weight, weight_out, gain_moe, weight_router, weight_gate, weight_up, weight_down):
    offset, seq_starts, source_rows, positions = dealt_tables(lengths, seq_perm, GROUP_TOKENS)
    inverse = jnp.zeros((GROUP_TOKENS,), jnp.int32).at[source_rows].set(positions)
    cosine, sine_table = angles(offset)
    head_repeat_count = QUERY_HEADS // KEY_VALUE_HEADS
    dealt_in = group_in[source_rows]
    attention_input = low(norm_rows(dealt_in, gain_attn))
    projected_rows = reduced_backward(matrix_product(attention_input, query_key_value_weight)).reshape(GROUP_TOKENS, KEY_VALUE_HEADS, head_repeat_count + 2, HEAD_WIDTH)
    query_rows = low(rotate(projected_rows[:, :, :head_repeat_count], cosine[:, None, None, :], sine_table[:, None, None, :]))
    head_keys = low(rotate(projected_rows[:, :, head_repeat_count], cosine[:, None, :], sine_table[:, None, :]))
    head_values = low(projected_rows[:, :, head_repeat_count + 1])
    block_total_count = GROUP_TOKENS // DEVICE_TOKENS
    block_base = jnp.arange(block_total_count, dtype=jnp.int32) * DEVICE_TOKENS
    local_start_rows = (seq_starts.reshape(block_total_count, DEVICE_TOKENS) - block_base[:, None]).astype(jnp.int32)
    blended_rows = lax.map(jax.checkpoint(attend_one_block), (query_rows.reshape(block_total_count, DEVICE_TOKENS, KEY_VALUE_HEADS, head_repeat_count, HEAD_WIDTH), head_keys.reshape(block_total_count, DEVICE_TOKENS, KEY_VALUE_HEADS, HEAD_WIDTH), head_values.reshape(block_total_count, DEVICE_TOKENS, KEY_VALUE_HEADS, HEAD_WIDTH), local_start_rows)).reshape(GROUP_TOKENS, QUERY_HEADS * HEAD_WIDTH)
    attn_out = matrix_product(blended_rows, weight_out.T)
    middle = dealt_in + RESIDUAL_SCALE * reduced_backward(attn_out)
    moe_in = low(norm_rows(middle, gain_moe))
    logits = reduced_backward(matrix_product(moe_in, weight_router))
    chosen = jnp.take_along_axis(logits, chosen_ids, axis=1)
    pair_gates = jax.nn.softmax(chosen, axis=-1)
    kept_pair = pair_places < CAP
    slot_index = jnp.where(kept_pair, chosen_ids * CAP + pair_places, EXPERT_COUNT * CAP).reshape(-1)
    pair_token = (positions[:, None] + jnp.zeros_like(chosen_ids)).reshape(-1)
    slot_token = jnp.full((EXPERT_COUNT * CAP,), GROUP_TOKENS, jnp.int32).at[slot_index].set(pair_token, mode='drop')
    slot_pair = jnp.full((EXPERT_COUNT * CAP,), GROUP_TOKENS * TOPK, jnp.int32).at[slot_index].set(jnp.arange(GROUP_TOKENS * TOPK, dtype=jnp.int32), mode='drop')
    padded_in = jnp.concatenate([moe_in, jnp.zeros((1, D), jnp.float32)], axis=0)
    routed = padded_in[slot_token].reshape(EXPERT_COUNT, CAP, D)
    gate_in = reduced_backward(jnp.einsum('ecd,def->ecf', routed, weight_gate, precision=HIGHEST))
    up_in = reduced_backward(jnp.einsum('ecd,def->ecf', routed, weight_up, precision=HIGHEST))
    hidden = low(jax.nn.silu(gate_in) * up_in)
    expert_out = reduced_backward(jnp.einsum('ecf,def->ecd', hidden, weight_down, precision=HIGHEST)).reshape(EXPERT_COUNT * CAP, D)
    padded_gates = jnp.concatenate([pair_gates.reshape(-1), jnp.zeros((1,), jnp.float32)], axis=0)
    weighted = padded_gates[slot_pair][:, None] * expert_out
    expert_sum = jnp.zeros((GROUP_TOKENS + 1, D), jnp.float32).at[slot_token].add(weighted)[:GROUP_TOKENS]
    block_rows = middle + RESIDUAL_SCALE * reduced_backward(expert_sum)
    return block_rows[inverse]

def reference(block_in, cotangent, seq_lengths, seq_order, expert_ids, places, attn_gain, w_qkv, w_out, moe_gain, w_router, w_gate, w_up, w_down):

    def forward(input_rows, gain_attn, query_key_value_weight, weight_out, gain_moe, weight_router, weight_gate, weight_up, weight_down):

        def one_group(inputs):
            return group_forward(inputs[0], inputs[1], inputs[2], inputs[3], inputs[4], gain_attn, query_key_value_weight, weight_out, gain_moe, weight_router, weight_gate, weight_up, weight_down)
        return lax.map(jax.checkpoint(one_group), (input_rows, seq_lengths, seq_order, expert_ids, places))
    primals = (block_in.astype(jnp.float32), attn_gain, w_qkv.astype(jnp.float32), w_out.astype(jnp.float32), moe_gain, w_router.astype(jnp.float32), w_gate.astype(jnp.float32), w_up.astype(jnp.float32), w_down.astype(jnp.float32))
    result, pullback = jax.vjp(forward, *primals)
    gradients = pullback(cotangent.astype(jnp.float32))
    return (result.astype(jnp.bfloat16), gradients[0], gradients[1], gradients[2], gradients[3], gradients[4], gradients[5], gradients[6], gradients[7], gradients[8])
```

```python
import functools

import jax
import jax.numpy as jnp
from jax import lax
from jax.experimental import pallas as pl
from jax.experimental.pallas import tpu as pltpu
from jax.sharding import PartitionSpec as P

HEAD_WIDTH = 64
QUERY_HEADS = 16
KEY_VALUE_HEADS = 8
EXPERT_COUNT = 32
TOPK = 8
EPSILON = 1e-06
RESIDUAL_SCALE = 0.22
SCORE_SCALE = 0.015625
ROPE_BASE = 10000.0
MASKED = -1e30
LANES = 128
MIB = 1024 * 1024
BF = jnp.bfloat16
F32 = jnp.float32
ANY = pl.BlockSpec(memory_space=pl.ANY)
FULL = pl.BlockSpec(memory_space=pltpu.VMEM)


def mm(a, b):
    return lax.dot_general(a, b, (((1,), (0,)), ((), ())), preferred_element_type=F32)


def mm_nt(a, b):
    return lax.dot_general(a, b, (((1,), (1,)), ((), ())), preferred_element_type=F32)


def mm_tn(a, b):
    return lax.dot_general(a, b, (((0,), (0,)), ((), ())), preferred_element_type=F32)


def iota(shape, dim):
    return lax.broadcasted_iota(jnp.int32, shape, dim)


def params(mib):
    return pltpu.CompilerParams(vmem_limit_bytes=mib * MIB)


def cost(flops, moved):
    return pl.CostEstimate(flops=int(flops), bytes_accessed=int(moved), transcendentals=0)


def row_scale(values):
    return lax.rsqrt(jnp.mean(values * values, axis=-1, keepdims=True) + EPSILON)


def swap_halves(values):
    width = values.shape[-1]
    half = HEAD_WIDTH // 2
    low = (iota(values.shape, 1) % HEAD_WIDTH) < half
    ahead = pltpu.roll(values, width - half, 1)
    behind = pltpu.roll(values, half, 1)
    return jnp.where(low, ahead, behind)


def masked_probs(q, k, row0, starts):
    rows, cols = q.shape[0], k.shape[0]
    scores = mm_nt(q, k) * SCORE_SCALE
    at = iota((rows, cols), 1)
    allowed = (at <= iota((rows, cols), 0) + row0) & (at >= starts)
    scores = jnp.where(allowed, scores, MASKED)
    top = jnp.max(scores, axis=-1, keepdims=True)
    raised = jnp.exp(scores - top)
    total = jnp.sum(raised, axis=-1, keepdims=True)
    return raised * (1.0 / total)


def front_kernel(nblk, *refs):
    xin = refs[:nblk]
    (src, starts, cos, sin, gain_a, gain_m, w_att) = refs[nblk : nblk + 7]
    (xd, attn, qkv, mixed, middle, moe) = refs[nblk + 7 :]
    tokens = xd.shape[0]
    half = tokens // 2
    qw = w_att.shape[2] * 2 // 3
    source = src[...]
    x = jnp.zeros((tokens, xd.shape[1]), F32)
    for j in range(nblk):
        pick = jnp.where(source == iota((tokens, tokens), 1) + j * tokens, 1.0, 0.0).astype(BF)
        x = x + mm(pick, xin[j][...])
    xd[...] = x.astype(BF)
    attn[...] = (x * row_scale(x) * gain_a[...]).astype(BF)
    groups = qw // (4 * HEAD_WIDTH)

    def project(j, carry):
        proj = mm(attn[...], w_att[j, :, :qw])
        cos_w = jnp.concatenate([cos[...]] * groups, axis=1)
        sin_w = jnp.concatenate([sin[...]] * groups, axis=1)
        turned = proj * cos_w + swap_halves(proj) * sin_w
        qkv[:, pl.ds(pl.multiple_of(j * qw, qw), qw)] = turned.astype(BF)
        return carry

    lax.fori_loop(0, nblk, project, 0)

    def group(g, carry):
        chunk = qkv[:, pl.ds(pl.multiple_of(g * 4 * HEAD_WIDTH, 4 * HEAD_WIDTH), 4 * HEAD_WIDTH)]
        k = chunk[:, 2 * HEAD_WIDTH : 3 * HEAD_WIDTH]
        v = chunk[:, 3 * HEAD_WIDTH :]
        for b in range(2):
            span = (b + 1) * half
            outs = []
            for h in range(2):
                q = chunk[b * half : (b + 1) * half, h * HEAD_WIDTH : (h + 1) * HEAD_WIDTH]
                probs = masked_probs(q, k[:span], b * half, starts[b * half : (b + 1) * half, :])
                outs.append(mm(probs.astype(BF), v[:span]))
            mixed[b * half : (b + 1) * half, pl.ds(pl.multiple_of(g * 2 * HEAD_WIDTH, 2 * HEAD_WIDTH), 2 * HEAD_WIDTH)] = (
                jnp.concatenate(outs, axis=1).astype(BF)
            )
        return carry

    lax.fori_loop(0, groups * nblk, group, 0)
    ow = w_att.shape[2] - qw
    out = jnp.zeros((tokens, xd.shape[1]), F32)
    for j in range(nblk):
        out = out + mm_nt(mixed[:, j * ow : (j + 1) * ow], w_att[j, :, qw:])
    mid = xd[...].astype(F32) + RESIDUAL_SCALE * out
    middle[...] = mid
    moe[...] = (mid * row_scale(mid) * gain_m[...]).astype(BF)


def front(xin, src, starts, cos, sin, gain_a, gain_m, w_att):
    tokens, width = xin[0].shape
    nblk = len(xin)
    qkv_width = nblk * w_att.shape[2] * 2 // 3
    head_width = nblk * w_att.shape[2] // 3
    shape = jax.ShapeDtypeStruct
    return pl.pallas_call(
        functools.partial(front_kernel, nblk),
        out_shape=(
            shape((tokens, width), BF),
            shape((tokens, width), BF),
            shape((tokens, qkv_width), BF),
            shape((tokens, head_width), BF),
            shape((tokens, width), F32),
            shape((tokens, width), BF),
        ),
        in_specs=[FULL] * (nblk + 7),
        out_specs=[FULL] * 6,
        compiler_params=params(48),
        cost_estimate=cost(10e9, 30 * MIB),
        name="attention_forward",
    )(*xin, src, starts, cos, sin, gain_a, gain_m, w_att)


def deal_kernel(nblk, *refs):
    cot = refs[:nblk]
    (src, ids, spots) = refs[nblk : nblk + 3]
    (dsum, dy, slot_cols, slot_rows, chosen) = refs[nblk + 3 :]
    tokens = cot[0].shape[0]

    def block(b, carry):
        at = pl.ds(pl.multiple_of(b * tokens, tokens), tokens)
        source = src[at, :]
        rows = jnp.zeros(cot[0].shape, F32)
        for j in range(nblk):
            pick = jnp.where(source == iota((tokens, tokens), 1) + j * tokens, 1.0, 0.0).astype(BF)
            rows = rows + mm(pick, cot[j][...])
        dsum[at, :] = (RESIDUAL_SCALE * rows).astype(BF)

        @pl.when(b == 0)
        def _():
            dy[...] = rows.astype(BF)

        lane = iota((tokens, LANES), 1)
        spot = jnp.zeros((tokens, LANES), F32)
        named = jnp.zeros((tokens, LANES), F32)
        own_ids = ids[at, :]
        own_spots = spots[at, :]
        for k in range(TOPK):
            hit = lane == own_ids[:, k : k + 1]
            named = jnp.where(hit, 1.0, named)
            spot = jnp.where(hit, own_spots[:, k : k + 1].astype(F32), spot)
        chosen[at, :] = named
        slot = jnp.where(named > 0.0, spot, -1.0)
        slot_cols[at, :] = slot
        slot_rows[:, at] = slot.T
        return carry

    lax.fori_loop(0, nblk, block, 0)


def deal(cot, src, ids, spots):
    tokens, width = cot[0].shape
    nblk = len(cot)
    total = nblk * tokens
    shape = jax.ShapeDtypeStruct
    return pl.pallas_call(
        functools.partial(deal_kernel, nblk),
        out_shape=(
            shape((total, width), BF),
            shape((tokens, width), BF),
            shape((total, LANES), F32),
            shape((LANES, total), F32),
            shape((total, LANES), F32),
        ),
        in_specs=[FULL] * (nblk + 3),
        out_specs=[FULL] * 5,
        compiler_params=params(40),
        cost_estimate=cost(9e9, 20 * MIB),
        name="deal_cotangent",
    )(*cot, src, ids, spots)


def router_kernel(nblk, *refs):
    moe = refs[:nblk]
    (w_router, chosen, gates, packed) = refs[nblk:]
    tokens = moe[0].shape[0]
    local = EXPERT_COUNT // nblk
    for j in range(nblk):
        at = slice(j * tokens, (j + 1) * tokens)
        logits = mm(moe[j][...], w_router[...])
        named = chosen[at, :] > 0.0
        logits = jnp.where(named, logits, MASKED)
        top = jnp.max(logits, axis=-1, keepdims=True)
        raised = jnp.where(named, jnp.exp(logits - top), 0.0)
        gate = raised / jnp.sum(raised, axis=-1, keepdims=True)
        gates[at, :] = gate
        lane = iota((tokens, LANES), 1)
        own = jnp.where(lane < local, gate, 0.0)
        high = own.astype(BF).astype(F32)
        rest = own - high
        mid = rest.astype(BF).astype(F32)
        low = rest - mid
        packed[at, :] = (high + pltpu.roll(mid, local, 1) + pltpu.roll(low, 2 * local, 1)).astype(BF)


def router(moe, w_router, chosen):
    tokens = moe[0].shape[0]
    nblk = len(moe)
    total = nblk * tokens
    shape = jax.ShapeDtypeStruct
    return pl.pallas_call(
        functools.partial(router_kernel, nblk),
        out_shape=(shape((total, LANES), F32), shape((total, LANES), BF)),
        in_specs=[FULL] * (nblk + 2),
        out_specs=[FULL] * 2,
        compiler_params=params(24),
        cost_estimate=cost(1e9, 7 * MIB),
        name="router",
    )(*moe, w_router, chosen)


def expert_kernel(nblk, base, first, last, local, capacity, *refs):
    moe_hbm = refs[:nblk]
    refs = refs[nblk:]
    if first:
        (dsum_hbm, slot_rows, slot_cols, packed, w) = refs[:5]
        refs = refs[5:]
    else:
        (dsum_hbm, slot_rows, slot_cols, packed, w, acc_in, accg_in) = refs[:7]
        refs = refs[7:]
    if last:
        (grads, sums, dgates) = refs[:3]
    else:
        (grads, acc_out, accg_out) = refs[:3]
    (moe, dsum, acc, accg, sel, selt, routed, dsl, dslot, y1, y2, sems) = refs[3:]
    step = pl.program_id(0)
    steps = pl.num_programs(0)
    e = base + step
    tokens, width = moe_hbm[0].shape
    total = nblk * tokens
    fe = w.shape[4]
    shard = w.shape[3]
    tile = 256
    tiles = width // tile
    copies = []
    for j in range(nblk):
        copies.append(
            pltpu.make_async_copy(moe_hbm[j], moe.at[pl.ds(j * tokens, tokens)], sems.at[j])
        )
    copies.append(pltpu.make_async_copy(dsum_hbm, dsum, sems.at[nblk]))
    loads = []
    if not first:
        loads.append(pltpu.make_async_copy(acc_in, acc, sems.at[nblk + 1]))
        loads.append(pltpu.make_async_copy(accg_in, accg, sems.at[nblk + 2]))

    @pl.when(step == 0)
    def _():
        for c in copies:
            c.start()
        for c in loads:
            c.start()
        if first:
            acc[...] = jnp.zeros(acc.shape, F32)
            accg[...] = jnp.zeros(accg.shape, F32)

    row = slot_rows[pl.ds(e, 1), :]
    lanes = iota((tokens, LANES), 1)
    for j in range(nblk):
        at = slice(j * tokens, (j + 1) * tokens)
        sel[:, at] = jnp.where(
            iota((capacity, tokens), 0).astype(F32) == row[:, at], 1.0, 0.0
        ).astype(BF)
        col = jnp.sum(jnp.where(lanes == e, slot_cols[at, :], 0.0), axis=1, keepdims=True)
        selt[at, :] = jnp.where(
            col == iota((tokens, capacity), 1).astype(F32), 1.0, 0.0
        ).astype(BF)

    @pl.when(step == 0)
    def _():
        for c in copies:
            c.wait()

    def dispatch(n, carry):
        at = pl.ds(pl.multiple_of(n * tile, tile), tile)
        routed[:, at] = mm(sel[...], moe[:, at]).astype(BF)
        dsl[:, at] = mm(sel[...], dsum[:, at]).astype(BF)
        return carry

    lax.fori_loop(0, tiles, dispatch, 0)
    lane = iota((capacity, LANES), 1)
    picked = mm(sel[...], packed[...])
    mine = (lane == e) | (lane == e + local) | (lane == e + 2 * local)
    gate = jnp.sum(jnp.where(mine, picked, 0.0), axis=1, keepdims=True)
    dslot[...] = (gate * dsl[...].astype(F32)).astype(BF)

    def weight(i):
        return w[:, 0, i].reshape(width, fe)

    per = tile // shard

    def weight_tile(i, n):
        return w[pl.ds(n * per, per), 0, i].reshape(tile, fe)

    gate_in = mm(routed[...], weight(0))
    up_in = mm(routed[...], weight(1))
    sig = jax.nn.sigmoid(gate_in)
    silu = gate_in * sig
    hidden = (silu * up_in).astype(BF)

    def down(n, inner):
        at = pl.ds(pl.multiple_of(n * tile, tile), tile)
        out = mm_nt(hidden, weight_tile(2, n))
        y1[:, at] = (gate * out).astype(BF)
        return inner + jnp.sum(dsl[:, at].astype(F32) * out, axis=1, keepdims=True)

    inner = lax.fori_loop(0, tiles, down, jnp.zeros((capacity, 1), F32))
    high = inner.astype(BF).astype(F32)
    rest = inner - high
    mid = rest.astype(BF).astype(F32)
    low = rest - mid
    spread = jnp.where(
        lane == e,
        high,
        jnp.where(lane == e + local, mid, jnp.where(lane == e + 2 * local, low, 0.0)),
    ).astype(BF)
    dhidden = mm(dslot[...], weight(2))
    dgate = (dhidden * up_in * sig * (1.0 + gate_in * (1.0 - sig))).astype(BF)
    dup = (dhidden * silu).astype(BF)

    def back(n, carry):
        at = pl.ds(pl.multiple_of(n * tile, tile), tile)
        devs = pl.ds(n * per, per)
        grads[devs, 0, 2] = mm_tn(dslot[:, at], hidden).astype(BF).reshape(per, shard, fe)
        rows = routed[:, at]
        grads[devs, 0, 0] = mm_tn(rows, dgate).astype(BF).reshape(per, shard, fe)
        grads[devs, 0, 1] = mm_tn(rows, dup).astype(BF).reshape(per, shard, fe)
        y2[:, at] = (mm_nt(dgate, weight_tile(0, n)) + mm_nt(dup, weight_tile(1, n))).astype(BF)
        return carry

    lax.fori_loop(0, tiles, back, 0)

    if not first:

        @pl.when(step == 0)
        def _():
            for c in loads:
                c.wait()

    def combine(b, carry):
        at = pl.ds(pl.multiple_of(b * tokens, tokens), tokens)
        chosen = selt[at, :]
        acc[0, at, :] += mm(chosen, y1[...])
        acc[1, at, :] += mm(chosen, y2[...])
        accg[at, :] += mm(chosen, spread)
        return carry

    lax.fori_loop(0, nblk, combine, 0)

    @pl.when(step == steps - 1)
    def _():
        if last:
            moe[...] = acc[0].astype(BF)
            dsum[...] = acc[1].astype(BF)
            outs = [
                pltpu.make_async_copy(moe, sums.at[0], sems.at[0]),
                pltpu.make_async_copy(dsum, sums.at[1], sems.at[1]),
                pltpu.make_async_copy(accg, dgates, sems.at[2]),
            ]
        else:
            outs = [
                pltpu.make_async_copy(acc, acc_out, sems.at[0]),
                pltpu.make_async_copy(accg, accg_out, sems.at[1]),
            ]
        for c in outs:
            c.start()
        for c in outs:
            c.wait()


def experts(moe, dsum, slot_rows, slot_cols, packed, w, carried, base, last, capacity):
    nblk = len(moe)
    tokens, width = moe[0].shape
    total = nblk * tokens
    cols, ne, three, shard, fe = w.shape
    local = EXPERT_COUNT // nblk
    first = carried is None
    shape = jax.ShapeDtypeStruct
    wspec = pl.BlockSpec((cols, 1, three, shard, fe), lambda s: (0, s, 0, 0, 0))
    ins = [*moe, dsum, slot_rows, slot_cols, packed, w]
    in_specs = [ANY] * (nblk + 1) + [FULL, FULL, FULL, wspec]
    aliases = {}
    if not first:
        ins += list(carried)
        in_specs += [ANY, ANY]
        aliases = {} if last else {len(ins) - 2: 1, len(ins) - 1: 2}
    if last:
        outs = (shape((2, total, width), BF), shape((total, LANES), F32))
    else:
        outs = (shape((2, total, width), F32), shape((total, LANES), F32))
    return pl.pallas_call(
        functools.partial(expert_kernel, nblk, base, first, last, local, capacity),
        grid=(ne,),
        out_shape=(shape(w.shape, BF), *outs),
        in_specs=in_specs,
        out_specs=[wspec, ANY, ANY],
        scratch_shapes=[
            pltpu.VMEM((total, width), BF),
            pltpu.VMEM((total, width), BF),
            pltpu.VMEM((2, total, width), F32),
            pltpu.VMEM((total, LANES), F32),
            pltpu.VMEM((capacity, total), BF),
            pltpu.VMEM((total, capacity), BF),
            pltpu.VMEM((capacity, width), BF),
            pltpu.VMEM((capacity, width), BF),
            pltpu.VMEM((capacity, width), BF),
            pltpu.VMEM((capacity, width), BF),
            pltpu.VMEM((capacity, width), BF),
            pltpu.SemaphoreType.DMA((nblk + 3,)),
        ],
        input_output_aliases=aliases,
        compiler_params=params(60),
        cost_estimate=cost(14e9 * ne, 40 * MIB),
        name="experts",
    )(*ins)


def back_kernel(nblk, *refs):
    dm = refs[:nblk]
    dg = refs[nblk : 2 * nblk]
    (gates, middle, moe, dy, mixed, qkv, attn, xd, w_att, w_router, starts, cos, sin, gain_a, gain_m) = refs[
        2 * nblk : 2 * nblk + 15
    ]
    (igrad, qkv_grad, out_grad, router_grad, gains) = refs[2 * nblk + 15 : 2 * nblk + 20]
    (dmid, dmix, dproj) = refs[2 * nblk + 20 :]
    tokens, width = xd.shape
    half = tokens // 2
    local = EXPERT_COUNT // nblk
    qw = w_att.shape[2] * 2 // 3
    ow = w_att.shape[2] - qw
    hw = HEAD_WIDTH
    lane = iota((tokens, LANES), 1)
    dgate = jnp.zeros((tokens, LANES), F32)
    for j in range(nblk):
        part = dg[j][...]
        part = part + pltpu.roll(part, LANES - local, 1) + pltpu.roll(part, LANES - 2 * local, 1)
        part = jnp.where(lane < local, part, 0.0)
        dgate = dgate + (part if j == 0 else pltpu.roll(part, j * local, 1))
    gate = gates[...]
    dchosen = gate * (dgate - jnp.sum(gate * dgate, axis=1, keepdims=True))
    dlogits = dchosen.astype(BF)
    router_grad[...] = mm_tn(moe[...], dlogits)
    dmoe = mm_nt(dlogits, w_router[...])
    for j in range(nblk):
        dmoe = dmoe + dm[j][...].astype(F32)
    mid = middle[...]
    r = row_scale(mid)
    scaled = dmoe * gain_m[...]
    inner = jnp.mean(scaled * mid, axis=-1, keepdims=True)
    dmid[...] = dy[...].astype(F32) + (r * scaled - mid * (r * r * r) * inner)
    gains[1:2, :] = jnp.sum(dmoe * mid * r, axis=0, keepdims=True)
    dattn = (RESIDUAL_SCALE * dmid[...]).astype(BF)
    for j in range(nblk):
        dmix[:, j * ow : (j + 1) * ow] = mm(dattn, w_att[j, :, qw:]).astype(BF)
        out_grad[j] = mm_tn(dattn, mixed[:, j * ow : (j + 1) * ow]).astype(BF)

    def group(g, carry):
        chunk = qkv[:, pl.ds(pl.multiple_of(g * 4 * hw, 4 * hw), 4 * hw)]
        dm_chunk = dmix[:, pl.ds(pl.multiple_of(g * 2 * hw, 2 * hw), 2 * hw)]
        k = chunk[:, 2 * hw : 3 * hw]
        v = chunk[:, 3 * hw :]
        dk = jnp.zeros((tokens, hw), F32)
        dv = jnp.zeros((tokens, hw), F32)
        dq = [[None, None], [None, None]]
        for b in range(2):
            span = (b + 1) * half
            rows = slice(b * half, (b + 1) * half)
            for h in range(2):
                q = chunk[rows, h * hw : (h + 1) * hw]
                dmh = dm_chunk[rows, h * hw : (h + 1) * hw]
                probs = masked_probs(q, k[:span], b * half, starts[rows, :])
                dprobs = mm_nt(dmh, v[:span])
                total = jnp.sum(probs * dprobs, axis=-1, keepdims=True)
                dscores = (probs * (dprobs - total) * SCORE_SCALE).astype(BF)
                dq[h][b] = mm(dscores, k[:span])
                dk_part = mm_tn(dscores, q)
                dv_part = mm_tn(probs.astype(BF), dmh)
                if span < tokens:
                    pad = jnp.zeros((tokens - span, hw), F32)
                    dk_part = jnp.concatenate([dk_part, pad], axis=0)
                    dv_part = jnp.concatenate([dv_part, pad], axis=0)
                dk = dk + dk_part
                dv = dv + dv_part
        d = jnp.concatenate(
            [
                jnp.concatenate(dq[0], axis=0),
                jnp.concatenate(dq[1], axis=0),
                dk,
                dv,
            ],
            axis=1,
        )
        d = d * cos[...] - swap_halves(d) * sin[...]
        dproj[:, pl.ds(pl.multiple_of(g * 4 * hw, 4 * hw), 4 * hw)] = d.astype(BF)
        return carry

    lax.fori_loop(0, nblk * qw // (4 * hw), group, 0)
    dattn_in = jnp.zeros((tokens, width), F32)
    for j in range(nblk):
        part = dproj[:, j * qw : (j + 1) * qw]
        qkv_grad[j] = mm_tn(attn[...], part).astype(BF)
        dattn_in = dattn_in + mm_nt(part, w_att[j, :, :qw])
    x = xd[...].astype(F32)
    r = row_scale(x)
    scaled = dattn_in * gain_a[...]
    inner = jnp.mean(scaled * x, axis=-1, keepdims=True)
    igrad[...] = (dmid[...] + (r * scaled - x * (r * r * r) * inner)).astype(BF)
    gains[0:1, :] = jnp.sum(dattn_in * x * r, axis=0, keepdims=True)


def backward(dm, dg, *rest):
    nblk = len(dm)
    tokens, width = dm[0].shape
    w_att = rest[8]
    qw = w_att.shape[2] * 2 // 3
    ow = w_att.shape[2] - qw
    shape = jax.ShapeDtypeStruct
    return pl.pallas_call(
        functools.partial(back_kernel, nblk),
        out_shape=(
            shape((tokens, width), BF),
            shape((nblk, width, qw), BF),
            shape((nblk, width, ow), BF),
            shape((width, LANES), F32),
            shape((2, width), F32),
        ),
        in_specs=[FULL] * (2 * nblk + 15),
        out_specs=[FULL] * 5,
        scratch_shapes=[
            pltpu.VMEM((tokens, width), F32),
            pltpu.VMEM((tokens, nblk * ow), BF),
            pltpu.VMEM((tokens, nblk * qw), BF),
        ],
        compiler_params=params(60),
        cost_estimate=cost(20e9, 40 * MIB),
        name="attention_backward",
    )(*dm, *dg, *rest)


def given_kernel(nblk, *refs):
    rows = refs[:nblk]
    src, out = refs[nblk:]
    tokens, width = out.shape
    total = jnp.zeros((tokens, width), F32)
    for j in range(nblk):
        at = src[:, j * tokens : (j + 1) * tokens]
        pick = jnp.where(iota((tokens, tokens), 0) == at, 1.0, 0.0).astype(BF)
        total = total + mm(pick, rows[j][...])
    out[...] = total.astype(out.dtype)


def to_given(rows, src_row, dtype):
    nblk = len(rows)
    return pl.pallas_call(
        functools.partial(given_kernel, nblk),
        out_shape=jax.ShapeDtypeStruct(rows[0].shape, dtype),
        in_specs=[FULL] * (nblk + 1),
        out_specs=FULL,
        compiler_params=params(24),
        cost_estimate=cost(2e9, 6 * MIB),
        name="to_given_order",
    )(*rows, src_row)


def swap_over(value, axis, size, step):
    return lax.ppermute(value, axis, [(i, i ^ step) for i in range(size)])


def spread_rows(value, axis, size, step=1):
    return [value] + [swap_over(value, axis, size, j) for j in range(step, size, step)]


def sum_over(value, axis, size):
    return functools.reduce(lambda a, b: a + b, spread_rows(value, axis, size))


def body(
    block_in,
    cotangent,
    seq_lengths,
    seq_order,
    expert_ids,
    places,
    attn_gain,
    w_qkv,
    w_out,
    moe_gain,
    w_router,
    w_gate,
    w_up,
    w_down,
):
    tokens = block_in.shape[1]
    width = block_in.shape[2]
    rows = lax.axis_size("row")
    cols = lax.axis_size("col")
    total = tokens * rows
    r = lax.axis_index("row")
    c = lax.axis_index("col")
    parity = c % 2
    local = w_gate.shape[1]
    shard = w_gate.shape[0]
    fe = w_gate.shape[2]
    capacity = total * TOPK // EXPERT_COUNT
    pairs = cols // 2
    qw = w_qkv.shape[1]
    ow = w_out.shape[1]

    stacked = jnp.stack([w_gate, w_up, w_down]).transpose(2, 0, 1, 3)
    chunk = 2
    gathered = [
        lax.all_gather(stacked[i : i + chunk], "col", axis=0) for i in range(0, local, chunk)
    ]

    given_in = spread_rows(block_in[0], "row", rows)

    w_own = jnp.concatenate([w_qkv, w_out], axis=1)
    w_half = jnp.stack(spread_rows(w_own, "col", cols, 2))
    w_rows = jnp.stack(spread_rows(w_half, "row", rows))
    w_other = swap_over(w_rows, "col", cols, 1)
    base = c // 2

    def join_parity(mine, other, axis):
        even = jnp.where(parity == 0, mine, other)
        odd = jnp.where(parity == 0, other, mine)
        both = jnp.stack([even, odd], axis=axis + 1)
        return jnp.concatenate(
            [lax.dynamic_slice_in_dim(both, base ^ i, 1, axis) for i in range(pairs)], axis=axis
        )

    w_att = join_parity(w_rows, w_other, 1).reshape(rows, cols * shard, qw + ow)

    lengths = seq_lengths[0]
    perm = seq_order[0]
    seq_ids = jnp.arange(lengths.shape[0], dtype=jnp.int32)
    picked = perm[:, None] == seq_ids[None, :]
    dealt_len = jnp.sum(jnp.where(picked, lengths[None, :], 0), axis=1)
    before = seq_ids[None, :] < perm[:, None]
    source_base = jnp.sum(jnp.where(before, lengths[None, :], 0), axis=1)
    upto = seq_ids[None, :] <= seq_ids[:, None]
    seq_ends = jnp.sum(jnp.where(upto, dealt_len[None, :], 0), axis=1)
    dealt_start = seq_ends - dealt_len
    turn = r * tokens
    pos = jnp.arange(total, dtype=jnp.int32) ^ turn
    inside = (pos[:, None] >= dealt_start[None, :]) & (pos[:, None] < seq_ends[None, :])
    seq_starts = jnp.sum(jnp.where(inside, dealt_start[None, :], 0), axis=1)
    offset = pos - seq_starts
    source = jnp.sum(jnp.where(inside, source_base[None, :], 0), axis=1) + offset
    source = source ^ turn
    src_col = source[:, None]
    src_row = source[None, :]
    own_offset = offset[:tokens]
    own_starts = (seq_starts[:tokens] - turn)[:, None]

    half = HEAD_WIDTH // 2
    frequency = ROPE_BASE ** (-jnp.arange(half, dtype=F32) * 2.0 / HEAD_WIDTH)
    turned = own_offset.astype(F32)[:, None] * frequency[None, :]
    cosine, sine = jnp.cos(turned), jnp.sin(turned)
    ones, zeros = jnp.ones_like(cosine), jnp.zeros_like(cosine)
    cos_w = jnp.concatenate([cosine] * 6 + [ones] * 2, axis=1)
    sin_w = jnp.concatenate([-sine, sine] * 3 + [zeros] * 2, axis=1)

    gain_a = attn_gain[None, :]
    gain_m = moe_gain[None, :]
    xd, attn, qkv, mixed, middle, moe_own = front(
        given_in, src_col[:tokens], own_starts, cos_w, sin_w, gain_a, gain_m, w_att
    )
    moe = spread_rows(moe_own, "row", rows)

    held = lax.optimization_barrier((cotangent[0], given_in[-1]))[0]
    given_cot = spread_rows(held, "row", rows)

    def by_block(table):
        blocks = table.reshape(rows, tokens, TOPK)
        return jnp.concatenate(
            [lax.dynamic_slice_in_dim(blocks, r ^ j, 1, 0) for j in range(rows)], axis=0
        ).reshape(total, TOPK)

    ids = by_block(expert_ids[0])
    spots = by_block(places[0])
    ids = ((ids // local) ^ r) * local + ids % local
    spots = jnp.where(spots < capacity, spots, -1)
    dsum, dy, slot_cols, slot_rows, chosen = deal(given_cot, src_col, ids, spots)

    router_half = jnp.stack(spread_rows(w_router, "col", cols, 2))
    router_full = join_parity(router_half, swap_over(router_half, "col", cols, 1), 0)
    router_blocks = router_full.reshape(width, rows, local)
    router_x = jnp.concatenate(
        [lax.dynamic_slice_in_dim(router_blocks, r ^ j, 1, 1) for j in range(rows)], axis=1
    ).reshape(width, EXPERT_COUNT)
    router_x = jnp.pad(router_x, ((0, 0), (0, LANES - EXPERT_COUNT)))
    gates, packed = router(moe, router_x, chosen)

    carried = None
    summed = []
    for i, w in enumerate(gathered):
        last = i == len(gathered) - 1
        grads, *carried = experts(
            moe, dsum, slot_rows, slot_cols, packed, w, carried, i * chunk, last, capacity
        )
        summed.append(lax.psum_scatter(grads, "col", scatter_dimension=0, tiled=False))
    sums, dgates = carried

    def send_blocks(value):
        blocks = value.reshape(rows, tokens, value.shape[-1])
        return [blocks[0]] + [swap_over(blocks[j], "row", rows, j) for j in range(1, rows)]

    dg = send_blocks(dgates)
    dm = send_blocks(sums[1])
    es = send_blocks(lax.optimization_barrier((sums[0], dm[-1]))[0])
    dm[0] = lax.optimization_barrier((dm[0], summed[0]))[0]
    igrad, qkv_part, out_part, router_part, gain_part = backward(
        dm,
        dg,
        gates[:tokens],
        middle,
        moe_own,
        dy,
        mixed,
        qkv,
        attn,
        xd,
        w_att,
        router_x,
        own_starts,
        cos_w,
        sin_w,
        gain_a,
        gain_m,
    )
    expert_sum = functools.reduce(lambda a, b: a + b, [v.astype(F32) for v in es])
    block_dealt = (middle + RESIDUAL_SCALE * expert_sum).astype(BF)
    igrad = lax.optimization_barrier((igrad, summed[1]))[0]
    block_out = to_given(spread_rows(block_dealt, "row", rows), src_row, BF)[None]
    input_grad = to_given(spread_rows(igrad, "row", rows), src_row, F32)[None]

    part = jnp.concatenate([qkv_part, out_part], axis=2).reshape(
        rows, pairs, 2, shard, qw + ow
    )
    mine = jnp.where(parity == 0, part[:, :, 0], part[:, :, 1])
    other = jnp.where(parity == 0, part[:, :, 1], part[:, :, 0])
    chip = (mine.astype(F32) + swap_over(other, "col", cols, 1).astype(F32)).astype(BF)
    row_sum = functools.reduce(
        lambda a, b: a + b,
        [chip[0].astype(F32)]
        + [swap_over(chip[j], "row", rows, j).astype(F32) for j in range(1, rows)],
    ).astype(BF)
    z_own = [
        lax.dynamic_index_in_dim(row_sum, base ^ i, 0, keepdims=False) for i in range(pairs)
    ]
    att_sum = functools.reduce(
        lambda a, b: a + b,
        [z_own[0].astype(F32)]
        + [swap_over(z_own[i], "col", cols, 2 * i).astype(F32) for i in range(1, pairs)],
    )
    qkv_grad = att_sum[:, :qw]
    out_grad = att_sum[:, qw:]

    blocks = router_part[:, :EXPERT_COUNT].reshape(width, rows, local)
    router_std = jnp.concatenate(
        [lax.dynamic_slice_in_dim(blocks, r ^ j, 1, 1) for j in range(rows)], axis=1
    ).reshape(width * EXPERT_COUNT // width, width)
    small = jnp.concatenate([router_std, gain_part], axis=0)
    small = sum_over(small, "row", rows)
    small = sum_over(small, "col", cols)
    router_all = small[:EXPERT_COUNT].reshape(width, EXPERT_COUNT)
    router_grad = lax.dynamic_slice_in_dim(router_all, c * shard, shard, 0)
    attn_gain_total = small[EXPERT_COUNT]
    moe_gain_total = small[EXPERT_COUNT + 1]

    grads = jnp.concatenate(summed, axis=0).astype(F32).transpose(1, 2, 0, 3)
    return (
        block_out,
        input_grad,
        attn_gain_total,
        qkv_grad,
        out_grad,
        moe_gain_total,
        router_grad,
        grads[0],
        grads[1],
        grads[2],
    )


def solution(mesh):
    tokens = P("col", "row", None)
    weight = P("col", "row")
    expert = P("col", "row", None)
    return jax.shard_map(
        body,
        mesh=mesh,
        in_specs=(
            tokens,
            tokens,
            P("col", None),
            P("col", None),
            P("col", None, None),
            P("col", None, None),
            P(),
            weight,
            weight,
            P(),
            P("col", None),
            expert,
            expert,
            expert,
        ),
        out_specs=(
            tokens,
            tokens,
            P(),
            weight,
            weight,
            P(),
            P("col", None),
            expert,
            expert,
            expert,
        ),
        check_vma=False,
    )
```

```python
import functools

import jax
import jax.numpy as jnp
from jax import lax
from jax.experimental import pallas as pl
from jax.experimental.pallas import tpu as pltpu
from jax.sharding import PartitionSpec as P

HEAD_WIDTH = 64
QUERY_HEADS = 16
KEY_VALUE_HEADS = 8
EXPERT_COUNT = 32
TOPK = 8
EPSILON = 1e-06
RESIDUAL_SCALE = 0.22
SCORE_SCALE = 0.015625
ROPE_BASE = 10000.0
MASKED = -1e30
LANES = 128
MIB = 1024 * 1024
BF = jnp.bfloat16
F32 = jnp.float32
ANY = pl.BlockSpec(memory_space=pl.ANY)
FULL = pl.BlockSpec(memory_space=pltpu.VMEM)


def mm(a, b):
    return lax.dot_general(a, b, (((1,), (0,)), ((), ())), preferred_element_type=F32)


def mm_nt(a, b):
    return lax.dot_general(a, b, (((1,), (1,)), ((), ())), preferred_element_type=F32)


def mm_tn(a, b):
    return lax.dot_general(a, b, (((0,), (0,)), ((), ())), preferred_element_type=F32)


def iota(shape, dim):
    return lax.broadcasted_iota(jnp.int32, shape, dim)


def params(mib):
    return pltpu.CompilerParams(vmem_limit_bytes=mib * MIB)


def cost(flops, moved):
    return pl.CostEstimate(flops=int(flops), bytes_accessed=int(moved), transcendentals=0)


def row_scale(values):
    return lax.rsqrt(jnp.mean(values * values, axis=-1, keepdims=True) + EPSILON)


def swap_halves(values):
    width = values.shape[-1]
    half = HEAD_WIDTH // 2
    low = (iota(values.shape, 1) % HEAD_WIDTH) < half
    ahead = pltpu.roll(values, width - half, 1)
    behind = pltpu.roll(values, half, 1)
    return jnp.where(low, ahead, behind)


def masked_probs(q, k, row0, starts):
    rows, cols = q.shape[0], k.shape[0]
    scores = mm_nt(q, k) * SCORE_SCALE
    at = iota((rows, cols), 1)
    allowed = (at <= iota((rows, cols), 0) + row0) & (at >= starts)
    scores = jnp.where(allowed, scores, MASKED)
    top = jnp.max(scores, axis=-1, keepdims=True)
    raised = jnp.exp(scores - top)
    total = jnp.sum(raised, axis=-1, keepdims=True)
    return raised * (1.0 / total)


def link(src, dst, sems, index, device):
    return pltpu.make_async_remote_copy(
        src_ref=src,
        dst_ref=dst,
        send_sem=sems.at[0, index],
        recv_sem=sems.at[1, index],
        device_id=device,
        device_id_type=pl.DeviceIdType.MESH,
    )


def greet(devices):
    barrier = pltpu.get_barrier_semaphore()
    for device in devices:
        pl.semaphore_signal(barrier, inc=1, device_id=device, device_id_type=pl.DeviceIdType.MESH)
    pl.semaphore_wait(barrier, len(devices))


class RowGather:
    count = 6

    def __init__(self, own, slot, sems, base, r, c):
        near, far = (r ^ 1, c), (r ^ 2, c)
        self.copies = {
            (1, 1): link(own(1), slot(1, 1), sems, base, near),
            (2, 0): link(own(0), slot(2, 0), sems, base + 1, far),
            (1, 0): link(own(0), slot(1, 0), sems, base + 2, near),
            (2, 1): link(own(1), slot(2, 1), sems, base + 3, far),
            (3, 0): link(slot(2, 0), slot(3, 0), sems, base + 4, near),
            (3, 1): link(slot(1, 1), slot(3, 1), sems, base + 5, far),
        }

    def start(self, half):
        order = ((2, 0), (1, 0)) if half == 0 else ((1, 1), (2, 1))
        for key in order:
            self.copies[key].start()

    def forward(self, half):
        self.copies[(2, 0) if half == 0 else (1, 1)].wait_recv()
        self.copies[(3, half)].start()

    def wait(self, *keys):
        for key in keys:
            self.copies[key].wait_recv()

    def drain(self):
        for copy in self.copies.values():
            copy.wait_send()


def front_kernel(
    xin,
    cot,
    w_own,
    src,
    starts,
    cos,
    sin,
    gain_a,
    gain_m,
    ids,
    spots,
    src_row,
    xd,
    attn,
    qkv,
    mixed,
    middle,
    moe_all,
    dsum,
    dy,
    slot_cols,
    slot_rows,
    chosen,
    w_att,
    moe,
    slot_given,
    mid16,
    xb,
    cb,
    sems,
    local_sems,
):
    nblk, tokens, width = xb.shape
    half = tokens // 2
    pairs = w_att.shape[1]
    qw = w_att.shape[4] * 2 // 3
    rank = w_att.shape[1] * 2 * w_att.shape[3]
    r = lax.axis_index("row")
    c = lax.axis_index("col")
    z = c // 2
    k = c % 2
    others = [(r, 2 * (z ^ i) + k) for i in range(1, pairs)]
    sibling = (r, c ^ 1)
    greet([(r ^ 1, c), (r ^ 2, c), sibling] + others)

    def cut(ref):
        return lambda h: ref.at[pl.ds(h * half, half)]

    def cut_slot(ref):
        return lambda j, h: ref.at[j, pl.ds(h * half, half)]

    def w_slot(j, h):
        return w_att.at[j, pl.ds(h * (pairs // 2), pairs // 2), k]

    n = RowGather.count
    xs = RowGather(cut(xin), cut_slot(xb), sems, 0, r, c)
    ws = RowGather(lambda h: w_slot(0, h), w_slot, sems, n, r, c)
    cs = RowGather(cut(cot), cut_slot(cb), sems, 2 * n, r, c)
    ms = RowGather(cut(moe), cut_slot(moe_all), sems, 3 * n, r, c)
    across = [
        link(w_own, w_att.at[0, z, k], sems, 4 * n + i, others[i]) for i in range(pairs - 1)
    ]
    base = 4 * n + pairs - 1
    share = [link(w_att.at[j, :, k], w_att.at[j, :, k], sems, base + j, sibling) for j in range(nblk)]
    keep = [
        pltpu.make_async_copy(w_own, w_att.at[0, z, k], local_sems.at[0]),
        pltpu.make_async_copy(xin, xb.at[0], local_sems.at[1]),
        pltpu.make_async_copy(cot, cb.at[0], local_sems.at[2]),
    ]
    for copy in across:
        copy.start()
    xs.start(1)
    xs.start(0)
    for copy in keep:
        copy.start()
    keep[0].wait()
    for copy in across:
        copy.wait_recv()
    ws.start(1)
    ws.start(0)
    share[0].start()
    xs.forward(0)
    xs.forward(1)
    keep[1].wait()

    source = src[:tokens, :]

    def pick(at, j):
        return jnp.where(at == iota((tokens, tokens), 1) + j * tokens, 1.0, 0.0).astype(BF)

    x = mm(pick(source, 0), xb[0])
    xs.wait((1, 0))
    x = x + mm(pick(source, 1), xb[1])
    xs.wait((2, 1))
    x = x + mm(pick(source, 2), xb[2])
    ws.forward(0)
    ws.forward(1)
    ws.wait((1, 0), (2, 1))
    share[1].start()
    share[2].start()
    xs.wait((3, 0), (3, 1))
    x = x + mm(pick(source, 3), xb[3])
    xd[...] = x.astype(BF)
    attn[...] = (x * row_scale(x) * gain_a[...]).astype(BF)
    groups = qw // (4 * HEAD_WIDTH)

    def project(j):
        proj = mm(attn[...], w_att[j, :, :, :, :qw].reshape(rank, qw))
        cos_w = jnp.concatenate([cos[...]] * groups, axis=1)
        sin_w = jnp.concatenate([sin[...]] * groups, axis=1)
        turned = proj * cos_w + swap_halves(proj) * sin_w
        qkv[:, pl.ds(pl.multiple_of(j * qw, qw), qw)] = turned.astype(BF)

    ws.wait((3, 0), (3, 1))
    share[3].start()
    cs.start(1)
    cs.start(0)
    for j in range(nblk):
        share[j].wait_recv()

    @pl.loop(0, nblk)
    def _(j):
        project(j)

    pair = 2 * HEAD_WIDTH
    for b in range(2):
        rows = slice(b * half, (b + 1) * half)
        span = (b + 1) * half

        @pl.loop(0, groups * nblk)
        def _(g):
            chunk = qkv[:span, pl.ds(pl.multiple_of(g * 2 * pair, 2 * pair), 2 * pair)]
            k_rows = chunk[:, pair : pair + HEAD_WIDTH]
            v_rows = chunk[:, pair + HEAD_WIDTH :]
            outs = []
            for h in range(2):
                q = chunk[b * half :, h * HEAD_WIDTH : (h + 1) * HEAD_WIDTH]
                probs = masked_probs(q, k_rows, b * half, starts[rows, :])
                outs.append(mm(probs.astype(BF), v_rows))
            mixed[rows, pl.ds(pl.multiple_of(g * pair, pair), pair)] = jnp.concatenate(
                outs, axis=1
            ).astype(BF)

        if b == 1:
            cs.forward(0)
            cs.forward(1)
            ms.forward(0)
        ow = w_att.shape[4] - qw
        out = jnp.zeros((half, width), F32)
        for j in range(nblk):
            w_out = w_att[j, :, :, :, qw:].reshape(rank, ow)
            out = out + mm_nt(mixed[rows, j * ow : (j + 1) * ow], w_out)
        mid = xd[rows, :].astype(F32) + RESIDUAL_SCALE * out
        middle[rows, :] = mid
        mid16[rows, :] = mid.astype(BF)
        moe[rows, :] = (mid * row_scale(mid) * gain_m[...]).astype(BF)
        ms.start(b)

    place = pltpu.make_async_copy(moe, moe_all.at[0], local_sems.at[3])
    place.start()
    keep[2].wait()
    cs.wait((1, 0), (2, 1), (3, 0), (3, 1))

    def deal_block(b):
        at = pl.ds(pl.multiple_of(b * tokens, tokens), tokens)
        source = src[at, :]
        dealt = mm(pick(source, 0), cb[0])
        for j in range(1, nblk):
            dealt = dealt + mm(pick(source, j), cb[j])
        dsum[at, :] = (RESIDUAL_SCALE * dealt).astype(BF)

        @pl.when(b == 0)
        def _():
            dy[...] = dealt.astype(BF)

        lane = iota((tokens, LANES), 1)
        spot = jnp.zeros((tokens, LANES), F32)
        named = jnp.zeros((tokens, LANES), F32)
        own_ids = ids[at, :]
        own_spots = spots[at, :]
        for i in range(TOPK):
            hit = lane == own_ids[:, i : i + 1]
            named = jnp.where(hit, 1.0, named)
            spot = jnp.where(hit, own_spots[:, i : i + 1].astype(F32), spot)
        chosen[at, :] = named
        slot = jnp.where(named > 0.0, spot, -1.0)
        slot_cols[at, :] = slot
        slot_rows[:, at] = slot.T

    for part in range(2):

        @pl.loop(part * nblk // 2, (part + 1) * nblk // 2)
        def _(b):
            deal_block(b)

        if part == 0:
            ms.forward(1)

    @pl.loop(0, nblk)
    def _(b):
        at = pl.ds(pl.multiple_of(b * tokens, tokens), tokens)
        found = jnp.zeros((tokens, LANES), F32)
        for j in range(nblk):
            part = slice(j * tokens, (j + 1) * tokens)
            match = iota((tokens, tokens), 0) + b * tokens == src_row[:, part]
            match = jnp.where(match, 1.0, 0.0).astype(BF)
            value = slot_cols[part, :] + 1.0
            high = jnp.floor(value * 0.0625)
            low = value - 16.0 * high
            found = found + 16.0 * mm(match, high.astype(BF)) + mm(match, low.astype(BF))
        slot_given[at, :] = found - 1.0

    ms.wait((1, 0), (2, 1), (3, 0), (3, 1))
    place.wait()
    for gather in (xs, ws, cs, ms):
        gather.drain()
    for copy in across + share:
        copy.wait_send()


def front(xin, cot, w_own, src, starts, cos, sin, gain_a, gain_m, ids, spots, src_row, nblk, pairs):
    tokens, width = xin.shape
    shard, both = w_own.shape
    total = nblk * tokens
    qkv_width = nblk * both * 2 // 3
    head_width = nblk * both // 3
    shape = jax.ShapeDtypeStruct
    count = 4 * RowGather.count + pairs - 1 + nblk
    return pl.pallas_call(
        front_kernel,
        out_shape=(
            shape((tokens, width), BF),
            shape((tokens, width), BF),
            shape((tokens, qkv_width), BF),
            shape((tokens, head_width), BF),
            shape((tokens, width), F32),
            shape((nblk, tokens, width), BF),
            shape((total, width), BF),
            shape((tokens, width), BF),
            shape((total, LANES), F32),
            shape((LANES, total), F32),
            shape((total, LANES), F32),
            shape((nblk, pairs, 2, shard, both), BF),
            shape((tokens, width), BF),
            shape((total, LANES), F32),
            shape((tokens, width), BF),
        ),
        in_specs=[ANY] * 3 + [FULL] * 9,
        out_specs=[FULL] * 5 + [ANY] + [FULL] * 9,
        scratch_shapes=[
            pltpu.VMEM((nblk, tokens, width), BF),
            pltpu.VMEM((nblk, tokens, width), BF),
            pltpu.SemaphoreType.DMA((2, count)),
            pltpu.SemaphoreType.DMA((4,)),
        ],
        compiler_params=pltpu.CompilerParams(
            vmem_limit_bytes=58 * MIB, collective_id=1, has_side_effects=True
        ),
        cost_estimate=cost(20e9, 60 * MIB),
        name="attention_forward",
    )(xin, cot, w_own, src, starts, cos, sin, gain_a, gain_m, ids, spots, src_row)


def router_kernel(moe, w_router, chosen, gates, packed):
    nblk, tokens, _ = moe.shape
    local = EXPERT_COUNT // nblk
    for j in range(nblk):
        at = slice(j * tokens, (j + 1) * tokens)
        logits = mm(moe[j], w_router[...])
        named = chosen[at, :] > 0.0
        logits = jnp.where(named, logits, MASKED)
        top = jnp.max(logits, axis=-1, keepdims=True)
        raised = jnp.where(named, jnp.exp(logits - top), 0.0)
        gate = raised / jnp.sum(raised, axis=-1, keepdims=True)
        gates[at, :] = gate
        lane = iota((tokens, LANES), 1)
        own = jnp.where(lane < local, gate, 0.0)
        high = own.astype(BF).astype(F32)
        rest = own - high
        mid = rest.astype(BF).astype(F32)
        low = rest - mid
        packed[at, :] = (high + pltpu.roll(mid, local, 1) + pltpu.roll(low, 2 * local, 1)).astype(BF)


def router(moe, w_router, chosen):
    nblk, tokens, _ = moe.shape
    total = nblk * tokens
    shape = jax.ShapeDtypeStruct
    return pl.pallas_call(
        router_kernel,
        out_shape=(shape((total, LANES), F32), shape((total, LANES), BF)),
        in_specs=[FULL] * 3,
        out_specs=[FULL] * 2,
        compiler_params=params(24),
        cost_estimate=cost(1e9, 7 * MIB),
        name="router",
    )(moe, w_router, chosen)


def expert_kernel(base, first, last, local, capacity, *refs):
    moe_hbm = refs[0]
    refs = refs[1:]
    if first:
        (dsum_hbm, slot_rows, slot_cols, slot_given, packed, w) = refs[:6]
        refs = refs[6:]
    else:
        (dsum_hbm, slot_rows, slot_cols, slot_given, packed, w, acc_in, accg_in) = refs[:8]
        refs = refs[8:]
    if last:
        (grads, es_out, dm_out, dgates) = refs[:4]
        refs = refs[4:]
    else:
        (grads, acc_out, accg_out) = refs[:3]
        refs = refs[3:]
    (moe, dsum, acc, accg, sel, selt, routed, dsl, dslot, y1, y2, sems) = refs
    step = pl.program_id(0)
    steps = pl.num_programs(0)
    e = base + step
    nblk, tokens, width = moe_hbm.shape
    total = nblk * tokens
    fe = w.shape[4]
    shard = w.shape[3]
    tile = 256
    tiles = width // tile
    copies = []
    for j in range(nblk):
        copies.append(
            pltpu.make_async_copy(moe_hbm.at[j], moe.at[pl.ds(j * tokens, tokens)], sems.at[j])
        )
    copies.append(pltpu.make_async_copy(dsum_hbm, dsum, sems.at[nblk]))
    loads = []
    if not first:
        loads.append(pltpu.make_async_copy(acc_in, acc, sems.at[nblk + 1]))
        loads.append(pltpu.make_async_copy(accg_in, accg, sems.at[nblk + 2]))

    @pl.when(step == 0)
    def _():
        for c in copies:
            c.start()
        for c in loads:
            c.start()
        if first:
            acc[...] = jnp.zeros(acc.shape, F32)
            accg[...] = jnp.zeros(accg.shape, F32)

    row = slot_rows[pl.ds(e, 1), :]
    lanes = iota((tokens, LANES), 1)
    for j in range(nblk):
        at = slice(j * tokens, (j + 1) * tokens)
        sel[:, at] = jnp.where(
            iota((capacity, tokens), 0).astype(F32) == row[:, at], 1.0, 0.0
        ).astype(BF)
        col = jnp.sum(jnp.where(lanes == e, slot_cols[at, :], 0.0), axis=1, keepdims=True)
        selt[at, :] = jnp.where(
            col == iota((tokens, capacity), 1).astype(F32), 1.0, 0.0
        ).astype(BF)

    @pl.when(step == 0)
    def _():
        for c in copies:
            c.wait()

    def dispatch(n, carry):
        at = pl.ds(pl.multiple_of(n * tile, tile), tile)
        routed[:, at] = mm(sel[...], moe[:, at]).astype(BF)
        dsl[:, at] = mm(sel[...], dsum[:, at]).astype(BF)
        return carry

    lax.fori_loop(0, tiles, dispatch, 0)
    lane = iota((capacity, LANES), 1)
    picked = mm(sel[...], packed[...])
    mine = (lane == e) | (lane == e + local) | (lane == e + 2 * local)
    gate = jnp.sum(jnp.where(mine, picked, 0.0), axis=1, keepdims=True)
    dslot[...] = (gate * dsl[...].astype(F32)).astype(BF)

    def weight(i):
        return w[:, 0, i].reshape(width, fe)

    per = tile // shard

    def weight_tile(i, n):
        return w[pl.ds(n * per, per), 0, i].reshape(tile, fe)

    gate_in = mm(routed[...], weight(0))
    up_in = mm(routed[...], weight(1))
    sig = jax.nn.sigmoid(gate_in)
    silu = gate_in * sig
    hidden = (silu * up_in).astype(BF)

    def down(n, inner):
        at = pl.ds(pl.multiple_of(n * tile, tile), tile)
        out = mm_nt(hidden, weight_tile(2, n))
        y1[:, at] = (gate * out).astype(BF)
        return inner + jnp.sum(dsl[:, at].astype(F32) * out, axis=1, keepdims=True)

    inner = lax.fori_loop(0, tiles, down, jnp.zeros((capacity, 1), F32))
    high = inner.astype(BF).astype(F32)
    rest = inner - high
    mid = rest.astype(BF).astype(F32)
    low = rest - mid
    spread = jnp.where(
        lane == e,
        high,
        jnp.where(lane == e + local, mid, jnp.where(lane == e + 2 * local, low, 0.0)),
    ).astype(BF)
    dhidden = mm(dslot[...], weight(2))
    dgate = (dhidden * up_in * sig * (1.0 + gate_in * (1.0 - sig))).astype(BF)
    dup = (dhidden * silu).astype(BF)

    def back(n, carry):
        at = pl.ds(pl.multiple_of(n * tile, tile), tile)
        devs = pl.ds(n * per, per)
        grads[devs, 0, 2] = mm_tn(dslot[:, at], hidden).astype(BF).reshape(per, shard, fe)
        rows = routed[:, at]
        grads[devs, 0, 0] = mm_tn(rows, dgate).astype(BF).reshape(per, shard, fe)
        grads[devs, 0, 1] = mm_tn(rows, dup).astype(BF).reshape(per, shard, fe)
        y2[:, at] = (mm_nt(dgate, weight_tile(0, n)) + mm_nt(dup, weight_tile(1, n))).astype(BF)
        return carry

    lax.fori_loop(0, tiles, back, 0)

    if not first:

        @pl.when(step == 0)
        def _():
            for c in loads:
                c.wait()

    def combine(b, carry):
        at = pl.ds(pl.multiple_of(b * tokens, tokens), tokens)
        chosen = selt[at, :]
        acc[1, at, :] += mm(chosen, y2[...])
        accg[at, :] += mm(chosen, spread)
        col = jnp.sum(jnp.where(lanes == e, slot_given[at, :], 0.0), axis=1, keepdims=True)
        given = jnp.where(col == iota((tokens, capacity), 1).astype(F32), 1.0, 0.0).astype(BF)
        acc[0, at, :] += mm(given, y1[...])
        return carry

    lax.fori_loop(0, nblk, combine, 0)

    @pl.when(step == steps - 1)
    def _():
        if last:
            moe[...] = acc[0].astype(BF)
            dsum[...] = acc[1].astype(BF)
            summed = accg[...]
            summed = (
                summed
                + pltpu.roll(summed, LANES - local, 1)
                + pltpu.roll(summed, LANES - 2 * local, 1)
            )
            dgates[...] = summed.T[:local, :]
            outs = []
            for j in range(nblk):
                part = pl.ds(j * tokens, tokens)
                outs.append(pltpu.make_async_copy(moe.at[part], es_out.at[j], sems.at[2 * j]))
                outs.append(pltpu.make_async_copy(dsum.at[part], dm_out.at[j], sems.at[2 * j + 1]))
        else:
            outs = [
                pltpu.make_async_copy(acc, acc_out, sems.at[0]),
                pltpu.make_async_copy(accg, accg_out, sems.at[1]),
            ]
        for c in outs:
            c.start()
        for c in outs:
            c.wait()


def experts(moe, dsum, slot_rows, slot_cols, slot_given, packed, w, carried, base, last, capacity):
    nblk, tokens, width = moe.shape
    total = nblk * tokens
    cols, ne, three, shard, fe = w.shape
    local = EXPERT_COUNT // nblk
    first = carried is None
    shape = jax.ShapeDtypeStruct
    wspec = pl.BlockSpec((cols, 1, three, shard, fe), lambda s: (0, s, 0, 0, 0))
    ins = [moe, dsum, slot_rows, slot_cols, slot_given, packed, w]
    in_specs = [ANY] * 2 + [FULL, FULL, FULL, FULL, wspec]
    aliases = {}
    if not first:
        ins += list(carried)
        in_specs += [ANY, ANY]
        aliases = {} if last else {len(ins) - 2: 1, len(ins) - 1: 2}
    if last:
        blocks = shape((nblk, tokens, width), BF)
        outs = (blocks, blocks, shape((local, total), F32))
        out_specs = [wspec, ANY, ANY, FULL]
    else:
        outs = (shape((2, total, width), F32), shape((total, LANES), F32))
        out_specs = [wspec, ANY, ANY]
    return pl.pallas_call(
        functools.partial(expert_kernel, base, first, last, local, capacity),
        grid=(ne,),
        out_shape=(shape(w.shape, BF), *outs),
        in_specs=in_specs,
        out_specs=out_specs,
        scratch_shapes=[
            pltpu.VMEM((total, width), BF),
            pltpu.VMEM((total, width), BF),
            pltpu.VMEM((2, total, width), F32),
            pltpu.VMEM((total, LANES), F32),
            pltpu.VMEM((capacity, total), BF),
            pltpu.VMEM((total, capacity), BF),
            pltpu.VMEM((capacity, width), BF),
            pltpu.VMEM((capacity, width), BF),
            pltpu.VMEM((capacity, width), BF),
            pltpu.VMEM((capacity, width), BF),
            pltpu.VMEM((capacity, width), BF),
            pltpu.SemaphoreType.DMA((2 * nblk,)),
        ],
        input_output_aliases=aliases,
        compiler_params=params(60),
        cost_estimate=cost(14e9 * ne, 40 * MIB),
        name="experts",
    )(*ins)


class RowScatter:
    count = 6

    def __init__(self, block, mixed_in, across, landed, sems, base, r, c):
        near, far = (r ^ 1, c), (r ^ 2, c)
        self.copies = {
            "diag0": link(block(3, 0), across(0), sems, base, near),
            "diag1": link(block(3, 1), across(1), sems, base + 1, far),
            "near0": link(block(1, 0), landed(1, 0), sems, base + 2, near),
            "far1": link(block(2, 1), landed(2, 1), sems, base + 3, far),
            "far0": link(mixed_in(0), landed(2, 0), sems, base + 4, far),
            "near1": link(mixed_in(1), landed(1, 1), sems, base + 5, near),
        }

    def start(self):
        for key in ("diag0", "diag1", "near0", "far1"):
            self.copies[key].start()

    def arrived(self, half):
        self.copies["diag0" if half == 0 else "diag1"].wait_recv()

    def send(self, half):
        self.copies["far0" if half == 0 else "near1"].start()

    def finish(self):
        for key in ("near0", "far1", "far0", "near1"):
            self.copies[key].wait_recv()

    def drain(self):
        for copy in self.copies.values():
            copy.wait_send()


def tree_sum(parts):
    while len(parts) > 1:
        parts = [parts[i] + parts[i + 1] for i in range(0, len(parts), 2)]
    return parts[0]


def plus(a, b):
    return (a.astype(F32) + b.astype(F32)).astype(BF)


def back_kernel(nblk, *refs):
    dm, es, dgates = refs[:3]
    mids = refs[3 : 3 + nblk]
    refs = refs[3 + nblk :]
    (gates, middle, moe, dy, mixed, qkv, attn, xd, w_att, w_router) = refs[:10]
    (starts, cos, sin, gain_a, gain_m, src_row) = refs[10:16]
    (block_out, input_grad, att_grad, small, e_across, e_landed) = refs[16:22]
    (own, d_across, d_landed, dg_land, e_mix, e_load, igb, dmid, dmix, dproj, dkv, wg, wg_sib) = refs[22:35]
    (w_across, w_landed, w_z, rowsum, s_own, s_sib, s_sum, s_row, s_chip, s_z, sems, lsems) = refs[35:]
    tokens, width = xd.shape
    half = tokens // 2
    local = EXPERT_COUNT // nblk
    pairs = w_att.shape[1]
    shard = w_att.shape[3]
    qw = w_att.shape[4] * 2 // 3
    ow = w_att.shape[4] - qw
    hw = HEAD_WIDTH
    r = lax.axis_index("row")
    c = lax.axis_index("col")
    z = c // 2
    k = c % 2
    row_peers = [(r ^ j, c) for j in range(1, nblk)]
    z_peers = [(r, 2 * (z ^ i) + k) for i in range(1, pairs)]
    sibling = (r, c ^ 1)
    greet(row_peers + z_peers + [sibling])

    def part(h):
        return pl.ds(h * half, half)

    zhalf = pairs // 2

    def zpart(h):
        return pl.ds(h * zhalf, zhalf)

    n = RowScatter.count
    dms = RowScatter(
        lambda j, h: dm.at[j, part(h)],
        lambda h: own.at[2 - h, part(h)],
        lambda h: d_across.at[h],
        lambda j, h: d_landed.at[j - 1, part(h)],
        sems,
        0,
        r,
        c,
    )
    ess = RowScatter(
        lambda j, h: es.at[j, part(h)],
        lambda h: e_mix.at[h],
        lambda h: e_across.at[h],
        lambda j, h: e_landed.at[j - 1, part(h)],
        sems,
        n,
        r,
        c,
    )
    wgs = RowScatter(
        lambda j, h: wg.at[j, zpart(h), k],
        lambda h: wg.at[2 - h, zpart(h), k],
        lambda h: w_across.at[h],
        lambda j, h: w_landed.at[j - 1, zpart(h)],
        sems,
        2 * n,
        r,
        c,
    )
    igs = RowGather(
        lambda h: igb.at[0, part(h)], lambda j, h: igb.at[j, part(h)], sems, 3 * n, r, c
    )
    at = 3 * n + RowGather.count
    dgs = [
        link(dgates.at[:, pl.ds(j * tokens, tokens)], dg_land.at[j - 1], sems, at + j - 1, (r ^ j, c))
        for j in range(1, nblk)
    ]
    at += nblk - 1
    wg_share = [
        link(wg.at[j, :, 1 - k], wg_sib.at[j], sems, at + j, sibling) for j in range(nblk)
    ]
    at += nblk
    wg_z = [
        link(rowsum.at[z ^ i], w_z.at[i - 1], sems, at + i - 1, z_peers[i - 1])
        for i in range(1, pairs)
    ]
    at += pairs - 1
    s_share = link(s_own, s_sib, sems, at, sibling)
    s_rows = [link(s_sum, s_row.at[j], sems, at + 1 + j, row_peers[j]) for j in range(nblk - 1)]
    at += nblk
    s_zs = [link(s_chip, s_z.at[i], sems, at + i, z_peers[i]) for i in range(pairs - 1)]

    dms.start()
    for copy in dgs:
        copy.start()
    loads = [
        pltpu.make_async_copy(dm.at[0], own.at[0], lsems.at[0]),
        pltpu.make_async_copy(dm.at[1, part(1)], own.at[1, part(1)], lsems.at[1]),
        pltpu.make_async_copy(dm.at[2, part(0)], own.at[2, part(0)], lsems.at[2]),
        pltpu.make_async_copy(middle, dmid, lsems.at[3]),
    ]
    for copy in loads:
        copy.start()

    def match(j):
        hit = iota((tokens, tokens), 0) == src_row[:, j * tokens : (j + 1) * tokens]
        return jnp.where(hit, 1.0, 0.0).astype(BF)

    total = jnp.zeros((tokens, width), F32)
    for j in range(nblk):
        get = pltpu.make_async_copy(mids[j], dmix, lsems.at[4])
        get.start()
        hit = match(j)
        get.wait()
        total = total + mm(hit, dmix[...])
    input_grad[...] = total
    for copy in loads:
        copy.wait()
    for h in range(2):
        dms.arrived(h)
        rows = part(h)
        own[2 - h, rows, :] = plus(own[2 - h, rows, :], d_across[h])
        dms.send(h)

    for copy in dgs:
        copy.wait_recv()
    parts = [dgates[:, :tokens]] + [dg_land[j] for j in range(nblk - 1)]
    pad = jnp.zeros((LANES - EXPERT_COUNT, tokens), F32)
    dgate = jnp.concatenate(parts + [pad], axis=0).T
    gate = gates[...]
    dchosen = gate * (dgate - jnp.sum(gate * dgate, axis=1, keepdims=True))
    dlogits = dchosen.astype(BF)
    router_t = mm_tn(dlogits, moe[...])
    for j in range(nblk):
        s_own[pl.ds(pl.multiple_of((r ^ j) * local, local), local), :] = router_t[
            j * local : (j + 1) * local, :
        ]
    dmoe = mm_nt(dlogits, w_router[...]) + own[0].astype(F32)
    dms.finish()
    ess.start()
    dmoe = dmoe + (d_landed[0].astype(F32) + d_landed[1].astype(F32))
    mid = dmid[...]
    rr = row_scale(mid)
    scaled = dmoe * gain_m[...]
    inner = jnp.mean(scaled * mid, axis=-1, keepdims=True)
    gain_m_part = jnp.sum(dmoe * mid * rr, axis=0, keepdims=True)
    dmid[...] = dy[...].astype(F32) + (rr * scaled - mid * (rr * rr * rr) * inner)
    dattn = (RESIDUAL_SCALE * dmid[...]).astype(BF)
    for j in range(nblk):
        cols = slice(j * ow, (j + 1) * ow)
        dmix[:, cols] = mm(dattn, w_att[j, :, :, :, qw:].reshape(width, ow)).astype(BF)
        wg[j, :, :, :, qw:] = (
            mm_tn(dattn, mixed[:, cols]).astype(BF).reshape(pairs, 2, shard, ow)
        )

    quad = 4 * hw
    groups = nblk * qw // quad
    gain_a_part = jnp.zeros((1, width), F32)
    e_loads = [
        pltpu.make_async_copy(es.at[2, part(0)], e_mix.at[0], lsems.at[5]),
        pltpu.make_async_copy(es.at[1, part(1)], e_mix.at[1], lsems.at[6]),
    ]
    for copy in e_loads:
        copy.start()
    for b in (1, 0):
        span = (b + 1) * half
        rows = slice(b * half, (b + 1) * half)

        @pl.loop(0, groups)
        def _(g):
            chunk = qkv[:span, pl.ds(pl.multiple_of(g * quad, quad), quad)]
            dm_chunk = dmix[rows, pl.ds(pl.multiple_of(g * 2 * hw, 2 * hw), 2 * hw)]
            k_rows = chunk[:, 2 * hw : 3 * hw]
            v_rows = chunk[:, 3 * hw :]
            dk = jnp.zeros((span, hw), F32)
            dv = jnp.zeros((span, hw), F32)
            dqs = []
            for h in range(2):
                q = chunk[b * half :, h * hw : (h + 1) * hw]
                dmh = dm_chunk[:, h * hw : (h + 1) * hw]
                probs = masked_probs(q, k_rows, b * half, starts[rows, :])
                dprobs = mm_nt(dmh, v_rows)
                total = jnp.sum(probs * dprobs, axis=-1, keepdims=True)
                dscores = (probs * (dprobs - total) * SCORE_SCALE).astype(BF)
                dqs.append(mm(dscores, k_rows))
                dk = dk + mm_tn(dscores, q)
                dv = dv + mm_tn(probs.astype(BF), dmh)
            dkv_new = jnp.concatenate([dk, dv], axis=1)
            pair = pl.ds(pl.multiple_of(g * 2 * hw, 2 * hw), 2 * hw)
            if b == 1:
                dkv[:, pair] = dkv_new[:half]
                dkv_own = dkv_new[half:]
            else:
                dkv_own = dkv_new + dkv[:, pair]
            d = jnp.concatenate(dqs + [dkv_own], axis=1)
            d = d * cos[rows, :] - swap_halves(d) * sin[rows, :]
            dproj[rows, pl.ds(pl.multiple_of(g * quad, quad), quad)] = d.astype(BF)

        dattn_in = jnp.zeros((half, width), F32)
        for j in range(nblk):
            dattn_in = dattn_in + mm_nt(
                dproj[rows, j * qw : (j + 1) * qw],
                w_att[j, :, :, :, :qw].reshape(width, qw),
            )
        x = xd[rows, :].astype(F32)
        rx = row_scale(x)
        scaled = dattn_in * gain_a[...]
        inner = jnp.mean(scaled * x, axis=-1, keepdims=True)
        igb[0, rows, :] = (dmid[rows, :] + (rx * scaled - x * (rx * rx * rx) * inner)).astype(BF)
        gain_a_part = gain_a_part + jnp.sum(dattn_in * x * rx, axis=0, keepdims=True)
        igs.start(b)
        if b == 1:
            for h in range(2):
                ess.arrived(h)
                get = pltpu.make_async_copy(e_across.at[h], e_load, lsems.at[7])
                get.start()
                get.wait()
                e_loads[h].wait()
                e_mix[h] = plus(e_mix[h], e_load[...])
                ess.send(h)

    s_own[EXPERT_COUNT : EXPERT_COUNT + 8, :] = jnp.concatenate(
        [gain_a_part, gain_m_part, jnp.zeros((6, width), F32)], axis=0
    )
    s_share.start()
    for j in range(nblk):
        wg[j, :, :, :, :qw] = (
            mm_tn(attn[...], dproj[:, j * qw : (j + 1) * qw])
            .astype(BF)
            .reshape(pairs, 2, shard, qw)
        )
        wg_share[j].start()
    igs.forward(1)
    igs.forward(0)
    s_share.wait_recv()
    s_sum[...] = s_own[...] + s_sib[...]
    for copy in s_rows:
        copy.start()
    for j in (3, 1, 2, 0):
        wg_share[j].wait_recv()
        wg[j, :, pl.ds(k, 1)] = plus(wg[j, :, pl.ds(k, 1)], wg_sib[j][:, None])
    wgs.start()

    ess.finish()
    e_gets = [
        pltpu.make_async_copy(es.at[0], own.at[0], lsems.at[0]),
        pltpu.make_async_copy(e_landed.at[0], own.at[1], lsems.at[1]),
        pltpu.make_async_copy(e_landed.at[1], own.at[2], lsems.at[2]),
    ]
    dms.drain()
    for copy in e_gets:
        copy.start()
    for copy in e_gets:
        copy.wait()
    summed = own[0].astype(F32) + (own[1].astype(F32) + own[2].astype(F32))
    block_out[...] = (input_grad[...] + RESIDUAL_SCALE * summed).astype(BF)

    for h in range(2):
        wgs.arrived(h)
        hz = zpart(h)
        wg[2 - h, hz, pl.ds(k, 1)] = plus(wg[2 - h, hz, pl.ds(k, 1)], w_across[h][:, None])
        wgs.send(h)
    for copy in s_rows:
        copy.wait_recv()
    s_chip[...] = tree_sum([s_sum[...]] + [s_row[j] for j in range(nblk - 1)])
    for copy in s_zs:
        copy.start()
    igs.wait((1, 0), (2, 1))
    total = mm(match(0), igb[0])
    for j in (1, 2):
        total = total + mm(match(j), igb[j])
    igs.wait((3, 0), (3, 1))
    total = total + mm(match(3), igb[3])
    input_grad[...] = total
    wgs.finish()
    rowsum[...] = (
        wg[0, :, pl.ds(k, 1)].reshape(rowsum.shape).astype(F32)
        + (w_landed[0].astype(F32) + w_landed[1].astype(F32))
    ).astype(BF)
    for copy in wg_z:
        copy.start()
    for copy in s_zs:
        copy.wait_recv()
    small[...] = tree_sum([s_chip[...]] + [s_z[i] for i in range(pairs - 1)])
    for copy in wg_z:
        copy.wait_recv()
    att_grad[...] = tree_sum(
        [rowsum[pl.ds(z, 1)].reshape(att_grad.shape).astype(F32)]
        + [w_z[i].astype(F32) for i in range(pairs - 1)]
    )
    for group in (ess, wgs, igs):
        group.drain()
    for copy in dgs + wg_share + wg_z + [s_share] + s_rows + s_zs:
        copy.wait_send()


def backward(dm, es, dgates, mids, *rest):
    nblk, tokens, width = dm.shape
    w_att = rest[8]
    pairs, shard, both = w_att.shape[1], w_att.shape[3], w_att.shape[4]
    half = tokens // 2
    local = EXPERT_COUNT // nblk
    shape = jax.ShapeDtypeStruct
    count = (
        3 * RowScatter.count
        + RowGather.count
        + (nblk - 1)
        + nblk
        + (pairs - 1)
        + 1
        + (nblk - 1)
        + (pairs - 1)
    )
    small = (EXPERT_COUNT + 8, width)
    outs = pl.pallas_call(
        functools.partial(back_kernel, nblk),
        out_shape=(
            shape((tokens, width), BF),
            shape((tokens, width), F32),
            shape((shard, both), F32),
            shape(small, F32),
            shape((2, half, width), BF),
            shape((2, tokens, width), BF),
        ),
        in_specs=[ANY] * 2 + [FULL] + [ANY] * nblk + [FULL, ANY] + [FULL] * 14,
        out_specs=[FULL] * 4 + [ANY] * 2,
        scratch_shapes=[
            pltpu.VMEM((3, tokens, width), BF),
            pltpu.VMEM((2, half, width), BF),
            pltpu.VMEM((2, tokens, width), BF),
            pltpu.VMEM((nblk - 1, local, tokens), F32),
            pltpu.VMEM((2, half, width), BF),
            pltpu.VMEM((half, width), BF),
            pltpu.VMEM((nblk, tokens, width), BF),
            pltpu.VMEM((tokens, width), F32),
            pltpu.VMEM((tokens, width), BF),
            pltpu.VMEM((tokens, 2 * width), BF),
            pltpu.VMEM((half, width), F32),
            pltpu.VMEM(w_att.shape, BF),
            pltpu.VMEM((nblk, pairs, shard, both), BF),
            pltpu.VMEM((2, pairs // 2, shard, both), BF),
            pltpu.VMEM((2, pairs, shard, both), BF),
            pltpu.VMEM((pairs - 1, shard, both), BF),
            pltpu.VMEM((pairs, shard, both), BF),
            pltpu.VMEM(small, F32),
            pltpu.VMEM(small, F32),
            pltpu.VMEM(small, F32),
            pltpu.VMEM((nblk - 1, *small), F32),
            pltpu.VMEM(small, F32),
            pltpu.VMEM((pairs - 1, *small), F32),
            pltpu.SemaphoreType.DMA((2, count)),
            pltpu.SemaphoreType.DMA((8,)),
        ],
        compiler_params=pltpu.CompilerParams(
            vmem_limit_bytes=62 * MIB, collective_id=2, has_side_effects=True
        ),
        cost_estimate=cost(60e9, 100 * MIB),
        name="attention_backward",
    )(dm, es, dgates, *mids, *rest)
    return outs[:4]


def swap_over(value, axis, size, step):
    return lax.ppermute(value, axis, [(i, i ^ step) for i in range(size)])


def spread_rows(value, axis, size, step=1):
    return [value] + [swap_over(value, axis, size, j) for j in range(step, size, step)]


def body(
    block_in,
    cotangent,
    seq_lengths,
    seq_order,
    expert_ids,
    places,
    attn_gain,
    w_qkv,
    w_out,
    moe_gain,
    w_router,
    w_gate,
    w_up,
    w_down,
):
    tokens = block_in.shape[1]
    width = block_in.shape[2]
    rows = lax.axis_size("row")
    cols = lax.axis_size("col")
    total = tokens * rows
    r = lax.axis_index("row")
    c = lax.axis_index("col")
    parity = c % 2
    local = w_gate.shape[1]
    shard = w_gate.shape[0]
    fe = w_gate.shape[2]
    capacity = total * TOPK // EXPERT_COUNT
    pairs = cols // 2
    qw = w_qkv.shape[1]
    ow = w_out.shape[1]

    stacked = jnp.stack([w_gate, w_up, w_down]).transpose(2, 0, 1, 3)
    chunk = 2
    gathered = [
        lax.all_gather(stacked[i : i + chunk], "col", axis=0) for i in range(0, local, chunk)
    ]

    w_own = jnp.concatenate([w_qkv, w_out], axis=1)
    base = c // 2

    def join_parity(mine, other, axis):
        even = jnp.where(parity == 0, mine, other)
        odd = jnp.where(parity == 0, other, mine)
        both = jnp.stack([even, odd], axis=axis + 1)
        return jnp.concatenate(
            [lax.dynamic_slice_in_dim(both, base ^ i, 1, axis) for i in range(pairs)], axis=axis
        )

    lengths = seq_lengths[0]
    perm = seq_order[0]
    seq_ids = jnp.arange(lengths.shape[0], dtype=jnp.int32)
    picked = perm[:, None] == seq_ids[None, :]
    dealt_len = jnp.sum(jnp.where(picked, lengths[None, :], 0), axis=1)
    before = seq_ids[None, :] < perm[:, None]
    source_base = jnp.sum(jnp.where(before, lengths[None, :], 0), axis=1)
    upto = seq_ids[None, :] <= seq_ids[:, None]
    seq_ends = jnp.sum(jnp.where(upto, dealt_len[None, :], 0), axis=1)
    dealt_start = seq_ends - dealt_len
    turn = r * tokens
    pos = jnp.arange(total, dtype=jnp.int32) ^ turn
    inside = (pos[:, None] >= dealt_start[None, :]) & (pos[:, None] < seq_ends[None, :])
    seq_starts = jnp.sum(jnp.where(inside, dealt_start[None, :], 0), axis=1)
    offset = pos - seq_starts
    source = jnp.sum(jnp.where(inside, source_base[None, :], 0), axis=1) + offset
    source = source ^ turn
    src_col = source[:, None]
    src_row = source[None, :]
    own_offset = offset[:tokens]
    own_starts = (seq_starts[:tokens] - turn)[:, None]

    half = HEAD_WIDTH // 2
    frequency = ROPE_BASE ** (-jnp.arange(half, dtype=F32) * 2.0 / HEAD_WIDTH)
    turned = own_offset.astype(F32)[:, None] * frequency[None, :]
    cosine, sine = jnp.cos(turned), jnp.sin(turned)
    ones, zeros = jnp.ones_like(cosine), jnp.zeros_like(cosine)
    cos_w = jnp.concatenate([cosine] * 6 + [ones] * 2, axis=1)
    sin_w = jnp.concatenate([-sine, sine] * 3 + [zeros] * 2, axis=1)

    gain_a = attn_gain[None, :]
    gain_m = moe_gain[None, :]
    def by_block(table):
        blocks = table.reshape(rows, tokens, TOPK)
        return jnp.concatenate(
            [lax.dynamic_slice_in_dim(blocks, r ^ j, 1, 0) for j in range(rows)], axis=0
        ).reshape(total, TOPK)

    ids = by_block(expert_ids[0])
    spots = by_block(places[0])
    ids = ((ids // local) ^ r) * local + ids % local
    spots = jnp.where(spots < capacity, spots, -1)
    (xd, attn, qkv, mixed, middle, moe, dsum, dy, slot_cols, slot_rows, chosen, w_att, moe_own, slot_given, mid16) = front(
        block_in[0],
        cotangent[0],
        w_own,
        src_col,
        own_starts,
        cos_w,
        sin_w,
        gain_a,
        gain_m,
        ids,
        spots,
        src_row,
        rows,
        pairs,
    )

    router_half = jnp.stack(spread_rows(w_router, "col", cols, 2))
    router_full = join_parity(router_half, swap_over(router_half, "col", cols, 1), 0)
    router_blocks = router_full.reshape(width, rows, local)
    router_x = jnp.concatenate(
        [lax.dynamic_slice_in_dim(router_blocks, r ^ j, 1, 1) for j in range(rows)], axis=1
    ).reshape(width, EXPERT_COUNT)
    router_x = jnp.pad(router_x, ((0, 0), (0, LANES - EXPERT_COUNT)))
    gates, packed = router(moe, router_x, chosen)

    mids = spread_rows(mid16, "row", rows)
    carried = None
    summed = []
    for i, w in enumerate(gathered):
        last = i == len(gathered) - 1
        if i == 2:
            w, *mids = lax.optimization_barrier((w, *mids))
        grads, *carried = experts(
            moe,
            dsum,
            slot_rows,
            slot_cols,
            slot_given,
            packed,
            w,
            carried,
            i * chunk,
            last,
            capacity,
        )
        summed.append(lax.psum_scatter(grads, "col", scatter_dimension=0, tiled=False))
    es, dm, dgates = carried
    dgates = lax.optimization_barrier((dgates, summed[0], summed[1]))[0]
    block_out, input_grad, att_grad, small = backward(
        dm,
        es,
        dgates,
        mids,
        gates[:tokens],
        middle,
        moe_own,
        dy,
        mixed,
        qkv,
        attn,
        xd,
        w_att,
        router_x,
        own_starts,
        cos_w,
        sin_w,
        gain_a,
        gain_m,
        src_row,
    )
    router_all = small[:EXPERT_COUNT].T
    router_grad = lax.dynamic_slice_in_dim(router_all, c * shard, shard, 0)
    grads = jnp.concatenate(summed, axis=0).astype(F32).transpose(1, 2, 0, 3)
    return (
        block_out[None],
        input_grad[None],
        small[EXPERT_COUNT],
        att_grad[:, :qw],
        att_grad[:, qw:],
        small[EXPERT_COUNT + 1],
        router_grad,
        grads[0],
        grads[1],
        grads[2],
    )


def solution(mesh):
    tokens = P("col", "row", None)
    weight = P("col", "row")
    expert = P("col", "row", None)
    return jax.shard_map(
        body,
        mesh=mesh,
        in_specs=(
            tokens,
            tokens,
            P("col", None),
            P("col", None),
            P("col", None, None),
            P("col", None, None),
            P(),
            weight,
            weight,
            P(),
            P("col", None),
            expert,
            expert,
            expert,
        ),
        out_specs=(
            tokens,
            tokens,
            P(),
            weight,
            weight,
            P(),
            P("col", None),
            expert,
            expert,
            expert,
        ),
        check_vma=False,
    )
```

```python
import functools

import jax
import jax.numpy as jnp
from jax import lax
from jax.experimental import pallas as pl
from jax.experimental.pallas import tpu as pltpu
from jax.sharding import PartitionSpec as P

HEAD_WIDTH = 64
QUERY_HEADS = 16
KEY_VALUE_HEADS = 8
EXPERT_COUNT = 32
TOPK = 8
EPSILON = 1e-06
RESIDUAL_SCALE = 0.22
SCORE_SCALE = 0.015625
ROPE_BASE = 10000.0
MASKED = -1e30
LANES = 128
MIB = 1024 * 1024
BF = jnp.bfloat16
F32 = jnp.float32
ANY = pl.BlockSpec(memory_space=pl.ANY)
FULL = pl.BlockSpec(memory_space=pltpu.VMEM)


def mm(a, b):
    return lax.dot_general(a, b, (((1,), (0,)), ((), ())), preferred_element_type=F32)


def mm_nt(a, b):
    return lax.dot_general(a, b, (((1,), (1,)), ((), ())), preferred_element_type=F32)


def mm_tn(a, b):
    return lax.dot_general(a, b, (((0,), (0,)), ((), ())), preferred_element_type=F32)


def iota(shape, dim):
    return lax.broadcasted_iota(jnp.int32, shape, dim)


def params(mib):
    return pltpu.CompilerParams(vmem_limit_bytes=mib * MIB)


def cost(flops, moved):
    return pl.CostEstimate(flops=int(flops), bytes_accessed=int(moved), transcendentals=0)


def row_scale(values):
    return lax.rsqrt(jnp.mean(values * values, axis=-1, keepdims=True) + EPSILON)


def swap_halves(values):
    width = values.shape[-1]
    half = HEAD_WIDTH // 2
    low = (iota(values.shape, 1) % HEAD_WIDTH) < half
    ahead = pltpu.roll(values, width - half, 1)
    behind = pltpu.roll(values, half, 1)
    return jnp.where(low, ahead, behind)


def attention_bias(row0, rows, cols, starts):
    at = iota((rows, cols), 1)
    allowed = (at <= iota((rows, cols), 0) + row0) & (at >= starts)
    return jnp.where(allowed, 0.0, MASKED)


def masked_probs(q, k, bias):
    scores = mm_nt(q, k) + bias
    raised = jnp.exp(scores - jnp.max(scores, axis=-1, keepdims=True))
    return raised * (1.0 / jnp.sum(raised, axis=-1, keepdims=True))


def link(src, dst, sems, index, device):
    return pltpu.make_async_remote_copy(
        src_ref=src,
        dst_ref=dst,
        send_sem=sems.at[0, index],
        recv_sem=sems.at[1, index],
        device_id=device,
        device_id_type=pl.DeviceIdType.MESH,
    )


def greet(devices):
    barrier = pltpu.get_barrier_semaphore()
    for device in devices:
        pl.semaphore_signal(barrier, inc=1, device_id=device, device_id_type=pl.DeviceIdType.MESH)
    pl.semaphore_wait(barrier, len(devices))


class RowGather:
    count = 6

    def __init__(self, own, slot, sems, base, r, c):
        near, far = (r ^ 1, c), (r ^ 2, c)
        self.copies = {
            (1, 1): link(own(1), slot(1, 1), sems, base, near),
            (2, 0): link(own(0), slot(2, 0), sems, base + 1, far),
            (1, 0): link(own(0), slot(1, 0), sems, base + 2, near),
            (2, 1): link(own(1), slot(2, 1), sems, base + 3, far),
            (3, 0): link(slot(2, 0), slot(3, 0), sems, base + 4, near),
            (3, 1): link(slot(1, 1), slot(3, 1), sems, base + 5, far),
        }

    def start(self, half):
        order = ((2, 0), (1, 0)) if half == 0 else ((1, 1), (2, 1))
        for key in order:
            self.copies[key].start()

    def forward(self, half):
        self.copies[(2, 0) if half == 0 else (1, 1)].wait_recv()
        self.copies[(3, half)].start()

    def wait(self, *keys):
        for key in keys:
            self.copies[key].wait_recv()

    def drain(self):
        for copy in self.copies.values():
            copy.wait_send()


def front_kernel(
    xin,
    w_half,
    src,
    starts,
    cos,
    sin,
    gain_a,
    gain_m,
    ids,
    spots,
    src_row,
    xd,
    attn,
    qkv,
    mixed,
    middle,
    moe_all,
    slot_cols,
    slot_rows,
    chosen,
    w_att,
    moe,
    slot_given,
    given_rows,
    mid16,
    w_router,
    xb,
    bias,
    sems,
    local_sems,
):
    nblk, tokens, width = xb.shape
    half = tokens // 2
    capacity = nblk * tokens * TOPK // EXPERT_COUNT
    pairs = w_att.shape[1]
    qw = w_att.shape[4] * 2 // 3
    rank = w_att.shape[1] * 2 * w_att.shape[3]
    r = lax.axis_index("row")
    c = lax.axis_index("col")
    z = c // 2
    k = c % 2
    both = w_att.shape[4]
    local = EXPERT_COUNT // nblk
    sibling = (r, c ^ 1)
    greet([(r ^ 1, c), (r ^ 2, c), sibling])

    def cut(ref):
        return lambda h: ref.at[pl.ds(h * half, half)]

    def cut_slot(ref):
        return lambda j, h: ref.at[j, pl.ds(h * half, half)]

    def w_slot(j, h):
        return w_att.at[j, pl.ds(h * (pairs // 2), pairs // 2), k]

    n = RowGather.count
    xs = RowGather(cut(xin), cut_slot(xb), sems, 0, r, c)
    ws = RowGather(lambda h: w_slot(0, h), w_slot, sems, n, r, c)
    ms = RowGather(cut(moe), cut_slot(moe_all), sems, 2 * n, r, c)
    base = 3 * n
    share = [link(w_att.at[j, :, k], w_att.at[j, :, k], sems, base + j, sibling) for j in range(nblk)]
    share.append(link(w_router.at[:, k], w_router.at[:, k], sems, base + nblk, sibling))
    xs.start(1)
    xs.start(0)
    keep = [pltpu.make_async_copy(xin, xb.at[0], local_sems.at[0])]
    for i in range(pairs):
        keep.append(
            pltpu.make_async_copy(
                w_half.at[i, :, pl.ds(0, both)], w_att.at[0, z ^ i, k], local_sems.at[2 + 2 * i]
            )
        )
        keep.append(
            pltpu.make_async_copy(
                w_half.at[i, :, pl.ds(both, LANES)], w_router.at[z ^ i, k], local_sems.at[3 + 2 * i]
            )
        )
    for copy in keep:
        copy.start()
    for copy in keep:
        copy.wait()
    ws.start(1)
    ws.start(0)
    share[0].start()
    share[nblk].start()
    xs.forward(0)
    xs.forward(1)

    source = src[:tokens, :]

    def pick(at, j):
        return jnp.where(at == iota((tokens, tokens), 1) + j * tokens, 1.0, 0.0).astype(BF)

    x = mm(pick(source, 0), xb[0])
    xs.wait((1, 0))
    x = x + mm(pick(source, 1), xb[1])
    xs.wait((2, 1))
    x = x + mm(pick(source, 2), xb[2])
    ws.forward(0)
    ws.forward(1)
    ws.wait((1, 0), (2, 1))
    share[1].start()
    share[2].start()
    xs.wait((3, 0), (3, 1))
    x = x + mm(pick(source, 3), xb[3])
    xd[...] = x.astype(BF)
    attn[...] = (x * row_scale(x) * gain_a[...]).astype(BF)
    groups = qw // (4 * HEAD_WIDTH)

    def project(j):
        proj = mm(attn[...], w_att[j, :, :, :, :qw].reshape(rank, qw))
        cos_w = jnp.concatenate([cos[...]] * groups, axis=1)
        sin_w = jnp.concatenate([sin[...]] * groups, axis=1)
        turned = proj * cos_w + swap_halves(proj) * sin_w
        qkv[:, pl.ds(pl.multiple_of(j * qw, qw), qw)] = turned.astype(BF)

    ws.wait((3, 0), (3, 1))
    share[3].start()
    for copy in share:
        copy.wait_recv()

    @pl.loop(0, nblk)
    def _(j):
        project(j)

    pair = 2 * HEAD_WIDTH
    for b in range(2):
        rows = slice(b * half, (b + 1) * half)
        span = (b + 1) * half
        bias[:, :span] = attention_bias(b * half, half, span, starts[rows, :])

        @pl.loop(0, groups * nblk)
        def _(g):
            chunk = qkv[:span, pl.ds(pl.multiple_of(g * 2 * pair, 2 * pair), 2 * pair)]
            k_rows = chunk[:, pair : pair + HEAD_WIDTH]
            v_rows = chunk[:, pair + HEAD_WIDTH :]
            outs = []
            for h in range(2):
                q = chunk[b * half :, h * HEAD_WIDTH : (h + 1) * HEAD_WIDTH]
                probs = masked_probs(q, k_rows, bias[:, :span])
                outs.append(mm(probs.astype(BF), v_rows))
            mixed[rows, pl.ds(pl.multiple_of(g * pair, pair), pair)] = jnp.concatenate(
                outs, axis=1
            ).astype(BF)

        if b == 1:
            ms.forward(0)
        ow = w_att.shape[4] - qw
        out = jnp.zeros((half, width), F32)
        for j in range(nblk):
            w_out = w_att[j, :, :, :, qw:].reshape(rank, ow)
            out = out + mm_nt(mixed[rows, j * ow : (j + 1) * ow], w_out)
        mid = xd[rows, :].astype(F32) + RESIDUAL_SCALE * out
        middle[rows, :] = mid
        mid16[rows, :] = mid.astype(BF)
        moe[rows, :] = (mid * row_scale(mid) * gain_m[...]).astype(BF)
        ms.start(b)

    place = pltpu.make_async_copy(moe, moe_all.at[0], local_sems.at[1])
    place.start()

    @pl.loop(0, nblk)
    def _(b):
        at = pl.ds(pl.multiple_of(b * tokens, tokens), tokens)
        lane = iota((tokens, LANES), 1)
        spot = jnp.zeros((tokens, LANES), F32)
        named = jnp.zeros((tokens, LANES), F32)
        there = pl.ds(pl.multiple_of((b ^ r) * tokens, tokens), tokens)
        own_ids = ids[there, :] ^ (r * local)
        own_spots = spots[there, :]
        for i in range(TOPK):
            hit = lane == own_ids[:, i : i + 1]
            named = jnp.where(hit, 1.0, named)
            spot = jnp.where(hit, own_spots[:, i : i + 1].astype(F32), spot)
        chosen[at, :] = named
        slot = jnp.where((named > 0.0) & (spot < capacity), spot, -1.0)
        slot_cols[at, :] = slot
        slot_rows[:, at] = slot.T[: slot_rows.shape[0], :]

    ms.forward(1)

    @pl.loop(0, nblk)
    def _(b):
        at = pl.ds(pl.multiple_of(b * tokens, tokens), tokens)
        found = jnp.zeros((tokens, LANES), F32)
        for j in range(nblk):
            part = slice(j * tokens, (j + 1) * tokens)
            match = iota((tokens, tokens), 0) + b * tokens == src_row[:, part]
            match = jnp.where(match, 1.0, 0.0).astype(BF)
            value = slot_cols[part, :] + 1.0
            high = jnp.floor(value * 0.0625)
            low = value - 16.0 * high
            found = found + 16.0 * mm(match, high.astype(BF)) + mm(match, low.astype(BF))
        slot_given[at, :] = found - 1.0
        given_rows[:, at] = (found - 1.0).T[: given_rows.shape[0], :]

    ms.wait((1, 0), (2, 1), (3, 0), (3, 1))
    place.wait()
    for gather in (xs, ws, ms):
        gather.drain()
    for copy in share:
        copy.wait_send()


def front(xin, w_half, src, starts, cos, sin, gain_a, gain_m, ids, spots, src_row, nblk, pairs):
    tokens, width = xin.shape
    shard, both = w_half.shape[1], w_half.shape[2] - LANES
    total = nblk * tokens
    qkv_width = nblk * both * 2 // 3
    head_width = nblk * both // 3
    shape = jax.ShapeDtypeStruct
    count = 3 * RowGather.count + nblk + 1
    local = EXPERT_COUNT // nblk
    return pl.pallas_call(
        front_kernel,
        out_shape=(
            shape((tokens, width), BF),
            shape((tokens, width), BF),
            shape((tokens, qkv_width), BF),
            shape((tokens, head_width), BF),
            shape((tokens, width), F32),
            shape((nblk, tokens, width), BF),
            shape((total, LANES), F32),
            shape((local, total), F32),
            shape((total, LANES), F32),
            shape((nblk, pairs, 2, shard, both), BF),
            shape((tokens, width), BF),
            shape((total, LANES), F32),
            shape((local, total), F32),
            shape((tokens, width), BF),
            shape((pairs, 2, shard, LANES), BF),
        ),
        in_specs=[ANY] * 2 + [FULL] * 9,
        out_specs=[FULL] * 5 + [ANY] + [FULL] * 9,
        scratch_shapes=[
            pltpu.VMEM((nblk, tokens, width), BF),
            pltpu.VMEM((tokens // 2, tokens), F32),
            pltpu.SemaphoreType.DMA((2, count)),
            pltpu.SemaphoreType.DMA((2 + 2 * pairs,)),
        ],
        compiler_params=pltpu.CompilerParams(
            vmem_limit_bytes=58 * MIB, collective_id=1, has_side_effects=True
        ),
        cost_estimate=cost(20e9, 60 * MIB),
        name="attention_forward",
    )(xin, w_half, src, starts, cos, sin, gain_a, gain_m, ids, spots, src_row)


def router_kernel(moe, w_router, chosen, gates, packed):
    nblk, tokens, _ = moe.shape
    local = EXPERT_COUNT // nblk
    for j in range(nblk):
        at = slice(j * tokens, (j + 1) * tokens)
        logits = mm(moe[j], w_router[...])
        named = chosen[at, :] > 0.0
        logits = jnp.where(named, logits, MASKED)
        top = jnp.max(logits, axis=-1, keepdims=True)
        raised = jnp.where(named, jnp.exp(logits - top), 0.0)
        gate = raised / jnp.sum(raised, axis=-1, keepdims=True)
        gates[at, :] = gate
        lane = iota((tokens, LANES), 1)
        own = jnp.where(lane < local, gate, 0.0)
        high = own.astype(BF).astype(F32)
        rest = own - high
        mid = rest.astype(BF).astype(F32)
        low = rest - mid
        packed[at, :] = (high + pltpu.roll(mid, local, 1) + pltpu.roll(low, 2 * local, 1)).astype(BF)


def router(moe, w_router, chosen):
    nblk, tokens, _ = moe.shape
    total = nblk * tokens
    shape = jax.ShapeDtypeStruct
    return pl.pallas_call(
        router_kernel,
        out_shape=(shape((total, LANES), F32), shape((total, LANES), BF)),
        in_specs=[FULL] * 3,
        out_specs=[FULL] * 2,
        compiler_params=params(24),
        cost_estimate=cost(1e9, 7 * MIB),
        name="router",
    )(moe, w_router, chosen)


class RowScatter:
    count = 6

    def __init__(self, block, mixed_in, across, landed, sems, base, r, c):
        near, far = (r ^ 1, c), (r ^ 2, c)
        self.copies = {
            "diag0": link(block(3, 0), across(0), sems, base, near),
            "diag1": link(block(3, 1), across(1), sems, base + 1, far),
            "near0": link(block(1, 0), landed(1, 0), sems, base + 2, near),
            "far1": link(block(2, 1), landed(2, 1), sems, base + 3, far),
        }
        if mixed_in is not None:
            self.copies["far0"] = link(mixed_in(0), landed(2, 0), sems, base + 4, far)
            self.copies["near1"] = link(mixed_in(1), landed(1, 1), sems, base + 5, near)

    def start(self):
        for key in ("diag0", "diag1", "near0", "far1"):
            self.copies[key].start()

    def arrived(self, half):
        self.copies["diag0" if half == 0 else "diag1"].wait_recv()

    def send(self, half):
        self.copies["far0" if half == 0 else "near1"].start()

    def finish(self):
        for key in self.copies:
            if not key.startswith("diag"):
                self.copies[key].wait_recv()

    def drain(self):
        for copy in self.copies.values():
            copy.wait_send()


def tree_sum(parts):
    while len(parts) > 1:
        parts = [parts[i] + parts[i + 1] for i in range(0, len(parts), 2)]
    return parts[0]


def plus(a, b):
    return (a.astype(F32) + b.astype(F32)).astype(BF)


def one_hot(hit):
    return jnp.where(hit, 1.0, 0.0).astype(BF)


def lane_column(table, index):
    return jnp.sum(jnp.where(iota(table.shape, 1) == index, table, 0.0), axis=1, keepdims=True)


def split_three(value):
    high = value.astype(BF).astype(F32)
    rest = value - high
    mid = rest.astype(BF).astype(F32)
    return high, mid, rest - mid


def forward_kernel(base, first, last, gathers, local, capacity, *refs):
    moe_hbm, slot_rows, slot_given, packed, w = refs[:5]
    refs = refs[5:]
    if not first:
        acc_in, refs = refs[0], refs[1:]
    if gathers:
        own_hbm, refs = refs[0], refs[1:]
    routed_out, gate_out, up_out, weight_out, acc_out = refs[:5]
    refs = refs[5:]
    if gathers:
        all_hbm, refs = refs[0], refs[1:]
    moe, acc, sel, given, y1, sems = refs[:6]
    step = pl.program_id(0)
    steps = pl.num_programs(0)
    e = base + step
    ne = y1.shape[0] // capacity
    nblk, tokens, width = moe_hbm.shape
    fe = w.shape[3] // 3
    copies = [
        pltpu.make_async_copy(moe_hbm.at[j], moe.at[pl.ds(j * tokens, tokens)], sems.at[j])
        for j in range(nblk)
    ]
    if not first:
        load = pltpu.make_async_copy(acc_in, acc, sems.at[nblk])
    if gathers:
        link_sems = refs[6]
        r = lax.axis_index("row")
        c = lax.axis_index("col")
        half = tokens // 2
        gather = RowGather(
            lambda h: own_hbm.at[pl.ds(h * half, half)],
            lambda j, h: all_hbm.at[j, pl.ds(h * half, half)],
            link_sems,
            0,
            r,
            c,
        )
        keep = pltpu.make_async_copy(own_hbm, all_hbm.at[0], sems.at[nblk + 1])

    @pl.when(step == 0)
    def _():
        for copy in copies:
            copy.start()
        if not first:
            load.start()
        if gathers:
            keep.start()
            greet([(r ^ 1, c), (r ^ 2, c)])
            gather.start(0)
            gather.start(1)

    row = slot_rows[pl.ds(e, 1), :]
    for j in range(nblk):
        at = slice(j * tokens, (j + 1) * tokens)
        sel[:, at] = one_hot(iota((capacity, tokens), 0).astype(F32) == row[:, at])

    @pl.when(step == 0)
    def _():
        for copy in copies:
            copy.wait()

    if gathers:

        @pl.when(step == steps - 1)
        def _():
            gather.forward(0)
            gather.forward(1)

    routed_out[0] = mm(sel[...], moe[...]).astype(BF)
    lane = iota((capacity, LANES), 1)
    picked = mm(sel[...], packed[...])
    mine = (lane == e) | (lane == e + local) | (lane == e + 2 * local)
    gate = jnp.sum(jnp.where(mine, picked, 0.0), axis=1, keepdims=True)
    weight_out[0] = jnp.broadcast_to(gate, (capacity, LANES))
    gate_up = mm(routed_out[0], w[:, 0, :, : 2 * fe].reshape(width, 2 * fe))
    gate_in = gate_up[:, :fe]
    up_in = gate_up[:, fe:]
    gate_out[0] = gate_in
    up_out[0] = up_in
    hidden = (gate_in * jax.nn.sigmoid(gate_in) * up_in).astype(BF)
    out = mm_nt(hidden, w[:, 0, :, 2 * fe :].reshape(width, fe))
    y1[pl.ds(pl.multiple_of(step * capacity, capacity), capacity), :] = (gate * out).astype(BF)

    @pl.when(step == steps - 1)
    def _():
        if not first:
            load.wait()

        def put(b):
            at = pl.ds(pl.multiple_of(b * tokens, tokens), tokens)
            if last:
                return pltpu.make_async_copy(moe.at[at], acc_out.at[b], sems.at[b])
            return pltpu.make_async_copy(acc.at[at], acc_out.at[at], sems.at[b])

        @pl.loop(0, nblk)
        def _(b):
            at = pl.ds(pl.multiple_of(b * tokens, tokens), tokens)
            slots = iota((tokens, capacity), 1).astype(F32)
            for i in range(ne):
                given[:, i * capacity : (i + 1) * capacity] = one_hot(
                    lane_column(slot_given[at, :], base + i) == slots
                )
            part = mm(given[...], y1[...])
            if not first:
                part = part + acc[at, :]
            if last:
                moe[at, :] = part.astype(BF)
            else:
                acc[at, :] = part
            put(b).start()

        if gathers:
            gather.wait((1, 0), (2, 1), (3, 0), (3, 1))
            keep.wait()
            gather.drain()
        for b in range(nblk):
            put(b).wait()


def experts_forward(moe, slot_rows, slot_given, packed, w, acc, own, base, last, capacity, key):
    nblk, tokens, width = moe.shape
    total = nblk * tokens
    cols, ne, shard, fe3 = w.shape
    fe = fe3 // 3
    local = EXPERT_COUNT // nblk
    first = acc is None
    gathers = own is not None
    shape = jax.ShapeDtypeStruct
    wspec = pl.BlockSpec((cols, 1, shard, fe3), lambda s: (0, s, 0, 0))

    def each(*dims):
        return pl.BlockSpec((1, *dims), lambda s: (s, 0, 0))

    ins = [moe, slot_rows, slot_given, packed, w]
    in_specs = [ANY, FULL, FULL, FULL, wspec]
    aliases = {}
    if not first:
        ins.append(acc)
        in_specs.append(ANY)
        if not last:
            aliases = {len(ins) - 1: 4}
    outs = [
        shape((ne, capacity, width), BF),
        shape((ne, capacity, fe), F32),
        shape((ne, capacity, fe), F32),
        shape((ne, capacity, LANES), F32),
        shape((nblk, tokens, width), BF) if last else shape((total, width), F32),
    ]
    out_specs = [each(capacity, width), each(capacity, fe), each(capacity, fe), each(capacity, LANES), ANY]
    scratch = [
        pltpu.VMEM((total, width), BF),
        pltpu.VMEM((total, width), F32),
        pltpu.VMEM((capacity, total), BF),
        pltpu.VMEM((tokens, ne * capacity), BF),
        pltpu.VMEM((ne * capacity, width), BF),
        pltpu.SemaphoreType.DMA((nblk + 2,)),
    ]
    options = dict(vmem_limit_bytes=58 * MIB)
    if gathers:
        ins.append(own)
        in_specs.append(ANY)
        outs.append(shape((nblk, tokens, width), BF))
        out_specs.append(ANY)
        scratch.append(pltpu.SemaphoreType.DMA((2, RowGather.count)))
        options.update(collective_id=key, has_side_effects=True)
    return pl.pallas_call(
        functools.partial(forward_kernel, base, first, last, gathers, local, capacity),
        grid=(ne,),
        out_shape=outs,
        in_specs=in_specs,
        out_specs=out_specs,
        scratch_shapes=scratch,
        input_output_aliases=aliases,
        compiler_params=pltpu.CompilerParams(**options),
        cost_estimate=cost(7e9 * ne, 30 * MIB),
        name="experts_forward",
    )(*ins)


def reverse_kernel(base, first, last, local, capacity, *refs):
    cot_hbm, given_rows, slot_cols, routed, gate_in_ref, up_in_ref, weight_ref, w = refs[:8]
    refs = refs[8:]
    if not first:
        acc_in, accg_in = refs[:2]
        refs = refs[2:]
    if last:
        es, refs = refs[0], refs[1:]
    grads, acc_out, accg_out = refs[:3]
    refs = refs[3:]
    if last:
        e_mix, e_across, e_landed = refs[:3]
        refs = refs[3:]
    cot, acc, accg, sel, chosen, spread, dsl, dslot, y2, sems = refs[:10]
    step = pl.program_id(0)
    steps = pl.num_programs(0)
    e = base + step
    nblk, tokens, width = cot_hbm.shape
    half = tokens // 2
    cols, _, shard, fe = w.shape
    fe = fe // 3
    ne = y2.shape[0] // capacity
    copies = [
        pltpu.make_async_copy(cot_hbm.at[j], cot.at[pl.ds(j * tokens, tokens)], sems.at[j])
        for j in range(nblk)
    ]
    if not first:
        loads = [
            pltpu.make_async_copy(acc_in, acc, sems.at[nblk]),
            pltpu.make_async_copy(accg_in, accg, sems.at[nblk + 1]),
        ]
    if last:
        e_vmem, link_sems = refs[10:]
        r = lax.axis_index("row")
        c = lax.axis_index("col")
        scatter = RowScatter(
            lambda j, h: es.at[j, pl.ds(h * half, half)],
            None,
            lambda h: e_across.at[h],
            lambda j, h: e_landed.at[h],
            link_sems,
            0,
            r,
            c,
        )

    @pl.when(step == 0)
    def _():
        for copy in copies:
            copy.start()
        if not first:
            for copy in loads:
                copy.start()
        if last:
            greet([(r ^ 1, c), (r ^ 2, c)])
            scatter.start()

    row = given_rows[pl.ds(e, 1), :]
    for j in range(nblk):
        at = slice(j * tokens, (j + 1) * tokens)
        sel[:, at] = one_hot(iota((capacity, tokens), 0).astype(F32) == row[:, at])

    @pl.when(step == 0)
    def _():
        for copy in copies:
            copy.wait()

    gate = weight_ref[0, :, :1]

    rows = (RESIDUAL_SCALE * mm(sel[...], cot[...])).astype(BF)
    dsl[...] = rows
    dslot[...] = (gate * rows.astype(F32)).astype(BF)
    gate_in = gate_in_ref[0]
    up_in = up_in_ref[0]
    sig = jax.nn.sigmoid(gate_in)
    silu = gate_in * sig
    hidden = (silu * up_in).astype(BF)
    dhidden = mm(dslot[...], w[:, 0, :, 2 * fe :].reshape(width, fe))
    dgate = (dhidden * up_in * sig * (1.0 + gate_in * (1.0 - sig))).astype(BF)
    dup = (dhidden * silu).astype(BF)
    both = jnp.concatenate([dgate, dup], axis=1)
    out = mm_nt(hidden, w[:, 0, :, 2 * fe :].reshape(width, fe))
    inner = jnp.sum(dsl[...].astype(F32) * out, axis=1, keepdims=True)
    grads[:, 0, :, 2 * fe :] = mm_tn(dslot[...], hidden).astype(BF).reshape(cols, shard, fe)
    grads[:, 0, :, : 2 * fe] = mm_tn(routed[0], both).astype(BF).reshape(cols, shard, 2 * fe)
    mine = pl.ds(pl.multiple_of(step * capacity, capacity), capacity)
    y2[mine, :] = mm_nt(both, w[:, 0, :, : 2 * fe].reshape(width, 2 * fe)).astype(BF)
    high, mid, low = split_three(inner)
    lane = iota((capacity, LANES), 1)
    spread[mine, :] = jnp.where(
        lane == e,
        high,
        jnp.where(lane == e + local, mid, jnp.where(lane == e + 2 * local, low, 0.0)),
    ).astype(BF)

    @pl.when(step == steps - 1)
    def _():
        if not first:
            for copy in loads:
                copy.wait()

        def put(b):
            at = pl.ds(pl.multiple_of(b * tokens, tokens), tokens)
            if last:
                return pltpu.make_async_copy(cot.at[at], acc_out.at[b], sems.at[b])
            return pltpu.make_async_copy(acc.at[at], acc_out.at[at], sems.at[b])

        @pl.loop(0, nblk)
        def _(b):
            at = pl.ds(pl.multiple_of(b * tokens, tokens), tokens)
            slots = iota((tokens, capacity), 1).astype(F32)
            for i in range(ne):
                chosen[:, i * capacity : (i + 1) * capacity] = one_hot(
                    lane_column(slot_cols[at, :], base + i) == slots
                )
            part = mm(chosen[...], y2[...])
            partg = mm(chosen[...], spread[...])
            if not first:
                part = part + acc[at, :]
                partg = partg + accg[at, :]
            if last:
                cot[at, :] = part.astype(BF)
            else:
                acc[at, :] = part
            accg[at, :] = partg
            put(b).start()

        if last:
            summed = accg[...]
            summed = (
                summed
                + pltpu.roll(summed, LANES - local, 1)
                + pltpu.roll(summed, LANES - 2 * local, 1)
            )
            accg_out[...] = summed.T[:local, :]
            for h in range(2):
                scatter.arrived(h)
                gets = [
                    pltpu.make_async_copy(
                        es.at[2 - h, pl.ds(h * half, half)], e_vmem.at[0], sems.at[nblk]
                    ),
                    pltpu.make_async_copy(e_across.at[h], e_vmem.at[1], sems.at[nblk + 1]),
                ]
                for copy in gets:
                    copy.start()
                for copy in gets:
                    copy.wait()
                e_vmem[0] = plus(e_vmem[0], e_vmem[1])
                back = pltpu.make_async_copy(e_vmem.at[0], e_mix.at[h], sems.at[nblk])
                back.start()
                back.wait()
            scatter.finish()
            scatter.drain()
        else:
            out_g = pltpu.make_async_copy(accg, accg_out, sems.at[nblk])
            out_g.start()
            out_g.wait()
        for b in range(nblk):
            put(b).wait()


def experts_reverse(cot, given_rows, slot_cols, kept, w, carried, es, base, last, capacity, key):
    nblk, tokens, width = cot.shape
    half = tokens // 2
    total = nblk * tokens
    cols, ne, shard, fe3 = w.shape
    fe = fe3 // 3
    local = EXPERT_COUNT // nblk
    first = carried is None
    shape = jax.ShapeDtypeStruct
    wspec = pl.BlockSpec((cols, 1, shard, fe3), lambda s: (0, s, 0, 0))

    def each(*dims):
        return pl.BlockSpec((1, *dims), lambda s: (s, 0, 0))

    ins = [cot, given_rows, slot_cols, *kept, w]
    in_specs = [
        ANY,
        FULL,
        FULL,
        each(capacity, width),
        each(capacity, fe),
        each(capacity, fe),
        each(capacity, LANES),
        wspec,
    ]
    aliases = {}
    if not first:
        ins += list(carried)
        in_specs += [ANY, ANY]
        if not last:
            aliases = {len(ins) - 2: 1, len(ins) - 1: 2}
    if last:
        outs = [
            shape(w.shape, BF),
            shape((nblk, tokens, width), BF),
            shape((local, total), F32),
            shape((2, half, width), BF),
            shape((2, half, width), BF),
            shape((2, half, width), BF),
        ]
        out_specs = [wspec, ANY, FULL, ANY, ANY, ANY]
        ins.append(es)
        in_specs.append(ANY)
    else:
        outs = [shape(w.shape, BF), shape((total, width), F32), shape((total, LANES), F32)]
        out_specs = [wspec, ANY, ANY]
    scratch = [
        pltpu.VMEM((total, width), BF),
        pltpu.VMEM((total, width), F32),
        pltpu.VMEM((total, LANES), F32),
        pltpu.VMEM((capacity, total), BF),
        pltpu.VMEM((tokens, ne * capacity), BF),
        pltpu.VMEM((ne * capacity, LANES), BF),
        pltpu.VMEM((capacity, width), BF),
        pltpu.VMEM((capacity, width), BF),
        pltpu.VMEM((ne * capacity, width), BF),
        pltpu.SemaphoreType.DMA((nblk + 2,)),
    ]
    options = dict(vmem_limit_bytes=58 * MIB)
    if last:
        scratch += [
            pltpu.VMEM((2, half, width), BF),
            pltpu.SemaphoreType.DMA((2, RowScatter.count)),
        ]
        options.update(collective_id=key, has_side_effects=True)
    return pl.pallas_call(
        functools.partial(reverse_kernel, base, first, last, local, capacity),
        grid=(ne,),
        out_shape=outs,
        in_specs=in_specs,
        out_specs=out_specs,
        scratch_shapes=scratch,
        input_output_aliases=aliases,
        compiler_params=pltpu.CompilerParams(**options),
        cost_estimate=cost(9e9 * ne, 40 * MIB),
        name="experts_reverse",
    )(*ins)


def back_kernel(nblk, *refs):
    dm, es, e_mix, e_half, dgates, mids, cot = refs[:7]
    refs = refs[7:]
    (gates, middle, moe, src_col, mixed, qkv, attn, xd, w_att, w_router) = refs[:10]
    (starts, cos, sin, gain_a, gain_m, src_row) = refs[10:16]
    (block_out, input_grad, att_grad, small, e_rest) = refs[16:21]
    (own, d_across, d_landed, dg_land, igb, dmid, dmix, dproj, dkv, bias, wg, wg_sib) = refs[21:33]
    (w_across, w_landed, w_z, rowsum, s_own, s_sib, s_sum, s_row, s_chip, s_z, sems, lsems) = refs[33:]
    tokens, width = xd.shape
    half = tokens // 2
    local = EXPERT_COUNT // nblk
    pairs = w_att.shape[1]
    shard = w_att.shape[3]
    qw = w_att.shape[4] * 2 // 3
    ow = w_att.shape[4] - qw
    hw = HEAD_WIDTH
    r = lax.axis_index("row")
    c = lax.axis_index("col")
    z = c // 2
    k = c % 2
    row_peers = [(r ^ j, c) for j in range(1, nblk)]
    z_peers = [(r, 2 * (z ^ i) + k) for i in range(1, pairs)]
    sibling = (r, c ^ 1)
    greet(row_peers + z_peers + [sibling])

    def part(h):
        return pl.ds(h * half, half)

    zhalf = pairs // 2

    def zpart(h):
        return pl.ds(h * zhalf, zhalf)

    n = RowScatter.count
    dms = RowScatter(
        lambda j, h: dm.at[j, part(h)],
        lambda h: own.at[2 - h, part(h)],
        lambda h: d_across.at[h],
        lambda j, h: d_landed.at[j - 1, part(h)],
        sems,
        0,
        r,
        c,
    )
    ess = [
        link(e_mix.at[0], e_rest.at[0], sems, n, (r ^ 2, c)),
        link(e_mix.at[1], e_rest.at[1], sems, n + 1, (r ^ 1, c)),
    ]
    wgs = RowScatter(
        lambda j, h: wg.at[j, zpart(h), k],
        lambda h: wg.at[2 - h, zpart(h), k],
        lambda h: w_across.at[h],
        lambda j, h: w_landed.at[j - 1, zpart(h)],
        sems,
        2 * n,
        r,
        c,
    )
    igs = RowGather(
        lambda h: igb.at[0, part(h)], lambda j, h: igb.at[j, part(h)], sems, 3 * n, r, c
    )
    at = 3 * n + RowGather.count
    dgs = [
        link(dgates.at[:, pl.ds(j * tokens, tokens)], dg_land.at[j - 1], sems, at + j - 1, (r ^ j, c))
        for j in range(1, nblk)
    ]
    at += nblk - 1
    wg_share = [
        link(wg.at[j, :, 1 - k], wg_sib.at[j], sems, at + j, sibling) for j in range(nblk)
    ]
    at += nblk
    wg_z = [
        link(rowsum.at[z ^ i], w_z.at[i - 1], sems, at + i - 1, z_peers[i - 1])
        for i in range(1, pairs)
    ]
    at += pairs - 1
    s_share = link(s_own, s_sib, sems, at, sibling)
    s_rows = [link(s_sum, s_row.at[j], sems, at + 1 + j, row_peers[j]) for j in range(nblk - 1)]
    at += nblk
    s_zs = [link(s_chip, s_z.at[i], sems, at + i, z_peers[i]) for i in range(pairs - 1)]

    dms.start()
    for copy in dgs:
        copy.start()
    loads = [
        pltpu.make_async_copy(dm.at[0], own.at[0], lsems.at[0]),
        pltpu.make_async_copy(dm.at[1, part(1)], own.at[1, part(1)], lsems.at[1]),
        pltpu.make_async_copy(dm.at[2, part(0)], own.at[2, part(0)], lsems.at[2]),
        pltpu.make_async_copy(middle, dmid, lsems.at[3]),
    ]
    for copy in loads:
        copy.start()

    def match(j):
        hit = iota((tokens, tokens), 0) == src_row[:, j * tokens : (j + 1) * tokens]
        return jnp.where(hit, 1.0, 0.0).astype(BF)

    total = jnp.zeros((tokens, width), F32)
    for j in range(nblk):
        get = pltpu.make_async_copy(mids.at[j], dmix, lsems.at[4])
        get.start()
        hit = match(j)
        get.wait()
        total = total + mm(hit, dmix[...])
    input_grad[...] = total
    dy = jnp.zeros((tokens, width), F32)
    for j in range(nblk):
        get = pltpu.make_async_copy(cot.at[j], dmix, lsems.at[4])
        get.start()
        hit = one_hot(src_col[...] == iota((tokens, tokens), 1) + j * tokens)
        get.wait()
        dy = dy + mm(hit, dmix[...])
    dproj[:, :width] = dy.astype(BF)
    for copy in loads:
        copy.wait()
    for h in range(2):
        dms.arrived(h)
        rows = part(h)
        own[2 - h, rows, :] = plus(own[2 - h, rows, :], d_across[h])
        dms.send(h)

    for copy in dgs:
        copy.wait_recv()
    parts = [dgates[:, :tokens]] + [dg_land[j] for j in range(nblk - 1)]
    pad = jnp.zeros((LANES - EXPERT_COUNT, tokens), F32)
    dgate = jnp.concatenate(parts + [pad], axis=0).T
    gate = gates[...]
    dchosen = gate * (dgate - jnp.sum(gate * dgate, axis=1, keepdims=True))
    dlogits = dchosen.astype(BF)
    router_t = mm_tn(dlogits, moe[...])
    for j in range(nblk):
        s_own[pl.ds(pl.multiple_of((r ^ j) * local, local), local), :] = router_t[
            j * local : (j + 1) * local, :
        ]
    dmoe = mm_nt(dlogits, w_router[...]) + own[0].astype(F32)
    dms.finish()
    for copy in ess:
        copy.start()
    dmoe = dmoe + (d_landed[0].astype(F32) + d_landed[1].astype(F32))
    mid = dmid[...]
    rr = row_scale(mid)
    scaled = dmoe * gain_m[...]
    inner = jnp.mean(scaled * mid, axis=-1, keepdims=True)
    gain_m_part = jnp.sum(dmoe * mid * rr, axis=0, keepdims=True)
    dmid[...] = dproj[:, :width].astype(F32) + (rr * scaled - mid * (rr * rr * rr) * inner)
    dattn = (RESIDUAL_SCALE * dmid[...]).astype(BF)
    for j in range(nblk):
        cols = slice(j * ow, (j + 1) * ow)
        dmix[:, cols] = mm(dattn, w_att[j, :, :, :, qw:].reshape(width, ow)).astype(BF)
        wg[j, :, :, :, qw:] = (
            mm_tn(dattn, mixed[:, cols]).astype(BF).reshape(pairs, 2, shard, ow)
        )

    quad = 4 * hw
    groups = nblk * qw // quad
    gain_a_part = jnp.zeros((1, width), F32)
    for b in (1, 0):
        span = (b + 1) * half
        rows = slice(b * half, (b + 1) * half)
        bias[:, :span] = attention_bias(b * half, half, span, starts[rows, :])

        @pl.loop(0, groups)
        def _(g):
            chunk = qkv[:span, pl.ds(pl.multiple_of(g * quad, quad), quad)]
            dm_chunk = dmix[rows, pl.ds(pl.multiple_of(g * 2 * hw, 2 * hw), 2 * hw)]
            k_rows = chunk[:, 2 * hw : 3 * hw]
            v_rows = chunk[:, 3 * hw :]
            dk = jnp.zeros((span, hw), F32)
            dv = jnp.zeros((span, hw), F32)
            dqs = []
            for h in range(2):
                q = chunk[b * half :, h * hw : (h + 1) * hw]
                dmh = dm_chunk[:, h * hw : (h + 1) * hw]
                probs = masked_probs(q, k_rows, bias[:, :span])
                dprobs = mm_nt(dmh, v_rows)
                total = jnp.sum(probs * dprobs, axis=-1, keepdims=True)
                dscores = (probs * (dprobs - total)).astype(BF)
                dqs.append(mm(dscores, k_rows))
                dk = dk + mm_tn(dscores, q)
                dv = dv + mm_tn(probs.astype(BF), dmh)
            dkv_new = jnp.concatenate([dk, dv], axis=1)
            pair = pl.ds(pl.multiple_of(g * 2 * hw, 2 * hw), 2 * hw)
            if b == 1:
                dkv[:, pair] = dkv_new[:half]
                dkv_own = dkv_new[half:]
            else:
                dkv_own = dkv_new + dkv[:, pair]
            d = jnp.concatenate(dqs + [dkv_own], axis=1)
            d = d * cos[rows, :] - swap_halves(d) * sin[rows, :]
            dproj[rows, pl.ds(pl.multiple_of(g * quad, quad), quad)] = d.astype(BF)

        dattn_in = jnp.zeros((half, width), F32)
        for j in range(nblk):
            dattn_in = dattn_in + mm_nt(
                dproj[rows, j * qw : (j + 1) * qw],
                w_att[j, :, :, :, :qw].reshape(width, qw),
            )
        x = xd[rows, :].astype(F32)
        rx = row_scale(x)
        scaled = dattn_in * gain_a[...]
        inner = jnp.mean(scaled * x, axis=-1, keepdims=True)
        igb[0, rows, :] = (dmid[rows, :] + (rx * scaled - x * (rx * rx * rx) * inner)).astype(BF)
        gain_a_part = gain_a_part + jnp.sum(dattn_in * x * rx, axis=0, keepdims=True)
        igs.start(b)

    s_own[EXPERT_COUNT : EXPERT_COUNT + 8, :] = jnp.concatenate(
        [gain_a_part, gain_m_part, jnp.zeros((6, width), F32)], axis=0
    )
    s_share.start()
    for j in range(nblk):
        wg[j, :, :, :, :qw] = (
            mm_tn(attn[...], dproj[:, j * qw : (j + 1) * qw])
            .astype(BF)
            .reshape(pairs, 2, shard, qw)
        )
        wg_share[j].start()
    igs.forward(1)
    igs.forward(0)
    s_share.wait_recv()
    s_sum[...] = s_own[...] + s_sib[...]
    for copy in s_rows:
        copy.start()
    for j in (3, 1, 2, 0):
        wg_share[j].wait_recv()
        wg[j, :, pl.ds(k, 1)] = plus(wg[j, :, pl.ds(k, 1)], wg_sib[j][:, None])
    wgs.start()

    for copy in ess:
        copy.wait_recv()
    e_gets = [
        pltpu.make_async_copy(es.at[0], own.at[0], lsems.at[0]),
        pltpu.make_async_copy(e_half.at[0], own.at[1, part(0)], lsems.at[1]),
        pltpu.make_async_copy(e_half.at[1], own.at[1, part(1)], lsems.at[2]),
        pltpu.make_async_copy(e_rest.at[0], own.at[2, part(0)], lsems.at[3]),
        pltpu.make_async_copy(e_rest.at[1], own.at[2, part(1)], lsems.at[4]),
    ]
    dms.drain()
    for copy in e_gets:
        copy.start()
    for copy in e_gets:
        copy.wait()
    rest = own[2].astype(F32)
    summed = own[0].astype(F32) + (own[1].astype(F32) + rest)
    block_out[...] = (input_grad[...] + RESIDUAL_SCALE * summed).astype(BF)

    for h in range(2):
        wgs.arrived(h)
        hz = zpart(h)
        wg[2 - h, hz, pl.ds(k, 1)] = plus(wg[2 - h, hz, pl.ds(k, 1)], w_across[h][:, None])
        wgs.send(h)
    for copy in s_rows:
        copy.wait_recv()
    s_chip[...] = tree_sum([s_sum[...]] + [s_row[j] for j in range(nblk - 1)])
    for copy in s_zs:
        copy.start()
    igs.wait((1, 0), (2, 1))
    total = mm(match(0), igb[0])
    for j in (1, 2):
        total = total + mm(match(j), igb[j])
    igs.wait((3, 0), (3, 1))
    total = total + mm(match(3), igb[3])
    input_grad[...] = total
    wgs.finish()
    rowsum[...] = (
        wg[0, :, pl.ds(k, 1)].reshape(rowsum.shape).astype(F32)
        + (w_landed[0].astype(F32) + w_landed[1].astype(F32))
    ).astype(BF)
    for copy in wg_z:
        copy.start()
    for copy in s_zs:
        copy.wait_recv()
    small[...] = tree_sum([s_chip[...]] + [s_z[i] for i in range(pairs - 1)])
    for copy in wg_z:
        copy.wait_recv()
    att_grad[...] = tree_sum(
        [rowsum[pl.ds(z, 1)].reshape(att_grad.shape).astype(F32)]
        + [w_z[i].astype(F32) for i in range(pairs - 1)]
    )
    for group in (wgs, igs):
        group.drain()
    for copy in ess + dgs + wg_share + wg_z + [s_share] + s_rows + s_zs:
        copy.wait_send()


def backward(dm, es, e_mix, e_half, dgates, mids, cot, *rest):
    nblk, tokens, width = dm.shape
    w_att = rest[8]
    pairs, shard, both = w_att.shape[1], w_att.shape[3], w_att.shape[4]
    half = tokens // 2
    local = EXPERT_COUNT // nblk
    shape = jax.ShapeDtypeStruct
    count = (
        3 * RowScatter.count
        + RowGather.count
        + (nblk - 1)
        + nblk
        + (pairs - 1)
        + 1
        + (nblk - 1)
        + (pairs - 1)
    )
    small = (EXPERT_COUNT + 8, width)
    outs = pl.pallas_call(
        functools.partial(back_kernel, nblk),
        out_shape=(
            shape((tokens, width), BF),
            shape((tokens, width), F32),
            shape((shard, both), F32),
            shape(small, F32),
            shape((2, half, width), BF),
        ),
        in_specs=[ANY] * 4 + [FULL] + [ANY] * 2 + [FULL, ANY] + [FULL] * 14,
        out_specs=[FULL] * 4 + [ANY],
        scratch_shapes=[
            pltpu.VMEM((3, tokens, width), BF),
            pltpu.VMEM((2, half, width), BF),
            pltpu.VMEM((2, tokens, width), BF),
            pltpu.VMEM((nblk - 1, local, tokens), F32),
            pltpu.VMEM((nblk, tokens, width), BF),
            pltpu.VMEM((tokens, width), F32),
            pltpu.VMEM((tokens, width), BF),
            pltpu.VMEM((tokens, 2 * width), BF),
            pltpu.VMEM((half, width), F32),
            pltpu.VMEM((half, tokens), F32),
            pltpu.VMEM(w_att.shape, BF),
            pltpu.VMEM((nblk, pairs, shard, both), BF),
            pltpu.VMEM((2, pairs // 2, shard, both), BF),
            pltpu.VMEM((2, pairs, shard, both), BF),
            pltpu.VMEM((pairs - 1, shard, both), BF),
            pltpu.VMEM((pairs, shard, both), BF),
            pltpu.VMEM(small, F32),
            pltpu.VMEM(small, F32),
            pltpu.VMEM(small, F32),
            pltpu.VMEM((nblk - 1, *small), F32),
            pltpu.VMEM(small, F32),
            pltpu.VMEM((pairs - 1, *small), F32),
            pltpu.SemaphoreType.DMA((2, count)),
            pltpu.SemaphoreType.DMA((8,)),
        ],
        compiler_params=pltpu.CompilerParams(
            vmem_limit_bytes=62 * MIB, collective_id=2, has_side_effects=True
        ),
        cost_estimate=cost(60e9, 100 * MIB),
        name="attention_backward",
    )(dm, es, e_mix, e_half, dgates, mids, cot, *rest)
    return outs[:4]


def swap_over(value, axis, size, step):
    return lax.ppermute(value, axis, [(i, i ^ step) for i in range(size)])


def spread_rows(value, axis, size, step=1):
    return [value] + [swap_over(value, axis, size, j) for j in range(step, size, step)]


def body(
    block_in,
    cotangent,
    seq_lengths,
    seq_order,
    expert_ids,
    places,
    attn_gain,
    w_qkv,
    w_out,
    moe_gain,
    w_router,
    w_gate,
    w_up,
    w_down,
):
    tokens = block_in.shape[1]
    width = block_in.shape[2]
    rows = lax.axis_size("row")
    cols = lax.axis_size("col")
    total = tokens * rows
    r = lax.axis_index("row")
    c = lax.axis_index("col")
    local = w_gate.shape[1]
    shard = w_gate.shape[0]
    fe = w_gate.shape[2]
    capacity = total * TOPK // EXPERT_COUNT
    pairs = cols // 2
    qw = w_qkv.shape[1]
    ow = w_out.shape[1]

    router_own = jnp.concatenate(
        [lax.dynamic_slice_in_dim(w_router, (r ^ j) * local, local, 1) for j in range(rows)], axis=1
    )
    router_own = jnp.pad(router_own, ((0, 0), (0, LANES - EXPERT_COUNT)))
    w_half = jnp.stack(
        spread_rows(jnp.concatenate([w_qkv, w_out, router_own], axis=1), "col", cols, 2)
    )

    stacked = jnp.concatenate([w_gate, w_up, w_down], axis=2).transpose(1, 0, 2)
    sizes = [local - 2 * (local * 3 // 8), local * 3 // 8, local * 3 // 8][::-1]
    bases = [sum(sizes[:i]) for i in range(len(sizes))]
    gathered = [
        lax.all_gather(stacked[i : i + n], "col", axis=0) for i, n in zip(bases, sizes)
    ]

    lengths = seq_lengths[0]
    perm = seq_order[0]
    seq_ids = jnp.arange(lengths.shape[0], dtype=jnp.int32)
    picked = perm[:, None] == seq_ids[None, :]
    dealt_len = jnp.sum(jnp.where(picked, lengths[None, :], 0), axis=1)
    before = seq_ids[None, :] < perm[:, None]
    source_base = jnp.sum(jnp.where(before, lengths[None, :], 0), axis=1)
    upto = seq_ids[None, :] <= seq_ids[:, None]
    seq_ends = jnp.sum(jnp.where(upto, dealt_len[None, :], 0), axis=1)
    dealt_start = seq_ends - dealt_len
    turn = r * tokens
    pos = jnp.arange(total, dtype=jnp.int32) ^ turn
    inside = (pos[:, None] >= dealt_start[None, :]) & (pos[:, None] < seq_ends[None, :])
    seq_starts = jnp.sum(jnp.where(inside, dealt_start[None, :], 0), axis=1)
    offset = pos - seq_starts
    source = jnp.sum(jnp.where(inside, source_base[None, :], 0), axis=1) + offset
    source = source ^ turn
    src_col = source[:, None]
    src_row = source[None, :]
    own_offset = offset[:tokens]
    own_starts = (seq_starts[:tokens] - turn)[:, None]

    half = HEAD_WIDTH // 2
    frequency = ROPE_BASE ** (-jnp.arange(half, dtype=F32) * 2.0 / HEAD_WIDTH)
    turned = own_offset.astype(F32)[:, None] * frequency[None, :]
    cosine, sine = jnp.cos(turned), jnp.sin(turned)
    ones, zeros = jnp.ones_like(cosine), jnp.zeros_like(cosine)
    cos_q, sin_q = cosine * SCORE_SCALE, sine * SCORE_SCALE
    cos_w = jnp.concatenate([cos_q] * 4 + [cosine] * 2 + [ones] * 2, axis=1)
    sin_w = jnp.concatenate([-sin_q, sin_q] * 2 + [-sine, sine] + [zeros] * 2, axis=1)

    gain_a = attn_gain[None, :]
    gain_m = moe_gain[None, :]
    (
        xd,
        attn,
        qkv,
        mixed,
        middle,
        moe,
        slot_cols,
        slot_rows,
        chosen,
        w_att,
        moe_own,
        slot_given,
        given_rows,
        mid16,
        router_x,
    ) = front(
        block_in[0],
        w_half,
        src_col,
        own_starts,
        cos_w,
        sin_w,
        gain_a,
        gain_m,
        expert_ids[0],
        places[0],
        src_row,
        rows,
        pairs,
    )

    router_x = router_x.reshape(width, LANES)
    gates, packed = router(moe, router_x, chosen)

    acc = carried = None
    summed = []
    final = len(gathered) - 1
    spare = [cotangent[0], mid16]
    full = []
    for i, w in enumerate(gathered):
        own = spare[i] if i < 2 else None
        if i > 0:
            w, *carried = lax.optimization_barrier((w, *carried))
        parts = experts_forward(
            moe, slot_rows, slot_given, packed, w, acc, own, bases[i], i == final, capacity, 3 + i
        )
        kept, acc = parts[:4], parts[4]
        full += parts[5:]
        rows_in = given_rows
        if i == final:
            rows_in = lax.optimization_barrier((given_rows, summed[0]))[0]
        grads, *carried = experts_reverse(
            full[0], rows_in, slot_cols, kept, w, carried, acc, bases[i], i == final, capacity, 7
        )
        summed.append(lax.psum_scatter(grads, "col", scatter_dimension=0, tiled=False))
    es = acc
    dm, dgates, e_mix, e_across, e_half = carried
    block_out, input_grad, att_grad, small = backward(
        dm,
        es,
        e_mix,
        e_half,
        dgates,
        full[1],
        full[0],
        gates[:tokens],
        middle,
        moe_own,
        src_col[:tokens],
        mixed,
        qkv,
        attn,
        xd,
        w_att,
        router_x,
        own_starts,
        cos_w,
        sin_w,
        gain_a,
        gain_m,
        src_row,
    )
    router_all = small[:EXPERT_COUNT].T
    router_grad = lax.dynamic_slice_in_dim(router_all, c * shard, shard, 0)
    def collect(i):
        parts = [g[:, :, i * fe : (i + 1) * fe] for g in summed]
        return jnp.concatenate(parts, axis=0).astype(F32).transpose(1, 0, 2)

    return (
        block_out[None],
        input_grad[None],
        small[EXPERT_COUNT],
        att_grad[:, :qw],
        att_grad[:, qw:],
        small[EXPERT_COUNT + 1],
        router_grad,
        collect(0),
        collect(1),
        collect(2),
    )


def solution(mesh):
    tokens = P("col", "row", None)
    weight = P("col", "row")
    expert = P("col", "row", None)
    return jax.shard_map(
        body,
        mesh=mesh,
        in_specs=(
            tokens,
            tokens,
            P("col", None),
            P("col", None),
            P("col", None, None),
            P("col", None, None),
            P(),
            weight,
            weight,
            P(),
            P("col", None),
            expert,
            expert,
            expert,
        ),
        out_specs=(
            tokens,
            tokens,
            P(),
            weight,
            weight,
            P(),
            P("col", None),
            expert,
            expert,
            expert,
        ),
        check_vma=False,
    )
```

```python
import functools

import jax
import jax.numpy as jnp
from jax import lax
from jax.experimental import pallas as pl
from jax.experimental.pallas import tpu as pltpu
from jax.sharding import PartitionSpec as P

HEAD_WIDTH = 64
QUERY_HEADS = 16
KEY_VALUE_HEADS = 8
EXPERT_COUNT = 32
TOPK = 8
EPSILON = 1e-06
RESIDUAL_SCALE = 0.22
SCORE_SCALE = 0.015625
ROPE_BASE = 10000.0
MASKED = -1e30
LANES = 128
MIB = 1024 * 1024
BF = jnp.bfloat16
F32 = jnp.float32
ANY = pl.BlockSpec(memory_space=pl.ANY)
FULL = pl.BlockSpec(memory_space=pltpu.VMEM)


def mm(a, b):
    return lax.dot_general(a, b, (((1,), (0,)), ((), ())), preferred_element_type=F32)


def mm_nt(a, b):
    return lax.dot_general(a, b, (((1,), (1,)), ((), ())), preferred_element_type=F32)


def mm_tn(a, b):
    return lax.dot_general(a, b, (((0,), (0,)), ((), ())), preferred_element_type=F32)


def iota(shape, dim):
    return lax.broadcasted_iota(jnp.int32, shape, dim)


def params(mib):
    return pltpu.CompilerParams(vmem_limit_bytes=mib * MIB)


def cost(flops, moved):
    return pl.CostEstimate(flops=int(flops), bytes_accessed=int(moved), transcendentals=0)


def row_scale(values):
    return lax.rsqrt(jnp.mean(values * values, axis=-1, keepdims=True) + EPSILON)


def swap_halves(values):
    width = values.shape[-1]
    half = HEAD_WIDTH // 2
    low = (iota(values.shape, 1) % HEAD_WIDTH) < half
    ahead = pltpu.roll(values, width - half, 1)
    behind = pltpu.roll(values, half, 1)
    return jnp.where(low, ahead, behind)


def attention_bias(row0, rows, cols, starts):
    at = iota((rows, cols), 1)
    allowed = (at <= iota((rows, cols), 0) + row0) & (at >= starts)
    return jnp.where(allowed, 0.0, MASKED)


def masked_probs(q, k, bias):
    scores = mm_nt(q, k) + bias
    raised = jnp.exp(scores - jnp.max(scores, axis=-1, keepdims=True))
    return raised * (1.0 / jnp.sum(raised, axis=-1, keepdims=True))


def link(src, dst, sems, index, device):
    return pltpu.make_async_remote_copy(
        src_ref=src,
        dst_ref=dst,
        send_sem=sems.at[0, index],
        recv_sem=sems.at[1, index],
        device_id=device,
        device_id_type=pl.DeviceIdType.MESH,
    )


def greet(devices):
    barrier = pltpu.get_barrier_semaphore()
    for device in devices:
        pl.semaphore_signal(barrier, inc=1, device_id=device, device_id_type=pl.DeviceIdType.MESH)
    pl.semaphore_wait(barrier, len(devices))


class RowGather:
    count = 6

    def __init__(self, own, slot, sems, base, r, c):
        near, far = (r ^ 1, c), (r ^ 2, c)
        self.copies = {
            (1, 1): link(own(1), slot(1, 1), sems, base, near),
            (2, 0): link(own(0), slot(2, 0), sems, base + 1, far),
            (1, 0): link(own(0), slot(1, 0), sems, base + 2, near),
            (2, 1): link(own(1), slot(2, 1), sems, base + 3, far),
            (3, 0): link(slot(2, 0), slot(3, 0), sems, base + 4, near),
            (3, 1): link(slot(1, 1), slot(3, 1), sems, base + 5, far),
        }

    def start(self, half):
        order = ((2, 0), (1, 0)) if half == 0 else ((1, 1), (2, 1))
        for key in order:
            self.copies[key].start()

    def forward(self, half):
        self.copies[(2, 0) if half == 0 else (1, 1)].wait_recv()
        self.copies[(3, half)].start()

    def wait(self, *keys):
        for key in keys:
            self.copies[key].wait_recv()

    def drain(self):
        for copy in self.copies.values():
            copy.wait_send()


def front_kernel(pairs, *refs):
    xin, cot, w_last = refs[:3]
    w_parts = refs[3 : 3 + pairs]
    refs = refs[3 + pairs :]
    src, starts, cos, sin, gain_a, gain_m, ids, spots, src_row = refs[:9]
    xd, attn, qkv, mixed, middle, moe_all, cot_first, slot_cols, slot_rows, gates, packed = refs[9:20]
    w_att, moe, slot_given, given_rows, mid16, w_router, w_next = refs[20:27]
    xb, bias, chosen, sems, local_sems = refs[27:]
    nblk, tokens, width = xb.shape
    half = tokens // 2
    capacity = nblk * tokens * TOPK // EXPERT_COUNT
    qw = w_att.shape[4] * 2 // 3
    rank = w_att.shape[1] * 2 * w_att.shape[3]
    r = lax.axis_index("row")
    c = lax.axis_index("col")
    z = c // 2
    k = c % 2
    both = w_att.shape[4]
    local = EXPERT_COUNT // nblk
    sibling = (r, c ^ 1)
    greet([(r ^ 1, c), (r ^ 2, c), sibling])

    def cut(ref):
        return lambda h: ref.at[pl.ds(h * half, half)]

    def cut_slot(ref):
        return lambda j, h: ref.at[j, pl.ds(h * half, half)]

    def w_slot(j, h):
        return w_att.at[j, pl.ds(h * (pairs // 2), pairs // 2), k]

    n = RowGather.count
    xs = RowGather(cut(xin), cut_slot(xb), sems, 0, r, c)
    ws = RowGather(lambda h: w_slot(0, h), w_slot, sems, n, r, c)
    ms = RowGather(cut(moe), cut_slot(moe_all), sems, 2 * n, r, c)
    base = 3 * n
    share = [link(w_att.at[j, :, k], w_att.at[j, :, k], sems, base + j, sibling) for j in range(nblk)]
    early = [
        link(cot.at[pl.ds(0, half)], cot_first.at[i], sems, base + nblk + 1 + i, (r ^ (1 + i), c))
        for i in range(2)
    ]
    share.append(link(w_router.at[:, k], w_router.at[:, k], sems, base + nblk, sibling))
    xs.start(1)
    xs.start(0)
    keep = [pltpu.make_async_copy(xin, xb.at[0], local_sems.at[0])]
    for i in range(pairs):
        keep.append(
            pltpu.make_async_copy(
                w_parts[i].at[:, pl.ds(0, both)], w_att.at[0, z ^ i, k], local_sems.at[2 + 2 * i]
            )
        )
        keep.append(
            pltpu.make_async_copy(
                w_parts[i].at[:, pl.ds(both, LANES)], w_router.at[z ^ i, k], local_sems.at[3 + 2 * i]
            )
        )
    for copy in keep:
        copy.start()
    seat = pltpu.make_async_copy(w_last, w_next.at[c], local_sems.at[2 + 2 * pairs])
    seat.start()
    for copy in keep:
        copy.wait()
    ws.start(1)
    ws.start(0)
    share[0].start()
    share[nblk].start()
    xs.forward(0)
    xs.forward(1)

    source = src[:tokens, :]

    def pick(at, j):
        return jnp.where(at == iota((tokens, tokens), 1) + j * tokens, 1.0, 0.0).astype(BF)

    x = mm(pick(source, 0), xb[0])
    xs.wait((1, 0))
    x = x + mm(pick(source, 1), xb[1])
    xs.wait((2, 1))
    x = x + mm(pick(source, 2), xb[2])
    ws.forward(0)
    ws.forward(1)
    ws.wait((1, 0), (2, 1))
    share[1].start()
    share[2].start()
    xs.wait((3, 0), (3, 1))
    x = x + mm(pick(source, 3), xb[3])
    xd[...] = x.astype(BF)
    attn[...] = (x * row_scale(x) * gain_a[...]).astype(BF)
    groups = qw // (4 * HEAD_WIDTH)

    def project(j):
        proj = mm(attn[...], w_att[j, :, :, :, :qw].reshape(rank, qw))
        cos_w = jnp.concatenate([cos[...]] * groups, axis=1)
        sin_w = jnp.concatenate([sin[...]] * groups, axis=1)
        turned = proj * cos_w + swap_halves(proj) * sin_w
        qkv[:, pl.ds(pl.multiple_of(j * qw, qw), qw)] = turned.astype(BF)

    ws.wait((3, 0), (3, 1))
    share[3].start()
    for copy in early:
        copy.start()
    for copy in share:
        copy.wait_recv()

    @pl.loop(0, nblk)
    def _(j):
        project(j)

    pair = 2 * HEAD_WIDTH
    for b in range(2):
        rows = slice(b * half, (b + 1) * half)
        span = (b + 1) * half
        bias[:, :span] = attention_bias(b * half, half, span, starts[rows, :])

        @pl.loop(0, groups * nblk)
        def _(g):
            chunk = qkv[:span, pl.ds(pl.multiple_of(g * 2 * pair, 2 * pair), 2 * pair)]
            k_rows = chunk[:, pair : pair + HEAD_WIDTH]
            v_rows = chunk[:, pair + HEAD_WIDTH :]
            outs = []
            for h in range(2):
                q = chunk[b * half :, h * HEAD_WIDTH : (h + 1) * HEAD_WIDTH]
                probs = masked_probs(q, k_rows, bias[:, :span])
                outs.append(mm(probs.astype(BF), v_rows))
            mixed[rows, pl.ds(pl.multiple_of(g * pair, pair), pair)] = jnp.concatenate(
                outs, axis=1
            ).astype(BF)

        if b == 1:
            ms.forward(0)
        ow = w_att.shape[4] - qw
        out = jnp.zeros((half, width), F32)
        for j in range(nblk):
            w_out = w_att[j, :, :, :, qw:].reshape(rank, ow)
            out = out + mm_nt(mixed[rows, j * ow : (j + 1) * ow], w_out)
        mid = xd[rows, :].astype(F32) + RESIDUAL_SCALE * out
        middle[rows, :] = mid
        mid16[rows, :] = mid.astype(BF)
        moe[rows, :] = (mid * row_scale(mid) * gain_m[...]).astype(BF)
        ms.start(b)

    place = pltpu.make_async_copy(moe, moe_all.at[0], local_sems.at[1])
    place.start()

    @pl.loop(0, nblk)
    def _(b):
        at = pl.ds(pl.multiple_of(b * tokens, tokens), tokens)
        there = pl.ds(pl.multiple_of((b ^ r) * tokens, tokens), tokens)
        expert = iota((EXPERT_COUNT, tokens), 0)
        spot = jnp.zeros((EXPERT_COUNT, tokens), F32)
        named = jnp.zeros((EXPERT_COUNT, tokens), F32)
        own_ids = ids[:, there] ^ (r * local)
        own_spots = spots[:, there].astype(F32)
        for i in range(TOPK):
            hit = expert == own_ids[i : i + 1, :]
            named = jnp.where(hit, 1.0, named)
            spot = jnp.where(hit, own_spots[i : i + 1, :], spot)
        slot = jnp.where((named > 0.0) & (spot < capacity), spot, -1.0)
        slot_rows[:, at] = slot[:local, :]
        rest = jnp.zeros((LANES - EXPERT_COUNT, tokens), F32)
        chosen[at, :] = jnp.concatenate([named, rest], axis=0).T
        slot_cols[at, :] = jnp.concatenate([slot, rest - 1.0], axis=0).T

    ms.forward(1)

    @pl.loop(0, nblk)
    def _(b):
        at = pl.ds(pl.multiple_of(b * tokens, tokens), tokens)
        found = jnp.zeros((tokens, LANES), F32)
        for j in range(nblk):
            part = slice(j * tokens, (j + 1) * tokens)
            match = iota((tokens, tokens), 0) + b * tokens == src_row[:, part]
            match = jnp.where(match, 1.0, 0.0).astype(BF)
            value = slot_cols[part, :] + 1.0
            high = jnp.floor(value * 0.0625)
            low = value - 16.0 * high
            found = found + 16.0 * mm(match, high.astype(BF)) + mm(match, low.astype(BF))
        slot_given[at, :] = found - 1.0
        given_rows[:, at] = (found - 1.0).T[: given_rows.shape[0], :]

    def gate_block(j, rows):
        at = slice(j * tokens, (j + 1) * tokens)
        logits = mm(rows, w_router[...].reshape(width, LANES))
        named = chosen[at, :] > 0.0
        logits = jnp.where(named, logits, MASKED)
        top = jnp.max(logits, axis=-1, keepdims=True)
        raised = jnp.where(named, jnp.exp(logits - top), 0.0)
        gate = raised / jnp.sum(raised, axis=-1, keepdims=True)
        if j == 0:
            gates[...] = gate
        own = jnp.where(iota((tokens, LANES), 1) < local, gate, 0.0)
        high, mid, low = split_three(own)
        packed[at, :] = (high + pltpu.roll(mid, local, 1) + pltpu.roll(low, 2 * local, 1)).astype(BF)

    gate_block(0, moe[...])
    place.wait()
    xs.drain()
    for j, keys in ((1, ((1, 0),)), (2, ((2, 1),)), (3, ((3, 0), (3, 1)))):
        ms.wait(*keys)
        get = pltpu.make_async_copy(moe_all.at[j], xb.at[j], local_sems.at[0])
        get.start()
        get.wait()
        gate_block(j, xb[j])
    seat.wait()
    for copy in early:
        copy.wait_recv()
    for gather in (ws, ms):
        gather.drain()
    for copy in share + early:
        copy.wait_send()


def front(xin, cot, w_last, w_parts, tables, nblk):
    tokens, width = xin.shape
    pairs = len(w_parts)
    shard, both = w_parts[0].shape[0], w_parts[0].shape[1] - LANES
    total = nblk * tokens
    qkv_width = nblk * both * 2 // 3
    head_width = nblk * both // 3
    shape = jax.ShapeDtypeStruct
    count = 3 * RowGather.count + nblk + 3
    local = EXPERT_COUNT // nblk
    return pl.pallas_call(
        functools.partial(front_kernel, pairs),
        out_shape=(
            shape((tokens, width), BF),
            shape((tokens, width), BF),
            shape((tokens, qkv_width), BF),
            shape((tokens, head_width), BF),
            shape((tokens, width), F32),
            shape((nblk, tokens, width), BF),
            shape((2, tokens // 2, width), BF),
            shape((total, LANES), F32),
            shape((local, total), F32),
            shape((tokens, LANES), F32),
            shape((total, LANES), BF),
            shape((nblk, pairs, 2, shard, both), BF),
            shape((tokens, width), BF),
            shape((total, LANES), F32),
            shape((local, total), F32),
            shape((tokens, width), BF),
            shape((pairs, 2, shard, LANES), BF),
            shape((2 * pairs, *w_last.shape), BF),
        ),
        in_specs=[ANY] * (3 + pairs) + [FULL] * 9,
        out_specs=[FULL] * 5 + [ANY] * 2 + [FULL] * 10 + [ANY],
        scratch_shapes=[
            pltpu.VMEM((nblk, tokens, width), BF),
            pltpu.VMEM((tokens // 2, tokens), F32),
            pltpu.VMEM((total, LANES), F32),
            pltpu.SemaphoreType.DMA((2, count)),
            pltpu.SemaphoreType.DMA((3 + 2 * pairs,)),
        ],
        compiler_params=pltpu.CompilerParams(
            vmem_limit_bytes=58 * MIB, collective_id=1, has_side_effects=True
        ),
        cost_estimate=cost(20e9, 60 * MIB),
        name="attention_forward",
    )(xin, cot, w_last, *w_parts, *tables)


class RowScatter:
    count = 6

    def __init__(self, block, mixed_in, across, landed, sems, base, r, c):
        near, far = (r ^ 1, c), (r ^ 2, c)
        self.copies = {
            "diag0": link(block(3, 0), across(0), sems, base, near),
            "diag1": link(block(3, 1), across(1), sems, base + 1, far),
            "near0": link(block(1, 0), landed(1, 0), sems, base + 2, near),
            "far1": link(block(2, 1), landed(2, 1), sems, base + 3, far),
        }
        if mixed_in is not None:
            self.copies["far0"] = link(mixed_in(0), landed(2, 0), sems, base + 4, far)
            self.copies["near1"] = link(mixed_in(1), landed(1, 1), sems, base + 5, near)

    def start(self):
        for key in ("diag0", "diag1", "near0", "far1"):
            self.copies[key].start()

    def arrived(self, half):
        self.copies["diag0" if half == 0 else "diag1"].wait_recv()

    def send(self, half):
        self.copies["far0" if half == 0 else "near1"].start()

    def finish(self):
        for key in self.copies:
            if not key.startswith("diag"):
                self.copies[key].wait_recv()

    def drain(self):
        for copy in self.copies.values():
            copy.wait_send()


def tree_sum(parts):
    while len(parts) > 1:
        parts = [parts[i] + parts[i + 1] for i in range(0, len(parts), 2)]
    return parts[0]


def plus(a, b):
    return (a.astype(F32) + b.astype(F32)).astype(BF)


def one_hot(hit):
    return jnp.where(hit, 1.0, 0.0).astype(BF)


def lane_column(table, index):
    return jnp.sum(jnp.where(iota(table.shape, 1) == index, table, 0.0), axis=1, keepdims=True)


def split_three(value):
    high = value.astype(BF).astype(F32)
    rest = value - high
    mid = rest.astype(BF).astype(F32)
    return high, mid, rest - mid


def forward_kernel(base, first, last, gathers, stage, local, capacity, *refs):
    moe_hbm, slot_rows, slot_given, packed, w = refs[:5]
    refs = refs[5:]
    if not first:
        acc_in, refs = refs[0], refs[1:]
    early = gathers == "rest"
    if gathers:
        own_hbm, refs = refs[0], refs[1:]
    if early:
        first_hbm, refs = refs[0], refs[1:]
    if stage:
        next_in, refs = refs[0], refs[1:]
    routed_out, gate_out, up_out, weight_out, acc_out = refs[:5]
    refs = refs[5:]
    if gathers:
        all_hbm, refs = refs[0], refs[1:]
    if stage:
        next_out, refs = refs[0], refs[1:]
    moe, acc, sel, given, y1, sems = refs[:6]
    step = pl.program_id(0)
    steps = pl.num_programs(0)
    e = base + step
    ne = y1.shape[0] // capacity
    nblk, tokens, width = moe_hbm.shape
    fe = w.shape[3] // 3
    copies = [
        pltpu.make_async_copy(moe_hbm.at[j], moe.at[pl.ds(j * tokens, tokens)], sems.at[j])
        for j in range(nblk)
    ]
    if not first:
        load = pltpu.make_async_copy(acc_in, acc, sems.at[nblk])
    if gathers:
        link_sems = refs[6]
        r = lax.axis_index("row")
        c = lax.axis_index("col")
        half = tokens // 2
        near, far = (r ^ 1, c), (r ^ 2, c)
        top, bottom = pl.ds(0, half), pl.ds(half, half)
        later = []
        greeted = [near, far]
        if stage:
            line = LineGather(stage, next_in, next_out, refs[7], r, c)
            greeted = greeted + line.devices
        if gathers == "rest":
            begin = [
                link(own_hbm.at[bottom], all_hbm.at[0], link_sems, 0, near),
                link(first_hbm.at[1], all_hbm.at[2], link_sems, 1, near),
                link(own_hbm.at[bottom], all_hbm.at[1], link_sems, 2, far),
            ]
            later = [link(all_hbm.at[0], all_hbm.at[3], link_sems, 3, far)]
        elif gathers == "sides":
            begin = [
                link(own_hbm, all_hbm.at[0], link_sems, 0, near),
                link(own_hbm, all_hbm.at[1], link_sems, 1, far),
            ]
        else:
            begin = [
                link(own_hbm.at[1, top], all_hbm.at[top], link_sems, 0, near),
                link(own_hbm.at[0, bottom], all_hbm.at[bottom], link_sems, 1, far),
            ]

    @pl.when(step == 0)
    def _():
        for copy in copies:
            copy.start()
        if not first:
            load.start()
        if gathers:
            greet(greeted)
            for copy in begin:
                copy.start()
            if stage:
                line.start()

    row = slot_rows[pl.ds(e, 1), :]
    for j in range(nblk):
        at = slice(j * tokens, (j + 1) * tokens)
        sel[:, at] = one_hot(iota((capacity, tokens), 0).astype(F32) == row[:, at])

    @pl.when(step == 0)
    def _():
        for copy in copies:
            copy.wait()

    if early:

        @pl.when(step == steps - 1)
        def _():
            begin[0].wait_recv()
            later[0].start()

    routed_out[0] = mm(sel[...], moe[...]).astype(BF)
    lane = iota((capacity, LANES), 1)
    picked = mm(sel[...], packed[...])
    mine = (lane == e) | (lane == e + local) | (lane == e + 2 * local)
    gate = jnp.sum(jnp.where(mine, picked, 0.0), axis=1, keepdims=True)
    weight_out[0] = jnp.broadcast_to(gate, (capacity, LANES))
    gate_up = mm(routed_out[0], w[:, 0, :, : 2 * fe].reshape(width, 2 * fe))
    gate_in = gate_up[:, :fe]
    up_in = gate_up[:, fe:]
    gate_out[0] = gate_in
    up_out[0] = up_in
    hidden = (gate_in * jax.nn.sigmoid(gate_in) * up_in).astype(BF)
    out = mm_nt(hidden, w[:, 0, :, 2 * fe :].reshape(width, fe))
    y1[pl.ds(pl.multiple_of(step * capacity, capacity), capacity), :] = (gate * out).astype(BF)

    @pl.when(step == steps - 1)
    def _():
        if not first:
            load.wait()

        def put(b):
            at = pl.ds(pl.multiple_of(b * tokens, tokens), tokens)
            if last:
                return pltpu.make_async_copy(moe.at[at], acc_out.at[b], sems.at[b])
            return pltpu.make_async_copy(acc.at[at], acc_out.at[at], sems.at[b])

        @pl.loop(0, nblk)
        def _(b):
            at = pl.ds(pl.multiple_of(b * tokens, tokens), tokens)
            slots = iota((tokens, capacity), 1).astype(F32)
            for i in range(ne):
                given[:, i * capacity : (i + 1) * capacity] = one_hot(
                    lane_column(slot_given[at, :], base + i) == slots
                )
            part = mm(given[...], y1[...])
            if not first:
                part = part + acc[at, :]
            if last:
                moe[at, :] = part.astype(BF)
            else:
                acc[at, :] = part
            put(b).start()

        if stage:
            line.finish()
        if gathers:
            for copy in begin[1:] if early else begin:
                copy.wait_recv()
            for copy in later:
                copy.wait_recv()
            for copy in begin + later:
                copy.wait_send()
        for b in range(nblk):
            put(b).wait()


def experts_forward(moe, slot_rows, slot_given, packed, w, acc, moved, later, base, last, capacity, key):
    nblk, tokens, width = moe.shape
    total = nblk * tokens
    cols, ne, shard, fe3 = w.shape
    fe = fe3 // 3
    local = EXPERT_COUNT // nblk
    first = acc is None
    gathers, *sent = moved
    landing = {"rest": (4, tokens // 2), "sides": (2, tokens), "corner": (tokens,)}[gathers]
    shape = jax.ShapeDtypeStruct
    wspec = pl.BlockSpec((cols, 1, shard, fe3), lambda s: (0, s, 0, 0))

    def each(*dims):
        return pl.BlockSpec((1, *dims), lambda s: (s, 0, 0))

    ins = [moe, slot_rows, slot_given, packed, w]
    in_specs = [ANY, FULL, FULL, FULL, wspec]
    aliases = {}
    if not first:
        ins.append(acc)
        in_specs.append(ANY)
        if not last:
            aliases = {len(ins) - 1: 4}
    outs = [
        shape((ne, capacity, width), BF),
        shape((ne, capacity, fe), F32),
        shape((ne, capacity, fe), F32),
        shape((ne, capacity, LANES), F32),
        shape((nblk, tokens, width), BF) if last else shape((total, width), F32),
    ]
    out_specs = [each(capacity, width), each(capacity, fe), each(capacity, fe), each(capacity, LANES), ANY]
    scratch = [
        pltpu.VMEM((total, width), BF),
        pltpu.VMEM((total, width), F32),
        pltpu.VMEM((capacity, total), BF),
        pltpu.VMEM((tokens, ne * capacity), BF),
        pltpu.VMEM((ne * capacity, width), BF),
        pltpu.SemaphoreType.DMA((nblk + 1,)),
    ]
    options = dict(vmem_limit_bytes=58 * MIB)
    ins += sent
    in_specs += [ANY] * len(sent)
    outs.append(shape((*landing, width), BF))
    out_specs.append(ANY)
    scratch.append(pltpu.SemaphoreType.DMA((2, 4)))
    stage, following = later
    if stage:
        aliases = {**aliases, len(ins): len(outs)}
        ins.append(following)
        in_specs.append(ANY)
        outs.append(shape(following.shape, BF))
        out_specs.append(ANY)
        scratch.append(LineGather.scratch(cols // 2))
    options.update(collective_id=key, has_side_effects=True)
    return pl.pallas_call(
        functools.partial(forward_kernel, base, first, last, gathers, stage, local, capacity),
        grid=(ne,),
        out_shape=outs,
        in_specs=in_specs,
        out_specs=out_specs,
        scratch_shapes=scratch,
        input_output_aliases=aliases,
        compiler_params=pltpu.CompilerParams(**options),
        cost_estimate=cost(7e9 * ne, 30 * MIB),
        name="experts_forward",
    )(*ins)


class LineGather:
    def __init__(self, stage, src, dst, sems, r, c):
        self.pairs = src.shape[0] // 2
        self.stage, self.src, self.dst, self.sems = stage, src, dst, sems
        self.z, self.k = c // 2, c % 2
        count = 2 * self.pairs
        hops = list(range(1, self.pairs))
        cut = [(len(hops) * i) // 3 for i in range(4)]
        self.hops = hops[cut[stage - 1] : cut[stage]] if stage < 4 else []
        self.swaps = []
        if stage == 4:
            self.devices = [(r, c ^ 1)]
            for i in range(self.pairs):
                slot = 2 * i + self.k
                self.swaps.append(link(src.at[slot], dst.at[slot], sems, i, (r, c ^ 1)))
        else:
            self.devices = [(r, (c + 2) % count), (r, (c - 2) % count)]

    def place(self, side):
        return self.z if side == 0 else self.pairs - 1 - self.z

    def copy(self, side, hop):
        at = jnp.maximum(self.place(side) - hop + 1, 0)
        slot = 2 * (at if side == 0 else self.pairs - 1 - at) + self.k
        src = self.src if hop == self.hops[0] else self.dst
        index = side * (self.pairs - 1) + hop - 1
        return link(src.at[slot], self.dst.at[slot], self.sems, index, self.devices[side])

    def sends(self, side, hop):
        return (self.place(side) >= hop - 1) & (self.place(side) <= self.pairs - 2)

    def hop(self, hop):
        for side in range(2):

            @pl.when(self.sends(side, hop))
            def _():
                self.copy(side, hop).start()

    def start(self):
        for copy in self.swaps:
            copy.start()
        if self.hops:
            self.hop(self.hops[0])

    def finish(self):
        for copy in self.swaps:
            copy.wait_recv()
        for hop in self.hops:
            for side in range(2):

                @pl.when(self.place(side) >= hop)
                def _():
                    self.copy(side, hop).wait_recv()

            if hop != self.hops[-1]:
                self.hop(hop + 1)
        for hop in self.hops:
            for side in range(2):

                @pl.when(self.sends(side, hop))
                def _():
                    self.copy(side, hop).wait_send()

        for copy in self.swaps:
            copy.wait_send()

    @staticmethod
    def scratch(pairs):
        return pltpu.SemaphoreType.DMA((2, 2 * pairs))


def cot_pieces(own, first, rest):
    half = own.shape[0] // 2
    return [
        own.at[pl.ds(0, half)],
        own.at[pl.ds(half, half)],
        first.at[0],
        rest.at[0],
        first.at[1],
        rest.at[1],
        rest.at[2],
        rest.at[3],
    ]


def reverse_kernel(base, first, last, stage, local, capacity, *refs):
    cot_own, cot_first, cot_rest, given_rows, slot_cols, routed, gate_in_ref, up_in_ref, weight_ref, w = refs[:10]
    refs = refs[10:]
    if not first:
        acc_in, accg_in = refs[:2]
        refs = refs[2:]
    if last:
        es, refs = refs[0], refs[1:]
    if stage:
        next_in, refs = refs[0], refs[1:]
    grads, acc_out, accg_out = refs[:3]
    refs = refs[3:]
    if last:
        e_mix, e_across, e_landed = refs[:3]
        refs = refs[3:]
    if stage:
        next_out, refs = refs[0], refs[1:]
    cot, acc, accg, sel, chosen, spread, dsl, dslot, y2, sems = refs[:10]
    step = pl.program_id(0)
    steps = pl.num_programs(0)
    e = base + step
    tokens, width = cot_own.shape
    nblk = cot.shape[0] // tokens
    half = tokens // 2
    cols, _, shard, fe = w.shape
    fe = fe // 3
    ne = y2.shape[0] // capacity
    copies = [
        pltpu.make_async_copy(piece, cot.at[pl.ds(j * half, half)], sems.at[j])
        for j, piece in enumerate(cot_pieces(cot_own, cot_first, cot_rest))
    ]
    if not first:
        loads = [
            pltpu.make_async_copy(acc_in, acc, sems.at[2 * nblk]),
            pltpu.make_async_copy(accg_in, accg, sems.at[2 * nblk + 1]),
        ]
    r = lax.axis_index("row")
    c = lax.axis_index("col")
    if stage:
        line = LineGather(stage, next_in, next_out, refs[10], r, c)
    if last:
        e_vmem, link_sems = refs[10:]
        scatter = RowScatter(
            lambda j, h: es.at[j, pl.ds(h * half, half)],
            None,
            lambda h: e_across.at[h],
            lambda j, h: e_landed.at[h],
            link_sems,
            0,
            r,
            c,
        )

    @pl.when(step == 0)
    def _():
        for copy in copies:
            copy.start()
        if not first:
            for copy in loads:
                copy.start()
        if last:
            greet([(r ^ 1, c), (r ^ 2, c)])
            scatter.start()
        if stage:
            greet(line.devices)
            line.start()

    row = given_rows[pl.ds(e, 1), :]
    for j in range(nblk):
        at = slice(j * tokens, (j + 1) * tokens)
        sel[:, at] = one_hot(iota((capacity, tokens), 0).astype(F32) == row[:, at])

    @pl.when(step == 0)
    def _():
        for copy in copies:
            copy.wait()

    gate = weight_ref[0, :, :1]

    rows = (RESIDUAL_SCALE * mm(sel[...], cot[...])).astype(BF)
    dsl[...] = rows
    dslot[...] = (gate * rows.astype(F32)).astype(BF)
    gate_in = gate_in_ref[0]
    up_in = up_in_ref[0]
    sig = jax.nn.sigmoid(gate_in)
    silu = gate_in * sig
    hidden = (silu * up_in).astype(BF)
    dhidden = mm(dslot[...], w[:, 0, :, 2 * fe :].reshape(width, fe))
    dgate = (dhidden * up_in * sig * (1.0 + gate_in * (1.0 - sig))).astype(BF)
    dup = (dhidden * silu).astype(BF)
    both = jnp.concatenate([dgate, dup], axis=1)
    out = mm_nt(hidden, w[:, 0, :, 2 * fe :].reshape(width, fe))
    inner = jnp.sum(dsl[...].astype(F32) * out, axis=1, keepdims=True)
    grads[:, 0, :, 2 * fe :] = mm_tn(dslot[...], hidden).astype(BF).reshape(cols, shard, fe)
    grads[:, 0, :, : 2 * fe] = mm_tn(routed[0], both).astype(BF).reshape(cols, shard, 2 * fe)
    mine = pl.ds(pl.multiple_of(step * capacity, capacity), capacity)
    y2[mine, :] = mm_nt(both, w[:, 0, :, : 2 * fe].reshape(width, 2 * fe)).astype(BF)
    high, mid, low = split_three(inner)
    lane = iota((capacity, LANES), 1)
    spread[mine, :] = jnp.where(
        lane == e,
        high,
        jnp.where(lane == e + local, mid, jnp.where(lane == e + 2 * local, low, 0.0)),
    ).astype(BF)

    @pl.when(step == steps - 1)
    def _():
        if not first:
            for copy in loads:
                copy.wait()

        def put(b):
            at = pl.ds(pl.multiple_of(b * tokens, tokens), tokens)
            if last:
                return pltpu.make_async_copy(cot.at[at], acc_out.at[b], sems.at[b])
            return pltpu.make_async_copy(acc.at[at], acc_out.at[at], sems.at[b])

        @pl.loop(0, nblk)
        def _(b):
            at = pl.ds(pl.multiple_of(b * tokens, tokens), tokens)
            slots = iota((tokens, capacity), 1).astype(F32)
            for i in range(ne):
                chosen[:, i * capacity : (i + 1) * capacity] = one_hot(
                    lane_column(slot_cols[at, :], base + i) == slots
                )
            part = mm(chosen[...], y2[...])
            partg = mm(chosen[...], spread[...])
            if not first:
                part = part + acc[at, :]
                partg = partg + accg[at, :]
            if last:
                cot[at, :] = part.astype(BF)
            else:
                acc[at, :] = part
            accg[at, :] = partg
            put(b).start()

        if last:
            summed = accg[...]
            summed = (
                summed
                + pltpu.roll(summed, LANES - local, 1)
                + pltpu.roll(summed, LANES - 2 * local, 1)
            )
            accg_out[...] = summed.T[:local, :]
            for h in range(2):
                scatter.arrived(h)
                gets = [
                    pltpu.make_async_copy(
                        es.at[2 - h, pl.ds(h * half, half)], e_vmem.at[0], sems.at[nblk]
                    ),
                    pltpu.make_async_copy(e_across.at[h], e_vmem.at[1], sems.at[nblk + 1]),
                ]
                for copy in gets:
                    copy.start()
                for copy in gets:
                    copy.wait()
                e_vmem[0] = plus(e_vmem[0], e_vmem[1])
                back = pltpu.make_async_copy(e_vmem.at[0], e_mix.at[h], sems.at[nblk])
                back.start()
                back.wait()
            scatter.finish()
            scatter.drain()
        else:
            out_g = pltpu.make_async_copy(accg, accg_out, sems.at[nblk])
            out_g.start()
            if stage:
                line.finish()
            out_g.wait()
        for b in range(nblk):
            put(b).wait()


def experts_reverse(cots, given_rows, slot_cols, kept, w, carried, es, later, base, last, capacity, key):
    tokens, width = cots[0].shape
    nblk = EXPERT_COUNT // given_rows.shape[0]
    half = tokens // 2
    total = nblk * tokens
    cols, ne, shard, fe3 = w.shape
    fe = fe3 // 3
    local = EXPERT_COUNT // nblk
    first = carried is None
    shape = jax.ShapeDtypeStruct
    wspec = pl.BlockSpec((cols, 1, shard, fe3), lambda s: (0, s, 0, 0))

    def each(*dims):
        return pl.BlockSpec((1, *dims), lambda s: (s, 0, 0))

    ins = [*cots, given_rows, slot_cols, *kept, w]
    in_specs = [
        ANY,
        ANY,
        ANY,
        FULL,
        FULL,
        each(capacity, width),
        each(capacity, fe),
        each(capacity, fe),
        each(capacity, LANES),
        wspec,
    ]
    aliases = {}
    if not first:
        ins += list(carried)
        in_specs += [ANY, ANY]
        if not last:
            aliases = {len(ins) - 2: 1, len(ins) - 1: 2}
    if last:
        outs = [
            shape(w.shape, BF),
            shape((nblk, tokens, width), BF),
            shape((local, total), F32),
            shape((2, half, width), BF),
            shape((2, half, width), BF),
            shape((2, half, width), BF),
        ]
        out_specs = [wspec, ANY, FULL, ANY, ANY, ANY]
        ins.append(es)
        in_specs.append(ANY)
    else:
        outs = [shape(w.shape, BF), shape((total, width), F32), shape((total, LANES), F32)]
        out_specs = [wspec, ANY, ANY]
    scratch = [
        pltpu.VMEM((total, width), BF),
        pltpu.VMEM((total, width), F32),
        pltpu.VMEM((total, LANES), F32),
        pltpu.VMEM((capacity, total), BF),
        pltpu.VMEM((tokens, ne * capacity), BF),
        pltpu.VMEM((ne * capacity, LANES), BF),
        pltpu.VMEM((capacity, width), BF),
        pltpu.VMEM((capacity, width), BF),
        pltpu.VMEM((ne * capacity, width), BF),
        pltpu.SemaphoreType.DMA((2 * nblk + 2,)),
    ]
    options = dict(vmem_limit_bytes=61 * MIB)
    if last:
        scratch += [
            pltpu.VMEM((2, half, width), BF),
            pltpu.SemaphoreType.DMA((2, RowScatter.count)),
        ]
        options.update(collective_id=key, has_side_effects=True)
    stage, following = later
    if stage:
        aliases = {**aliases, len(ins): len(outs)}
        ins.append(following)
        in_specs.append(ANY)
        outs.append(shape(following.shape, BF))
        out_specs.append(ANY)
        scratch.append(LineGather.scratch(cols // 2))
        options.update(collective_id=key, has_side_effects=True)
    return pl.pallas_call(
        functools.partial(reverse_kernel, base, first, last, stage, local, capacity),
        grid=(ne,),
        out_shape=outs,
        in_specs=in_specs,
        out_specs=out_specs,
        scratch_shapes=scratch,
        input_output_aliases=aliases,
        compiler_params=pltpu.CompilerParams(**options),
        cost_estimate=cost(9e9 * ne, 40 * MIB),
        name="experts_reverse",
    )(*ins)


class WeightScatter:
    def __init__(self, full, mate, across, landed, own, others, sems, base, r, c):
        nblk, self.pairs = full.shape[0], full.shape[1]
        self.full, self.mate, self.across, self.landed = full, mate, across, landed
        self.own, self.others = own, others
        self.z, self.k = c // 2, c % 2
        z, k, step = self.z, self.k, self.pairs // 2
        self.part = lambda h: pl.ds(h * step, step)
        self.shares = [
            link(full.at[j, :, 1 - k], mate.at[j], sems, base + j, (r, c ^ 1)) for j in range(nblk)
        ]
        self.rows = RowScatter(
            lambda j, h: full.at[j, self.part(h), k],
            lambda h: full.at[2 - h, self.part(h), k],
            lambda h: across.at[h],
            lambda j, h: landed.at[j - 1, self.part(h)],
            sems,
            base + nblk,
            r,
            c,
        )
        self.line = [
            link(
                own.at[z ^ i],
                others.at[i - 1],
                sems,
                base + nblk + RowScatter.count + i - 1,
                (r, 2 * (z ^ i) + k),
            )
            for i in range(1, self.pairs)
        ]

    def share(self, j):
        self.shares[j].start()

    def join(self):
        mine = pl.ds(self.k, 1)
        for j in (3, 1, 2, 0):
            self.shares[j].wait_recv()
            self.full[j, :, mine] = plus(self.full[j, :, mine], self.mate[j][:, None])
        self.rows.start()

    def middle(self):
        mine = pl.ds(self.k, 1)
        for h in range(2):
            self.rows.arrived(h)
            at = self.part(h)
            self.full[2 - h, at, mine] = plus(self.full[2 - h, at, mine], self.across[h][:, None])
            self.rows.send(h)

    def settle(self):
        self.rows.finish()
        self.own[...] = (
            self.full[0, :, pl.ds(self.k, 1)].reshape(self.own.shape).astype(F32)
            + (self.landed[0].astype(F32) + self.landed[1].astype(F32))
        ).astype(BF)
        for copy in self.line:
            copy.start()

    def result(self):
        for copy in self.line:
            copy.wait_recv()
        shape = self.own.shape[1:]
        return tree_sum(
            [self.own[pl.ds(self.z, 1)].reshape(shape).astype(F32)]
            + [self.others[i].astype(F32) for i in range(self.pairs - 1)]
        )

    def drain(self):
        self.rows.drain()
        for copy in self.shares + self.line:
            copy.wait_send()

    @staticmethod
    def count(nblk, pairs):
        return nblk + RowScatter.count + pairs - 1

    @staticmethod
    def scratch(nblk, pairs, shard, width):
        return [
            pltpu.VMEM((nblk, pairs, 2, shard, width), BF),
            pltpu.VMEM((nblk, pairs, shard, width), BF),
            pltpu.VMEM((2, pairs // 2, shard, width), BF),
            pltpu.VMEM((2, pairs, shard, width), BF),
            pltpu.VMEM((pairs, shard, width), BF),
            pltpu.VMEM((pairs - 1, shard, width), BF),
        ]


class SmallSum:
    def __init__(self, own, mate, chip, row_in, row, line_in, sems, base, sliced, r, c):
        pairs = line_in.shape[0] + 1
        self.refs = (own, mate, chip, row_in, row, line_in)
        self.z, self.sliced = c // 2, sliced
        z, k = c // 2, c % 2
        self.share = link(own, mate, sems, base, (r, c ^ 1))
        count = row_in.shape[0]
        self.rows = [
            link(chip, row_in.at[j], sems, base + 1 + j, (r ^ (j + 1), c)) for j in range(count)
        ]
        self.line = [
            link(
                row.at[z ^ i] if sliced else row,
                line_in.at[i - 1],
                sems,
                base + count + i,
                (r, 2 * (z ^ i) + k),
            )
            for i in range(1, pairs)
        ]

    def over_row(self):
        own, mate, chip = self.refs[:3]
        self.share.wait_recv()
        chip[...] = own[...] + mate[...]
        for copy in self.rows:
            copy.start()

    def over_line(self):
        chip, row_in, row = self.refs[2:5]
        for copy in self.rows:
            copy.wait_recv()
        row[...] = tree_sum([chip[...]] + [row_in[j] for j in range(row_in.shape[0])])
        for copy in self.line:
            copy.start()

    def result(self):
        row, line_in = self.refs[4:]
        for copy in self.line:
            copy.wait_recv()
        own = row[pl.ds(self.z, 1)].reshape(row.shape[1:]) if self.sliced else row[...]
        return tree_sum([own] + [line_in[i] for i in range(line_in.shape[0])])

    def drain(self):
        for copy in [self.share] + self.rows + self.line:
            copy.wait_send()

    @staticmethod
    def scratch(nblk, pairs, shape, sliced):
        whole = (pairs, *shape) if sliced else shape
        return [
            pltpu.VMEM(whole, F32),
            pltpu.VMEM(whole, F32),
            pltpu.VMEM(whole, F32),
            pltpu.VMEM((nblk - 1, *whole), F32),
            pltpu.VMEM(whole, F32),
            pltpu.VMEM((pairs - 1, *shape), F32),
        ]


def back_kernel(nblk, *refs):
    dm, es, e_mix, e_half, dgates, mid_own, mid_sides, mid_corner = refs[:8]
    cots = cot_pieces(*refs[8:11])
    refs = refs[11:]
    mids = [mid_own, mid_sides.at[0], mid_sides.at[1], mid_corner]
    (gates, middle, moe, src_col, mixed, qkv, attn, xd, w_att, w_router) = refs[:10]
    (starts, cos, sin, gain_a, gain_m, src_row) = refs[10:16]
    (block_out, input_grad, qkv_grad, out_grad, router_out, gains_out, e_rest) = refs[16:23]
    (own, d_across, d_landed, dg_land, igb, dmid, dmix, dproj, dkv, bias) = refs[23:33]
    refs = refs[33:]
    sems, lsems = refs[24:]
    tokens, width = xd.shape
    half = tokens // 2
    local = EXPERT_COUNT // nblk
    pairs = w_att.shape[1]
    shard = w_att.shape[3]
    qw = w_att.shape[4] * 2 // 3
    ow = w_att.shape[4] - qw
    hw = HEAD_WIDTH
    r = lax.axis_index("row")
    c = lax.axis_index("col")
    z = c // 2
    k = c % 2
    row_peers = [(r ^ j, c) for j in range(1, nblk)]
    z_peers = [(r, 2 * (z ^ i) + k) for i in range(1, pairs)]
    sibling = (r, c ^ 1)
    greet(row_peers + z_peers + [sibling])

    def part(h):
        return pl.ds(h * half, half)

    n = RowScatter.count
    dms = RowScatter(
        lambda j, h: dm.at[j, part(h)],
        lambda h: own.at[2 - h, part(h)],
        lambda h: d_across.at[h],
        lambda j, h: d_landed.at[j - 1, part(h)],
        sems,
        0,
        r,
        c,
    )
    ess = [
        link(e_mix.at[0], e_rest.at[0], sems, n, (r ^ 2, c)),
        link(e_mix.at[1], e_rest.at[1], sems, n + 1, (r ^ 1, c)),
    ]
    igs = RowGather(
        lambda h: igb.at[0, part(h)], lambda j, h: igb.at[j, part(h)], sems, 3 * n, r, c
    )
    at = 3 * n + RowGather.count
    dgs = [
        link(dgates.at[:, pl.ds(j * tokens, tokens)], dg_land.at[j - 1], sems, at + j - 1, (r ^ j, c))
        for j in range(1, nblk)
    ]
    at += nblk - 1
    wos = WeightScatter(*refs[:6], sems, at, r, c)
    at += WeightScatter.count(nblk, pairs)
    wqs = WeightScatter(*refs[6:12], sems, at, r, c)
    at += WeightScatter.count(nblk, pairs)
    wo, wq = refs[0], refs[6]
    routers = SmallSum(*refs[12:18], sems, at, True, r, c)
    at += nblk + pairs - 1
    gains = SmallSum(*refs[18:24], sems, at, False, r, c)

    dms.start()
    for copy in dgs:
        copy.start()
    loads = [
        pltpu.make_async_copy(dm.at[0], own.at[0], lsems.at[0]),
        pltpu.make_async_copy(dm.at[1, part(1)], own.at[1, part(1)], lsems.at[1]),
        pltpu.make_async_copy(dm.at[2, part(0)], own.at[2, part(0)], lsems.at[2]),
        pltpu.make_async_copy(middle, dmid, lsems.at[3]),
    ]
    for copy in loads:
        copy.start()

    def match(j):
        hit = iota((tokens, tokens), 0) == src_row[:, j * tokens : (j + 1) * tokens]
        return jnp.where(hit, 1.0, 0.0).astype(BF)

    total = jnp.zeros((tokens, width), F32)
    for j in range(nblk):
        get = pltpu.make_async_copy(mids[j], dmix, lsems.at[4])
        get.start()
        hit = match(j)
        get.wait()
        total = total + mm(hit, dmix[...])
    input_grad[...] = total
    dy = jnp.zeros((tokens, width), F32)
    for j in range(nblk):
        gets = [
            pltpu.make_async_copy(cots[2 * j], dmix.at[pl.ds(0, half)], lsems.at[4]),
            pltpu.make_async_copy(cots[2 * j + 1], dmix.at[pl.ds(half, half)], lsems.at[5]),
        ]
        for copy in gets:
            copy.start()
        hit = one_hot(src_col[...] == iota((tokens, tokens), 1) + j * tokens)
        for copy in gets:
            copy.wait()
        dy = dy + mm(hit, dmix[...])
    dproj[:, :width] = dy.astype(BF)
    for copy in loads:
        copy.wait()
    for h in range(2):
        dms.arrived(h)
        rows = part(h)
        own[2 - h, rows, :] = plus(own[2 - h, rows, :], d_across[h])
        dms.send(h)

    for copy in dgs:
        copy.wait_recv()
    parts = [dgates[:, :tokens]] + [dg_land[j] for j in range(nblk - 1)]
    pad = jnp.zeros((LANES - EXPERT_COUNT, tokens), F32)
    dgate = jnp.concatenate(parts + [pad], axis=0).T
    gate = gates[...]
    dchosen = gate * (dgate - jnp.sum(gate * dgate, axis=1, keepdims=True))
    dlogits = dchosen.astype(BF)
    router_t = mm_tn(dlogits, moe[...])
    for i in range(pairs):
        for j in range(nblk):
            refs[12][i, pl.ds(pl.multiple_of((r ^ j) * local, local), local), :] = router_t[
                j * local : (j + 1) * local, i * 2 * shard : (i + 1) * 2 * shard
            ]
    routers.share.start()
    dmoe = mm_nt(dlogits, w_router[...]) + own[0].astype(F32)
    dms.finish()
    for copy in ess:
        copy.start()
    dmoe = dmoe + (d_landed[0].astype(F32) + d_landed[1].astype(F32))
    mid = dmid[...]
    rr = row_scale(mid)
    scaled = dmoe * gain_m[...]
    inner = jnp.mean(scaled * mid, axis=-1, keepdims=True)
    gain_m_part = jnp.sum(dmoe * mid * rr, axis=0, keepdims=True)
    dmid[...] = dproj[:, :width].astype(F32) + (rr * scaled - mid * (rr * rr * rr) * inner)
    dattn = (RESIDUAL_SCALE * dmid[...]).astype(BF)
    for j in range(nblk):
        cols = slice(j * ow, (j + 1) * ow)
        dmix[:, cols] = mm(dattn, w_att[j, :, :, :, qw:].reshape(width, ow)).astype(BF)
        wo[j] = mm_tn(dattn, mixed[:, cols]).astype(BF).reshape(pairs, 2, shard, ow)
        wos.share(j)
    routers.over_row()

    quad = 4 * hw
    groups = nblk * qw // quad
    gain_a_part = jnp.zeros((1, width), F32)
    for b in (1, 0):
        span = (b + 1) * half
        rows = slice(b * half, (b + 1) * half)
        bias[:, :span] = attention_bias(b * half, half, span, starts[rows, :])

        @pl.loop(0, groups)
        def _(g):
            chunk = qkv[:span, pl.ds(pl.multiple_of(g * quad, quad), quad)]
            dm_chunk = dmix[rows, pl.ds(pl.multiple_of(g * 2 * hw, 2 * hw), 2 * hw)]
            k_rows = chunk[:, 2 * hw : 3 * hw]
            v_rows = chunk[:, 3 * hw :]
            dk = jnp.zeros((span, hw), F32)
            dv = jnp.zeros((span, hw), F32)
            dqs = []
            for h in range(2):
                q = chunk[b * half :, h * hw : (h + 1) * hw]
                dmh = dm_chunk[:, h * hw : (h + 1) * hw]
                probs = masked_probs(q, k_rows, bias[:, :span])
                dprobs = mm_nt(dmh, v_rows)
                total = jnp.sum(probs * dprobs, axis=-1, keepdims=True)
                dscores = (probs * (dprobs - total)).astype(BF)
                dqs.append(mm(dscores, k_rows))
                dk = dk + mm_tn(dscores, q)
                dv = dv + mm_tn(probs.astype(BF), dmh)
            dkv_new = jnp.concatenate([dk, dv], axis=1)
            pair = pl.ds(pl.multiple_of(g * 2 * hw, 2 * hw), 2 * hw)
            if b == 1:
                dkv[:, pair] = dkv_new[:half]
                dkv_own = dkv_new[half:]
            else:
                dkv_own = dkv_new + dkv[:, pair]
            d = jnp.concatenate(dqs + [dkv_own], axis=1)
            d = d * cos[rows, :] - swap_halves(d) * sin[rows, :]
            dproj[rows, pl.ds(pl.multiple_of(g * quad, quad), quad)] = d.astype(BF)

        dattn_in = jnp.zeros((half, width), F32)
        for j in range(nblk):
            dattn_in = dattn_in + mm_nt(
                dproj[rows, j * qw : (j + 1) * qw],
                w_att[j, :, :, :, :qw].reshape(width, qw),
            )
        x = xd[rows, :].astype(F32)
        rx = row_scale(x)
        scaled = dattn_in * gain_a[...]
        inner = jnp.mean(scaled * x, axis=-1, keepdims=True)
        igb[0, rows, :] = (dmid[rows, :] + (rx * scaled - x * (rx * rx * rx) * inner)).astype(BF)
        gain_a_part = gain_a_part + jnp.sum(dattn_in * x * rx, axis=0, keepdims=True)
        igs.start(b)
        if b == 1:
            wos.join()
            routers.over_line()

    refs[18][...] = jnp.concatenate(
        [gain_a_part, gain_m_part, jnp.zeros((6, width), F32)], axis=0
    )
    gains.share.start()
    wos.middle()
    for j in range(nblk):
        wq[j] = (
            mm_tn(attn[...], dproj[:, j * qw : (j + 1) * qw])
            .astype(BF)
            .reshape(pairs, 2, shard, qw)
        )
        wqs.share(j)
    igs.forward(1)
    igs.forward(0)
    gains.over_row()
    wqs.join()

    for copy in ess:
        copy.wait_recv()
    e_gets = [
        pltpu.make_async_copy(es.at[0], own.at[0], lsems.at[0]),
        pltpu.make_async_copy(e_half.at[0], own.at[1, part(0)], lsems.at[1]),
        pltpu.make_async_copy(e_half.at[1], own.at[1, part(1)], lsems.at[2]),
        pltpu.make_async_copy(e_rest.at[0], own.at[2, part(0)], lsems.at[3]),
        pltpu.make_async_copy(e_rest.at[1], own.at[2, part(1)], lsems.at[4]),
    ]
    dms.drain()
    for copy in e_gets:
        copy.start()
    for copy in e_gets:
        copy.wait()
    rest = own[2].astype(F32)
    summed = own[0].astype(F32) + (own[1].astype(F32) + rest)
    block_out[...] = (input_grad[...] + RESIDUAL_SCALE * summed).astype(BF)

    wos.settle()
    wqs.middle()
    gains.over_line()
    igs.wait((1, 0), (2, 1))
    total = mm(match(0), igb[0])
    for j in (1, 2):
        total = total + mm(match(j), igb[j])
    router_out[...] = routers.result()
    out_grad[...] = wos.result()
    wqs.settle()
    igs.wait((3, 0), (3, 1))
    input_grad[...] = total + mm(match(3), igb[3])
    gains_out[...] = gains.result()
    qkv_grad[...] = wqs.result()
    for group in (wos, wqs, igs, routers, gains):
        group.drain()
    for copy in ess + dgs:
        copy.wait_send()


def backward(dm, es, e_mix, e_half, dgates, mids, cots, *rest):
    nblk, tokens, width = dm.shape
    w_att = rest[8]
    pairs, shard, both = w_att.shape[1], w_att.shape[3], w_att.shape[4]
    half = tokens // 2
    local = EXPERT_COUNT // nblk
    shape = jax.ShapeDtypeStruct
    count = (
        3 * RowScatter.count
        + RowGather.count
        + (nblk - 1)
        + 2 * WeightScatter.count(nblk, pairs)
        + 2 * (nblk + pairs - 1)
    )
    router_part = (EXPERT_COUNT, 2 * shard)
    outs = pl.pallas_call(
        functools.partial(back_kernel, nblk),
        out_shape=(
            shape((tokens, width), BF),
            shape((tokens, width), F32),
            shape((shard, both * 2 // 3), F32),
            shape((shard, both // 3), F32),
            shape(router_part, F32),
            shape((8, width), F32),
            shape((2, half, width), BF),
        ),
        in_specs=[ANY] * 4 + [FULL] + [ANY] * 6 + [FULL, ANY] + [FULL] * 14,
        out_specs=[FULL] * 6 + [ANY],
        scratch_shapes=[
            pltpu.VMEM((3, tokens, width), BF),
            pltpu.VMEM((2, half, width), BF),
            pltpu.VMEM((2, tokens, width), BF),
            pltpu.VMEM((nblk - 1, local, tokens), F32),
            pltpu.VMEM((nblk, tokens, width), BF),
            pltpu.VMEM((tokens, width), F32),
            pltpu.VMEM((tokens, width), BF),
            pltpu.VMEM((tokens, 2 * width), BF),
            pltpu.VMEM((half, width), F32),
            pltpu.VMEM((half, tokens), F32),
            *WeightScatter.scratch(nblk, pairs, shard, both // 3),
            *WeightScatter.scratch(nblk, pairs, shard, both * 2 // 3),
            *SmallSum.scratch(nblk, pairs, router_part, True),
            *SmallSum.scratch(nblk, pairs, (8, width), False),
            pltpu.SemaphoreType.DMA((2, count)),
            pltpu.SemaphoreType.DMA((8,)),
        ],
        compiler_params=pltpu.CompilerParams(
            vmem_limit_bytes=62 * MIB, collective_id=2, has_side_effects=True
        ),
        cost_estimate=cost(60e9, 100 * MIB),
        name="attention_backward",
    )(dm, es, e_mix, e_half, dgates, *mids, *cots, *rest)
    return outs[:6]


def collect_kernel(*refs):
    parts, outs = refs[:-3], refs[-3:]
    rows = jnp.concatenate([part[...].astype(F32) for part in parts], axis=0)
    fe = outs[0].shape[2]
    for i in range(3):
        outs[i][...] = jnp.swapaxes(rows[:, :, i * fe : (i + 1) * fe], 0, 1)


def collect(parts):
    count = sum(part.shape[0] for part in parts)
    _, shard, fe3 = parts[0].shape
    step = min(16, shard)
    out = jax.ShapeDtypeStruct((shard, count, fe3 // 3), F32)
    return pl.pallas_call(
        collect_kernel,
        grid=(shard // step,),
        out_shape=[out] * 3,
        in_specs=[pl.BlockSpec((part.shape[0], step, fe3), lambda i: (0, i, 0)) for part in parts],
        out_specs=[pl.BlockSpec((step, count, fe3 // 3), lambda i: (i, 0, 0))] * 3,
        compiler_params=params(32),
        cost_estimate=cost(1e6, 9 * MIB),
        name="collect",
    )(*parts)


def swap_over(value, axis, size, step):
    return lax.ppermute(value, axis, [(i, i ^ step) for i in range(size)])


def spread_rows(value, axis, size, step=1):
    return [value] + [swap_over(value, axis, size, j) for j in range(step, size, step)]


def body(
    block_in,
    cotangent,
    seq_lengths,
    seq_order,
    expert_ids,
    places,
    attn_gain,
    w_qkv,
    w_out,
    moe_gain,
    w_router,
    w_gate,
    w_up,
    w_down,
):
    tokens = block_in.shape[1]
    width = block_in.shape[2]
    rows = lax.axis_size("row")
    cols = lax.axis_size("col")
    total = tokens * rows
    r = lax.axis_index("row")
    c = lax.axis_index("col")
    local = w_gate.shape[1]
    shard = w_gate.shape[0]
    fe = w_gate.shape[2]
    capacity = total * TOPK // EXPERT_COUNT
    pairs = cols // 2
    qw = w_qkv.shape[1]
    ow = w_out.shape[1]

    router_own = jnp.concatenate(
        [lax.dynamic_slice_in_dim(w_router, (r ^ j) * local, local, 1) for j in range(rows)], axis=1
    )
    router_own = jnp.pad(router_own, ((0, 0), (0, LANES - EXPERT_COUNT)))
    w_parts = spread_rows(jnp.concatenate([w_qkv, w_out, router_own], axis=1), "col", cols, 2)

    stacked = jnp.concatenate([w_gate, w_up, w_down], axis=2).transpose(1, 0, 2)
    sizes = [local // 4, local - 5 * local // 8, 3 * local // 8]
    bases = [sum(sizes[:i]) for i in range(len(sizes))]
    pieces = [stacked[i : i + n] for i, n in zip(bases, sizes)]
    pieces[0], pieces[1], *w_parts = lax.optimization_barrier((pieces[0], pieces[1], *w_parts))
    gathered = [lax.all_gather(piece, "col", axis=0) for piece in pieces[:-1]]

    lengths = seq_lengths[0]
    perm = seq_order[0]
    seq_ids = jnp.arange(lengths.shape[0], dtype=jnp.int32)
    picked = perm[:, None] == seq_ids[None, :]
    dealt_len = jnp.sum(jnp.where(picked, lengths[None, :], 0), axis=1)
    before = seq_ids[None, :] < perm[:, None]
    source_base = jnp.sum(jnp.where(before, lengths[None, :], 0), axis=1)
    upto = seq_ids[None, :] <= seq_ids[:, None]
    seq_ends = jnp.sum(jnp.where(upto, dealt_len[None, :], 0), axis=1)
    dealt_start = seq_ends - dealt_len
    turn = r * tokens
    pos = jnp.arange(total, dtype=jnp.int32) ^ turn
    inside = (pos[:, None] >= dealt_start[None, :]) & (pos[:, None] < seq_ends[None, :])
    seq_starts = jnp.sum(jnp.where(inside, dealt_start[None, :], 0), axis=1)
    offset = pos - seq_starts
    source = jnp.sum(jnp.where(inside, source_base[None, :], 0), axis=1) + offset
    source = source ^ turn
    src_col = source[:, None]
    src_row = source[None, :]
    own_offset = offset[:tokens]
    own_starts = (seq_starts[:tokens] - turn)[:, None]

    half = HEAD_WIDTH // 2
    frequency = ROPE_BASE ** (-jnp.arange(half, dtype=F32) * 2.0 / HEAD_WIDTH)
    turned = own_offset.astype(F32)[:, None] * frequency[None, :]
    cosine, sine = jnp.cos(turned), jnp.sin(turned)
    ones, zeros = jnp.ones_like(cosine), jnp.zeros_like(cosine)
    cos_q, sin_q = cosine * SCORE_SCALE, sine * SCORE_SCALE
    cos_w = jnp.concatenate([cos_q] * 4 + [cosine] * 2 + [ones] * 2, axis=1)
    sin_w = jnp.concatenate([-sin_q, sin_q] * 2 + [-sine, sine] + [zeros] * 2, axis=1)

    gain_a = attn_gain[None, :]
    gain_m = moe_gain[None, :]
    (
        xd,
        attn,
        qkv,
        mixed,
        middle,
        moe,
        cot_first,
        slot_cols,
        slot_rows,
        gates,
        packed,
        w_att,
        moe_own,
        slot_given,
        given_rows,
        mid16,
        router_x,
        following,
    ) = front(
        block_in[0],
        cotangent[0],
        pieces[-1],
        w_parts,
        [
            src_col,
            own_starts,
            cos_w,
            sin_w,
            gain_a,
            gain_m,
            expert_ids[0].T,
            places[0].T,
            src_row,
        ],
        rows,
    )
    router_x = router_x.reshape(width, LANES)

    acc = carried = None
    summed = []
    final = len(sizes) - 1
    full = []
    for i in range(len(sizes)):
        w = gathered[i] if i < final else following
        moved = [("rest", cotangent[0], cot_first), ("sides", mid16)]
        moved = moved[i] if i < 2 else ("corner", full[1])
        if i > 0:
            w, *carried = lax.optimization_barrier((w, *carried))
        stage = 2 * i + 1 if i < final else 0
        parts = experts_forward(
            moe, slot_rows, slot_given, packed, w, acc, moved, (stage, following), bases[i], i == final, capacity, 3 + i
        )
        kept, acc = parts[:4], parts[4]
        full.append(parts[5])
        if i == 1:
            held, acc = lax.optimization_barrier((held, acc))
            summed.append(lax.psum_scatter(held, "col", scatter_dimension=0, tiled=False))
        if stage:
            following = parts[6]
            stage += 1
        rows_in = given_rows
        if i == final:
            rows_in = lax.optimization_barrier((given_rows, summed[0]))[0]
        grads, *carried = experts_reverse(
            (cotangent[0], cot_first, full[0]), rows_in, slot_cols, kept, w, carried, acc, (stage, following), bases[i], i == final, capacity, 6 + i
        )
        if stage:
            following = carried.pop()
        if i == 0:
            held = grads
        else:
            summed.append(lax.psum_scatter(grads, "col", scatter_dimension=0, tiled=False))
    es = acc
    dm, dgates, e_mix, e_across, e_half = carried
    block_out, input_grad, qkv_grad, out_grad, router_part, gains = backward(
        dm,
        es,
        e_mix,
        e_half,
        dgates,
        [mid16, full[1], full[2]],
        (cotangent[0], cot_first, full[0]),
        gates,
        middle,
        moe_own,
        src_col[:tokens],
        mixed,
        qkv,
        attn,
        xd,
        w_att,
        router_x,
        own_starts,
        cos_w,
        sin_w,
        gain_a,
        gain_m,
        src_row,
    )
    router_grad = lax.dynamic_slice_in_dim(router_part, c % 2 * shard, shard, 1).T

    gate_grad, up_grad, down_grad = collect(summed)
    return (
        block_out[None],
        input_grad[None],
        gains[0],
        qkv_grad,
        out_grad,
        gains[1],
        router_grad,
        gate_grad,
        up_grad,
        down_grad,
    )


def solution(mesh):
    tokens = P("col", "row", None)
    weight = P("col", "row")
    expert = P("col", "row", None)
    return jax.shard_map(
        body,
        mesh=mesh,
        in_specs=(
            tokens,
            tokens,
            P("col", None),
            P("col", None),
            P("col", None, None),
            P("col", None, None),
            P(),
            weight,
            weight,
            P(),
            P("col", None),
            expert,
            expert,
            expert,
        ),
        out_specs=(
            tokens,
            tokens,
            P(),
            weight,
            weight,
            P(),
            P("col", None),
            expert,
            expert,
            expert,
        ),
        check_vma=False,
    )
```

```python
import functools

import jax
import jax.numpy as jnp
from jax import lax
from jax.experimental import pallas as pl
from jax.experimental.pallas import tpu as pltpu
from jax.sharding import PartitionSpec as P

HEAD_WIDTH = 64
QUERY_HEADS = 16
KEY_VALUE_HEADS = 8
EXPERT_COUNT = 32
TOPK = 8
EPSILON = 1e-06
RESIDUAL_SCALE = 0.22
SCORE_SCALE = 0.015625
ROPE_BASE = 10000.0
MASKED = -1e30
LANES = 128
MIB = 1024 * 1024
BF = jnp.bfloat16
F32 = jnp.float32
ANY = pl.BlockSpec(memory_space=pl.ANY)
FULL = pl.BlockSpec(memory_space=pltpu.VMEM)


def mm(a, b):
    return lax.dot_general(a, b, (((1,), (0,)), ((), ())), preferred_element_type=F32)


def mm_nt(a, b):
    return lax.dot_general(a, b, (((1,), (1,)), ((), ())), preferred_element_type=F32)


def mm_tn(a, b):
    return lax.dot_general(a, b, (((0,), (0,)), ((), ())), preferred_element_type=F32)


def iota(shape, dim):
    return lax.broadcasted_iota(jnp.int32, shape, dim)


def params(mib):
    return pltpu.CompilerParams(vmem_limit_bytes=mib * MIB)


def cost(flops, moved):
    return pl.CostEstimate(flops=int(flops), bytes_accessed=int(moved), transcendentals=0)


def row_scale(values):
    return lax.rsqrt(jnp.mean(values * values, axis=-1, keepdims=True) + EPSILON)


def swap_halves(values):
    width = values.shape[-1]
    half = HEAD_WIDTH // 2
    low = (iota(values.shape, 1) % HEAD_WIDTH) < half
    ahead = pltpu.roll(values, width - half, 1)
    behind = pltpu.roll(values, half, 1)
    return jnp.where(low, ahead, behind)


def attention_bias(row0, rows, cols, starts):
    at = iota((rows, cols), 1)
    allowed = (at <= iota((rows, cols), 0) + row0) & (at >= starts)
    return jnp.where(allowed, 0.0, MASKED)


def masked_probs(q, k, bias):
    scores = mm_nt(q, k) + bias
    raised = jnp.exp(scores - jnp.max(scores, axis=-1, keepdims=True))
    return raised * (1.0 / jnp.sum(raised, axis=-1, keepdims=True))


def link(src, dst, sems, index, device):
    return pltpu.make_async_remote_copy(
        src_ref=src,
        dst_ref=dst,
        send_sem=sems.at[0, index],
        recv_sem=sems.at[1, index],
        device_id=device,
        device_id_type=pl.DeviceIdType.MESH,
    )


def greet(devices):
    barrier = pltpu.get_barrier_semaphore()
    for device in devices:
        pl.semaphore_signal(barrier, inc=1, device_id=device, device_id_type=pl.DeviceIdType.MESH)
    pl.semaphore_wait(barrier, len(devices))


class RowGather:
    count = 6

    def __init__(self, own, slot, sems, base, r, c):
        near, far = (r ^ 1, c), (r ^ 2, c)
        self.copies = {
            (1, 1): link(own(1), slot(1, 1), sems, base, near),
            (2, 0): link(own(0), slot(2, 0), sems, base + 1, far),
            (1, 0): link(own(0), slot(1, 0), sems, base + 2, near),
            (2, 1): link(own(1), slot(2, 1), sems, base + 3, far),
            (3, 0): link(slot(2, 0), slot(3, 0), sems, base + 4, near),
            (3, 1): link(slot(1, 1), slot(3, 1), sems, base + 5, far),
        }

    def start(self, half):
        order = ((2, 0), (1, 0)) if half == 0 else ((1, 1), (2, 1))
        for key in order:
            self.copies[key].start()

    def forward(self, half):
        self.copies[(2, 0) if half == 0 else (1, 1)].wait_recv()
        self.copies[(3, half)].start()

    def wait(self, *keys):
        for key in keys:
            self.copies[key].wait_recv()

    def drain(self):
        for copy in self.copies.values():
            copy.wait_send()


def front_kernel(pairs, *refs):
    xin, cot, w_last = refs[:3]
    w_parts = refs[3 : 3 + pairs]
    refs = refs[3 + pairs :]
    src, starts, cos, sin, gain_a, gain_m, ids, spots, src_row = refs[:9]
    xd, attn, qkv, mixed, middle, moe_all, cot_first, slot_cols, slot_rows, gates, packed = refs[9:20]
    w_att, moe, slot_given, given_rows, mid16, w_router, w_next = refs[20:27]
    xb, bias, chosen, sems, local_sems = refs[27:]
    nblk, tokens, width = xb.shape
    half = tokens // 2
    capacity = nblk * tokens * TOPK // EXPERT_COUNT
    qw = w_att.shape[4] * 2 // 3
    rank = w_att.shape[1] * 2 * w_att.shape[3]
    r = lax.axis_index("row")
    c = lax.axis_index("col")
    z = c // 2
    k = c % 2
    both = w_att.shape[4]
    local = EXPERT_COUNT // nblk
    sibling = (r, c ^ 1)
    greet([(r ^ 1, c), (r ^ 2, c), sibling])

    def cut(ref):
        return lambda h: ref.at[pl.ds(h * half, half)]

    def cut_slot(ref):
        return lambda j, h: ref.at[j, pl.ds(h * half, half)]

    def w_slot(j, h):
        return w_att.at[j, pl.ds(h * (pairs // 2), pairs // 2), k]

    n = RowGather.count
    xs = RowGather(cut(xin), cut_slot(xb), sems, 0, r, c)
    ws = RowGather(lambda h: w_slot(0, h), w_slot, sems, n, r, c)
    ms = RowGather(cut(moe), cut_slot(moe_all), sems, 2 * n, r, c)
    base = 3 * n
    share = [link(w_att.at[j, :, k], w_att.at[j, :, k], sems, base + j, sibling) for j in range(nblk)]
    early = [
        link(cot.at[pl.ds(0, half)], cot_first.at[i], sems, base + nblk + 1 + i, (r ^ (1 + i), c))
        for i in range(2)
    ]
    share.append(link(w_router.at[:, k], w_router.at[:, k], sems, base + nblk, sibling))
    xs.start(1)
    xs.start(0)
    keep = [pltpu.make_async_copy(xin, xb.at[0], local_sems.at[0])]
    for i in range(pairs):
        keep.append(
            pltpu.make_async_copy(
                w_parts[i].at[:, pl.ds(0, both)], w_att.at[0, z ^ i, k], local_sems.at[2 + 2 * i]
            )
        )
        keep.append(
            pltpu.make_async_copy(
                w_parts[i].at[:, pl.ds(both, LANES)], w_router.at[z ^ i, k], local_sems.at[3 + 2 * i]
            )
        )
    for copy in keep:
        copy.start()
    seat = pltpu.make_async_copy(w_last, w_next.at[c], local_sems.at[2 + 2 * pairs])
    seat.start()
    for copy in keep:
        copy.wait()
    ws.start(1)
    ws.start(0)
    share[0].start()
    share[nblk].start()
    xs.forward(0)
    xs.forward(1)

    source = src[:tokens, :]

    def pick(at, j):
        return jnp.where(at == iota((tokens, tokens), 1) + j * tokens, 1.0, 0.0).astype(BF)

    x = mm(pick(source, 0), xb[0])
    xs.wait((1, 0))
    x = x + mm(pick(source, 1), xb[1])
    xs.wait((2, 1))
    x = x + mm(pick(source, 2), xb[2])
    ws.forward(0)
    ws.forward(1)
    ws.wait((1, 0), (2, 1))
    share[1].start()
    share[2].start()
    xs.wait((3, 0), (3, 1))
    x = x + mm(pick(source, 3), xb[3])
    xd[...] = x.astype(BF)
    attn[...] = (x * row_scale(x) * gain_a[...]).astype(BF)
    groups = qw // (4 * HEAD_WIDTH)

    def project(j):
        proj = mm(attn[...], w_att[j, :, :, :, :qw].reshape(rank, qw))
        cos_w = jnp.concatenate([cos[...]] * groups, axis=1)
        sin_w = jnp.concatenate([sin[...]] * groups, axis=1)
        turned = proj * cos_w + swap_halves(proj) * sin_w
        qkv[:, pl.ds(pl.multiple_of(j * qw, qw), qw)] = turned.astype(BF)

    ws.wait((3, 0), (3, 1))
    share[3].start()
    for copy in early:
        copy.start()
    for copy in share:
        copy.wait_recv()

    @pl.loop(0, nblk)
    def _(j):
        project(j)

    pair = 2 * HEAD_WIDTH
    for b in range(2):
        rows = slice(b * half, (b + 1) * half)
        span = (b + 1) * half
        bias[:, :span] = attention_bias(b * half, half, span, starts[rows, :])

        @pl.loop(0, groups * nblk)
        def _(g):
            chunk = qkv[:span, pl.ds(pl.multiple_of(g * 2 * pair, 2 * pair), 2 * pair)]
            k_rows = chunk[:, pair : pair + HEAD_WIDTH]
            v_rows = chunk[:, pair + HEAD_WIDTH :]
            outs = []
            for h in range(2):
                q = chunk[b * half :, h * HEAD_WIDTH : (h + 1) * HEAD_WIDTH]
                probs = masked_probs(q, k_rows, bias[:, :span])
                outs.append(mm(probs.astype(BF), v_rows))
            mixed[rows, pl.ds(pl.multiple_of(g * pair, pair), pair)] = jnp.concatenate(
                outs, axis=1
            ).astype(BF)

        if b == 1:
            ms.forward(0)
        ow = w_att.shape[4] - qw
        out = jnp.zeros((half, width), F32)
        for j in range(nblk):
            w_out = w_att[j, :, :, :, qw:].reshape(rank, ow)
            out = out + mm_nt(mixed[rows, j * ow : (j + 1) * ow], w_out)
        mid = xd[rows, :].astype(F32) + RESIDUAL_SCALE * out
        middle[rows, :] = mid
        mid16[rows, :] = mid.astype(BF)
        moe[rows, :] = (mid * row_scale(mid) * gain_m[...]).astype(BF)
        ms.start(b)

    place = pltpu.make_async_copy(moe, moe_all.at[0], local_sems.at[1])
    place.start()

    @pl.loop(0, nblk)
    def _(b):
        at = pl.ds(pl.multiple_of(b * tokens, tokens), tokens)
        there = pl.ds(pl.multiple_of((b ^ r) * tokens, tokens), tokens)
        expert = iota((EXPERT_COUNT, tokens), 0)
        spot = jnp.zeros((EXPERT_COUNT, tokens), F32)
        named = jnp.zeros((EXPERT_COUNT, tokens), F32)
        own_ids = ids[:, there] ^ (r * local)
        own_spots = spots[:, there].astype(F32)
        for i in range(TOPK):
            hit = expert == own_ids[i : i + 1, :]
            named = jnp.where(hit, 1.0, named)
            spot = jnp.where(hit, own_spots[i : i + 1, :], spot)
        slot = jnp.where((named > 0.0) & (spot < capacity), spot, -1.0)
        slot_rows[:, at] = slot[:local, :]
        rest = jnp.zeros((LANES - EXPERT_COUNT, tokens), F32)
        chosen[at, :] = jnp.concatenate([named, rest], axis=0).T
        slot_cols[at, :] = jnp.concatenate([slot, rest - 1.0], axis=0).T

    ms.forward(1)

    @pl.loop(0, nblk)
    def _(b):
        at = pl.ds(pl.multiple_of(b * tokens, tokens), tokens)
        found = jnp.zeros((tokens, LANES), F32)
        for j in range(nblk):
            part = slice(j * tokens, (j + 1) * tokens)
            match = iota((tokens, tokens), 0) + b * tokens == src_row[:, part]
            match = jnp.where(match, 1.0, 0.0).astype(BF)
            value = slot_cols[part, :] + 1.0
            high = jnp.floor(value * 0.0625)
            low = value - 16.0 * high
            found = found + 16.0 * mm(match, high.astype(BF)) + mm(match, low.astype(BF))
        slot_given[at, :] = found - 1.0
        given_rows[:, at] = (found - 1.0).T[: given_rows.shape[0], :]

    def gate_block(j, rows):
        at = slice(j * tokens, (j + 1) * tokens)
        logits = mm(rows, w_router[...].reshape(width, LANES))
        named = chosen[at, :] > 0.0
        logits = jnp.where(named, logits, MASKED)
        top = jnp.max(logits, axis=-1, keepdims=True)
        raised = jnp.where(named, jnp.exp(logits - top), 0.0)
        gate = raised / jnp.sum(raised, axis=-1, keepdims=True)
        if j == 0:
            gates[...] = gate
        own = jnp.where(iota((tokens, LANES), 1) < local, gate, 0.0)
        high, mid, low = split_three(own)
        packed[at, :] = (high + pltpu.roll(mid, local, 1) + pltpu.roll(low, 2 * local, 1)).astype(BF)

    gate_block(0, moe[...])
    place.wait()
    xs.drain()
    for j, keys in ((1, ((1, 0),)), (2, ((2, 1),)), (3, ((3, 0), (3, 1)))):
        ms.wait(*keys)
        get = pltpu.make_async_copy(moe_all.at[j], xb.at[j], local_sems.at[0])
        get.start()
        get.wait()
        gate_block(j, xb[j])
    seat.wait()
    for copy in early:
        copy.wait_recv()
    for gather in (ws, ms):
        gather.drain()
    for copy in share + early:
        copy.wait_send()


def front(xin, cot, w_last, w_parts, tables, nblk):
    tokens, width = xin.shape
    pairs = len(w_parts)
    shard, both = w_parts[0].shape[0], w_parts[0].shape[1] - LANES
    total = nblk * tokens
    qkv_width = nblk * both * 2 // 3
    head_width = nblk * both // 3
    shape = jax.ShapeDtypeStruct
    count = 3 * RowGather.count + nblk + 3
    local = EXPERT_COUNT // nblk
    return pl.pallas_call(
        functools.partial(front_kernel, pairs),
        out_shape=(
            shape((tokens, width), BF),
            shape((tokens, width), BF),
            shape((tokens, qkv_width), BF),
            shape((tokens, head_width), BF),
            shape((tokens, width), F32),
            shape((nblk, tokens, width), BF),
            shape((2, tokens // 2, width), BF),
            shape((total, LANES), F32),
            shape((local, total), F32),
            shape((tokens, LANES), F32),
            shape((total, LANES), BF),
            shape((nblk, pairs, 2, shard, both), BF),
            shape((tokens, width), BF),
            shape((total, LANES), F32),
            shape((local, total), F32),
            shape((tokens, width), BF),
            shape((pairs, 2, shard, LANES), BF),
            shape((2 * pairs, *w_last.shape), BF),
        ),
        in_specs=[ANY] * (3 + pairs) + [FULL] * 9,
        out_specs=[FULL] * 5 + [ANY] * 2 + [FULL] * 10 + [ANY],
        scratch_shapes=[
            pltpu.VMEM((nblk, tokens, width), BF),
            pltpu.VMEM((tokens // 2, tokens), F32),
            pltpu.VMEM((total, LANES), F32),
            pltpu.SemaphoreType.DMA((2, count)),
            pltpu.SemaphoreType.DMA((3 + 2 * pairs,)),
        ],
        compiler_params=pltpu.CompilerParams(
            vmem_limit_bytes=58 * MIB, collective_id=1, has_side_effects=True
        ),
        cost_estimate=cost(20e9, 60 * MIB),
        name="attention_forward",
    )(xin, cot, w_last, *w_parts, *tables)


class RowScatter:
    count = 6

    def __init__(self, block, mixed_in, across, landed, sems, base, r, c):
        near, far = (r ^ 1, c), (r ^ 2, c)
        self.copies = {
            "diag0": link(block(3, 0), across(0), sems, base, near),
            "diag1": link(block(3, 1), across(1), sems, base + 1, far),
            "near0": link(block(1, 0), landed(1, 0), sems, base + 2, near),
            "far1": link(block(2, 1), landed(2, 1), sems, base + 3, far),
        }
        if mixed_in is not None:
            self.copies["far0"] = link(mixed_in(0), landed(2, 0), sems, base + 4, far)
            self.copies["near1"] = link(mixed_in(1), landed(1, 1), sems, base + 5, near)

    def start(self):
        for key in ("diag0", "diag1", "near0", "far1"):
            self.copies[key].start()

    def arrived(self, half):
        self.copies["diag0" if half == 0 else "diag1"].wait_recv()

    def send(self, half):
        self.copies["far0" if half == 0 else "near1"].start()

    def finish(self):
        for key in self.copies:
            if not key.startswith("diag"):
                self.copies[key].wait_recv()

    def drain(self):
        for copy in self.copies.values():
            copy.wait_send()


def tree_sum(parts):
    while len(parts) > 1:
        parts = [parts[i] + parts[i + 1] for i in range(0, len(parts), 2)]
    return parts[0]


def plus(a, b):
    return (a.astype(F32) + b.astype(F32)).astype(BF)


def one_hot(hit):
    return jnp.where(hit, 1.0, 0.0).astype(BF)


def lane_column(table, index):
    return jnp.sum(jnp.where(iota(table.shape, 1) == index, table, 0.0), axis=1, keepdims=True)


def split_three(value):
    high = value.astype(BF).astype(F32)
    rest = value - high
    mid = rest.astype(BF).astype(F32)
    return high, mid, rest - mid


def forward_kernel(base, first, last, gathers, stage, local, capacity, *refs):
    moe_hbm, slot_rows, slot_given, packed, w = refs[:5]
    refs = refs[5:]
    if not first:
        acc_in, refs = refs[0], refs[1:]
    early = gathers == "rest"
    if gathers:
        own_hbm, refs = refs[0], refs[1:]
    if early:
        first_hbm, refs = refs[0], refs[1:]
    if stage:
        next_in, refs = refs[0], refs[1:]
    routed_out, gate_out, up_out, weight_out, acc_out = refs[:5]
    refs = refs[5:]
    if gathers:
        all_hbm, refs = refs[0], refs[1:]
    if stage:
        next_out, refs = refs[0], refs[1:]
    moe, acc, sel, given, y1, sems = refs[:6]
    step = pl.program_id(0)
    steps = pl.num_programs(0)
    e = base + step
    ne = y1.shape[0] // capacity
    nblk, tokens, width = moe_hbm.shape
    fe = w.shape[3] // 3
    copies = [
        pltpu.make_async_copy(moe_hbm.at[j], moe.at[pl.ds(j * tokens, tokens)], sems.at[j])
        for j in range(nblk)
    ]
    if not first:
        load = pltpu.make_async_copy(acc_in, acc, sems.at[nblk])
    if gathers:
        link_sems = refs[6]
        r = lax.axis_index("row")
        c = lax.axis_index("col")
        half = tokens // 2
        near, far = (r ^ 1, c), (r ^ 2, c)
        top, bottom = pl.ds(0, half), pl.ds(half, half)
        later = []
        greeted = [near, far]
        if stage:
            line = LineGather(stage, next_in, next_out, refs[7], r, c)
            greeted = greeted + line.devices
        if gathers == "rest":
            begin = [
                link(own_hbm.at[bottom], all_hbm.at[0], link_sems, 0, near),
                link(first_hbm.at[1], all_hbm.at[2], link_sems, 1, near),
                link(own_hbm.at[bottom], all_hbm.at[1], link_sems, 2, far),
            ]
            later = [link(all_hbm.at[0], all_hbm.at[3], link_sems, 3, far)]
        elif gathers == "sides":
            begin = [
                link(own_hbm, all_hbm.at[0], link_sems, 0, near),
                link(own_hbm, all_hbm.at[1], link_sems, 1, far),
            ]
        else:
            begin = [
                link(own_hbm.at[1, top], all_hbm.at[top], link_sems, 0, near),
                link(own_hbm.at[0, bottom], all_hbm.at[bottom], link_sems, 1, far),
            ]

    @pl.when(step == 0)
    def _():
        for copy in copies:
            copy.start()
        if not first:
            load.start()
        if gathers:
            greet(greeted)
            for copy in begin:
                copy.start()
            if stage:
                line.start()

    row = slot_rows[pl.ds(e, 1), :]
    for j in range(nblk):
        at = slice(j * tokens, (j + 1) * tokens)
        sel[:, at] = one_hot(iota((capacity, tokens), 0).astype(F32) == row[:, at])

    @pl.when(step == 0)
    def _():
        for copy in copies:
            copy.wait()

    if stage:

        @pl.when(step == steps - 1)
        def _():
            line.advance()

    if early:

        @pl.when(step == steps - 1)
        def _():
            begin[0].wait_recv()
            later[0].start()

    routed_out[0] = mm(sel[...], moe[...]).astype(BF)
    lane = iota((capacity, LANES), 1)
    picked = mm(sel[...], packed[...])
    mine = (lane == e) | (lane == e + local) | (lane == e + 2 * local)
    gate = jnp.sum(jnp.where(mine, picked, 0.0), axis=1, keepdims=True)
    weight_out[0] = jnp.broadcast_to(gate, (capacity, LANES))
    gate_up = mm(routed_out[0], w[:, 0, :, : 2 * fe].reshape(width, 2 * fe))
    gate_in = gate_up[:, :fe]
    up_in = gate_up[:, fe:]
    gate_out[0] = gate_in
    up_out[0] = up_in
    hidden = (gate_in * jax.nn.sigmoid(gate_in) * up_in).astype(BF)
    out = mm_nt(hidden, w[:, 0, :, 2 * fe :].reshape(width, fe))
    y1[pl.ds(pl.multiple_of(step * capacity, capacity), capacity), :] = (gate * out).astype(BF)

    @pl.when(step == steps - 1)
    def _():
        if not first:
            load.wait()

        def put(b):
            at = pl.ds(pl.multiple_of(b * tokens, tokens), tokens)
            if last:
                return pltpu.make_async_copy(moe.at[at], acc_out.at[b], sems.at[b])
            return pltpu.make_async_copy(acc.at[at], acc_out.at[at], sems.at[b])

        @pl.loop(0, nblk)
        def _(b):
            at = pl.ds(pl.multiple_of(b * tokens, tokens), tokens)
            slots = iota((tokens, capacity), 1).astype(F32)
            for i in range(ne):
                given[:, i * capacity : (i + 1) * capacity] = one_hot(
                    lane_column(slot_given[at, :], base + i) == slots
                )
            part = mm(given[...], y1[...])
            if not first:
                part = part + acc[at, :]
            if last:
                moe[at, :] = part.astype(BF)
            else:
                acc[at, :] = part
            put(b).start()

        if stage:
            line.finish()
        if gathers:
            for copy in begin[1:] if early else begin:
                copy.wait_recv()
            for copy in later:
                copy.wait_recv()
            for copy in begin + later:
                copy.wait_send()
        for b in range(nblk):
            put(b).wait()


def experts_forward(moe, slot_rows, slot_given, packed, w, acc, moved, later, base, last, capacity, key):
    nblk, tokens, width = moe.shape
    total = nblk * tokens
    cols, ne, shard, fe3 = w.shape
    fe = fe3 // 3
    local = EXPERT_COUNT // nblk
    first = acc is None
    gathers, *sent = moved
    landing = {"rest": (4, tokens // 2), "sides": (2, tokens), "corner": (tokens,)}[gathers]
    shape = jax.ShapeDtypeStruct
    wspec = pl.BlockSpec((cols, 1, shard, fe3), lambda s: (0, s, 0, 0))

    def each(*dims):
        return pl.BlockSpec((1, *dims), lambda s: (s, 0, 0))

    ins = [moe, slot_rows, slot_given, packed, w]
    in_specs = [ANY, FULL, FULL, FULL, wspec]
    aliases = {}
    if not first:
        ins.append(acc)
        in_specs.append(ANY)
        if not last:
            aliases = {len(ins) - 1: 4}
    outs = [
        shape((ne, capacity, width), BF),
        shape((ne, capacity, fe), F32),
        shape((ne, capacity, fe), F32),
        shape((ne, capacity, LANES), F32),
        shape((nblk, tokens, width), BF) if last else shape((total, width), F32),
    ]
    out_specs = [each(capacity, width), each(capacity, fe), each(capacity, fe), each(capacity, LANES), ANY]
    scratch = [
        pltpu.VMEM((total, width), BF),
        pltpu.VMEM((total, width), F32),
        pltpu.VMEM((capacity, total), BF),
        pltpu.VMEM((tokens, ne * capacity), BF),
        pltpu.VMEM((ne * capacity, width), BF),
        pltpu.SemaphoreType.DMA((nblk + 1,)),
    ]
    options = dict(vmem_limit_bytes=58 * MIB)
    ins += sent
    in_specs += [ANY] * len(sent)
    outs.append(shape((*landing, width), BF))
    out_specs.append(ANY)
    scratch.append(pltpu.SemaphoreType.DMA((2, 4)))
    stage, following = later
    if stage:
        aliases = {**aliases, len(ins): len(outs)}
        ins.append(following)
        in_specs.append(ANY)
        outs.append(shape(following.shape, BF))
        out_specs.append(ANY)
        scratch.append(LineGather.scratch(cols // 2, following.shape[1]))
    options.update(collective_id=key, has_side_effects=True)
    return pl.pallas_call(
        functools.partial(forward_kernel, base, first, last, gathers, stage, local, capacity),
        grid=(ne,),
        out_shape=outs,
        in_specs=in_specs,
        out_specs=out_specs,
        scratch_shapes=scratch,
        input_output_aliases=aliases,
        compiler_params=pltpu.CompilerParams(**options),
        cost_estimate=cost(7e9 * ne, 30 * MIB),
        name="experts_forward",
    )(*ins)


class LineGather:
    def __init__(self, stage, src, dst, sems, r, c):
        self.pairs, self.count = src.shape[0] // 2, src.shape[1]
        self.stage, self.src, self.dst, self.sems = stage, src, dst, sems
        self.z, self.k = c // 2, c % 2
        slots = []
        for slot in range(self.pairs + self.count - 2):
            moves = [(slot - e + 1, e) for e in range(self.count)]
            slots.append([(hop, e) for hop, e in moves if 1 <= hop < self.pairs])
        self.slots = [slots[:1], slots[1:-1], slots[-1:], []][stage - 1]
        self.swaps = []
        if stage == 4:
            self.devices = [(r, c ^ 1)]
            for i in range(self.pairs):
                slot = 2 * i + self.k
                self.swaps.append(link(src.at[slot], dst.at[slot], sems, i, (r, c ^ 1)))
        else:
            devices = 2 * self.pairs
            self.devices = [(r, (c + 2) % devices), (r, (c - 2) % devices)]

    def place(self, side):
        return self.z if side == 0 else self.pairs - 1 - self.z

    def copy(self, side, hop, e):
        at = jnp.maximum(self.place(side) - hop + 1, 0)
        slot = 2 * (at if side == 0 else self.pairs - 1 - at) + self.k
        here = any((hop - 1, e) in moves for moves in self.slots)
        src = self.dst if here else self.src
        index = (side * (self.pairs - 1) + hop - 1) * self.count + e
        return link(
            src.at[slot, e], self.dst.at[slot, e], self.sems, index, self.devices[side]
        )

    def sends(self, side, hop):
        return (self.place(side) >= hop - 1) & (self.place(side) <= self.pairs - 2)

    def send(self, moves):
        for hop, e in moves:
            for side in range(2):

                @pl.when(self.sends(side, hop))
                def _():
                    self.copy(side, hop, e).start()

    def start(self):
        for copy in self.swaps:
            copy.start()
        if self.slots:
            self.send(self.slots[0])

    def land(self, number):
        for hop, e in self.slots[number]:
            for side in range(2):

                @pl.when(self.place(side) >= hop)
                def _():
                    self.copy(side, hop, e).wait_recv()

        if number + 1 < len(self.slots):
            self.send(self.slots[number + 1])

    def advance(self):
        if len(self.slots) > 1:
            self.land(0)

    def finish(self):
        for copy in self.swaps:
            copy.wait_recv()
        for number in range(1 if len(self.slots) > 1 else 0, len(self.slots)):
            self.land(number)
        for moves in self.slots:
            for hop, e in moves:
                for side in range(2):

                    @pl.when(self.sends(side, hop))
                    def _():
                        self.copy(side, hop, e).wait_send()

        for copy in self.swaps:
            copy.wait_send()

    @staticmethod
    def scratch(pairs, count):
        return pltpu.SemaphoreType.DMA((2, max(2 * (pairs - 1) * count, pairs)))


def cot_pieces(own, first, rest):
    half = own.shape[0] // 2
    return [
        own.at[pl.ds(0, half)],
        own.at[pl.ds(half, half)],
        first.at[0],
        rest.at[0],
        first.at[1],
        rest.at[1],
        rest.at[2],
        rest.at[3],
    ]


def reverse_kernel(base, first, last, stage, local, capacity, *refs):
    cot_own, cot_first, cot_rest, given_rows, slot_cols, routed, gate_in_ref, up_in_ref, weight_ref, w = refs[:10]
    refs = refs[10:]
    if not first:
        acc_in, accg_in = refs[:2]
        refs = refs[2:]
    if last:
        es, refs = refs[0], refs[1:]
    if stage:
        next_in, refs = refs[0], refs[1:]
    grads, acc_out, accg_out = refs[:3]
    refs = refs[3:]
    if last:
        e_mix, e_across, e_landed = refs[:3]
        refs = refs[3:]
    if stage:
        next_out, refs = refs[0], refs[1:]
    cot, acc, accg, sel, chosen, spread, dsl, dslot, y2, sems = refs[:10]
    step = pl.program_id(0)
    steps = pl.num_programs(0)
    e = base + step
    tokens, width = cot_own.shape
    nblk = cot.shape[0] // tokens
    half = tokens // 2
    cols, _, shard, fe = w.shape
    fe = fe // 3
    ne = y2.shape[0] // capacity
    copies = [
        pltpu.make_async_copy(piece, cot.at[pl.ds(j * half, half)], sems.at[j])
        for j, piece in enumerate(cot_pieces(cot_own, cot_first, cot_rest))
    ]
    if not first:
        loads = [
            pltpu.make_async_copy(acc_in, acc, sems.at[2 * nblk]),
            pltpu.make_async_copy(accg_in, accg, sems.at[2 * nblk + 1]),
        ]
    r = lax.axis_index("row")
    c = lax.axis_index("col")
    if stage:
        line = LineGather(stage, next_in, next_out, refs[10], r, c)
    if last:
        e_vmem, link_sems = refs[10:]
        scatter = RowScatter(
            lambda j, h: es.at[j, pl.ds(h * half, half)],
            None,
            lambda h: e_across.at[h],
            lambda j, h: e_landed.at[h],
            link_sems,
            0,
            r,
            c,
        )

    @pl.when(step == 0)
    def _():
        for copy in copies:
            copy.start()
        if not first:
            for copy in loads:
                copy.start()
        if last:
            greet([(r ^ 1, c), (r ^ 2, c)])
            scatter.start()
        if stage:
            greet(line.devices)
            line.start()

    row = given_rows[pl.ds(e, 1), :]
    for j in range(nblk):
        at = slice(j * tokens, (j + 1) * tokens)
        sel[:, at] = one_hot(iota((capacity, tokens), 0).astype(F32) == row[:, at])

    @pl.when(step == 0)
    def _():
        for copy in copies:
            copy.wait()

    gate = weight_ref[0, :, :1]

    rows = (RESIDUAL_SCALE * mm(sel[...], cot[...])).astype(BF)
    dsl[...] = rows
    dslot[...] = (gate * rows.astype(F32)).astype(BF)
    gate_in = gate_in_ref[0]
    up_in = up_in_ref[0]
    sig = jax.nn.sigmoid(gate_in)
    silu = gate_in * sig
    hidden = (silu * up_in).astype(BF)
    if stage:

        @pl.when(step == (steps - 1) // 2)
        def _():
            line.advance()

    dhidden = mm(dslot[...], w[:, 0, :, 2 * fe :].reshape(width, fe))
    dgate = (dhidden * up_in * sig * (1.0 + gate_in * (1.0 - sig))).astype(BF)
    dup = (dhidden * silu).astype(BF)
    both = jnp.concatenate([dgate, dup], axis=1)
    out = mm_nt(hidden, w[:, 0, :, 2 * fe :].reshape(width, fe))
    inner = jnp.sum(dsl[...].astype(F32) * out, axis=1, keepdims=True)
    grads[:, 0, :, 2 * fe :] = mm_tn(dslot[...], hidden).astype(BF).reshape(cols, shard, fe)
    grads[:, 0, :, : 2 * fe] = mm_tn(routed[0], both).astype(BF).reshape(cols, shard, 2 * fe)
    mine = pl.ds(pl.multiple_of(step * capacity, capacity), capacity)
    y2[mine, :] = mm_nt(both, w[:, 0, :, : 2 * fe].reshape(width, 2 * fe)).astype(BF)
    high, mid, low = split_three(inner)
    lane = iota((capacity, LANES), 1)
    spread[mine, :] = jnp.where(
        lane == e,
        high,
        jnp.where(lane == e + local, mid, jnp.where(lane == e + 2 * local, low, 0.0)),
    ).astype(BF)

    @pl.when(step == steps - 1)
    def _():
        if not first:
            for copy in loads:
                copy.wait()

        def put(b):
            at = pl.ds(pl.multiple_of(b * tokens, tokens), tokens)
            if last:
                return pltpu.make_async_copy(cot.at[at], acc_out.at[b], sems.at[b])
            return pltpu.make_async_copy(acc.at[at], acc_out.at[at], sems.at[b])

        @pl.loop(0, nblk)
        def _(b):
            at = pl.ds(pl.multiple_of(b * tokens, tokens), tokens)
            slots = iota((tokens, capacity), 1).astype(F32)
            for i in range(ne):
                chosen[:, i * capacity : (i + 1) * capacity] = one_hot(
                    lane_column(slot_cols[at, :], base + i) == slots
                )
            part = mm(chosen[...], y2[...])
            partg = mm(chosen[...], spread[...])
            if not first:
                part = part + acc[at, :]
                partg = partg + accg[at, :]
            if last:
                cot[at, :] = part.astype(BF)
            else:
                acc[at, :] = part
            accg[at, :] = partg
            put(b).start()

        if last:
            summed = accg[...]
            summed = (
                summed
                + pltpu.roll(summed, LANES - local, 1)
                + pltpu.roll(summed, LANES - 2 * local, 1)
            )
            accg_out[...] = summed.T[:local, :]
            for h in range(2):
                scatter.arrived(h)
                gets = [
                    pltpu.make_async_copy(
                        es.at[2 - h, pl.ds(h * half, half)], e_vmem.at[0], sems.at[nblk]
                    ),
                    pltpu.make_async_copy(e_across.at[h], e_vmem.at[1], sems.at[nblk + 1]),
                ]
                for copy in gets:
                    copy.start()
                for copy in gets:
                    copy.wait()
                e_vmem[0] = plus(e_vmem[0], e_vmem[1])
                back = pltpu.make_async_copy(e_vmem.at[0], e_mix.at[h], sems.at[nblk])
                back.start()
                back.wait()
            scatter.finish()
            scatter.drain()
        else:
            out_g = pltpu.make_async_copy(accg, accg_out, sems.at[nblk])
            out_g.start()
            if stage:
                line.finish()
            out_g.wait()
        for b in range(nblk):
            put(b).wait()


def experts_reverse(cots, given_rows, slot_cols, kept, w, carried, es, later, base, last, capacity, key):
    tokens, width = cots[0].shape
    nblk = EXPERT_COUNT // given_rows.shape[0]
    half = tokens // 2
    total = nblk * tokens
    cols, ne, shard, fe3 = w.shape
    fe = fe3 // 3
    local = EXPERT_COUNT // nblk
    first = carried is None
    shape = jax.ShapeDtypeStruct
    wspec = pl.BlockSpec((cols, 1, shard, fe3), lambda s: (0, s, 0, 0))

    def each(*dims):
        return pl.BlockSpec((1, *dims), lambda s: (s, 0, 0))

    ins = [*cots, given_rows, slot_cols, *kept, w]
    in_specs = [
        ANY,
        ANY,
        ANY,
        FULL,
        FULL,
        each(capacity, width),
        each(capacity, fe),
        each(capacity, fe),
        each(capacity, LANES),
        wspec,
    ]
    aliases = {}
    if not first:
        ins += list(carried)
        in_specs += [ANY, ANY]
        if not last:
            aliases = {len(ins) - 2: 1, len(ins) - 1: 2}
    if last:
        outs = [
            shape(w.shape, BF),
            shape((nblk, tokens, width), BF),
            shape((local, total), F32),
            shape((2, half, width), BF),
            shape((2, half, width), BF),
            shape((2, half, width), BF),
        ]
        out_specs = [wspec, ANY, FULL, ANY, ANY, ANY]
        ins.append(es)
        in_specs.append(ANY)
    else:
        outs = [shape(w.shape, BF), shape((total, width), F32), shape((total, LANES), F32)]
        out_specs = [wspec, ANY, ANY]
    scratch = [
        pltpu.VMEM((total, width), BF),
        pltpu.VMEM((total, width), F32),
        pltpu.VMEM((total, LANES), F32),
        pltpu.VMEM((capacity, total), BF),
        pltpu.VMEM((tokens, ne * capacity), BF),
        pltpu.VMEM((ne * capacity, LANES), BF),
        pltpu.VMEM((capacity, width), BF),
        pltpu.VMEM((capacity, width), BF),
        pltpu.VMEM((ne * capacity, width), BF),
        pltpu.SemaphoreType.DMA((2 * nblk + 2,)),
    ]
    options = dict(vmem_limit_bytes=61 * MIB)
    if last:
        scratch += [
            pltpu.VMEM((2, half, width), BF),
            pltpu.SemaphoreType.DMA((2, RowScatter.count)),
        ]
        options.update(collective_id=key, has_side_effects=True)
    stage, following = later
    if stage:
        aliases = {**aliases, len(ins): len(outs)}
        ins.append(following)
        in_specs.append(ANY)
        outs.append(shape(following.shape, BF))
        out_specs.append(ANY)
        scratch.append(LineGather.scratch(cols // 2, following.shape[1]))
        options.update(collective_id=key, has_side_effects=True)
    return pl.pallas_call(
        functools.partial(reverse_kernel, base, first, last, stage, local, capacity),
        grid=(ne,),
        out_shape=outs,
        in_specs=in_specs,
        out_specs=out_specs,
        scratch_shapes=scratch,
        input_output_aliases=aliases,
        compiler_params=pltpu.CompilerParams(**options),
        cost_estimate=cost(9e9 * ne, 40 * MIB),
        name="experts_reverse",
    )(*ins)


class WeightScatter:
    def __init__(self, full, mate, across, landed, own, others, sems, base, r, c):
        nblk, self.pairs = full.shape[0], full.shape[1]
        self.full, self.mate, self.across, self.landed = full, mate, across, landed
        self.own, self.others = own, others
        self.z, self.k = c // 2, c % 2
        z, k, step = self.z, self.k, self.pairs // 2
        self.part = lambda h: pl.ds(h * step, step)
        self.shares = [
            link(full.at[j, :, 1 - k], mate.at[j], sems, base + j, (r, c ^ 1)) for j in range(nblk)
        ]
        self.rows = RowScatter(
            lambda j, h: full.at[j, self.part(h), k],
            lambda h: full.at[2 - h, self.part(h), k],
            lambda h: across.at[h],
            lambda j, h: landed.at[j - 1, self.part(h)],
            sems,
            base + nblk,
            r,
            c,
        )
        self.line = [
            link(
                own.at[z ^ i],
                others.at[i - 1],
                sems,
                base + nblk + RowScatter.count + i - 1,
                (r, 2 * (z ^ i) + k),
            )
            for i in range(1, self.pairs)
        ]

    def share(self, j):
        self.shares[j].start()

    def join(self):
        mine = pl.ds(self.k, 1)
        for j in (3, 1, 2, 0):
            self.shares[j].wait_recv()
            self.full[j, :, mine] = plus(self.full[j, :, mine], self.mate[j][:, None])
        self.rows.start()

    def middle(self):
        mine = pl.ds(self.k, 1)
        for h in range(2):
            self.rows.arrived(h)
            at = self.part(h)
            self.full[2 - h, at, mine] = plus(self.full[2 - h, at, mine], self.across[h][:, None])
            self.rows.send(h)

    def settle(self):
        self.rows.finish()
        self.own[...] = (
            self.full[0, :, pl.ds(self.k, 1)].reshape(self.own.shape).astype(F32)
            + (self.landed[0].astype(F32) + self.landed[1].astype(F32))
        ).astype(BF)
        for copy in self.line:
            copy.start()

    def result(self):
        for copy in self.line:
            copy.wait_recv()
        shape = self.own.shape[1:]
        return tree_sum(
            [self.own[pl.ds(self.z, 1)].reshape(shape).astype(F32)]
            + [self.others[i].astype(F32) for i in range(self.pairs - 1)]
        )

    def drain(self):
        self.rows.drain()
        for copy in self.shares + self.line:
            copy.wait_send()

    @staticmethod
    def count(nblk, pairs):
        return nblk + RowScatter.count + pairs - 1

    @staticmethod
    def scratch(nblk, pairs, shard, width):
        return [
            pltpu.VMEM((nblk, pairs, 2, shard, width), BF),
            pltpu.VMEM((nblk, pairs, shard, width), BF),
            pltpu.VMEM((2, pairs // 2, shard, width), BF),
            pltpu.VMEM((2, pairs, shard, width), BF),
            pltpu.VMEM((pairs, shard, width), BF),
            pltpu.VMEM((pairs - 1, shard, width), BF),
        ]


class SmallSum:
    def __init__(self, own, mate, chip, row_in, row, line_in, sems, base, sliced, r, c):
        pairs = line_in.shape[0] + 1
        self.refs = (own, mate, chip, row_in, row, line_in)
        self.z, self.sliced = c // 2, sliced
        z, k = c // 2, c % 2
        self.share = link(own, mate, sems, base, (r, c ^ 1))
        count = row_in.shape[0]
        self.rows = [
            link(chip, row_in.at[j], sems, base + 1 + j, (r ^ (j + 1), c)) for j in range(count)
        ]
        self.line = [
            link(
                row.at[z ^ i] if sliced else row,
                line_in.at[i - 1],
                sems,
                base + count + i,
                (r, 2 * (z ^ i) + k),
            )
            for i in range(1, pairs)
        ]

    def over_row(self):
        own, mate, chip = self.refs[:3]
        self.share.wait_recv()
        chip[...] = own[...] + mate[...]
        for copy in self.rows:
            copy.start()

    def over_line(self):
        chip, row_in, row = self.refs[2:5]
        for copy in self.rows:
            copy.wait_recv()
        row[...] = tree_sum([chip[...]] + [row_in[j] for j in range(row_in.shape[0])])
        for copy in self.line:
            copy.start()

    def result(self):
        row, line_in = self.refs[4:]
        for copy in self.line:
            copy.wait_recv()
        own = row[pl.ds(self.z, 1)].reshape(row.shape[1:]) if self.sliced else row[...]
        return tree_sum([own] + [line_in[i] for i in range(line_in.shape[0])])

    def drain(self):
        for copy in [self.share] + self.rows + self.line:
            copy.wait_send()

    @staticmethod
    def scratch(nblk, pairs, shape, sliced):
        whole = (pairs, *shape) if sliced else shape
        return [
            pltpu.VMEM(whole, F32),
            pltpu.VMEM(whole, F32),
            pltpu.VMEM(whole, F32),
            pltpu.VMEM((nblk - 1, *whole), F32),
            pltpu.VMEM(whole, F32),
            pltpu.VMEM((pairs - 1, *shape), F32),
        ]


def back_kernel(nblk, *refs):
    dm, es, e_mix, e_half, dgates, mid_own, mid_sides, mid_corner = refs[:8]
    cots = cot_pieces(*refs[8:11])
    refs = refs[11:]
    mids = [mid_own, mid_sides.at[0], mid_sides.at[1], mid_corner]
    (gates, middle, moe, src_col, mixed, qkv, attn, xd, w_att, w_router) = refs[:10]
    (starts, cos, sin, gain_a, gain_m, src_row) = refs[10:16]
    (block_out, input_grad, qkv_grad, out_grad, router_out, gains_out, e_rest) = refs[16:23]
    (own, d_across, d_landed, dg_land, igb, dmid, dmix, dproj, dkv, bias) = refs[23:33]
    refs = refs[33:]
    sems, lsems = refs[24:]
    tokens, width = xd.shape
    half = tokens // 2
    local = EXPERT_COUNT // nblk
    pairs = w_att.shape[1]
    shard = w_att.shape[3]
    qw = w_att.shape[4] * 2 // 3
    ow = w_att.shape[4] - qw
    hw = HEAD_WIDTH
    r = lax.axis_index("row")
    c = lax.axis_index("col")
    z = c // 2
    k = c % 2
    row_peers = [(r ^ j, c) for j in range(1, nblk)]
    z_peers = [(r, 2 * (z ^ i) + k) for i in range(1, pairs)]
    sibling = (r, c ^ 1)
    greet(row_peers + z_peers + [sibling])

    def part(h):
        return pl.ds(h * half, half)

    n = RowScatter.count
    dms = RowScatter(
        lambda j, h: dm.at[j, part(h)],
        lambda h: own.at[2 - h, part(h)],
        lambda h: d_across.at[h],
        lambda j, h: d_landed.at[j - 1, part(h)],
        sems,
        0,
        r,
        c,
    )
    ess = [
        link(e_mix.at[0], e_rest.at[0], sems, n, (r ^ 2, c)),
        link(e_mix.at[1], e_rest.at[1], sems, n + 1, (r ^ 1, c)),
    ]
    igs = RowGather(
        lambda h: igb.at[0, part(h)], lambda j, h: igb.at[j, part(h)], sems, 3 * n, r, c
    )
    at = 3 * n + RowGather.count
    dgs = [
        link(dgates.at[:, pl.ds(j * tokens, tokens)], dg_land.at[j - 1], sems, at + j - 1, (r ^ j, c))
        for j in range(1, nblk)
    ]
    at += nblk - 1
    wos = WeightScatter(*refs[:6], sems, at, r, c)
    at += WeightScatter.count(nblk, pairs)
    wqs = WeightScatter(*refs[6:12], sems, at, r, c)
    at += WeightScatter.count(nblk, pairs)
    wo, wq = refs[0], refs[6]
    routers = SmallSum(*refs[12:18], sems, at, True, r, c)
    at += nblk + pairs - 1
    gains = SmallSum(*refs[18:24], sems, at, False, r, c)

    dms.start()
    for copy in dgs:
        copy.start()
    loads = [
        pltpu.make_async_copy(dm.at[0], own.at[0], lsems.at[0]),
        pltpu.make_async_copy(dm.at[1, part(1)], own.at[1, part(1)], lsems.at[1]),
        pltpu.make_async_copy(dm.at[2, part(0)], own.at[2, part(0)], lsems.at[2]),
        pltpu.make_async_copy(middle, dmid, lsems.at[3]),
    ]
    for copy in loads:
        copy.start()

    def match(j):
        hit = iota((tokens, tokens), 0) == src_row[:, j * tokens : (j + 1) * tokens]
        return jnp.where(hit, 1.0, 0.0).astype(BF)

    total = jnp.zeros((tokens, width), F32)
    for j in range(nblk):
        get = pltpu.make_async_copy(mids[j], dmix, lsems.at[4])
        get.start()
        hit = match(j)
        get.wait()
        total = total + mm(hit, dmix[...])
    input_grad[...] = total
    dy = jnp.zeros((tokens, width), F32)
    for j in range(nblk):
        gets = [
            pltpu.make_async_copy(cots[2 * j], dmix.at[pl.ds(0, half)], lsems.at[4]),
            pltpu.make_async_copy(cots[2 * j + 1], dmix.at[pl.ds(half, half)], lsems.at[5]),
        ]
        for copy in gets:
            copy.start()
        hit = one_hot(src_col[...] == iota((tokens, tokens), 1) + j * tokens)
        for copy in gets:
            copy.wait()
        dy = dy + mm(hit, dmix[...])
    dproj[:, :width] = dy.astype(BF)
    for copy in loads:
        copy.wait()
    for h in range(2):
        dms.arrived(h)
        rows = part(h)
        own[2 - h, rows, :] = plus(own[2 - h, rows, :], d_across[h])
        dms.send(h)

    for copy in dgs:
        copy.wait_recv()
    parts = [dgates[:, :tokens]] + [dg_land[j] for j in range(nblk - 1)]
    pad = jnp.zeros((LANES - EXPERT_COUNT, tokens), F32)
    dgate = jnp.concatenate(parts + [pad], axis=0).T
    gate = gates[...]
    dchosen = gate * (dgate - jnp.sum(gate * dgate, axis=1, keepdims=True))
    dlogits = dchosen.astype(BF)
    router_t = mm_tn(dlogits, moe[...])
    for i in range(pairs):
        for j in range(nblk):
            refs[12][i, pl.ds(pl.multiple_of((r ^ j) * local, local), local), :] = router_t[
                j * local : (j + 1) * local, i * 2 * shard : (i + 1) * 2 * shard
            ]
    routers.share.start()
    dmoe = mm_nt(dlogits, w_router[...]) + own[0].astype(F32)
    dms.finish()
    for copy in ess:
        copy.start()
    dmoe = dmoe + (d_landed[0].astype(F32) + d_landed[1].astype(F32))
    mid = dmid[...]
    rr = row_scale(mid)
    scaled = dmoe * gain_m[...]
    inner = jnp.mean(scaled * mid, axis=-1, keepdims=True)
    gain_m_part = jnp.sum(dmoe * mid * rr, axis=0, keepdims=True)
    dmid[...] = dproj[:, :width].astype(F32) + (rr * scaled - mid * (rr * rr * rr) * inner)
    dattn = (RESIDUAL_SCALE * dmid[...]).astype(BF)
    for j in range(nblk):
        cols = slice(j * ow, (j + 1) * ow)
        dmix[:, cols] = mm(dattn, w_att[j, :, :, :, qw:].reshape(width, ow)).astype(BF)
        wo[j] = mm_tn(dattn, mixed[:, cols]).astype(BF).reshape(pairs, 2, shard, ow)
        wos.share(j)
    routers.over_row()

    quad = 4 * hw
    groups = nblk * qw // quad
    gain_a_part = jnp.zeros((1, width), F32)
    for b in (1, 0):
        span = (b + 1) * half
        rows = slice(b * half, (b + 1) * half)
        bias[:, :span] = attention_bias(b * half, half, span, starts[rows, :])

        @pl.loop(0, groups)
        def _(g):
            chunk = qkv[:span, pl.ds(pl.multiple_of(g * quad, quad), quad)]
            dm_chunk = dmix[rows, pl.ds(pl.multiple_of(g * 2 * hw, 2 * hw), 2 * hw)]
            k_rows = chunk[:, 2 * hw : 3 * hw]
            v_rows = chunk[:, 3 * hw :]
            dk = jnp.zeros((span, hw), F32)
            dv = jnp.zeros((span, hw), F32)
            dqs = []
            for h in range(2):
                q = chunk[b * half :, h * hw : (h + 1) * hw]
                dmh = dm_chunk[:, h * hw : (h + 1) * hw]
                probs = masked_probs(q, k_rows, bias[:, :span])
                dprobs = mm_nt(dmh, v_rows)
                total = jnp.sum(probs * dprobs, axis=-1, keepdims=True)
                dscores = (probs * (dprobs - total)).astype(BF)
                dqs.append(mm(dscores, k_rows))
                dk = dk + mm_tn(dscores, q)
                dv = dv + mm_tn(probs.astype(BF), dmh)
            dkv_new = jnp.concatenate([dk, dv], axis=1)
            pair = pl.ds(pl.multiple_of(g * 2 * hw, 2 * hw), 2 * hw)
            if b == 1:
                dkv[:, pair] = dkv_new[:half]
                dkv_own = dkv_new[half:]
            else:
                dkv_own = dkv_new + dkv[:, pair]
            d = jnp.concatenate(dqs + [dkv_own], axis=1)
            d = d * cos[rows, :] - swap_halves(d) * sin[rows, :]
            dproj[rows, pl.ds(pl.multiple_of(g * quad, quad), quad)] = d.astype(BF)

        dattn_in = jnp.zeros((half, width), F32)
        for j in range(nblk):
            dattn_in = dattn_in + mm_nt(
                dproj[rows, j * qw : (j + 1) * qw],
                w_att[j, :, :, :, :qw].reshape(width, qw),
            )
        x = xd[rows, :].astype(F32)
        rx = row_scale(x)
        scaled = dattn_in * gain_a[...]
        inner = jnp.mean(scaled * x, axis=-1, keepdims=True)
        igb[0, rows, :] = (dmid[rows, :] + (rx * scaled - x * (rx * rx * rx) * inner)).astype(BF)
        gain_a_part = gain_a_part + jnp.sum(dattn_in * x * rx, axis=0, keepdims=True)
        igs.start(b)
        if b == 1:
            wos.join()
            routers.over_line()

    refs[18][...] = jnp.concatenate(
        [gain_a_part, gain_m_part, jnp.zeros((6, width), F32)], axis=0
    )
    gains.share.start()
    wos.middle()
    for j in range(nblk):
        wq[j] = (
            mm_tn(attn[...], dproj[:, j * qw : (j + 1) * qw])
            .astype(BF)
            .reshape(pairs, 2, shard, qw)
        )
        wqs.share(j)
    igs.forward(1)
    igs.forward(0)
    gains.over_row()
    wqs.join()

    for copy in ess:
        copy.wait_recv()
    e_gets = [
        pltpu.make_async_copy(es.at[0], own.at[0], lsems.at[0]),
        pltpu.make_async_copy(e_half.at[0], own.at[1, part(0)], lsems.at[1]),
        pltpu.make_async_copy(e_half.at[1], own.at[1, part(1)], lsems.at[2]),
        pltpu.make_async_copy(e_rest.at[0], own.at[2, part(0)], lsems.at[3]),
        pltpu.make_async_copy(e_rest.at[1], own.at[2, part(1)], lsems.at[4]),
    ]
    dms.drain()
    for copy in e_gets:
        copy.start()
    for copy in e_gets:
        copy.wait()
    rest = own[2].astype(F32)
    summed = own[0].astype(F32) + (own[1].astype(F32) + rest)
    block_out[...] = (input_grad[...] + RESIDUAL_SCALE * summed).astype(BF)

    wos.settle()
    wqs.middle()
    gains.over_line()
    igs.wait((1, 0), (2, 1))
    total = mm(match(0), igb[0])
    for j in (1, 2):
        total = total + mm(match(j), igb[j])
    router_out[...] = routers.result()
    out_grad[...] = wos.result()
    wqs.settle()
    igs.wait((3, 0), (3, 1))
    input_grad[...] = total + mm(match(3), igb[3])
    gains_out[...] = gains.result()
    qkv_grad[...] = wqs.result()
    for group in (wos, wqs, igs, routers, gains):
        group.drain()
    for copy in ess + dgs:
        copy.wait_send()


def backward(dm, es, e_mix, e_half, dgates, mids, cots, *rest):
    nblk, tokens, width = dm.shape
    w_att = rest[8]
    pairs, shard, both = w_att.shape[1], w_att.shape[3], w_att.shape[4]
    half = tokens // 2
    local = EXPERT_COUNT // nblk
    shape = jax.ShapeDtypeStruct
    count = (
        3 * RowScatter.count
        + RowGather.count
        + (nblk - 1)
        + 2 * WeightScatter.count(nblk, pairs)
        + 2 * (nblk + pairs - 1)
    )
    router_part = (EXPERT_COUNT, 2 * shard)
    outs = pl.pallas_call(
        functools.partial(back_kernel, nblk),
        out_shape=(
            shape((tokens, width), BF),
            shape((tokens, width), F32),
            shape((shard, both * 2 // 3), F32),
            shape((shard, both // 3), F32),
            shape(router_part, F32),
            shape((8, width), F32),
            shape((2, half, width), BF),
        ),
        in_specs=[ANY] * 4 + [FULL] + [ANY] * 6 + [FULL, ANY] + [FULL] * 14,
        out_specs=[FULL] * 6 + [ANY],
        scratch_shapes=[
            pltpu.VMEM((3, tokens, width), BF),
            pltpu.VMEM((2, half, width), BF),
            pltpu.VMEM((2, tokens, width), BF),
            pltpu.VMEM((nblk - 1, local, tokens), F32),
            pltpu.VMEM((nblk, tokens, width), BF),
            pltpu.VMEM((tokens, width), F32),
            pltpu.VMEM((tokens, width), BF),
            pltpu.VMEM((tokens, 2 * width), BF),
            pltpu.VMEM((half, width), F32),
            pltpu.VMEM((half, tokens), F32),
            *WeightScatter.scratch(nblk, pairs, shard, both // 3),
            *WeightScatter.scratch(nblk, pairs, shard, both * 2 // 3),
            *SmallSum.scratch(nblk, pairs, router_part, True),
            *SmallSum.scratch(nblk, pairs, (8, width), False),
            pltpu.SemaphoreType.DMA((2, count)),
            pltpu.SemaphoreType.DMA((8,)),
        ],
        compiler_params=pltpu.CompilerParams(
            vmem_limit_bytes=62 * MIB, collective_id=2, has_side_effects=True
        ),
        cost_estimate=cost(60e9, 100 * MIB),
        name="attention_backward",
    )(dm, es, e_mix, e_half, dgates, *mids, *cots, *rest)
    return outs[:6]


def collect_kernel(*refs):
    parts, outs = refs[:-3], refs[-3:]
    rows = jnp.concatenate([part[...].astype(F32) for part in parts], axis=0)
    fe = outs[0].shape[2]
    for i in range(3):
        outs[i][...] = jnp.swapaxes(rows[:, :, i * fe : (i + 1) * fe], 0, 1)


def collect(parts):
    count = sum(part.shape[0] for part in parts)
    _, shard, fe3 = parts[0].shape
    step = min(16, shard)
    out = jax.ShapeDtypeStruct((shard, count, fe3 // 3), F32)
    return pl.pallas_call(
        collect_kernel,
        grid=(shard // step,),
        out_shape=[out] * 3,
        in_specs=[pl.BlockSpec((part.shape[0], step, fe3), lambda i: (0, i, 0)) for part in parts],
        out_specs=[pl.BlockSpec((step, count, fe3 // 3), lambda i: (i, 0, 0))] * 3,
        compiler_params=params(32),
        cost_estimate=cost(1e6, 9 * MIB),
        name="collect",
    )(*parts)


def swap_over(value, axis, size, step):
    return lax.ppermute(value, axis, [(i, i ^ step) for i in range(size)])


def spread_rows(value, axis, size, step=1):
    return [value] + [swap_over(value, axis, size, j) for j in range(step, size, step)]


def body(
    block_in,
    cotangent,
    seq_lengths,
    seq_order,
    expert_ids,
    places,
    attn_gain,
    w_qkv,
    w_out,
    moe_gain,
    w_router,
    w_gate,
    w_up,
    w_down,
):
    tokens = block_in.shape[1]
    width = block_in.shape[2]
    rows = lax.axis_size("row")
    cols = lax.axis_size("col")
    total = tokens * rows
    r = lax.axis_index("row")
    c = lax.axis_index("col")
    local = w_gate.shape[1]
    shard = w_gate.shape[0]
    fe = w_gate.shape[2]
    capacity = total * TOPK // EXPERT_COUNT
    pairs = cols // 2
    qw = w_qkv.shape[1]
    ow = w_out.shape[1]

    router_own = jnp.concatenate(
        [lax.dynamic_slice_in_dim(w_router, (r ^ j) * local, local, 1) for j in range(rows)], axis=1
    )
    router_own = jnp.pad(router_own, ((0, 0), (0, LANES - EXPERT_COUNT)))
    w_parts = spread_rows(jnp.concatenate([w_qkv, w_out, router_own], axis=1), "col", cols, 2)

    stacked = jnp.concatenate([w_gate, w_up, w_down], axis=2).transpose(1, 0, 2)
    sizes = [3 * local // 8, 3 * local // 8, local // 4]
    bases = [sum(sizes[:i]) for i in range(len(sizes))]
    pieces = [stacked[i : i + n] for i, n in zip(bases, sizes)]
    pieces[0], pieces[1], *w_parts = lax.optimization_barrier((pieces[0], pieces[1], *w_parts))
    gathered = [lax.all_gather(piece, "col", axis=0) for piece in pieces[:-1]]

    lengths = seq_lengths[0]
    perm = seq_order[0]
    seq_ids = jnp.arange(lengths.shape[0], dtype=jnp.int32)
    picked = perm[:, None] == seq_ids[None, :]
    dealt_len = jnp.sum(jnp.where(picked, lengths[None, :], 0), axis=1)
    before = seq_ids[None, :] < perm[:, None]
    source_base = jnp.sum(jnp.where(before, lengths[None, :], 0), axis=1)
    upto = seq_ids[None, :] <= seq_ids[:, None]
    seq_ends = jnp.sum(jnp.where(upto, dealt_len[None, :], 0), axis=1)
    dealt_start = seq_ends - dealt_len
    turn = r * tokens
    pos = jnp.arange(total, dtype=jnp.int32) ^ turn
    inside = (pos[:, None] >= dealt_start[None, :]) & (pos[:, None] < seq_ends[None, :])
    seq_starts = jnp.sum(jnp.where(inside, dealt_start[None, :], 0), axis=1)
    offset = pos - seq_starts
    source = jnp.sum(jnp.where(inside, source_base[None, :], 0), axis=1) + offset
    source = source ^ turn
    src_col = source[:, None]
    src_row = source[None, :]
    own_offset = offset[:tokens]
    own_starts = (seq_starts[:tokens] - turn)[:, None]

    half = HEAD_WIDTH // 2
    frequency = ROPE_BASE ** (-jnp.arange(half, dtype=F32) * 2.0 / HEAD_WIDTH)
    turned = own_offset.astype(F32)[:, None] * frequency[None, :]
    cosine, sine = jnp.cos(turned), jnp.sin(turned)
    ones, zeros = jnp.ones_like(cosine), jnp.zeros_like(cosine)
    cos_q, sin_q = cosine * SCORE_SCALE, sine * SCORE_SCALE
    cos_w = jnp.concatenate([cos_q] * 4 + [cosine] * 2 + [ones] * 2, axis=1)
    sin_w = jnp.concatenate([-sin_q, sin_q] * 2 + [-sine, sine] + [zeros] * 2, axis=1)

    gain_a = attn_gain[None, :]
    gain_m = moe_gain[None, :]
    (
        xd,
        attn,
        qkv,
        mixed,
        middle,
        moe,
        cot_first,
        slot_cols,
        slot_rows,
        gates,
        packed,
        w_att,
        moe_own,
        slot_given,
        given_rows,
        mid16,
        router_x,
        following,
    ) = front(
        block_in[0],
        cotangent[0],
        pieces[-1],
        w_parts,
        [
            src_col,
            own_starts,
            cos_w,
            sin_w,
            gain_a,
            gain_m,
            expert_ids[0].T,
            places[0].T,
            src_row,
        ],
        rows,
    )
    router_x = router_x.reshape(width, LANES)

    acc = carried = None
    summed = []
    final = len(sizes) - 1
    full = []
    for i in range(len(sizes)):
        w = gathered[i] if i < final else following
        moved = [("rest", cotangent[0], cot_first), ("sides", mid16)]
        moved = moved[i] if i < 2 else ("corner", full[1])
        if i > 0:
            w, *carried = lax.optimization_barrier((w, *carried))
        stage = (1, 3, 0)[i]
        parts = experts_forward(
            moe, slot_rows, slot_given, packed, w, acc, moved, (stage, following), bases[i], i == final, capacity, 3 + i
        )
        kept, acc = parts[:4], parts[4]
        full.append(parts[5])
        if stage:
            following = parts[6]
        stage = (2, 4, 0)[i]
        rows_in = given_rows
        if i == final:
            rows_in = lax.optimization_barrier((given_rows, summed[0]))[0]
        grads, *carried = experts_reverse(
            (cotangent[0], cot_first, full[0]), rows_in, slot_cols, kept, w, carried, acc, (stage, following), bases[i], i == final, capacity, 6 + i
        )
        if stage:
            following = carried.pop()
        summed.append(lax.psum_scatter(grads, "col", scatter_dimension=0, tiled=False))
    es = acc
    dm, dgates, e_mix, e_across, e_half = carried
    block_out, input_grad, qkv_grad, out_grad, router_part, gains = backward(
        dm,
        es,
        e_mix,
        e_half,
        dgates,
        [mid16, full[1], full[2]],
        (cotangent[0], cot_first, full[0]),
        gates,
        middle,
        moe_own,
        src_col[:tokens],
        mixed,
        qkv,
        attn,
        xd,
        w_att,
        router_x,
        own_starts,
        cos_w,
        sin_w,
        gain_a,
        gain_m,
        src_row,
    )
    router_grad = lax.dynamic_slice_in_dim(router_part, c % 2 * shard, shard, 1).T

    gate_grad, up_grad, down_grad = collect(summed)
    return (
        block_out[None],
        input_grad[None],
        gains[0],
        qkv_grad,
        out_grad,
        gains[1],
        router_grad,
        gate_grad,
        up_grad,
        down_grad,
    )


def solution(mesh):
    tokens = P("col", "row", None)
    weight = P("col", "row")
    expert = P("col", "row", None)
    return jax.shard_map(
        body,
        mesh=mesh,
        in_specs=(
            tokens,
            tokens,
            P("col", None),
            P("col", None),
            P("col", None, None),
            P("col", None, None),
            P(),
            weight,
            weight,
            P(),
            P("col", None),
            expert,
            expert,
            expert,
        ),
        out_specs=(
            tokens,
            tokens,
            P(),
            weight,
            weight,
            P(),
            P("col", None),
            expert,
            expert,
            expert,
        ),
        check_vma=False,
    )
```

```python
import functools

import jax
import jax.numpy as jnp
from jax import lax
from jax.experimental import pallas as pl
from jax.experimental.pallas import tpu as pltpu
from jax.sharding import PartitionSpec as P

HEAD_WIDTH = 64
QUERY_HEADS = 16
KEY_VALUE_HEADS = 8
EXPERT_COUNT = 32
TOPK = 8
EPSILON = 1e-06
RESIDUAL_SCALE = 0.22
SCORE_SCALE = 0.015625
ROPE_BASE = 10000.0
MASKED = -1e30
LANES = 128
MIB = 1024 * 1024
BF = jnp.bfloat16
F32 = jnp.float32
ANY = pl.BlockSpec(memory_space=pl.ANY)
FULL = pl.BlockSpec(memory_space=pltpu.VMEM)


def mm(a, b):
    return lax.dot_general(a, b, (((1,), (0,)), ((), ())), preferred_element_type=F32)


def mm_nt(a, b):
    return lax.dot_general(a, b, (((1,), (1,)), ((), ())), preferred_element_type=F32)


def mm_tn(a, b):
    return lax.dot_general(a, b, (((0,), (0,)), ((), ())), preferred_element_type=F32)


def iota(shape, dim):
    return lax.broadcasted_iota(jnp.int32, shape, dim)


def params(mib):
    return pltpu.CompilerParams(vmem_limit_bytes=mib * MIB)


def cost(flops, moved):
    return pl.CostEstimate(flops=int(flops), bytes_accessed=int(moved), transcendentals=0)


def row_scale(values):
    return lax.rsqrt(jnp.mean(values * values, axis=-1, keepdims=True) + EPSILON)


def swap_halves(values):
    width = values.shape[-1]
    half = HEAD_WIDTH // 2
    low = (iota(values.shape, 1) % HEAD_WIDTH) < half
    ahead = pltpu.roll(values, width - half, 1)
    behind = pltpu.roll(values, half, 1)
    return jnp.where(low, ahead, behind)


def attention_bias(row0, rows, cols, starts):
    at = iota((rows, cols), 1)
    allowed = (at <= iota((rows, cols), 0) + row0) & (at >= starts)
    return jnp.where(allowed, 0.0, MASKED)


def masked_probs(q, k, bias):
    scores = mm_nt(q, k) + bias
    raised = jnp.exp(scores - jnp.max(scores, axis=-1, keepdims=True))
    return raised * (1.0 / jnp.sum(raised, axis=-1, keepdims=True))


def link(src, dst, sems, index, device):
    return pltpu.make_async_remote_copy(
        src_ref=src,
        dst_ref=dst,
        send_sem=sems.at[0, index],
        recv_sem=sems.at[1, index],
        device_id=device,
        device_id_type=pl.DeviceIdType.MESH,
    )


def greet(devices):
    barrier = pltpu.get_barrier_semaphore()
    for device in devices:
        pl.semaphore_signal(barrier, inc=1, device_id=device, device_id_type=pl.DeviceIdType.MESH)
    pl.semaphore_wait(barrier, len(devices))


class RowGather:
    count = 6

    def __init__(self, own, slot, sems, base, r, c):
        near, far = (r ^ 1, c), (r ^ 2, c)
        self.copies = {
            (1, 1): link(own(1), slot(1, 1), sems, base, near),
            (2, 0): link(own(0), slot(2, 0), sems, base + 1, far),
            (1, 0): link(own(0), slot(1, 0), sems, base + 2, near),
            (2, 1): link(own(1), slot(2, 1), sems, base + 3, far),
            (3, 0): link(slot(2, 0), slot(3, 0), sems, base + 4, near),
            (3, 1): link(slot(1, 1), slot(3, 1), sems, base + 5, far),
        }

    def start(self, half):
        order = ((2, 0), (1, 0)) if half == 0 else ((1, 1), (2, 1))
        for key in order:
            self.copies[key].start()

    def forward(self, half):
        self.copies[(2, 0) if half == 0 else (1, 1)].wait_recv()
        self.copies[(3, half)].start()

    def wait(self, *keys):
        for key in keys:
            self.copies[key].wait_recv()

    def drain(self):
        for copy in self.copies.values():
            copy.wait_send()


def front_kernel(pairs, *refs):
    xin, cot, w_last = refs[:3]
    w_parts = refs[3 : 3 + pairs]
    refs = refs[3 + pairs :]
    src, starts, cos, sin, gain_a, gain_m, ids, spots, src_row = refs[:9]
    xd, attn, qkv, mixed, middle, moe_all, cot_first, slot_cols, slot_rows, gates, packed = refs[9:20]
    w_att, moe, slot_given, given_rows, mid16, w_router, w_next = refs[20:27]
    xb, bias, chosen, sems, local_sems = refs[27:]
    nblk, tokens, width = xb.shape
    half = tokens // 2
    capacity = nblk * tokens * TOPK // EXPERT_COUNT
    qw = w_att.shape[4] * 2 // 3
    rank = w_att.shape[1] * 2 * w_att.shape[3]
    r = lax.axis_index("row")
    c = lax.axis_index("col")
    z = c // 2
    k = c % 2
    both = w_att.shape[4]
    local = EXPERT_COUNT // nblk
    sibling = (r, c ^ 1)
    greet([(r ^ 1, c), (r ^ 2, c), sibling])

    def cut(ref):
        return lambda h: ref.at[pl.ds(h * half, half)]

    def cut_slot(ref):
        return lambda j, h: ref.at[j, pl.ds(h * half, half)]

    def w_slot(j, h):
        return w_att.at[j, pl.ds(h * (pairs // 2), pairs // 2), k]

    n = RowGather.count
    xs = RowGather(cut(xin), cut_slot(xb), sems, 0, r, c)
    ws = RowGather(lambda h: w_slot(0, h), w_slot, sems, n, r, c)
    ms = RowGather(cut(moe), cut_slot(moe_all), sems, 2 * n, r, c)
    base = 3 * n
    share = [link(w_att.at[j, :, k], w_att.at[j, :, k], sems, base + j, sibling) for j in range(nblk)]
    early = [
        link(cot.at[pl.ds(0, half)], cot_first.at[i], sems, base + nblk + 1 + i, (r ^ (1 + i), c))
        for i in range(2)
    ]
    share.append(link(w_router.at[:, k], w_router.at[:, k], sems, base + nblk, sibling))
    xs.start(1)
    xs.start(0)
    keep = [pltpu.make_async_copy(xin, xb.at[0], local_sems.at[0])]
    for i in range(pairs):
        keep.append(
            pltpu.make_async_copy(
                w_parts[i].at[:, pl.ds(0, both)], w_att.at[0, z ^ i, k], local_sems.at[2 + 2 * i]
            )
        )
        keep.append(
            pltpu.make_async_copy(
                w_parts[i].at[:, pl.ds(both, LANES)], w_router.at[z ^ i, k], local_sems.at[3 + 2 * i]
            )
        )
    for copy in keep:
        copy.start()
    seat = pltpu.make_async_copy(w_last, w_next.at[c], local_sems.at[2 + 2 * pairs])
    seat.start()
    for copy in keep:
        copy.wait()
    ws.start(1)
    ws.start(0)
    share[0].start()
    share[nblk].start()
    xs.forward(0)
    xs.forward(1)

    source = src[:tokens, :]

    def pick(at, j):
        return jnp.where(at == iota((tokens, tokens), 1) + j * tokens, 1.0, 0.0).astype(BF)

    x = mm(pick(source, 0), xb[0])
    xs.wait((1, 0))
    x = x + mm(pick(source, 1), xb[1])
    xs.wait((2, 1))
    x = x + mm(pick(source, 2), xb[2])
    ws.forward(0)
    ws.forward(1)
    ws.wait((1, 0), (2, 1))
    share[1].start()
    share[2].start()
    xs.wait((3, 0), (3, 1))
    x = x + mm(pick(source, 3), xb[3])
    xd[...] = x.astype(BF)
    attn[...] = (x * row_scale(x) * gain_a[...]).astype(BF)
    groups = qw // (4 * HEAD_WIDTH)

    def project(j):
        proj = mm(attn[...], w_att[j, :, :, :, :qw].reshape(rank, qw))
        cos_w = jnp.concatenate([cos[...]] * groups, axis=1)
        sin_w = jnp.concatenate([sin[...]] * groups, axis=1)
        turned = proj * cos_w + swap_halves(proj) * sin_w
        qkv[:, pl.ds(pl.multiple_of(j * qw, qw), qw)] = turned.astype(BF)

    ws.wait((3, 0), (3, 1))
    share[3].start()
    for copy in early:
        copy.start()
    for copy in share:
        copy.wait_recv()

    @pl.loop(0, nblk)
    def _(j):
        project(j)

    pair = 2 * HEAD_WIDTH
    for b in range(2):
        rows = slice(b * half, (b + 1) * half)
        span = (b + 1) * half
        bias[:, :span] = attention_bias(b * half, half, span, starts[rows, :])

        @pl.loop(0, groups * nblk)
        def _(g):
            chunk = qkv[:span, pl.ds(pl.multiple_of(g * 2 * pair, 2 * pair), 2 * pair)]
            k_rows = chunk[:, pair : pair + HEAD_WIDTH]
            v_rows = chunk[:, pair + HEAD_WIDTH :]
            outs = []
            for h in range(2):
                q = chunk[b * half :, h * HEAD_WIDTH : (h + 1) * HEAD_WIDTH]
                probs = masked_probs(q, k_rows, bias[:, :span])
                outs.append(mm(probs.astype(BF), v_rows))
            mixed[rows, pl.ds(pl.multiple_of(g * pair, pair), pair)] = jnp.concatenate(
                outs, axis=1
            ).astype(BF)

        if b == 1:
            ms.forward(0)
        ow = w_att.shape[4] - qw
        out = jnp.zeros((half, width), F32)
        for j in range(nblk):
            w_out = w_att[j, :, :, :, qw:].reshape(rank, ow)
            out = out + mm_nt(mixed[rows, j * ow : (j + 1) * ow], w_out)
        mid = xd[rows, :].astype(F32) + RESIDUAL_SCALE * out
        middle[rows, :] = mid
        mid16[rows, :] = mid.astype(BF)
        moe[rows, :] = (mid * row_scale(mid) * gain_m[...]).astype(BF)
        ms.start(b)

    place = pltpu.make_async_copy(moe, moe_all.at[0], local_sems.at[1])
    place.start()

    @pl.loop(0, nblk)
    def _(b):
        at = pl.ds(pl.multiple_of(b * tokens, tokens), tokens)
        there = pl.ds(pl.multiple_of((b ^ r) * tokens, tokens), tokens)
        expert = iota((EXPERT_COUNT, tokens), 0)
        spot = jnp.zeros((EXPERT_COUNT, tokens), F32)
        named = jnp.zeros((EXPERT_COUNT, tokens), F32)
        own_ids = ids[:, there] ^ (r * local)
        own_spots = spots[:, there].astype(F32)
        for i in range(TOPK):
            hit = expert == own_ids[i : i + 1, :]
            named = jnp.where(hit, 1.0, named)
            spot = jnp.where(hit, own_spots[i : i + 1, :], spot)
        slot = jnp.where((named > 0.0) & (spot < capacity), spot, -1.0)
        slot_rows[:, at] = slot[:local, :]
        rest = jnp.zeros((LANES - EXPERT_COUNT, tokens), F32)
        chosen[at, :] = jnp.concatenate([named, rest], axis=0).T
        slot_cols[at, :] = jnp.concatenate([slot, rest - 1.0], axis=0).T

    ms.forward(1)

    @pl.loop(0, nblk)
    def _(b):
        at = pl.ds(pl.multiple_of(b * tokens, tokens), tokens)
        found = jnp.zeros((tokens, LANES), F32)
        for j in range(nblk):
            part = slice(j * tokens, (j + 1) * tokens)
            match = iota((tokens, tokens), 0) + b * tokens == src_row[:, part]
            match = jnp.where(match, 1.0, 0.0).astype(BF)
            value = slot_cols[part, :] + 1.0
            high = jnp.floor(value * 0.0625)
            low = value - 16.0 * high
            found = found + 16.0 * mm(match, high.astype(BF)) + mm(match, low.astype(BF))
        slot_given[at, :] = found - 1.0
        given_rows[:, at] = (found - 1.0).T[: given_rows.shape[0], :]

    def gate_block(j, rows):
        at = slice(j * tokens, (j + 1) * tokens)
        logits = mm(rows, w_router[...].reshape(width, LANES))
        named = chosen[at, :] > 0.0
        logits = jnp.where(named, logits, MASKED)
        top = jnp.max(logits, axis=-1, keepdims=True)
        raised = jnp.where(named, jnp.exp(logits - top), 0.0)
        gate = raised / jnp.sum(raised, axis=-1, keepdims=True)
        if j == 0:
            gates[...] = gate
        own = jnp.where(iota((tokens, LANES), 1) < local, gate, 0.0)
        high, mid, low = split_three(own)
        packed[at, :] = (high + pltpu.roll(mid, local, 1) + pltpu.roll(low, 2 * local, 1)).astype(BF)

    gate_block(0, moe[...])
    place.wait()
    xs.drain()
    for j, keys in ((1, ((1, 0),)), (2, ((2, 1),)), (3, ((3, 0), (3, 1)))):
        ms.wait(*keys)
        get = pltpu.make_async_copy(moe_all.at[j], xb.at[j], local_sems.at[0])
        get.start()
        get.wait()
        gate_block(j, xb[j])
    seat.wait()
    for copy in early:
        copy.wait_recv()
    for gather in (ws, ms):
        gather.drain()
    for copy in share + early:
        copy.wait_send()


def front(xin, cot, w_last, w_parts, tables, nblk):
    tokens, width = xin.shape
    pairs = len(w_parts)
    shard, both = w_parts[0].shape[0], w_parts[0].shape[1] - LANES
    total = nblk * tokens
    qkv_width = nblk * both * 2 // 3
    head_width = nblk * both // 3
    shape = jax.ShapeDtypeStruct
    count = 3 * RowGather.count + nblk + 3
    local = EXPERT_COUNT // nblk
    return pl.pallas_call(
        functools.partial(front_kernel, pairs),
        out_shape=(
            shape((tokens, width), BF),
            shape((tokens, width), BF),
            shape((tokens, qkv_width), BF),
            shape((tokens, head_width), BF),
            shape((tokens, width), F32),
            shape((nblk, tokens, width), BF),
            shape((2, tokens // 2, width), BF),
            shape((total, LANES), F32),
            shape((local, total), F32),
            shape((tokens, LANES), F32),
            shape((total, LANES), BF),
            shape((nblk, pairs, 2, shard, both), BF),
            shape((tokens, width), BF),
            shape((total, LANES), F32),
            shape((local, total), F32),
            shape((tokens, width), BF),
            shape((pairs, 2, shard, LANES), BF),
            shape((2 * pairs, *w_last.shape), BF),
        ),
        in_specs=[ANY] * (3 + pairs) + [FULL] * 9,
        out_specs=[FULL] * 5 + [ANY] * 2 + [FULL] * 10 + [ANY],
        scratch_shapes=[
            pltpu.VMEM((nblk, tokens, width), BF),
            pltpu.VMEM((tokens // 2, tokens), F32),
            pltpu.VMEM((total, LANES), F32),
            pltpu.SemaphoreType.DMA((2, count)),
            pltpu.SemaphoreType.DMA((3 + 2 * pairs,)),
        ],
        compiler_params=pltpu.CompilerParams(
            vmem_limit_bytes=58 * MIB, collective_id=1, has_side_effects=True
        ),
        cost_estimate=cost(20e9, 60 * MIB),
        name="attention_forward",
    )(xin, cot, w_last, *w_parts, *tables)


class RowScatter:
    count = 6

    def __init__(self, block, mixed_in, across, landed, sems, base, r, c):
        near, far = (r ^ 1, c), (r ^ 2, c)
        self.copies = {
            "diag0": link(block(3, 0), across(0), sems, base, near),
            "diag1": link(block(3, 1), across(1), sems, base + 1, far),
            "near0": link(block(1, 0), landed(1, 0), sems, base + 2, near),
            "far1": link(block(2, 1), landed(2, 1), sems, base + 3, far),
        }
        if mixed_in is not None:
            self.copies["far0"] = link(mixed_in(0), landed(2, 0), sems, base + 4, far)
            self.copies["near1"] = link(mixed_in(1), landed(1, 1), sems, base + 5, near)

    def start(self):
        for key in ("diag0", "diag1", "near0", "far1"):
            self.copies[key].start()

    def arrived(self, half):
        self.copies["diag0" if half == 0 else "diag1"].wait_recv()

    def send(self, half):
        self.copies["far0" if half == 0 else "near1"].start()

    def finish(self):
        for key in self.copies:
            if not key.startswith("diag"):
                self.copies[key].wait_recv()

    def drain(self):
        for copy in self.copies.values():
            copy.wait_send()


def tree_sum(parts):
    while len(parts) > 1:
        parts = [parts[i] + parts[i + 1] for i in range(0, len(parts), 2)]
    return parts[0]


def plus(a, b):
    return (a.astype(F32) + b.astype(F32)).astype(BF)


def one_hot(hit):
    return jnp.where(hit, 1.0, 0.0).astype(BF)


def lane_column(table, index):
    return jnp.sum(jnp.where(iota(table.shape, 1) == index, table, 0.0), axis=1, keepdims=True)


def split_three(value):
    high = value.astype(BF).astype(F32)
    rest = value - high
    mid = rest.astype(BF).astype(F32)
    return high, mid, rest - mid


def forward_kernel(base, first, last, gathers, stage, local, capacity, *refs):
    moe_hbm, slot_rows, slot_given, packed, w = refs[:5]
    refs = refs[5:]
    if not first:
        acc_in, refs = refs[0], refs[1:]
    early = gathers == "rest"
    if gathers:
        own_hbm, refs = refs[0], refs[1:]
    if early:
        first_hbm, refs = refs[0], refs[1:]
    if stage:
        next_in, refs = refs[0], refs[1:]
    routed_out, gate_out, up_out, weight_out, acc_out = refs[:5]
    refs = refs[5:]
    if gathers:
        all_hbm, refs = refs[0], refs[1:]
    if stage:
        next_out, refs = refs[0], refs[1:]
    moe, acc, sel, given, y1, sems = refs[:6]
    step = pl.program_id(0)
    steps = pl.num_programs(0)
    e = base + step
    ne = y1.shape[0] // capacity
    nblk, tokens, width = moe_hbm.shape
    fe = w.shape[3] // 3
    copies = [
        pltpu.make_async_copy(moe_hbm.at[j], moe.at[pl.ds(j * tokens, tokens)], sems.at[j])
        for j in range(nblk)
    ]
    if not first:
        load = pltpu.make_async_copy(acc_in, acc, sems.at[nblk])
    if gathers:
        link_sems = refs[6]
        r = lax.axis_index("row")
        c = lax.axis_index("col")
        half = tokens // 2
        near, far = (r ^ 1, c), (r ^ 2, c)
        top, bottom = pl.ds(0, half), pl.ds(half, half)
        later = []
        greeted = [near, far]
        if stage:
            line = LineGather(stage, next_in, next_out, refs[7], r, c)
            greeted = greeted + line.devices
        if gathers == "rest":
            begin = [
                link(own_hbm.at[bottom], all_hbm.at[0], link_sems, 0, near),
                link(first_hbm.at[1], all_hbm.at[2], link_sems, 1, near),
                link(own_hbm.at[bottom], all_hbm.at[1], link_sems, 2, far),
            ]
            later = [link(all_hbm.at[0], all_hbm.at[3], link_sems, 3, far)]
        elif gathers == "sides":
            begin = [
                link(own_hbm, all_hbm.at[0], link_sems, 0, near),
                link(own_hbm, all_hbm.at[1], link_sems, 1, far),
            ]
        else:
            begin = [
                link(own_hbm.at[1, top], all_hbm.at[top], link_sems, 0, near),
                link(own_hbm.at[0, bottom], all_hbm.at[bottom], link_sems, 1, far),
            ]

    @pl.when(step == 0)
    def _():
        for copy in copies:
            copy.start()
        if not first:
            load.start()
        if gathers:
            greet(greeted)
            for copy in begin:
                copy.start()
            if stage:
                line.start()

    row = slot_rows[pl.ds(e, 1), :]
    for j in range(nblk):
        at = slice(j * tokens, (j + 1) * tokens)
        sel[:, at] = one_hot(iota((capacity, tokens), 0).astype(F32) == row[:, at])

    @pl.when(step == 0)
    def _():
        for copy in copies:
            copy.wait()

    if stage:

        @pl.when(step == steps - 1)
        def _():
            line.advance()

    if early:

        @pl.when(step == steps - 1)
        def _():
            begin[0].wait_recv()
            later[0].start()

    routed_out[0] = mm(sel[...], moe[...]).astype(BF)
    lane = iota((capacity, LANES), 1)
    picked = mm(sel[...], packed[...])
    mine = (lane == e) | (lane == e + local) | (lane == e + 2 * local)
    gate = jnp.sum(jnp.where(mine, picked, 0.0), axis=1, keepdims=True)
    weight_out[0] = jnp.broadcast_to(gate, (capacity, LANES))
    gate_up = mm(routed_out[0], w[:, 0, :, : 2 * fe].reshape(width, 2 * fe))
    gate_in = gate_up[:, :fe]
    up_in = gate_up[:, fe:]
    gate_out[0] = gate_in
    up_out[0] = up_in
    hidden = (gate_in * jax.nn.sigmoid(gate_in) * up_in).astype(BF)
    out = mm_nt(hidden, w[:, 0, :, 2 * fe :].reshape(width, fe))
    y1[pl.ds(pl.multiple_of(step * capacity, capacity), capacity), :] = (gate * out).astype(BF)

    @pl.when(step == steps - 1)
    def _():
        if not first:
            load.wait()

        def put(b):
            at = pl.ds(pl.multiple_of(b * tokens, tokens), tokens)
            if last:
                return pltpu.make_async_copy(moe.at[at], acc_out.at[b], sems.at[b])
            return pltpu.make_async_copy(acc.at[at], acc_out.at[at], sems.at[b])

        @pl.loop(0, nblk)
        def _(b):
            at = pl.ds(pl.multiple_of(b * tokens, tokens), tokens)
            slots = iota((tokens, capacity), 1).astype(F32)
            for i in range(ne):
                given[:, i * capacity : (i + 1) * capacity] = one_hot(
                    lane_column(slot_given[at, :], base + i) == slots
                )
            part = mm(given[...], y1[...])
            if not first:
                part = part + acc[at, :]
            if last:
                moe[at, :] = part.astype(BF)
            else:
                acc[at, :] = part
            put(b).start()

        if stage:
            line.finish()
        if gathers:
            for copy in begin[1:] if early else begin:
                copy.wait_recv()
            for copy in later:
                copy.wait_recv()
            for copy in begin + later:
                copy.wait_send()
        for b in range(nblk):
            put(b).wait()


def experts_forward(moe, slot_rows, slot_given, packed, w, acc, moved, later, base, last, capacity, key):
    nblk, tokens, width = moe.shape
    total = nblk * tokens
    cols, ne, shard, fe3 = w.shape
    fe = fe3 // 3
    local = EXPERT_COUNT // nblk
    first = acc is None
    gathers, *sent = moved
    landing = {"rest": (4, tokens // 2), "sides": (2, tokens), "corner": (tokens,)}[gathers]
    shape = jax.ShapeDtypeStruct
    wspec = pl.BlockSpec((cols, 1, shard, fe3), lambda s: (0, s, 0, 0))

    def each(*dims):
        return pl.BlockSpec((1, *dims), lambda s: (s, 0, 0))

    ins = [moe, slot_rows, slot_given, packed, w]
    in_specs = [ANY, FULL, FULL, FULL, wspec]
    aliases = {}
    if not first:
        ins.append(acc)
        in_specs.append(ANY)
        if not last:
            aliases = {len(ins) - 1: 4}
    outs = [
        shape((ne, capacity, width), BF),
        shape((ne, capacity, fe), F32),
        shape((ne, capacity, fe), F32),
        shape((ne, capacity, LANES), F32),
        shape((nblk, tokens, width), BF) if last else shape((total, width), F32),
    ]
    out_specs = [each(capacity, width), each(capacity, fe), each(capacity, fe), each(capacity, LANES), ANY]
    scratch = [
        pltpu.VMEM((total, width), BF),
        pltpu.VMEM((total, width), F32),
        pltpu.VMEM((capacity, total), BF),
        pltpu.VMEM((tokens, ne * capacity), BF),
        pltpu.VMEM((ne * capacity, width), BF),
        pltpu.SemaphoreType.DMA((nblk + 1,)),
    ]
    options = dict(vmem_limit_bytes=58 * MIB)
    ins += sent
    in_specs += [ANY] * len(sent)
    outs.append(shape((*landing, width), BF))
    out_specs.append(ANY)
    scratch.append(pltpu.SemaphoreType.DMA((2, 4)))
    stage, following = later
    if stage:
        aliases = {**aliases, len(ins): len(outs)}
        ins.append(following)
        in_specs.append(ANY)
        outs.append(shape(following.shape, BF))
        out_specs.append(ANY)
        scratch.append(LineGather.scratch(cols // 2, following.shape[1]))
    options.update(collective_id=key, has_side_effects=True)
    return pl.pallas_call(
        functools.partial(forward_kernel, base, first, last, gathers, stage, local, capacity),
        grid=(ne,),
        out_shape=outs,
        in_specs=in_specs,
        out_specs=out_specs,
        scratch_shapes=scratch,
        input_output_aliases=aliases,
        compiler_params=pltpu.CompilerParams(**options),
        cost_estimate=cost(7e9 * ne, 30 * MIB),
        name="experts_forward",
    )(*ins)


class LineGather:
    def __init__(self, stage, src, dst, sems, r, c):
        self.pairs, self.count = src.shape[0] // 2, src.shape[1]
        self.stage, self.src, self.dst, self.sems = stage, src, dst, sems
        self.z, self.k = c // 2, c % 2
        slots = []
        for slot in range(self.pairs + self.count - 2):
            moves = [(slot - e + 1, e) for e in range(self.count)]
            slots.append([(hop, e) for hop, e in moves if 1 <= hop < self.pairs])
        self.slots = [slots[:1], slots[1:-1], slots[-1:], []][stage - 1]
        self.swaps = []
        if stage == 4:
            self.devices = [(r, c ^ 1)]
            for i in range(self.pairs):
                slot = 2 * i + self.k
                self.swaps.append(link(src.at[slot], dst.at[slot], sems, i, (r, c ^ 1)))
        else:
            devices = 2 * self.pairs
            self.devices = [(r, (c + 2) % devices), (r, (c - 2) % devices)]

    def place(self, side):
        return self.z if side == 0 else self.pairs - 1 - self.z

    def copy(self, side, hop, e):
        at = jnp.maximum(self.place(side) - hop + 1, 0)
        slot = 2 * (at if side == 0 else self.pairs - 1 - at) + self.k
        here = any((hop - 1, e) in moves for moves in self.slots)
        src = self.dst if here else self.src
        index = (side * (self.pairs - 1) + hop - 1) * self.count + e
        return link(
            src.at[slot, e], self.dst.at[slot, e], self.sems, index, self.devices[side]
        )

    def sends(self, side, hop):
        return (self.place(side) >= hop - 1) & (self.place(side) <= self.pairs - 2)

    def send(self, moves):
        for hop, e in moves:
            for side in range(2):

                @pl.when(self.sends(side, hop))
                def _():
                    self.copy(side, hop, e).start()

    def start(self):
        for copy in self.swaps:
            copy.start()
        if self.slots:
            self.send(self.slots[0])

    def land(self, number):
        for hop, e in self.slots[number]:
            for side in range(2):

                @pl.when(self.place(side) >= hop)
                def _():
                    self.copy(side, hop, e).wait_recv()

        if number + 1 < len(self.slots):
            self.send(self.slots[number + 1])

    def advance(self):
        if len(self.slots) > 1:
            self.land(0)

    def finish(self):
        for copy in self.swaps:
            copy.wait_recv()
        for number in range(1 if len(self.slots) > 1 else 0, len(self.slots)):
            self.land(number)
        for moves in self.slots:
            for hop, e in moves:
                for side in range(2):

                    @pl.when(self.sends(side, hop))
                    def _():
                        self.copy(side, hop, e).wait_send()

        for copy in self.swaps:
            copy.wait_send()

    @staticmethod
    def scratch(pairs, count):
        return pltpu.SemaphoreType.DMA((2, max(2 * (pairs - 1) * count, pairs)))


def cot_pieces(own, first, rest):
    half = own.shape[0] // 2
    return [
        own.at[pl.ds(0, half)],
        own.at[pl.ds(half, half)],
        first.at[0],
        rest.at[0],
        first.at[1],
        rest.at[1],
        rest.at[2],
        rest.at[3],
    ]


def reverse_kernel(base, first, last, stage, local, capacity, *refs):
    cot_own, cot_first, cot_rest, given_rows, slot_cols, routed, gate_in_ref, up_in_ref, weight_ref, w = refs[:10]
    refs = refs[10:]
    if not first:
        acc_in, accg_in = refs[:2]
        refs = refs[2:]
    if last:
        es, refs = refs[0], refs[1:]
    if stage:
        next_in, refs = refs[0], refs[1:]
    grads, acc_out, accg_out = refs[:3]
    refs = refs[3:]
    if last:
        e_mix, e_across, e_landed = refs[:3]
        refs = refs[3:]
    if stage:
        next_out, refs = refs[0], refs[1:]
    cot, acc, accg, sel, chosen, spread, dsl, dslot, y2, sems = refs[:10]
    step = pl.program_id(0)
    steps = pl.num_programs(0)
    e = base + step
    tokens, width = cot_own.shape
    nblk = cot.shape[0] // tokens
    half = tokens // 2
    cols, _, shard, fe = w.shape
    fe = fe // 3
    ne = y2.shape[0] // capacity
    copies = [
        pltpu.make_async_copy(piece, cot.at[pl.ds(j * half, half)], sems.at[j])
        for j, piece in enumerate(cot_pieces(cot_own, cot_first, cot_rest))
    ]
    if not first:
        loads = [
            pltpu.make_async_copy(acc_in, acc, sems.at[2 * nblk]),
            pltpu.make_async_copy(accg_in, accg, sems.at[2 * nblk + 1]),
        ]
    r = lax.axis_index("row")
    c = lax.axis_index("col")
    if stage:
        line = LineGather(stage, next_in, next_out, refs[10], r, c)
    if last:
        e_vmem, link_sems = refs[10:]
        scatter = RowScatter(
            lambda j, h: es.at[j, pl.ds(h * half, half)],
            None,
            lambda h: e_across.at[h],
            lambda j, h: e_landed.at[h],
            link_sems,
            0,
            r,
            c,
        )

    @pl.when(step == 0)
    def _():
        for copy in copies:
            copy.start()
        if not first:
            for copy in loads:
                copy.start()
        if last:
            greet([(r ^ 1, c), (r ^ 2, c)])
            scatter.start()
        if stage:
            greet(line.devices)
            line.start()

    row = given_rows[pl.ds(e, 1), :]
    for j in range(nblk):
        at = slice(j * tokens, (j + 1) * tokens)
        sel[:, at] = one_hot(iota((capacity, tokens), 0).astype(F32) == row[:, at])

    @pl.when(step == 0)
    def _():
        for copy in copies:
            copy.wait()

    gate = weight_ref[0, :, :1]

    rows = (RESIDUAL_SCALE * mm(sel[...], cot[...])).astype(BF)
    dsl[...] = rows
    dslot[...] = (gate * rows.astype(F32)).astype(BF)
    gate_in = gate_in_ref[0]
    up_in = up_in_ref[0]
    sig = jax.nn.sigmoid(gate_in)
    silu = gate_in * sig
    hidden = (silu * up_in).astype(BF)
    if stage:

        @pl.when(step == (steps - 1) // 2)
        def _():
            line.advance()

    dhidden = mm(dslot[...], w[:, 0, :, 2 * fe :].reshape(width, fe))
    dgate = (dhidden * up_in * sig * (1.0 + gate_in * (1.0 - sig))).astype(BF)
    dup = (dhidden * silu).astype(BF)
    both = jnp.concatenate([dgate, dup], axis=1)
    out = mm_nt(hidden, w[:, 0, :, 2 * fe :].reshape(width, fe))
    inner = jnp.sum(dsl[...].astype(F32) * out, axis=1, keepdims=True)
    grads[:, 0, :, 2 * fe :] = mm_tn(dslot[...], hidden).astype(BF).reshape(cols, shard, fe)
    grads[:, 0, :, : 2 * fe] = mm_tn(routed[0], both).astype(BF).reshape(cols, shard, 2 * fe)
    mine = pl.ds(pl.multiple_of(step * capacity, capacity), capacity)
    y2[mine, :] = mm_nt(both, w[:, 0, :, : 2 * fe].reshape(width, 2 * fe)).astype(BF)
    high, mid, low = split_three(inner)
    lane = iota((capacity, LANES), 1)
    spread[mine, :] = jnp.where(
        lane == e,
        high,
        jnp.where(lane == e + local, mid, jnp.where(lane == e + 2 * local, low, 0.0)),
    ).astype(BF)

    @pl.when(step == steps - 1)
    def _():
        if not first:
            for copy in loads:
                copy.wait()

        def put(b):
            at = pl.ds(pl.multiple_of(b * tokens, tokens), tokens)
            if last:
                return pltpu.make_async_copy(cot.at[at], acc_out.at[b], sems.at[b])
            return pltpu.make_async_copy(acc.at[at], acc_out.at[at], sems.at[b])

        @pl.loop(0, nblk)
        def _(b):
            at = pl.ds(pl.multiple_of(b * tokens, tokens), tokens)
            slots = iota((tokens, capacity), 1).astype(F32)
            for i in range(ne):
                chosen[:, i * capacity : (i + 1) * capacity] = one_hot(
                    lane_column(slot_cols[at, :], base + i) == slots
                )
            part = mm(chosen[...], y2[...])
            partg = mm(chosen[...], spread[...])
            if not first:
                part = part + acc[at, :]
                partg = partg + accg[at, :]
            if last:
                cot[at, :] = part.astype(BF)
            else:
                acc[at, :] = part
            accg[at, :] = partg
            put(b).start()

        if last:
            summed = accg[...]
            summed = (
                summed
                + pltpu.roll(summed, LANES - local, 1)
                + pltpu.roll(summed, LANES - 2 * local, 1)
            )
            accg_out[...] = summed.T[:local, :]
            for h in range(2):
                scatter.arrived(h)
                gets = [
                    pltpu.make_async_copy(
                        es.at[2 - h, pl.ds(h * half, half)], e_vmem.at[0], sems.at[nblk]
                    ),
                    pltpu.make_async_copy(e_across.at[h], e_vmem.at[1], sems.at[nblk + 1]),
                ]
                for copy in gets:
                    copy.start()
                for copy in gets:
                    copy.wait()
                e_vmem[0] = plus(e_vmem[0], e_vmem[1])
                back = pltpu.make_async_copy(e_vmem.at[0], e_mix.at[h], sems.at[nblk])
                back.start()
                back.wait()
            scatter.finish()
            scatter.drain()
        else:
            out_g = pltpu.make_async_copy(accg, accg_out, sems.at[nblk])
            out_g.start()
            if stage:
                line.finish()
            out_g.wait()
        for b in range(nblk):
            put(b).wait()


def experts_reverse(cots, given_rows, slot_cols, kept, w, carried, es, later, base, last, capacity, key):
    tokens, width = cots[0].shape
    nblk = EXPERT_COUNT // given_rows.shape[0]
    half = tokens // 2
    total = nblk * tokens
    cols, ne, shard, fe3 = w.shape
    fe = fe3 // 3
    local = EXPERT_COUNT // nblk
    first = carried is None
    shape = jax.ShapeDtypeStruct
    wspec = pl.BlockSpec((cols, 1, shard, fe3), lambda s: (0, s, 0, 0))

    def each(*dims):
        return pl.BlockSpec((1, *dims), lambda s: (s, 0, 0))

    ins = [*cots, given_rows, slot_cols, *kept, w]
    in_specs = [
        ANY,
        ANY,
        ANY,
        FULL,
        FULL,
        each(capacity, width),
        each(capacity, fe),
        each(capacity, fe),
        each(capacity, LANES),
        wspec,
    ]
    aliases = {}
    if not first:
        ins += list(carried)
        in_specs += [ANY, ANY]
        if not last:
            aliases = {len(ins) - 2: 1, len(ins) - 1: 2}
    if last:
        outs = [
            shape(w.shape, BF),
            shape((nblk, tokens, width), BF),
            shape((local, total), F32),
            shape((2, half, width), BF),
            shape((2, half, width), BF),
            shape((2, half, width), BF),
        ]
        out_specs = [wspec, ANY, FULL, ANY, ANY, ANY]
        ins.append(es)
        in_specs.append(ANY)
    else:
        outs = [shape(w.shape, BF), shape((total, width), F32), shape((total, LANES), F32)]
        out_specs = [wspec, ANY, ANY]
    scratch = [
        pltpu.VMEM((total, width), BF),
        pltpu.VMEM((total, width), F32),
        pltpu.VMEM((total, LANES), F32),
        pltpu.VMEM((capacity, total), BF),
        pltpu.VMEM((tokens, ne * capacity), BF),
        pltpu.VMEM((ne * capacity, LANES), BF),
        pltpu.VMEM((capacity, width), BF),
        pltpu.VMEM((capacity, width), BF),
        pltpu.VMEM((ne * capacity, width), BF),
        pltpu.SemaphoreType.DMA((2 * nblk + 2,)),
    ]
    options = dict(vmem_limit_bytes=61 * MIB)
    if last:
        scratch += [
            pltpu.VMEM((2, half, width), BF),
            pltpu.SemaphoreType.DMA((2, RowScatter.count)),
        ]
        options.update(collective_id=key, has_side_effects=True)
    stage, following = later
    if stage:
        aliases = {**aliases, len(ins): len(outs)}
        ins.append(following)
        in_specs.append(ANY)
        outs.append(shape(following.shape, BF))
        out_specs.append(ANY)
        scratch.append(LineGather.scratch(cols // 2, following.shape[1]))
        options.update(collective_id=key, has_side_effects=True)
    return pl.pallas_call(
        functools.partial(reverse_kernel, base, first, last, stage, local, capacity),
        grid=(ne,),
        out_shape=outs,
        in_specs=in_specs,
        out_specs=out_specs,
        scratch_shapes=scratch,
        input_output_aliases=aliases,
        compiler_params=pltpu.CompilerParams(**options),
        cost_estimate=cost(9e9 * ne, 40 * MIB),
        name="experts_reverse",
    )(*ins)


class WeightScatter:
    def __init__(self, full, mate, across, landed, own, others, sems, base, r, c):
        nblk, self.pairs = full.shape[0], full.shape[1]
        self.full, self.mate, self.across, self.landed = full, mate, across, landed
        self.own, self.others = own, others
        self.z, self.k = c // 2, c % 2
        z, k, step = self.z, self.k, self.pairs // 2
        self.part = lambda h: pl.ds(h * step, step)
        self.shares = [
            link(full.at[j, :, 1 - k], mate.at[j], sems, base + j, (r, c ^ 1)) for j in range(nblk)
        ]
        self.rows = RowScatter(
            lambda j, h: full.at[j, self.part(h), k],
            lambda h: full.at[2 - h, self.part(h), k],
            lambda h: across.at[h],
            lambda j, h: landed.at[j - 1, self.part(h)],
            sems,
            base + nblk,
            r,
            c,
        )
        self.line = [
            link(
                own.at[z ^ i],
                others.at[i - 1],
                sems,
                base + nblk + RowScatter.count + i - 1,
                (r, 2 * (z ^ i) + k),
            )
            for i in range(1, self.pairs)
        ]

    def share(self, j):
        self.shares[j].start()

    def join(self):
        mine = pl.ds(self.k, 1)
        for j in (3, 1, 2, 0):
            self.shares[j].wait_recv()
            self.full[j, :, mine] = plus(self.full[j, :, mine], self.mate[j][:, None])
        self.rows.start()

    def middle(self):
        mine = pl.ds(self.k, 1)
        for h in range(2):
            self.rows.arrived(h)
            at = self.part(h)
            self.full[2 - h, at, mine] = plus(self.full[2 - h, at, mine], self.across[h][:, None])
            self.rows.send(h)

    def settle(self):
        self.rows.finish()
        self.own[...] = (
            self.full[0, :, pl.ds(self.k, 1)].reshape(self.own.shape).astype(F32)
            + (self.landed[0].astype(F32) + self.landed[1].astype(F32))
        ).astype(BF)
        for copy in self.line:
            copy.start()

    def result(self):
        for copy in self.line:
            copy.wait_recv()
        shape = self.own.shape[1:]
        return tree_sum(
            [self.own[pl.ds(self.z, 1)].reshape(shape).astype(F32)]
            + [self.others[i].astype(F32) for i in range(self.pairs - 1)]
        )

    def drain(self):
        self.rows.drain()
        for copy in self.shares + self.line:
            copy.wait_send()

    @staticmethod
    def count(nblk, pairs):
        return nblk + RowScatter.count + pairs - 1

    @staticmethod
    def scratch(nblk, pairs, shard, width):
        return [
            pltpu.VMEM((nblk, pairs, 2, shard, width), BF),
            pltpu.VMEM((nblk, pairs, shard, width), BF),
            pltpu.VMEM((2, pairs // 2, shard, width), BF),
            pltpu.VMEM((2, pairs, shard, width), BF),
            pltpu.VMEM((pairs, shard, width), BF),
            pltpu.VMEM((pairs - 1, shard, width), BF),
        ]


class SmallSum:
    def __init__(self, own, mate, chip, row_in, row, line_in, sems, base, sliced, r, c):
        pairs = line_in.shape[0] + 1
        self.refs = (own, mate, chip, row_in, row, line_in)
        self.z, self.sliced = c // 2, sliced
        z, k = c // 2, c % 2
        self.share = link(own, mate, sems, base, (r, c ^ 1))
        count = row_in.shape[0]
        self.rows = [
            link(chip, row_in.at[j], sems, base + 1 + j, (r ^ (j + 1), c)) for j in range(count)
        ]
        self.line = [
            link(
                row.at[z ^ i] if sliced else row,
                line_in.at[i - 1],
                sems,
                base + count + i,
                (r, 2 * (z ^ i) + k),
            )
            for i in range(1, pairs)
        ]

    def over_row(self):
        own, mate, chip = self.refs[:3]
        self.share.wait_recv()
        chip[...] = own[...] + mate[...]
        for copy in self.rows:
            copy.start()

    def over_line(self):
        chip, row_in, row = self.refs[2:5]
        for copy in self.rows:
            copy.wait_recv()
        row[...] = tree_sum([chip[...]] + [row_in[j] for j in range(row_in.shape[0])])
        for copy in self.line:
            copy.start()

    def result(self):
        row, line_in = self.refs[4:]
        for copy in self.line:
            copy.wait_recv()
        own = row[pl.ds(self.z, 1)].reshape(row.shape[1:]) if self.sliced else row[...]
        return tree_sum([own] + [line_in[i] for i in range(line_in.shape[0])])

    def drain(self):
        for copy in [self.share] + self.rows + self.line:
            copy.wait_send()

    @staticmethod
    def scratch(nblk, pairs, shape, sliced):
        whole = (pairs, *shape) if sliced else shape
        return [
            pltpu.VMEM(whole, F32),
            pltpu.VMEM(whole, F32),
            pltpu.VMEM(whole, F32),
            pltpu.VMEM((nblk - 1, *whole), F32),
            pltpu.VMEM(whole, F32),
            pltpu.VMEM((pairs - 1, *shape), F32),
        ]


def back_kernel(nblk, *refs):
    dm, es, e_mix, e_half, dgates, mid_own, mid_sides, mid_corner = refs[:8]
    cots = cot_pieces(*refs[8:11])
    refs = refs[11:]
    mids = [mid_own, mid_sides.at[0], mid_sides.at[1], mid_corner]
    (gates, middle, moe, src_col, mixed, qkv, attn, xd, w_att, w_router) = refs[:10]
    (starts, cos, sin, gain_a, gain_m, src_row) = refs[10:16]
    (block_out, input_grad, qkv_grad, out_grad, router_out, gains_out, e_rest) = refs[16:23]
    (own, d_across, d_landed, dg_land, igb, dmid, dmix, dproj, dkv, bias) = refs[23:33]
    refs = refs[33:]
    sems, lsems = refs[24:]
    tokens, width = xd.shape
    half = tokens // 2
    local = EXPERT_COUNT // nblk
    pairs = w_att.shape[1]
    shard = w_att.shape[3]
    qw = w_att.shape[4] * 2 // 3
    ow = w_att.shape[4] - qw
    hw = HEAD_WIDTH
    r = lax.axis_index("row")
    c = lax.axis_index("col")
    z = c // 2
    k = c % 2
    row_peers = [(r ^ j, c) for j in range(1, nblk)]
    z_peers = [(r, 2 * (z ^ i) + k) for i in range(1, pairs)]
    sibling = (r, c ^ 1)
    greet(row_peers + z_peers + [sibling])

    def part(h):
        return pl.ds(h * half, half)

    n = RowScatter.count
    dms = RowScatter(
        lambda j, h: dm.at[j, part(h)],
        lambda h: own.at[2 - h, part(h)],
        lambda h: d_across.at[h],
        lambda j, h: d_landed.at[j - 1, part(h)],
        sems,
        0,
        r,
        c,
    )
    ess = [
        link(e_mix.at[0], e_rest.at[0], sems, n, (r ^ 2, c)),
        link(e_mix.at[1], e_rest.at[1], sems, n + 1, (r ^ 1, c)),
    ]
    igs = RowGather(
        lambda h: igb.at[0, part(h)], lambda j, h: igb.at[j, part(h)], sems, 3 * n, r, c
    )
    at = 3 * n + RowGather.count
    dgs = [
        link(dgates.at[:, pl.ds(j * tokens, tokens)], dg_land.at[j - 1], sems, at + j - 1, (r ^ j, c))
        for j in range(1, nblk)
    ]
    at += nblk - 1
    wos = WeightScatter(*refs[:6], sems, at, r, c)
    at += WeightScatter.count(nblk, pairs)
    wqs = WeightScatter(*refs[6:12], sems, at, r, c)
    at += WeightScatter.count(nblk, pairs)
    wo, wq = refs[0], refs[6]
    routers = SmallSum(*refs[12:18], sems, at, True, r, c)
    at += nblk + pairs - 1
    gains = SmallSum(*refs[18:24], sems, at, False, r, c)

    dms.start()
    for copy in dgs:
        copy.start()
    loads = [
        pltpu.make_async_copy(dm.at[0], own.at[0], lsems.at[0]),
        pltpu.make_async_copy(dm.at[1, part(1)], own.at[1, part(1)], lsems.at[1]),
        pltpu.make_async_copy(dm.at[2, part(0)], own.at[2, part(0)], lsems.at[2]),
        pltpu.make_async_copy(middle, dmid, lsems.at[3]),
    ]
    for copy in loads:
        copy.start()

    def match(j):
        hit = iota((tokens, tokens), 0) == src_row[:, j * tokens : (j + 1) * tokens]
        return jnp.where(hit, 1.0, 0.0).astype(BF)

    total = jnp.zeros((tokens, width), F32)
    for j in range(nblk):
        get = pltpu.make_async_copy(mids[j], dmix, lsems.at[4])
        get.start()
        hit = match(j)
        get.wait()
        total = total + mm(hit, dmix[...])
    input_grad[...] = total
    dy = jnp.zeros((tokens, width), F32)
    for j in range(nblk):
        gets = [
            pltpu.make_async_copy(cots[2 * j], dmix.at[pl.ds(0, half)], lsems.at[4]),
            pltpu.make_async_copy(cots[2 * j + 1], dmix.at[pl.ds(half, half)], lsems.at[5]),
        ]
        for copy in gets:
            copy.start()
        hit = one_hot(src_col[...] == iota((tokens, tokens), 1) + j * tokens)
        for copy in gets:
            copy.wait()
        dy = dy + mm(hit, dmix[...])
    dproj[:, :width] = dy.astype(BF)
    for copy in loads:
        copy.wait()
    for h in range(2):
        dms.arrived(h)
        rows = part(h)
        own[2 - h, rows, :] = plus(own[2 - h, rows, :], d_across[h])
        dms.send(h)

    for copy in dgs:
        copy.wait_recv()
    parts = [dgates[:, :tokens]] + [dg_land[j] for j in range(nblk - 1)]
    pad = jnp.zeros((LANES - EXPERT_COUNT, tokens), F32)
    dgate = jnp.concatenate(parts + [pad], axis=0).T
    gate = gates[...]
    dchosen = gate * (dgate - jnp.sum(gate * dgate, axis=1, keepdims=True))
    dlogits = dchosen.astype(BF)
    router_t = mm_tn(dlogits, moe[...])
    for i in range(pairs):
        for j in range(nblk):
            refs[12][i, pl.ds(pl.multiple_of((r ^ j) * local, local), local), :] = router_t[
                j * local : (j + 1) * local, i * 2 * shard : (i + 1) * 2 * shard
            ]
    routers.share.start()
    dmoe = mm_nt(dlogits, w_router[...]) + own[0].astype(F32)
    dms.finish()
    for copy in ess:
        copy.start()
    dmoe = dmoe + (d_landed[0].astype(F32) + d_landed[1].astype(F32))
    mid = dmid[...]
    rr = row_scale(mid)
    scaled = dmoe * gain_m[...]
    inner = jnp.mean(scaled * mid, axis=-1, keepdims=True)
    gain_m_part = jnp.sum(dmoe * mid * rr, axis=0, keepdims=True)
    dmid[...] = dproj[:, :width].astype(F32) + (rr * scaled - mid * (rr * rr * rr) * inner)
    dattn = (RESIDUAL_SCALE * dmid[...]).astype(BF)
    for j in range(nblk):
        cols = slice(j * ow, (j + 1) * ow)
        dmix[:, cols] = mm(dattn, w_att[j, :, :, :, qw:].reshape(width, ow)).astype(BF)
        wo[j] = mm_tn(dattn, mixed[:, cols]).astype(BF).reshape(pairs, 2, shard, ow)
        wos.share(j)
    routers.over_row()

    quad = 4 * hw
    groups = nblk * qw // quad
    gain_a_part = jnp.zeros((1, width), F32)
    for b in (1, 0):
        span = (b + 1) * half
        rows = slice(b * half, (b + 1) * half)
        bias[:, :span] = attention_bias(b * half, half, span, starts[rows, :])

        @pl.loop(0, groups)
        def _(g):
            chunk = qkv[:span, pl.ds(pl.multiple_of(g * quad, quad), quad)]
            dm_chunk = dmix[rows, pl.ds(pl.multiple_of(g * 2 * hw, 2 * hw), 2 * hw)]
            k_rows = chunk[:, 2 * hw : 3 * hw]
            v_rows = chunk[:, 3 * hw :]
            dk = jnp.zeros((span, hw), F32)
            dv = jnp.zeros((span, hw), F32)
            dqs = []
            for h in range(2):
                q = chunk[b * half :, h * hw : (h + 1) * hw]
                dmh = dm_chunk[:, h * hw : (h + 1) * hw]
                probs = masked_probs(q, k_rows, bias[:, :span])
                dprobs = mm_nt(dmh, v_rows)
                total = jnp.sum(probs * dprobs, axis=-1, keepdims=True)
                dscores = (probs * (dprobs - total)).astype(BF)
                dqs.append(mm(dscores, k_rows))
                dk = dk + mm_tn(dscores, q)
                dv = dv + mm_tn(probs.astype(BF), dmh)
            dkv_new = jnp.concatenate([dk, dv], axis=1)
            pair = pl.ds(pl.multiple_of(g * 2 * hw, 2 * hw), 2 * hw)
            if b == 1:
                dkv[:, pair] = dkv_new[:half]
                dkv_own = dkv_new[half:]
            else:
                dkv_own = dkv_new + dkv[:, pair]
            d = jnp.concatenate(dqs + [dkv_own], axis=1)
            d = d * cos[rows, :] - swap_halves(d) * sin[rows, :]
            dproj[rows, pl.ds(pl.multiple_of(g * quad, quad), quad)] = d.astype(BF)

        dattn_in = jnp.zeros((half, width), F32)
        for j in range(nblk):
            dattn_in = dattn_in + mm_nt(
                dproj[rows, j * qw : (j + 1) * qw],
                w_att[j, :, :, :, :qw].reshape(width, qw),
            )
        x = xd[rows, :].astype(F32)
        rx = row_scale(x)
        scaled = dattn_in * gain_a[...]
        inner = jnp.mean(scaled * x, axis=-1, keepdims=True)
        igb[0, rows, :] = (dmid[rows, :] + (rx * scaled - x * (rx * rx * rx) * inner)).astype(BF)
        gain_a_part = gain_a_part + jnp.sum(dattn_in * x * rx, axis=0, keepdims=True)
        igs.start(b)
        if b == 1:
            wos.join()
            routers.over_line()

    refs[18][...] = jnp.concatenate(
        [gain_a_part, gain_m_part, jnp.zeros((6, width), F32)], axis=0
    )
    gains.share.start()
    wos.middle()
    for j in range(nblk):
        wq[j] = (
            mm_tn(attn[...], dproj[:, j * qw : (j + 1) * qw])
            .astype(BF)
            .reshape(pairs, 2, shard, qw)
        )
        wqs.share(j)
    igs.forward(1)
    igs.forward(0)
    gains.over_row()
    wqs.join()

    for copy in ess:
        copy.wait_recv()
    e_gets = [
        pltpu.make_async_copy(es.at[0], own.at[0], lsems.at[0]),
        pltpu.make_async_copy(e_half.at[0], own.at[1, part(0)], lsems.at[1]),
        pltpu.make_async_copy(e_half.at[1], own.at[1, part(1)], lsems.at[2]),
        pltpu.make_async_copy(e_rest.at[0], own.at[2, part(0)], lsems.at[3]),
        pltpu.make_async_copy(e_rest.at[1], own.at[2, part(1)], lsems.at[4]),
    ]
    dms.drain()
    for copy in e_gets:
        copy.start()
    for copy in e_gets:
        copy.wait()
    rest = own[2].astype(F32)
    summed = own[0].astype(F32) + (own[1].astype(F32) + rest)
    block_out[...] = (input_grad[...] + RESIDUAL_SCALE * summed).astype(BF)

    wos.settle()
    wqs.middle()
    gains.over_line()
    igs.wait((1, 0), (2, 1))
    total = mm(match(0), igb[0])
    for j in (1, 2):
        total = total + mm(match(j), igb[j])
    router_out[...] = routers.result()
    out_grad[...] = wos.result()
    wqs.settle()
    igs.wait((3, 0), (3, 1))
    input_grad[...] = total + mm(match(3), igb[3])
    gains_out[...] = gains.result()
    qkv_grad[...] = wqs.result()
    for group in (wos, wqs, igs, routers, gains):
        group.drain()
    for copy in ess + dgs:
        copy.wait_send()


def backward(dm, es, e_mix, e_half, dgates, mids, cots, *rest):
    nblk, tokens, width = dm.shape
    w_att = rest[8]
    pairs, shard, both = w_att.shape[1], w_att.shape[3], w_att.shape[4]
    half = tokens // 2
    local = EXPERT_COUNT // nblk
    shape = jax.ShapeDtypeStruct
    count = (
        3 * RowScatter.count
        + RowGather.count
        + (nblk - 1)
        + 2 * WeightScatter.count(nblk, pairs)
        + 2 * (nblk + pairs - 1)
    )
    router_part = (EXPERT_COUNT, 2 * shard)
    outs = pl.pallas_call(
        functools.partial(back_kernel, nblk),
        out_shape=(
            shape((tokens, width), BF),
            shape((tokens, width), F32),
            shape((shard, both * 2 // 3), F32),
            shape((shard, both // 3), F32),
            shape(router_part, F32),
            shape((8, width), F32),
            shape((2, half, width), BF),
        ),
        in_specs=[ANY] * 4 + [FULL] + [ANY] * 6 + [FULL, ANY] + [FULL] * 14,
        out_specs=[FULL] * 6 + [ANY],
        scratch_shapes=[
            pltpu.VMEM((3, tokens, width), BF),
            pltpu.VMEM((2, half, width), BF),
            pltpu.VMEM((2, tokens, width), BF),
            pltpu.VMEM((nblk - 1, local, tokens), F32),
            pltpu.VMEM((nblk, tokens, width), BF),
            pltpu.VMEM((tokens, width), F32),
            pltpu.VMEM((tokens, width), BF),
            pltpu.VMEM((tokens, 2 * width), BF),
            pltpu.VMEM((half, width), F32),
            pltpu.VMEM((half, tokens), F32),
            *WeightScatter.scratch(nblk, pairs, shard, both // 3),
            *WeightScatter.scratch(nblk, pairs, shard, both * 2 // 3),
            *SmallSum.scratch(nblk, pairs, router_part, True),
            *SmallSum.scratch(nblk, pairs, (8, width), False),
            pltpu.SemaphoreType.DMA((2, count)),
            pltpu.SemaphoreType.DMA((8,)),
        ],
        compiler_params=pltpu.CompilerParams(
            vmem_limit_bytes=62 * MIB, collective_id=2, has_side_effects=True
        ),
        cost_estimate=cost(60e9, 100 * MIB),
        name="attention_backward",
    )(dm, es, e_mix, e_half, dgates, *mids, *cots, *rest)
    return outs[:6]


def collect_kernel(*refs):
    parts, outs = refs[:-3], refs[-3:]
    rows = jnp.concatenate([part[...].astype(F32) for part in parts], axis=0)
    fe = outs[0].shape[2]
    for i in range(3):
        outs[i][...] = jnp.swapaxes(rows[:, :, i * fe : (i + 1) * fe], 0, 1)


def collect(parts):
    count = sum(part.shape[0] for part in parts)
    _, shard, fe3 = parts[0].shape
    step = min(16, shard)
    out = jax.ShapeDtypeStruct((shard, count, fe3 // 3), F32)
    return pl.pallas_call(
        collect_kernel,
        grid=(shard // step,),
        out_shape=[out] * 3,
        in_specs=[pl.BlockSpec((part.shape[0], step, fe3), lambda i: (0, i, 0)) for part in parts],
        out_specs=[pl.BlockSpec((step, count, fe3 // 3), lambda i: (i, 0, 0))] * 3,
        compiler_params=params(32),
        cost_estimate=cost(1e6, 9 * MIB),
        name="collect",
    )(*parts)


def swap_over(value, axis, size, step):
    return lax.ppermute(value, axis, [(i, i ^ step) for i in range(size)])


def spread_rows(value, axis, size, step=1):
    return [value] + [swap_over(value, axis, size, j) for j in range(step, size, step)]


def body(
    block_in,
    cotangent,
    seq_lengths,
    seq_order,
    expert_ids,
    places,
    attn_gain,
    w_qkv,
    w_out,
    moe_gain,
    w_router,
    w_gate,
    w_up,
    w_down,
):
    tokens = block_in.shape[1]
    width = block_in.shape[2]
    rows = lax.axis_size("row")
    cols = lax.axis_size("col")
    total = tokens * rows
    r = lax.axis_index("row")
    c = lax.axis_index("col")
    local = w_gate.shape[1]
    shard = w_gate.shape[0]
    fe = w_gate.shape[2]
    capacity = total * TOPK // EXPERT_COUNT
    pairs = cols // 2
    qw = w_qkv.shape[1]
    ow = w_out.shape[1]

    router_own = jnp.concatenate(
        [lax.dynamic_slice_in_dim(w_router, (r ^ j) * local, local, 1) for j in range(rows)], axis=1
    )
    router_own = jnp.pad(router_own, ((0, 0), (0, LANES - EXPERT_COUNT)))
    w_parts = spread_rows(jnp.concatenate([w_qkv, w_out, router_own], axis=1), "col", cols, 2)

    stacked = jnp.concatenate([w_gate, w_up, w_down], axis=2).transpose(1, 0, 2)
    sizes = [3 * local // 8, 3 * local // 8, local // 4]
    bases = [sum(sizes[:i]) for i in range(len(sizes))]
    pieces = [stacked[i : i + n] for i, n in zip(bases, sizes)]

    lengths = seq_lengths[0]
    perm = seq_order[0]
    seq_ids = jnp.arange(lengths.shape[0], dtype=jnp.int32)
    picked = perm[:, None] == seq_ids[None, :]
    dealt_len = jnp.sum(jnp.where(picked, lengths[None, :], 0), axis=1)
    before = seq_ids[None, :] < perm[:, None]
    source_base = jnp.sum(jnp.where(before, lengths[None, :], 0), axis=1)
    upto = seq_ids[None, :] <= seq_ids[:, None]
    seq_ends = jnp.sum(jnp.where(upto, dealt_len[None, :], 0), axis=1)
    dealt_start = seq_ends - dealt_len
    turn = r * tokens
    pos = jnp.arange(total, dtype=jnp.int32) ^ turn
    inside = (pos[:, None] >= dealt_start[None, :]) & (pos[:, None] < seq_ends[None, :])
    seq_starts = jnp.sum(jnp.where(inside, dealt_start[None, :], 0), axis=1)
    offset = pos - seq_starts
    source = jnp.sum(jnp.where(inside, source_base[None, :], 0), axis=1) + offset
    source = source ^ turn
    src_col = source[:, None]
    src_row = source[None, :]
    own_offset = offset[:tokens]
    own_starts = (seq_starts[:tokens] - turn)[:, None]

    half = HEAD_WIDTH // 2
    frequency = ROPE_BASE ** (-jnp.arange(half, dtype=F32) * 2.0 / HEAD_WIDTH)
    turned = own_offset.astype(F32)[:, None] * frequency[None, :]
    cosine, sine = jnp.cos(turned), jnp.sin(turned)
    ones, zeros = jnp.ones_like(cosine), jnp.zeros_like(cosine)
    cos_q, sin_q = cosine * SCORE_SCALE, sine * SCORE_SCALE
    cos_w = jnp.concatenate([cos_q] * 4 + [cosine] * 2 + [ones] * 2, axis=1)
    sin_w = jnp.concatenate([-sin_q, sin_q] * 2 + [-sine, sine] + [zeros] * 2, axis=1)

    tables = (src_col, src_row, own_starts, cos_w, sin_w)
    count = len(w_parts)
    ready = lax.optimization_barrier((pieces[0], pieces[1], *w_parts, *tables))
    pieces[:2], w_parts, tables = ready[:2], ready[2 : 2 + count], ready[2 + count :]
    src_col, src_row, own_starts, cos_w, sin_w = tables
    gathered = [lax.all_gather(piece, "col", axis=0) for piece in pieces[:-1]]

    gain_a = attn_gain[None, :]
    gain_m = moe_gain[None, :]
    (
        xd,
        attn,
        qkv,
        mixed,
        middle,
        moe,
        cot_first,
        slot_cols,
        slot_rows,
        gates,
        packed,
        w_att,
        moe_own,
        slot_given,
        given_rows,
        mid16,
        router_x,
        following,
    ) = front(
        block_in[0],
        cotangent[0],
        pieces[-1],
        w_parts,
        [
            src_col,
            own_starts,
            cos_w,
            sin_w,
            gain_a,
            gain_m,
            expert_ids[0].T,
            places[0].T,
            src_row,
        ],
        rows,
    )
    router_x = router_x.reshape(width, LANES)

    acc = carried = None
    summed = []
    final = len(sizes) - 1
    full = []
    for i in range(len(sizes)):
        w = gathered[i] if i < final else following
        moved = [("rest", cotangent[0], cot_first), ("sides", mid16)]
        moved = moved[i] if i < 2 else ("corner", full[1])
        if i > 0:
            w, *carried = lax.optimization_barrier((w, *carried))
        stage = (1, 3, 0)[i]
        parts = experts_forward(
            moe, slot_rows, slot_given, packed, w, acc, moved, (stage, following), bases[i], i == final, capacity, 3 + i
        )
        kept, acc = parts[:4], parts[4]
        full.append(parts[5])
        if stage:
            following = parts[6]
        stage = (2, 4, 0)[i]
        rows_in = given_rows
        if i == final:
            rows_in = lax.optimization_barrier((given_rows, summed[0]))[0]
        grads, *carried = experts_reverse(
            (cotangent[0], cot_first, full[0]), rows_in, slot_cols, kept, w, carried, acc, (stage, following), bases[i], i == final, capacity, 6 + i
        )
        if stage:
            following = carried.pop()
        summed.append(lax.psum_scatter(grads, "col", scatter_dimension=0, tiled=False))
    es = acc
    dm, dgates, e_mix, e_across, e_half = carried
    block_out, input_grad, qkv_grad, out_grad, router_part, gains = backward(
        dm,
        es,
        e_mix,
        e_half,
        dgates,
        [mid16, full[1], full[2]],
        (cotangent[0], cot_first, full[0]),
        gates,
        middle,
        moe_own,
        src_col[:tokens],
        mixed,
        qkv,
        attn,
        xd,
        w_att,
        router_x,
        own_starts,
        cos_w,
        sin_w,
        gain_a,
        gain_m,
        src_row,
    )
    router_grad = lax.dynamic_slice_in_dim(router_part, c % 2 * shard, shard, 1).T

    gate_grad, up_grad, down_grad = collect(summed)
    return (
        block_out[None],
        input_grad[None],
        gains[0],
        qkv_grad,
        out_grad,
        gains[1],
        router_grad,
        gate_grad,
        up_grad,
        down_grad,
    )


def solution(mesh):
    tokens = P("col", "row", None)
    weight = P("col", "row")
    expert = P("col", "row", None)
    return jax.shard_map(
        body,
        mesh=mesh,
        in_specs=(
            tokens,
            tokens,
            P("col", None),
            P("col", None),
            P("col", None, None),
            P("col", None, None),
            P(),
            weight,
            weight,
            P(),
            P("col", None),
            expert,
            expert,
            expert,
        ),
        out_specs=(
            tokens,
            tokens,
            P(),
            weight,
            weight,
            P(),
            P("col", None),
            expert,
            expert,
            expert,
        ),
        check_vma=False,
    )
```

```python
import functools

import jax
import jax.numpy as jnp
from jax import lax
from jax.experimental import pallas as pl
from jax.experimental.pallas import tpu as pltpu
from jax.sharding import PartitionSpec as P

HEAD_WIDTH = 64
QUERY_HEADS = 16
KEY_VALUE_HEADS = 8
EXPERT_COUNT = 32
TOPK = 8
EPSILON = 1e-06
RESIDUAL_SCALE = 0.22
SCORE_SCALE = 0.015625
ROPE_BASE = 10000.0
MASKED = -1e30
LANES = 128
MIB = 1024 * 1024
BF = jnp.bfloat16
F32 = jnp.float32
ANY = pl.BlockSpec(memory_space=pl.ANY)
FULL = pl.BlockSpec(memory_space=pltpu.VMEM)


def mm(a, b):
    return lax.dot_general(a, b, (((1,), (0,)), ((), ())), preferred_element_type=F32)


def mm_nt(a, b):
    return lax.dot_general(a, b, (((1,), (1,)), ((), ())), preferred_element_type=F32)


def mm_tn(a, b):
    return lax.dot_general(a, b, (((0,), (0,)), ((), ())), preferred_element_type=F32)


def iota(shape, dim):
    return lax.broadcasted_iota(jnp.int32, shape, dim)


def params(mib):
    return pltpu.CompilerParams(vmem_limit_bytes=mib * MIB)


def cost(flops, moved):
    return pl.CostEstimate(flops=int(flops), bytes_accessed=int(moved), transcendentals=0)


def row_scale(values):
    return lax.rsqrt(jnp.mean(values * values, axis=-1, keepdims=True) + EPSILON)


def swap_halves(values):
    width = values.shape[-1]
    half = HEAD_WIDTH // 2
    low = (iota(values.shape, 1) % HEAD_WIDTH) < half
    ahead = pltpu.roll(values, width - half, 1)
    behind = pltpu.roll(values, half, 1)
    return jnp.where(low, ahead, behind)


def attention_bias(row0, rows, cols, starts):
    at = iota((rows, cols), 1)
    allowed = (at <= iota((rows, cols), 0) + row0) & (at >= starts)
    return jnp.where(allowed, 0.0, MASKED)


def masked_probs(q, k, bias):
    scores = mm_nt(q, k) + bias
    raised = jnp.exp(scores - jnp.max(scores, axis=-1, keepdims=True))
    return raised * (1.0 / jnp.sum(raised, axis=-1, keepdims=True))


def link(src, dst, sems, index, device):
    return pltpu.make_async_remote_copy(
        src_ref=src,
        dst_ref=dst,
        send_sem=sems.at[0, index],
        recv_sem=sems.at[1, index],
        device_id=device,
        device_id_type=pl.DeviceIdType.MESH,
    )


def greet(devices):
    barrier = pltpu.get_barrier_semaphore()
    for device in devices:
        pl.semaphore_signal(barrier, inc=1, device_id=device, device_id_type=pl.DeviceIdType.MESH)
    pl.semaphore_wait(barrier, len(devices))


class RowGather:
    count = 6

    def __init__(self, own, slot, sems, base, r, c):
        near, far = (r ^ 1, c), (r ^ 2, c)
        self.copies = {
            (1, 1): link(own(1), slot(1, 1), sems, base, near),
            (2, 0): link(own(0), slot(2, 0), sems, base + 1, far),
            (1, 0): link(own(0), slot(1, 0), sems, base + 2, near),
            (2, 1): link(own(1), slot(2, 1), sems, base + 3, far),
            (3, 0): link(slot(2, 0), slot(3, 0), sems, base + 4, near),
            (3, 1): link(slot(1, 1), slot(3, 1), sems, base + 5, far),
        }

    def start(self, half):
        order = ((2, 0), (1, 0)) if half == 0 else ((1, 1), (2, 1))
        for key in order:
            self.copies[key].start()

    def forward(self, half):
        self.copies[(2, 0) if half == 0 else (1, 1)].wait_recv()
        self.copies[(3, half)].start()

    def wait(self, *keys):
        for key in keys:
            self.copies[key].wait_recv()

    def drain(self):
        for copy in self.copies.values():
            copy.wait_send()


def front_kernel(pairs, *refs):
    xin, cot, w_last = refs[:3]
    w_parts = refs[3 : 3 + pairs]
    refs = refs[3 + pairs :]
    src, starts, cos, sin, gain_a, gain_m, ids, spots, src_row = refs[:9]
    xd, attn, qkv, mixed, middle, moe_all, cot_first, slot_cols, slot_rows, gates, packed = refs[9:20]
    w_att, moe, slot_given, given_rows, mid16, w_router, w_next = refs[20:27]
    xb, bias, chosen, sems, local_sems = refs[27:]
    nblk, tokens, width = xb.shape
    half = tokens // 2
    capacity = nblk * tokens * TOPK // EXPERT_COUNT
    qw = w_att.shape[4] * 2 // 3
    rank = w_att.shape[1] * 2 * w_att.shape[3]
    r = lax.axis_index("row")
    c = lax.axis_index("col")
    z = c // 2
    k = c % 2
    both = w_att.shape[4]
    local = EXPERT_COUNT // nblk
    sibling = (r, c ^ 1)
    greet([(r ^ 1, c), (r ^ 2, c), sibling])

    def cut(ref):
        return lambda h: ref.at[pl.ds(h * half, half)]

    def cut_slot(ref):
        return lambda j, h: ref.at[j, pl.ds(h * half, half)]

    def w_slot(j, h):
        return w_att.at[j, pl.ds(h * (pairs // 2), pairs // 2), k]

    n = RowGather.count
    xs = RowGather(cut(xin), cut_slot(xb), sems, 0, r, c)
    ws = RowGather(lambda h: w_slot(0, h), w_slot, sems, n, r, c)
    ms = RowGather(cut(moe), cut_slot(moe_all), sems, 2 * n, r, c)
    base = 3 * n
    share = [link(w_att.at[j, :, k], w_att.at[j, :, k], sems, base + j, sibling) for j in range(nblk)]
    early = [
        link(cot.at[pl.ds(0, half)], cot_first.at[i], sems, base + nblk + 1 + i, (r ^ (1 + i), c))
        for i in range(2)
    ]
    share.append(link(w_router.at[:, k], w_router.at[:, k], sems, base + nblk, sibling))
    xs.start(1)
    xs.start(0)
    keep = [pltpu.make_async_copy(xin, xb.at[0], local_sems.at[0])]
    for i in range(pairs):
        keep.append(
            pltpu.make_async_copy(
                w_parts[i].at[:, pl.ds(0, both)], w_att.at[0, z ^ i, k], local_sems.at[2 + 2 * i]
            )
        )
        keep.append(
            pltpu.make_async_copy(
                w_parts[i].at[:, pl.ds(both, LANES)], w_router.at[z ^ i, k], local_sems.at[3 + 2 * i]
            )
        )
    for copy in keep:
        copy.start()
    seat = pltpu.make_async_copy(w_last, w_next.at[c], local_sems.at[2 + 2 * pairs])
    seat.start()
    for copy in keep:
        copy.wait()
    ws.start(1)
    ws.start(0)
    share[0].start()
    share[nblk].start()
    xs.forward(0)
    xs.forward(1)

    source = src[:tokens, :]

    def pick(at, j):
        return jnp.where(at == iota((tokens, tokens), 1) + j * tokens, 1.0, 0.0).astype(BF)

    x = mm(pick(source, 0), xb[0])
    xs.wait((1, 0))
    x = x + mm(pick(source, 1), xb[1])
    xs.wait((2, 1))
    x = x + mm(pick(source, 2), xb[2])
    ws.forward(0)
    ws.forward(1)
    ws.wait((1, 0), (2, 1))
    share[1].start()
    share[2].start()
    xs.wait((3, 0), (3, 1))
    x = x + mm(pick(source, 3), xb[3])
    xd[...] = x.astype(BF)
    attn[...] = (x * row_scale(x) * gain_a[...]).astype(BF)
    groups = qw // (4 * HEAD_WIDTH)

    def project(j):
        proj = mm(attn[...], w_att[j, :, :, :, :qw].reshape(rank, qw))
        cos_w = jnp.concatenate([cos[...]] * groups, axis=1)
        sin_w = jnp.concatenate([sin[...]] * groups, axis=1)
        turned = proj * cos_w + swap_halves(proj) * sin_w
        qkv[:, pl.ds(pl.multiple_of(j * qw, qw), qw)] = turned.astype(BF)

    ws.wait((3, 0), (3, 1))
    share[3].start()
    for copy in early:
        copy.start()
    for copy in share:
        copy.wait_recv()

    @pl.loop(0, nblk)
    def _(j):
        project(j)

    pair = 2 * HEAD_WIDTH
    for b in range(2):
        rows = slice(b * half, (b + 1) * half)
        span = (b + 1) * half
        bias[:, :span] = attention_bias(b * half, half, span, starts[rows, :])

        @pl.loop(0, groups * nblk)
        def _(g):
            chunk = qkv[:span, pl.ds(pl.multiple_of(g * 2 * pair, 2 * pair), 2 * pair)]
            k_rows = chunk[:, pair : pair + HEAD_WIDTH]
            v_rows = chunk[:, pair + HEAD_WIDTH :]
            outs = []
            for h in range(2):
                q = chunk[b * half :, h * HEAD_WIDTH : (h + 1) * HEAD_WIDTH]
                probs = masked_probs(q, k_rows, bias[:, :span])
                outs.append(mm(probs.astype(BF), v_rows))
            mixed[rows, pl.ds(pl.multiple_of(g * pair, pair), pair)] = jnp.concatenate(
                outs, axis=1
            ).astype(BF)

        if b == 1:
            ms.forward(0)
        ow = w_att.shape[4] - qw
        out = jnp.zeros((half, width), F32)
        for j in range(nblk):
            w_out = w_att[j, :, :, :, qw:].reshape(rank, ow)
            out = out + mm_nt(mixed[rows, j * ow : (j + 1) * ow], w_out)
        mid = xd[rows, :].astype(F32) + RESIDUAL_SCALE * out
        middle[rows, :] = mid
        mid16[rows, :] = mid.astype(BF)
        moe[rows, :] = (mid * row_scale(mid) * gain_m[...]).astype(BF)
        ms.start(b)

    place = pltpu.make_async_copy(moe, moe_all.at[0], local_sems.at[1])
    place.start()

    @pl.loop(0, nblk)
    def _(b):
        at = pl.ds(pl.multiple_of(b * tokens, tokens), tokens)
        there = pl.ds(pl.multiple_of((b ^ r) * tokens, tokens), tokens)
        expert = iota((EXPERT_COUNT, tokens), 0)
        spot = jnp.zeros((EXPERT_COUNT, tokens), F32)
        named = jnp.zeros((EXPERT_COUNT, tokens), F32)
        own_ids = ids[:, there] ^ (r * local)
        own_spots = spots[:, there].astype(F32)
        for i in range(TOPK):
            hit = expert == own_ids[i : i + 1, :]
            named = jnp.where(hit, 1.0, named)
            spot = jnp.where(hit, own_spots[i : i + 1, :], spot)
        slot = jnp.where((named > 0.0) & (spot < capacity), spot, -1.0)
        slot_rows[:, at] = slot[:local, :]
        rest = jnp.zeros((LANES - EXPERT_COUNT, tokens), F32)
        chosen[at, :] = jnp.concatenate([named, rest], axis=0).T
        slot_cols[at, :] = jnp.concatenate([slot, rest - 1.0], axis=0).T

    ms.forward(1)

    @pl.loop(0, nblk)
    def _(b):
        at = pl.ds(pl.multiple_of(b * tokens, tokens), tokens)
        found = jnp.zeros((tokens, LANES), F32)
        for j in range(nblk):
            part = slice(j * tokens, (j + 1) * tokens)
            match = iota((tokens, tokens), 0) + b * tokens == src_row[:, part]
            match = jnp.where(match, 1.0, 0.0).astype(BF)
            value = slot_cols[part, :] + 1.0
            high = jnp.floor(value * 0.0625)
            low = value - 16.0 * high
            found = found + 16.0 * mm(match, high.astype(BF)) + mm(match, low.astype(BF))
        slot_given[at, :] = found - 1.0
        given_rows[:, at] = (found - 1.0).T[: given_rows.shape[0], :]

    def gate_block(j, rows):
        at = slice(j * tokens, (j + 1) * tokens)
        logits = mm(rows, w_router[...].reshape(width, LANES))
        named = chosen[at, :] > 0.0
        logits = jnp.where(named, logits, MASKED)
        top = jnp.max(logits, axis=-1, keepdims=True)
        raised = jnp.where(named, jnp.exp(logits - top), 0.0)
        gate = raised / jnp.sum(raised, axis=-1, keepdims=True)
        if j == 0:
            gates[...] = gate
        own = jnp.where(iota((tokens, LANES), 1) < local, gate, 0.0)
        high, mid, low = split_three(own)
        packed[at, :] = (high + pltpu.roll(mid, local, 1) + pltpu.roll(low, 2 * local, 1)).astype(BF)

    gate_block(0, moe[...])
    place.wait()
    xs.drain()
    for j, keys in ((1, ((1, 0),)), (2, ((2, 1),)), (3, ((3, 0), (3, 1)))):
        ms.wait(*keys)
        get = pltpu.make_async_copy(moe_all.at[j], xb.at[j], local_sems.at[0])
        get.start()
        get.wait()
        gate_block(j, xb[j])
    seat.wait()
    for copy in early:
        copy.wait_recv()
    for gather in (ws, ms):
        gather.drain()
    for copy in share + early:
        copy.wait_send()


def front(xin, cot, w_last, w_parts, tables, nblk):
    tokens, width = xin.shape
    pairs = len(w_parts)
    shard, both = w_parts[0].shape[0], w_parts[0].shape[1] - LANES
    total = nblk * tokens
    qkv_width = nblk * both * 2 // 3
    head_width = nblk * both // 3
    shape = jax.ShapeDtypeStruct
    count = 3 * RowGather.count + nblk + 3
    local = EXPERT_COUNT // nblk
    return pl.pallas_call(
        functools.partial(front_kernel, pairs),
        out_shape=(
            shape((tokens, width), BF),
            shape((tokens, width), BF),
            shape((tokens, qkv_width), BF),
            shape((tokens, head_width), BF),
            shape((tokens, width), F32),
            shape((nblk, tokens, width), BF),
            shape((2, tokens // 2, width), BF),
            shape((total, LANES), F32),
            shape((local, total), F32),
            shape((tokens, LANES), F32),
            shape((total, LANES), BF),
            shape((nblk, pairs, 2, shard, both), BF),
            shape((tokens, width), BF),
            shape((total, LANES), F32),
            shape((local, total), F32),
            shape((tokens, width), BF),
            shape((pairs, 2, shard, LANES), BF),
            shape((2 * pairs, *w_last.shape), BF),
        ),
        in_specs=[ANY] * (3 + pairs) + [FULL] * 9,
        out_specs=[FULL] * 5 + [ANY] * 2 + [FULL] * 10 + [ANY],
        scratch_shapes=[
            pltpu.VMEM((nblk, tokens, width), BF),
            pltpu.VMEM((tokens // 2, tokens), F32),
            pltpu.VMEM((total, LANES), F32),
            pltpu.SemaphoreType.DMA((2, count)),
            pltpu.SemaphoreType.DMA((3 + 2 * pairs,)),
        ],
        compiler_params=pltpu.CompilerParams(
            vmem_limit_bytes=58 * MIB, collective_id=1, has_side_effects=True
        ),
        cost_estimate=cost(20e9, 60 * MIB),
        name="attention_forward",
    )(xin, cot, w_last, *w_parts, *tables)


class RowScatter:
    count = 6

    def __init__(self, block, mixed_in, across, landed, sems, base, r, c):
        near, far = (r ^ 1, c), (r ^ 2, c)
        self.copies = {
            "diag0": link(block(3, 0), across(0), sems, base, near),
            "diag1": link(block(3, 1), across(1), sems, base + 1, far),
            "near0": link(block(1, 0), landed(1, 0), sems, base + 2, near),
            "far1": link(block(2, 1), landed(2, 1), sems, base + 3, far),
        }
        if mixed_in is not None:
            self.copies["far0"] = link(mixed_in(0), landed(2, 0), sems, base + 4, far)
            self.copies["near1"] = link(mixed_in(1), landed(1, 1), sems, base + 5, near)

    def start(self):
        for key in ("diag0", "diag1", "near0", "far1"):
            self.copies[key].start()

    def arrived(self, half):
        self.copies["diag0" if half == 0 else "diag1"].wait_recv()

    def send(self, half):
        self.copies["far0" if half == 0 else "near1"].start()

    def finish(self):
        for key in self.copies:
            if not key.startswith("diag"):
                self.copies[key].wait_recv()

    def drain(self):
        for copy in self.copies.values():
            copy.wait_send()


def tree_sum(parts):
    while len(parts) > 1:
        parts = [parts[i] + parts[i + 1] for i in range(0, len(parts), 2)]
    return parts[0]


def plus(a, b):
    return (a.astype(F32) + b.astype(F32)).astype(BF)


def one_hot(hit):
    return jnp.where(hit, 1.0, 0.0).astype(BF)


def lane_column(table, index):
    return jnp.sum(jnp.where(iota(table.shape, 1) == index, table, 0.0), axis=1, keepdims=True)


def split_three(value):
    high = value.astype(BF).astype(F32)
    rest = value - high
    mid = rest.astype(BF).astype(F32)
    return high, mid, rest - mid


def forward_kernel(base, first, last, gathers, stage, local, capacity, *refs):
    moe_hbm, slot_rows, slot_given, packed, w = refs[:5]
    refs = refs[5:]
    if not first:
        acc_in, refs = refs[0], refs[1:]
    early = gathers == "rest"
    if gathers:
        own_hbm, refs = refs[0], refs[1:]
    if early:
        first_hbm, refs = refs[0], refs[1:]
    if stage:
        next_in, refs = refs[0], refs[1:]
    routed_out, gate_out, up_out, weight_out, acc_out = refs[:5]
    refs = refs[5:]
    if gathers:
        all_hbm, refs = refs[0], refs[1:]
    if stage:
        next_out, refs = refs[0], refs[1:]
    moe, acc, sel, given, y1, sems = refs[:6]
    step = pl.program_id(0)
    steps = pl.num_programs(0)
    e = base + step
    ne = y1.shape[0] // capacity
    nblk, tokens, width = moe_hbm.shape
    fe = w.shape[3] // 3
    copies = [
        pltpu.make_async_copy(moe_hbm.at[j], moe.at[pl.ds(j * tokens, tokens)], sems.at[j])
        for j in range(nblk)
    ]
    if not first:
        load = pltpu.make_async_copy(acc_in, acc, sems.at[nblk])
    if gathers:
        link_sems = refs[6]
        r = lax.axis_index("row")
        c = lax.axis_index("col")
        half = tokens // 2
        near, far = (r ^ 1, c), (r ^ 2, c)
        top, bottom = pl.ds(0, half), pl.ds(half, half)
        later = []
        greeted = [near, far]
        if stage:
            line = LineGather(stage, next_in, next_out, refs[7], r, c)
            greeted = greeted + line.devices
        if gathers == "rest":
            begin = [
                link(own_hbm.at[bottom], all_hbm.at[0], link_sems, 0, near),
                link(first_hbm.at[1], all_hbm.at[2], link_sems, 1, near),
                link(own_hbm.at[bottom], all_hbm.at[1], link_sems, 2, far),
            ]
            later = [link(all_hbm.at[0], all_hbm.at[3], link_sems, 3, far)]
        elif gathers == "sides":
            begin = [
                link(own_hbm, all_hbm.at[0], link_sems, 0, near),
                link(own_hbm, all_hbm.at[1], link_sems, 1, far),
            ]
        else:
            begin = [
                link(own_hbm.at[1, top], all_hbm.at[top], link_sems, 0, near),
                link(own_hbm.at[0, bottom], all_hbm.at[bottom], link_sems, 1, far),
            ]

    @pl.when(step == 0)
    def _():
        for copy in copies:
            copy.start()
        if not first:
            load.start()
        if gathers:
            greet(greeted)
            for copy in begin:
                copy.start()
            if stage:
                line.start()

    row = slot_rows[pl.ds(e, 1), :]
    for j in range(nblk):
        at = slice(j * tokens, (j + 1) * tokens)
        sel[:, at] = one_hot(iota((capacity, tokens), 0).astype(F32) == row[:, at])

    @pl.when(step == 0)
    def _():
        for copy in copies:
            copy.wait()

    if stage:

        @pl.when(step == steps - 1)
        def _():
            line.advance()

    if early:

        @pl.when(step == steps - 1)
        def _():
            begin[0].wait_recv()
            later[0].start()

    routed_out[0] = mm(sel[...], moe[...]).astype(BF)
    lane = iota((capacity, LANES), 1)
    picked = mm(sel[...], packed[...])
    mine = (lane == e) | (lane == e + local) | (lane == e + 2 * local)
    gate = jnp.sum(jnp.where(mine, picked, 0.0), axis=1, keepdims=True)
    weight_out[0] = jnp.broadcast_to(gate, (capacity, LANES))
    gate_up = mm(routed_out[0], w[:, 0, :, : 2 * fe].reshape(width, 2 * fe))
    gate_in = gate_up[:, :fe]
    up_in = gate_up[:, fe:]
    gate_out[0] = gate_in
    up_out[0] = up_in
    hidden = (gate_in * jax.nn.sigmoid(gate_in) * up_in).astype(BF)
    out = mm_nt(hidden, w[:, 0, :, 2 * fe :].reshape(width, fe))
    y1[pl.ds(pl.multiple_of(step * capacity, capacity), capacity), :] = (gate * out).astype(BF)

    @pl.when(step == steps - 1)
    def _():
        if not first:
            load.wait()

        def put(b):
            at = pl.ds(pl.multiple_of(b * tokens, tokens), tokens)
            if last:
                return pltpu.make_async_copy(moe.at[at], acc_out.at[b], sems.at[b])
            return pltpu.make_async_copy(acc.at[at], acc_out.at[at], sems.at[b])

        @pl.loop(0, nblk)
        def _(b):
            at = pl.ds(pl.multiple_of(b * tokens, tokens), tokens)
            slots = iota((tokens, capacity), 1).astype(F32)
            for i in range(ne):
                given[:, i * capacity : (i + 1) * capacity] = one_hot(
                    lane_column(slot_given[at, :], base + i) == slots
                )
            part = mm(given[...], y1[...])
            if not first:
                part = part + acc[at, :]
            if last:
                moe[at, :] = part.astype(BF)
            else:
                acc[at, :] = part
            put(b).start()

        if stage:
            line.finish()
        if gathers:
            for copy in begin[1:] if early else begin:
                copy.wait_recv()
            for copy in later:
                copy.wait_recv()
            for copy in begin + later:
                copy.wait_send()
        for b in range(nblk):
            put(b).wait()


def experts_forward(moe, slot_rows, slot_given, packed, w, acc, moved, later, base, last, capacity, key):
    nblk, tokens, width = moe.shape
    total = nblk * tokens
    cols, ne, shard, fe3 = w.shape
    fe = fe3 // 3
    local = EXPERT_COUNT // nblk
    first = acc is None
    gathers, *sent = moved
    landing = {"rest": (4, tokens // 2), "sides": (2, tokens), "corner": (tokens,)}[gathers]
    shape = jax.ShapeDtypeStruct
    wspec = pl.BlockSpec((cols, 1, shard, fe3), lambda s: (0, s, 0, 0))

    def each(*dims):
        return pl.BlockSpec((1, *dims), lambda s: (s, 0, 0))

    ins = [moe, slot_rows, slot_given, packed, w]
    in_specs = [ANY, FULL, FULL, FULL, wspec]
    aliases = {}
    if not first:
        ins.append(acc)
        in_specs.append(ANY)
        if not last:
            aliases = {len(ins) - 1: 4}
    outs = [
        shape((ne, capacity, width), BF),
        shape((ne, capacity, fe), F32),
        shape((ne, capacity, fe), F32),
        shape((ne, capacity, LANES), F32),
        shape((nblk, tokens, width), BF) if last else shape((total, width), F32),
    ]
    out_specs = [each(capacity, width), each(capacity, fe), each(capacity, fe), each(capacity, LANES), ANY]
    scratch = [
        pltpu.VMEM((total, width), BF),
        pltpu.VMEM((total, width), F32),
        pltpu.VMEM((capacity, total), BF),
        pltpu.VMEM((tokens, ne * capacity), BF),
        pltpu.VMEM((ne * capacity, width), BF),
        pltpu.SemaphoreType.DMA((nblk + 1,)),
    ]
    options = dict(vmem_limit_bytes=58 * MIB)
    ins += sent
    in_specs += [ANY] * len(sent)
    outs.append(shape((*landing, width), BF))
    out_specs.append(ANY)
    scratch.append(pltpu.SemaphoreType.DMA((2, 4)))
    stage, following = later
    if stage:
        aliases = {**aliases, len(ins): len(outs)}
        ins.append(following)
        in_specs.append(ANY)
        outs.append(shape(following.shape, BF))
        out_specs.append(ANY)
        scratch.append(LineGather.scratch(cols // 2, following.shape[1]))
    options.update(collective_id=key, has_side_effects=True)
    return pl.pallas_call(
        functools.partial(forward_kernel, base, first, last, gathers, stage, local, capacity),
        grid=(ne,),
        out_shape=outs,
        in_specs=in_specs,
        out_specs=out_specs,
        scratch_shapes=scratch,
        input_output_aliases=aliases,
        compiler_params=pltpu.CompilerParams(**options),
        cost_estimate=cost(7e9 * ne, 30 * MIB),
        name="experts_forward",
    )(*ins)


class LineGather:
    def __init__(self, stage, src, dst, sems, r, c):
        self.pairs, self.count = src.shape[0] // 2, src.shape[1]
        self.stage, self.src, self.dst, self.sems = stage, src, dst, sems
        self.z, self.k = c // 2, c % 2
        slots = []
        for slot in range(self.pairs + self.count - 2):
            moves = [(slot - e + 1, e) for e in range(self.count)]
            slots.append([(hop, e) for hop, e in moves if 1 <= hop < self.pairs])
        self.slots = [slots[:1], slots[1:-1], slots[-1:], []][stage - 1]
        self.swaps = []
        if stage == 4:
            self.devices = [(r, c ^ 1)]
            for i in range(self.pairs):
                slot = 2 * i + self.k
                self.swaps.append(link(src.at[slot], dst.at[slot], sems, i, (r, c ^ 1)))
        else:
            devices = 2 * self.pairs
            self.devices = [(r, (c + 2) % devices), (r, (c - 2) % devices)]

    def place(self, side):
        return self.z if side == 0 else self.pairs - 1 - self.z

    def copy(self, side, hop, e):
        at = jnp.maximum(self.place(side) - hop + 1, 0)
        slot = 2 * (at if side == 0 else self.pairs - 1 - at) + self.k
        here = any((hop - 1, e) in moves for moves in self.slots)
        src = self.dst if here else self.src
        index = (side * (self.pairs - 1) + hop - 1) * self.count + e
        return link(
            src.at[slot, e], self.dst.at[slot, e], self.sems, index, self.devices[side]
        )

    def sends(self, side, hop):
        return (self.place(side) >= hop - 1) & (self.place(side) <= self.pairs - 2)

    def send(self, moves):
        for hop, e in moves:
            for side in range(2):

                @pl.when(self.sends(side, hop))
                def _():
                    self.copy(side, hop, e).start()

    def start(self):
        for copy in self.swaps:
            copy.start()
        if self.slots:
            self.send(self.slots[0])

    def land(self, number):
        for hop, e in self.slots[number]:
            for side in range(2):

                @pl.when(self.place(side) >= hop)
                def _():
                    self.copy(side, hop, e).wait_recv()

        if number + 1 < len(self.slots):
            self.send(self.slots[number + 1])

    def advance(self):
        if len(self.slots) > 1:
            self.land(0)

    def finish(self):
        for copy in self.swaps:
            copy.wait_recv()
        for number in range(1 if len(self.slots) > 1 else 0, len(self.slots)):
            self.land(number)
        for moves in self.slots:
            for hop, e in moves:
                for side in range(2):

                    @pl.when(self.sends(side, hop))
                    def _():
                        self.copy(side, hop, e).wait_send()

        for copy in self.swaps:
            copy.wait_send()

    @staticmethod
    def scratch(pairs, count):
        return pltpu.SemaphoreType.DMA((2, max(2 * (pairs - 1) * count, pairs)))


def cot_pieces(own, first, rest):
    half = own.shape[0] // 2
    return [
        own.at[pl.ds(0, half)],
        own.at[pl.ds(half, half)],
        first.at[0],
        rest.at[0],
        first.at[1],
        rest.at[1],
        rest.at[2],
        rest.at[3],
    ]


def reverse_kernel(base, first, last, stage, local, capacity, *refs):
    cot_own, cot_first, cot_rest, given_rows, slot_cols, routed, gate_in_ref, up_in_ref, weight_ref, w = refs[:10]
    refs = refs[10:]
    if not first:
        acc_in, accg_in = refs[:2]
        refs = refs[2:]
    if last:
        es, refs = refs[0], refs[1:]
    if stage:
        next_in, refs = refs[0], refs[1:]
    grads, acc_out, accg_out = refs[:3]
    refs = refs[3:]
    if last:
        e_mix, e_across, e_landed = refs[:3]
        refs = refs[3:]
    if stage:
        next_out, refs = refs[0], refs[1:]
    cot, acc, accg, sel, chosen, spread, dsl, dslot, y2, sems = refs[:10]
    step = pl.program_id(0)
    steps = pl.num_programs(0)
    e = base + step
    tokens, width = cot_own.shape
    nblk = cot.shape[0] // tokens
    half = tokens // 2
    cols, _, shard, fe = w.shape
    fe = fe // 3
    ne = y2.shape[0] // capacity
    copies = [
        pltpu.make_async_copy(piece, cot.at[pl.ds(j * half, half)], sems.at[j])
        for j, piece in enumerate(cot_pieces(cot_own, cot_first, cot_rest))
    ]
    if not first:
        loads = [
            pltpu.make_async_copy(acc_in, acc, sems.at[2 * nblk]),
            pltpu.make_async_copy(accg_in, accg, sems.at[2 * nblk + 1]),
        ]
    r = lax.axis_index("row")
    c = lax.axis_index("col")
    if stage:
        line = LineGather(stage, next_in, next_out, refs[10], r, c)
    if last:
        e_vmem, link_sems = refs[10:]
        scatter = RowScatter(
            lambda j, h: es.at[j, pl.ds(h * half, half)],
            None,
            lambda h: e_across.at[h],
            lambda j, h: e_landed.at[h],
            link_sems,
            0,
            r,
            c,
        )

    @pl.when(step == 0)
    def _():
        for copy in copies:
            copy.start()
        if not first:
            for copy in loads:
                copy.start()
        if last:
            greet([(r ^ 1, c), (r ^ 2, c)])
            scatter.start()
        if stage:
            greet(line.devices)
            line.start()

    row = given_rows[pl.ds(e, 1), :]
    for j in range(nblk):
        at = slice(j * tokens, (j + 1) * tokens)
        sel[:, at] = one_hot(iota((capacity, tokens), 0).astype(F32) == row[:, at])

    @pl.when(step == 0)
    def _():
        for copy in copies:
            copy.wait()

    gate = weight_ref[0, :, :1]

    rows = (RESIDUAL_SCALE * mm(sel[...], cot[...])).astype(BF)
    dsl[...] = rows
    dslot[...] = (gate * rows.astype(F32)).astype(BF)
    gate_in = gate_in_ref[0]
    up_in = up_in_ref[0]
    sig = jax.nn.sigmoid(gate_in)
    silu = gate_in * sig
    hidden = (silu * up_in).astype(BF)
    if stage:

        @pl.when(step == (steps - 1) // 2)
        def _():
            line.advance()

    dhidden = mm(dslot[...], w[:, 0, :, 2 * fe :].reshape(width, fe))
    dgate = (dhidden * up_in * sig * (1.0 + gate_in * (1.0 - sig))).astype(BF)
    dup = (dhidden * silu).astype(BF)
    both = jnp.concatenate([dgate, dup], axis=1)
    out = mm_nt(hidden, w[:, 0, :, 2 * fe :].reshape(width, fe))
    inner = jnp.sum(dsl[...].astype(F32) * out, axis=1, keepdims=True)
    grads[:, 0, :, 2 * fe :] = mm_tn(dslot[...], hidden).astype(BF).reshape(cols, shard, fe)
    grads[:, 0, :, : 2 * fe] = mm_tn(routed[0], both).astype(BF).reshape(cols, shard, 2 * fe)
    mine = pl.ds(pl.multiple_of(step * capacity, capacity), capacity)
    y2[mine, :] = mm_nt(both, w[:, 0, :, : 2 * fe].reshape(width, 2 * fe)).astype(BF)
    high, mid, low = split_three(inner)
    lane = iota((capacity, LANES), 1)
    spread[mine, :] = jnp.where(
        lane == e,
        high,
        jnp.where(lane == e + local, mid, jnp.where(lane == e + 2 * local, low, 0.0)),
    ).astype(BF)

    @pl.when(step == steps - 1)
    def _():
        if not first:
            for copy in loads:
                copy.wait()

        def put(b):
            at = pl.ds(pl.multiple_of(b * tokens, tokens), tokens)
            if last:
                return pltpu.make_async_copy(cot.at[at], acc_out.at[b], sems.at[b])
            return pltpu.make_async_copy(acc.at[at], acc_out.at[at], sems.at[b])

        @pl.loop(0, nblk)
        def _(b):
            at = pl.ds(pl.multiple_of(b * tokens, tokens), tokens)
            slots = iota((tokens, capacity), 1).astype(F32)
            for i in range(ne):
                chosen[:, i * capacity : (i + 1) * capacity] = one_hot(
                    lane_column(slot_cols[at, :], base + i) == slots
                )
            part = mm(chosen[...], y2[...])
            partg = mm(chosen[...], spread[...])
            if not first:
                part = part + acc[at, :]
                partg = partg + accg[at, :]
            if last:
                cot[at, :] = part.astype(BF)
            else:
                acc[at, :] = part
            accg[at, :] = partg
            put(b).start()

        if last:
            summed = accg[...]
            summed = (
                summed
                + pltpu.roll(summed, LANES - local, 1)
                + pltpu.roll(summed, LANES - 2 * local, 1)
            )
            accg_out[...] = summed.T[:local, :]
            for h in range(2):
                scatter.arrived(h)
                gets = [
                    pltpu.make_async_copy(
                        es.at[2 - h, pl.ds(h * half, half)], e_vmem.at[0], sems.at[nblk]
                    ),
                    pltpu.make_async_copy(e_across.at[h], e_vmem.at[1], sems.at[nblk + 1]),
                ]
                for copy in gets:
                    copy.start()
                for copy in gets:
                    copy.wait()
                e_vmem[0] = plus(e_vmem[0], e_vmem[1])
                back = pltpu.make_async_copy(e_vmem.at[0], e_mix.at[h], sems.at[nblk])
                back.start()
                back.wait()
            scatter.finish()
            scatter.drain()
        else:
            out_g = pltpu.make_async_copy(accg, accg_out, sems.at[nblk])
            out_g.start()
            if stage:
                line.finish()
            out_g.wait()
        for b in range(nblk):
            put(b).wait()


def experts_reverse(cots, given_rows, slot_cols, kept, w, carried, es, later, base, last, capacity, key):
    tokens, width = cots[0].shape
    nblk = EXPERT_COUNT // given_rows.shape[0]
    half = tokens // 2
    total = nblk * tokens
    cols, ne, shard, fe3 = w.shape
    fe = fe3 // 3
    local = EXPERT_COUNT // nblk
    first = carried is None
    shape = jax.ShapeDtypeStruct
    wspec = pl.BlockSpec((cols, 1, shard, fe3), lambda s: (0, s, 0, 0))

    def each(*dims):
        return pl.BlockSpec((1, *dims), lambda s: (s, 0, 0))

    ins = [*cots, given_rows, slot_cols, *kept, w]
    in_specs = [
        ANY,
        ANY,
        ANY,
        FULL,
        FULL,
        each(capacity, width),
        each(capacity, fe),
        each(capacity, fe),
        each(capacity, LANES),
        wspec,
    ]
    aliases = {}
    if not first:
        ins += list(carried)
        in_specs += [ANY, ANY]
        if not last:
            aliases = {len(ins) - 2: 1, len(ins) - 1: 2}
    if last:
        outs = [
            shape(w.shape, BF),
            shape((nblk, tokens, width), BF),
            shape((local, total), F32),
            shape((2, half, width), BF),
            shape((2, half, width), BF),
            shape((2, half, width), BF),
        ]
        out_specs = [wspec, ANY, FULL, ANY, ANY, ANY]
        ins.append(es)
        in_specs.append(ANY)
    else:
        outs = [shape(w.shape, BF), shape((total, width), F32), shape((total, LANES), F32)]
        out_specs = [wspec, ANY, ANY]
    scratch = [
        pltpu.VMEM((total, width), BF),
        pltpu.VMEM((total, width), F32),
        pltpu.VMEM((total, LANES), F32),
        pltpu.VMEM((capacity, total), BF),
        pltpu.VMEM((tokens, ne * capacity), BF),
        pltpu.VMEM((ne * capacity, LANES), BF),
        pltpu.VMEM((capacity, width), BF),
        pltpu.VMEM((capacity, width), BF),
        pltpu.VMEM((ne * capacity, width), BF),
        pltpu.SemaphoreType.DMA((2 * nblk + 2,)),
    ]
    options = dict(vmem_limit_bytes=61 * MIB)
    if last:
        scratch += [
            pltpu.VMEM((2, half, width), BF),
            pltpu.SemaphoreType.DMA((2, RowScatter.count)),
        ]
        options.update(collective_id=key, has_side_effects=True)
    stage, following = later
    if stage:
        aliases = {**aliases, len(ins): len(outs)}
        ins.append(following)
        in_specs.append(ANY)
        outs.append(shape(following.shape, BF))
        out_specs.append(ANY)
        scratch.append(LineGather.scratch(cols // 2, following.shape[1]))
        options.update(collective_id=key, has_side_effects=True)
    return pl.pallas_call(
        functools.partial(reverse_kernel, base, first, last, stage, local, capacity),
        grid=(ne,),
        out_shape=outs,
        in_specs=in_specs,
        out_specs=out_specs,
        scratch_shapes=scratch,
        input_output_aliases=aliases,
        compiler_params=pltpu.CompilerParams(**options),
        cost_estimate=cost(9e9 * ne, 40 * MIB),
        name="experts_reverse",
    )(*ins)


class WeightScatter:
    def __init__(self, full, mate, across, landed, own, others, sems, base, r, c):
        nblk, self.pairs = full.shape[0], full.shape[1]
        self.full, self.mate, self.across, self.landed = full, mate, across, landed
        self.own, self.others = own, others
        self.z, self.k = c // 2, c % 2
        z, k, step = self.z, self.k, self.pairs // 2
        self.part = lambda h: pl.ds(h * step, step)
        self.shares = [
            link(full.at[j, :, 1 - k], mate.at[j], sems, base + j, (r, c ^ 1)) for j in range(nblk)
        ]
        self.rows = RowScatter(
            lambda j, h: full.at[j, self.part(h), k],
            lambda h: full.at[2 - h, self.part(h), k],
            lambda h: across.at[h],
            lambda j, h: landed.at[j - 1, self.part(h)],
            sems,
            base + nblk,
            r,
            c,
        )
        self.line = [
            link(
                own.at[z ^ i],
                others.at[i - 1],
                sems,
                base + nblk + RowScatter.count + i - 1,
                (r, 2 * (z ^ i) + k),
            )
            for i in range(1, self.pairs)
        ]

    def share(self, j):
        self.shares[j].start()

    def join(self):
        mine = pl.ds(self.k, 1)
        for j in (3, 1, 2, 0):
            self.shares[j].wait_recv()
            self.full[j, :, mine] = plus(self.full[j, :, mine], self.mate[j][:, None])
        self.rows.start()

    def middle(self):
        mine = pl.ds(self.k, 1)
        for h in range(2):
            self.rows.arrived(h)
            at = self.part(h)
            self.full[2 - h, at, mine] = plus(self.full[2 - h, at, mine], self.across[h][:, None])
            self.rows.send(h)

    def settle(self):
        self.rows.finish()
        self.own[...] = (
            self.full[0, :, pl.ds(self.k, 1)].reshape(self.own.shape).astype(F32)
            + (self.landed[0].astype(F32) + self.landed[1].astype(F32))
        ).astype(BF)
        for copy in self.line:
            copy.start()

    def result(self):
        for copy in self.line:
            copy.wait_recv()
        shape = self.own.shape[1:]
        return tree_sum(
            [self.own[pl.ds(self.z, 1)].reshape(shape).astype(F32)]
            + [self.others[i].astype(F32) for i in range(self.pairs - 1)]
        )

    def drain(self):
        self.rows.drain()
        for copy in self.shares + self.line:
            copy.wait_send()

    @staticmethod
    def count(nblk, pairs):
        return nblk + RowScatter.count + pairs - 1

    @staticmethod
    def scratch(nblk, pairs, shard, width):
        return [
            pltpu.VMEM((nblk, pairs, 2, shard, width), BF),
            pltpu.VMEM((nblk, pairs, shard, width), BF),
            pltpu.VMEM((2, pairs // 2, shard, width), BF),
            pltpu.VMEM((2, pairs, shard, width), BF),
            pltpu.VMEM((pairs, shard, width), BF),
            pltpu.VMEM((pairs - 1, shard, width), BF),
        ]


class SmallSum:
    def __init__(self, own, mate, chip, row_in, row, line_in, sems, base, sliced, r, c):
        pairs = line_in.shape[0] + 1
        self.refs = (own, mate, chip, row_in, row, line_in)
        self.z, self.sliced = c // 2, sliced
        z, k = c // 2, c % 2
        self.share = link(own, mate, sems, base, (r, c ^ 1))
        count = row_in.shape[0]
        self.rows = [
            link(chip, row_in.at[j], sems, base + 1 + j, (r ^ (j + 1), c)) for j in range(count)
        ]
        self.line = [
            link(
                row.at[z ^ i] if sliced else row,
                line_in.at[i - 1],
                sems,
                base + count + i,
                (r, 2 * (z ^ i) + k),
            )
            for i in range(1, pairs)
        ]

    def over_row(self):
        own, mate, chip = self.refs[:3]
        self.share.wait_recv()
        chip[...] = own[...] + mate[...]
        for copy in self.rows:
            copy.start()

    def over_line(self):
        chip, row_in, row = self.refs[2:5]
        for copy in self.rows:
            copy.wait_recv()
        row[...] = tree_sum([chip[...]] + [row_in[j] for j in range(row_in.shape[0])])
        for copy in self.line:
            copy.start()

    def result(self):
        row, line_in = self.refs[4:]
        for copy in self.line:
            copy.wait_recv()
        own = row[pl.ds(self.z, 1)].reshape(row.shape[1:]) if self.sliced else row[...]
        return tree_sum([own] + [line_in[i] for i in range(line_in.shape[0])])

    def drain(self):
        for copy in [self.share] + self.rows + self.line:
            copy.wait_send()

    @staticmethod
    def scratch(nblk, pairs, shape, sliced):
        whole = (pairs, *shape) if sliced else shape
        return [
            pltpu.VMEM(whole, F32),
            pltpu.VMEM(whole, F32),
            pltpu.VMEM(whole, F32),
            pltpu.VMEM((nblk - 1, *whole), F32),
            pltpu.VMEM(whole, F32),
            pltpu.VMEM((pairs - 1, *shape), F32),
        ]


def back_kernel(nblk, *refs):
    dm, es, e_mix, e_half, dgates, mid_own, mid_sides, mid_corner = refs[:8]
    cots = cot_pieces(*refs[8:11])
    refs = refs[11:]
    mids = [mid_own, mid_sides.at[0], mid_sides.at[1], mid_corner]
    (gates, middle, moe, src_col, mixed, qkv, attn, xd, w_att, w_router) = refs[:10]
    (starts, cos, sin, gain_a, gain_m, src_row) = refs[10:16]
    (block_out, input_grad, qkv_grad, out_grad, router_out, gains_out, e_rest) = refs[16:23]
    (own, d_across, d_landed, dg_land, igb, dmid, dmix, dproj, dkv, bias) = refs[23:33]
    refs = refs[33:]
    sems, lsems = refs[24:]
    tokens, width = xd.shape
    half = tokens // 2
    local = EXPERT_COUNT // nblk
    pairs = w_att.shape[1]
    shard = w_att.shape[3]
    qw = w_att.shape[4] * 2 // 3
    ow = w_att.shape[4] - qw
    hw = HEAD_WIDTH
    r = lax.axis_index("row")
    c = lax.axis_index("col")
    z = c // 2
    k = c % 2
    row_peers = [(r ^ j, c) for j in range(1, nblk)]
    z_peers = [(r, 2 * (z ^ i) + k) for i in range(1, pairs)]
    sibling = (r, c ^ 1)
    greet(row_peers + z_peers + [sibling])

    def part(h):
        return pl.ds(h * half, half)

    n = RowScatter.count
    dms = RowScatter(
        lambda j, h: dm.at[j, part(h)],
        lambda h: own.at[2 - h, part(h)],
        lambda h: d_across.at[h],
        lambda j, h: d_landed.at[j - 1, part(h)],
        sems,
        0,
        r,
        c,
    )
    ess = [
        link(e_mix.at[0], e_rest.at[0], sems, n, (r ^ 2, c)),
        link(e_mix.at[1], e_rest.at[1], sems, n + 1, (r ^ 1, c)),
    ]
    igs = RowGather(
        lambda h: igb.at[0, part(h)], lambda j, h: igb.at[j, part(h)], sems, 3 * n, r, c
    )
    at = 3 * n + RowGather.count
    dgs = [
        link(dgates.at[:, pl.ds(j * tokens, tokens)], dg_land.at[j - 1], sems, at + j - 1, (r ^ j, c))
        for j in range(1, nblk)
    ]
    at += nblk - 1
    wos = WeightScatter(*refs[:6], sems, at, r, c)
    at += WeightScatter.count(nblk, pairs)
    wqs = WeightScatter(*refs[6:12], sems, at, r, c)
    at += WeightScatter.count(nblk, pairs)
    wo, wq = refs[0], refs[6]
    routers = SmallSum(*refs[12:18], sems, at, True, r, c)
    at += nblk + pairs - 1
    gains = SmallSum(*refs[18:24], sems, at, False, r, c)

    dms.start()
    for copy in dgs:
        copy.start()
    loads = [
        pltpu.make_async_copy(dm.at[0], own.at[0], lsems.at[0]),
        pltpu.make_async_copy(dm.at[1, part(1)], own.at[1, part(1)], lsems.at[1]),
        pltpu.make_async_copy(dm.at[2, part(0)], own.at[2, part(0)], lsems.at[2]),
        pltpu.make_async_copy(middle, dmid, lsems.at[3]),
    ]
    for copy in loads:
        copy.start()

    def match(j):
        hit = iota((tokens, tokens), 0) == src_row[:, j * tokens : (j + 1) * tokens]
        return jnp.where(hit, 1.0, 0.0).astype(BF)

    total = jnp.zeros((tokens, width), F32)
    for j in range(nblk):
        get = pltpu.make_async_copy(mids[j], dmix, lsems.at[4])
        get.start()
        hit = match(j)
        get.wait()
        total = total + mm(hit, dmix[...])
    input_grad[...] = total
    dy = jnp.zeros((tokens, width), F32)
    for j in range(nblk):
        gets = [
            pltpu.make_async_copy(cots[2 * j], dmix.at[pl.ds(0, half)], lsems.at[4]),
            pltpu.make_async_copy(cots[2 * j + 1], dmix.at[pl.ds(half, half)], lsems.at[5]),
        ]
        for copy in gets:
            copy.start()
        hit = one_hot(src_col[...] == iota((tokens, tokens), 1) + j * tokens)
        for copy in gets:
            copy.wait()
        dy = dy + mm(hit, dmix[...])
    dproj[:, :width] = dy.astype(BF)
    for copy in loads:
        copy.wait()
    for h in range(2):
        dms.arrived(h)
        rows = part(h)
        own[2 - h, rows, :] = plus(own[2 - h, rows, :], d_across[h])
        dms.send(h)

    for copy in dgs:
        copy.wait_recv()
    parts = [dgates[:, :tokens]] + [dg_land[j] for j in range(nblk - 1)]
    pad = jnp.zeros((LANES - EXPERT_COUNT, tokens), F32)
    dgate = jnp.concatenate(parts + [pad], axis=0).T
    gate = gates[...]
    dchosen = gate * (dgate - jnp.sum(gate * dgate, axis=1, keepdims=True))
    dlogits = dchosen.astype(BF)
    router_t = mm_tn(dlogits, moe[...])
    for i in range(pairs):
        for j in range(nblk):
            refs[12][i, pl.ds(pl.multiple_of((r ^ j) * local, local), local), :] = router_t[
                j * local : (j + 1) * local, i * 2 * shard : (i + 1) * 2 * shard
            ]
    routers.share.start()
    dmoe = mm_nt(dlogits, w_router[...]) + own[0].astype(F32)
    dms.finish()
    for copy in ess:
        copy.start()
    dmoe = dmoe + (d_landed[0].astype(F32) + d_landed[1].astype(F32))
    mid = dmid[...]
    rr = row_scale(mid)
    scaled = dmoe * gain_m[...]
    inner = jnp.mean(scaled * mid, axis=-1, keepdims=True)
    gain_m_part = jnp.sum(dmoe * mid * rr, axis=0, keepdims=True)
    dmid[...] = dproj[:, :width].astype(F32) + (rr * scaled - mid * (rr * rr * rr) * inner)
    dattn = (RESIDUAL_SCALE * dmid[...]).astype(BF)
    for j in range(nblk):
        cols = slice(j * ow, (j + 1) * ow)
        dmix[:, cols] = mm(dattn, w_att[j, :, :, :, qw:].reshape(width, ow)).astype(BF)
        wo[j] = mm_tn(dattn, mixed[:, cols]).astype(BF).reshape(pairs, 2, shard, ow)
        wos.share(j)
    routers.over_row()
    wos.join()

    quad = 4 * hw
    groups = nblk * qw // quad
    gain_a_part = jnp.zeros((1, width), F32)
    for b in (1, 0):
        span = (b + 1) * half
        rows = slice(b * half, (b + 1) * half)
        bias[:, :span] = attention_bias(b * half, half, span, starts[rows, :])

        @pl.loop(0, groups)
        def _(g):
            chunk = qkv[:span, pl.ds(pl.multiple_of(g * quad, quad), quad)]
            dm_chunk = dmix[rows, pl.ds(pl.multiple_of(g * 2 * hw, 2 * hw), 2 * hw)]
            k_rows = chunk[:, 2 * hw : 3 * hw]
            v_rows = chunk[:, 3 * hw :]
            dk = jnp.zeros((span, hw), F32)
            dv = jnp.zeros((span, hw), F32)
            dqs = []
            for h in range(2):
                q = chunk[b * half :, h * hw : (h + 1) * hw]
                dmh = dm_chunk[:, h * hw : (h + 1) * hw]
                probs = masked_probs(q, k_rows, bias[:, :span])
                dprobs = mm_nt(dmh, v_rows)
                total = jnp.sum(probs * dprobs, axis=-1, keepdims=True)
                dscores = (probs * (dprobs - total)).astype(BF)
                dqs.append(mm(dscores, k_rows))
                dk = dk + mm_tn(dscores, q)
                dv = dv + mm_tn(probs.astype(BF), dmh)
            dkv_new = jnp.concatenate([dk, dv], axis=1)
            pair = pl.ds(pl.multiple_of(g * 2 * hw, 2 * hw), 2 * hw)
            if b == 1:
                dkv[:, pair] = dkv_new[:half]
                dkv_own = dkv_new[half:]
            else:
                dkv_own = dkv_new + dkv[:, pair]
            d = jnp.concatenate(dqs + [dkv_own], axis=1)
            d = d * cos[rows, :] - swap_halves(d) * sin[rows, :]
            dproj[rows, pl.ds(pl.multiple_of(g * quad, quad), quad)] = d.astype(BF)

        dattn_in = jnp.zeros((half, width), F32)
        for j in range(nblk):
            dattn_in = dattn_in + mm_nt(
                dproj[rows, j * qw : (j + 1) * qw],
                w_att[j, :, :, :, :qw].reshape(width, qw),
            )
        x = xd[rows, :].astype(F32)
        rx = row_scale(x)
        scaled = dattn_in * gain_a[...]
        inner = jnp.mean(scaled * x, axis=-1, keepdims=True)
        igb[0, rows, :] = (dmid[rows, :] + (rx * scaled - x * (rx * rx * rx) * inner)).astype(BF)
        gain_a_part = gain_a_part + jnp.sum(dattn_in * x * rx, axis=0, keepdims=True)
        igs.start(b)
        if b == 1:
            wos.middle()
            routers.over_line()

    refs[18][...] = jnp.concatenate(
        [gain_a_part, gain_m_part, jnp.zeros((6, width), F32)], axis=0
    )
    gains.share.start()
    wos.settle()
    for j in range(nblk):
        wq[j] = (
            mm_tn(attn[...], dproj[:, j * qw : (j + 1) * qw])
            .astype(BF)
            .reshape(pairs, 2, shard, qw)
        )
        wqs.share(j)
    igs.forward(1)
    igs.forward(0)
    gains.over_row()
    wqs.join()

    for copy in ess:
        copy.wait_recv()
    e_gets = [
        pltpu.make_async_copy(es.at[0], own.at[0], lsems.at[0]),
        pltpu.make_async_copy(e_half.at[0], own.at[1, part(0)], lsems.at[1]),
        pltpu.make_async_copy(e_half.at[1], own.at[1, part(1)], lsems.at[2]),
        pltpu.make_async_copy(e_rest.at[0], own.at[2, part(0)], lsems.at[3]),
        pltpu.make_async_copy(e_rest.at[1], own.at[2, part(1)], lsems.at[4]),
    ]
    dms.drain()
    for copy in e_gets:
        copy.start()
    for copy in e_gets:
        copy.wait()
    rest = own[2].astype(F32)
    summed = own[0].astype(F32) + (own[1].astype(F32) + rest)
    block_out[...] = (input_grad[...] + RESIDUAL_SCALE * summed).astype(BF)

    wqs.middle()
    gains.over_line()
    igs.wait((1, 0), (2, 1))
    total = mm(match(0), igb[0])
    for j in (1, 2):
        total = total + mm(match(j), igb[j])
    router_out[...] = routers.result()
    out_grad[...] = wos.result()
    wqs.settle()
    igs.wait((3, 0), (3, 1))
    input_grad[...] = total + mm(match(3), igb[3])
    gains_out[...] = gains.result()
    qkv_grad[...] = wqs.result()
    for group in (wos, wqs, igs, routers, gains):
        group.drain()
    for copy in ess + dgs:
        copy.wait_send()


def backward(dm, es, e_mix, e_half, dgates, mids, cots, *rest):
    nblk, tokens, width = dm.shape
    w_att = rest[8]
    pairs, shard, both = w_att.shape[1], w_att.shape[3], w_att.shape[4]
    half = tokens // 2
    local = EXPERT_COUNT // nblk
    shape = jax.ShapeDtypeStruct
    count = (
        3 * RowScatter.count
        + RowGather.count
        + (nblk - 1)
        + 2 * WeightScatter.count(nblk, pairs)
        + 2 * (nblk + pairs - 1)
    )
    router_part = (EXPERT_COUNT, 2 * shard)
    outs = pl.pallas_call(
        functools.partial(back_kernel, nblk),
        out_shape=(
            shape((tokens, width), BF),
            shape((tokens, width), F32),
            shape((shard, both * 2 // 3), F32),
            shape((shard, both // 3), F32),
            shape(router_part, F32),
            shape((8, width), F32),
            shape((2, half, width), BF),
        ),
        in_specs=[ANY] * 4 + [FULL] + [ANY] * 6 + [FULL, ANY] + [FULL] * 14,
        out_specs=[FULL] * 6 + [ANY],
        scratch_shapes=[
            pltpu.VMEM((3, tokens, width), BF),
            pltpu.VMEM((2, half, width), BF),
            pltpu.VMEM((2, tokens, width), BF),
            pltpu.VMEM((nblk - 1, local, tokens), F32),
            pltpu.VMEM((nblk, tokens, width), BF),
            pltpu.VMEM((tokens, width), F32),
            pltpu.VMEM((tokens, width), BF),
            pltpu.VMEM((tokens, 2 * width), BF),
            pltpu.VMEM((half, width), F32),
            pltpu.VMEM((half, tokens), F32),
            *WeightScatter.scratch(nblk, pairs, shard, both // 3),
            *WeightScatter.scratch(nblk, pairs, shard, both * 2 // 3),
            *SmallSum.scratch(nblk, pairs, router_part, True),
            *SmallSum.scratch(nblk, pairs, (8, width), False),
            pltpu.SemaphoreType.DMA((2, count)),
            pltpu.SemaphoreType.DMA((8,)),
        ],
        compiler_params=pltpu.CompilerParams(
            vmem_limit_bytes=62 * MIB, collective_id=2, has_side_effects=True
        ),
        cost_estimate=cost(60e9, 100 * MIB),
        name="attention_backward",
    )(dm, es, e_mix, e_half, dgates, *mids, *cots, *rest)
    return outs[:6]


def collect_kernel(*refs):
    parts, outs = refs[:-3], refs[-3:]
    rows = jnp.concatenate([part[...].astype(F32) for part in parts], axis=0)
    fe = outs[0].shape[2]
    for i in range(3):
        outs[i][...] = jnp.swapaxes(rows[:, :, i * fe : (i + 1) * fe], 0, 1)


def collect(parts):
    count = sum(part.shape[0] for part in parts)
    _, shard, fe3 = parts[0].shape
    step = min(16, shard)
    out = jax.ShapeDtypeStruct((shard, count, fe3 // 3), F32)
    return pl.pallas_call(
        collect_kernel,
        grid=(shard // step,),
        out_shape=[out] * 3,
        in_specs=[pl.BlockSpec((part.shape[0], step, fe3), lambda i: (0, i, 0)) for part in parts],
        out_specs=[pl.BlockSpec((step, count, fe3 // 3), lambda i: (i, 0, 0))] * 3,
        compiler_params=params(32),
        cost_estimate=cost(1e6, 9 * MIB),
        name="collect",
    )(*parts)


def swap_over(value, axis, size, step):
    return lax.ppermute(value, axis, [(i, i ^ step) for i in range(size)])


def spread_rows(value, axis, size, step=1):
    return [value] + [swap_over(value, axis, size, j) for j in range(step, size, step)]


def body(
    block_in,
    cotangent,
    seq_lengths,
    seq_order,
    expert_ids,
    places,
    attn_gain,
    w_qkv,
    w_out,
    moe_gain,
    w_router,
    w_gate,
    w_up,
    w_down,
):
    tokens = block_in.shape[1]
    width = block_in.shape[2]
    rows = lax.axis_size("row")
    cols = lax.axis_size("col")
    total = tokens * rows
    r = lax.axis_index("row")
    c = lax.axis_index("col")
    local = w_gate.shape[1]
    shard = w_gate.shape[0]
    fe = w_gate.shape[2]
    capacity = total * TOPK // EXPERT_COUNT
    pairs = cols // 2
    qw = w_qkv.shape[1]
    ow = w_out.shape[1]

    router_own = jnp.concatenate(
        [lax.dynamic_slice_in_dim(w_router, (r ^ j) * local, local, 1) for j in range(rows)], axis=1
    )
    router_own = jnp.pad(router_own, ((0, 0), (0, LANES - EXPERT_COUNT)))
    w_parts = spread_rows(jnp.concatenate([w_qkv, w_out, router_own], axis=1), "col", cols, 2)

    stacked = jnp.concatenate([w_gate, w_up, w_down], axis=2).transpose(1, 0, 2)
    sizes = [3 * local // 8, 3 * local // 8, local // 4]
    bases = [sum(sizes[:i]) for i in range(len(sizes))]
    pieces = [stacked[i : i + n] for i, n in zip(bases, sizes)]

    lengths = seq_lengths[0]
    perm = seq_order[0]
    seq_ids = jnp.arange(lengths.shape[0], dtype=jnp.int32)
    picked = perm[:, None] == seq_ids[None, :]
    dealt_len = jnp.sum(jnp.where(picked, lengths[None, :], 0), axis=1)
    before = seq_ids[None, :] < perm[:, None]
    source_base = jnp.sum(jnp.where(before, lengths[None, :], 0), axis=1)
    upto = seq_ids[None, :] <= seq_ids[:, None]
    seq_ends = jnp.sum(jnp.where(upto, dealt_len[None, :], 0), axis=1)
    dealt_start = seq_ends - dealt_len
    turn = r * tokens
    pos = jnp.arange(total, dtype=jnp.int32) ^ turn
    inside = (pos[:, None] >= dealt_start[None, :]) & (pos[:, None] < seq_ends[None, :])
    seq_starts = jnp.sum(jnp.where(inside, dealt_start[None, :], 0), axis=1)
    offset = pos - seq_starts
    source = jnp.sum(jnp.where(inside, source_base[None, :], 0), axis=1) + offset
    source = source ^ turn
    src_col = source[:, None]
    src_row = source[None, :]
    own_offset = offset[:tokens]
    own_starts = (seq_starts[:tokens] - turn)[:, None]

    half = HEAD_WIDTH // 2
    frequency = ROPE_BASE ** (-jnp.arange(half, dtype=F32) * 2.0 / HEAD_WIDTH)
    turned = own_offset.astype(F32)[:, None] * frequency[None, :]
    cosine, sine = jnp.cos(turned), jnp.sin(turned)
    ones, zeros = jnp.ones_like(cosine), jnp.zeros_like(cosine)
    cos_q, sin_q = cosine * SCORE_SCALE, sine * SCORE_SCALE
    cos_w = jnp.concatenate([cos_q] * 4 + [cosine] * 2 + [ones] * 2, axis=1)
    sin_w = jnp.concatenate([-sin_q, sin_q] * 2 + [-sine, sine] + [zeros] * 2, axis=1)

    tables = (src_col, src_row, own_starts, cos_w, sin_w)
    count = len(w_parts)
    ready = lax.optimization_barrier((pieces[0], pieces[1], *w_parts, *tables))
    pieces[:2], w_parts, tables = ready[:2], ready[2 : 2 + count], ready[2 + count :]
    src_col, src_row, own_starts, cos_w, sin_w = tables
    gathered = [lax.all_gather(piece, "col", axis=0) for piece in pieces[:-1]]

    gain_a = attn_gain[None, :]
    gain_m = moe_gain[None, :]
    (
        xd,
        attn,
        qkv,
        mixed,
        middle,
        moe,
        cot_first,
        slot_cols,
        slot_rows,
        gates,
        packed,
        w_att,
        moe_own,
        slot_given,
        given_rows,
        mid16,
        router_x,
        following,
    ) = front(
        block_in[0],
        cotangent[0],
        pieces[-1],
        w_parts,
        [
            src_col,
            own_starts,
            cos_w,
            sin_w,
            gain_a,
            gain_m,
            expert_ids[0].T,
            places[0].T,
            src_row,
        ],
        rows,
    )
    router_x = router_x.reshape(width, LANES)

    acc = carried = None
    summed = []
    final = len(sizes) - 1
    full = []
    for i in range(len(sizes)):
        w = gathered[i] if i < final else following
        moved = [("rest", cotangent[0], cot_first), ("sides", mid16)]
        moved = moved[i] if i < 2 else ("corner", full[1])
        if i > 0:
            w, *carried = lax.optimization_barrier((w, *carried))
        stage = (1, 3, 0)[i]
        parts = experts_forward(
            moe, slot_rows, slot_given, packed, w, acc, moved, (stage, following), bases[i], i == final, capacity, 3 + i
        )
        kept, acc = parts[:4], parts[4]
        full.append(parts[5])
        if stage:
            following = parts[6]
        stage = (2, 4, 0)[i]
        rows_in = given_rows
        if i == final:
            rows_in = lax.optimization_barrier((given_rows, summed[0]))[0]
        grads, *carried = experts_reverse(
            (cotangent[0], cot_first, full[0]), rows_in, slot_cols, kept, w, carried, acc, (stage, following), bases[i], i == final, capacity, 6 + i
        )
        if stage:
            following = carried.pop()
        summed.append(lax.psum_scatter(grads, "col", scatter_dimension=0, tiled=False))
    es = acc
    dm, dgates, e_mix, e_across, e_half = carried
    block_out, input_grad, qkv_grad, out_grad, router_part, gains = backward(
        dm,
        es,
        e_mix,
        e_half,
        dgates,
        [mid16, full[1], full[2]],
        (cotangent[0], cot_first, full[0]),
        gates,
        middle,
        moe_own,
        src_col[:tokens],
        mixed,
        qkv,
        attn,
        xd,
        w_att,
        router_x,
        own_starts,
        cos_w,
        sin_w,
        gain_a,
        gain_m,
        src_row,
    )
    router_grad = lax.dynamic_slice_in_dim(router_part, c % 2 * shard, shard, 1).T

    gate_grad, up_grad, down_grad = collect(summed)
    return (
        block_out[None],
        input_grad[None],
        gains[0],
        qkv_grad,
        out_grad,
        gains[1],
        router_grad,
        gate_grad,
        up_grad,
        down_grad,
    )


def solution(mesh):
    tokens = P("col", "row", None)
    weight = P("col", "row")
    expert = P("col", "row", None)
    return jax.shard_map(
        body,
        mesh=mesh,
        in_specs=(
            tokens,
            tokens,
            P("col", None),
            P("col", None),
            P("col", None, None),
            P("col", None, None),
            P(),
            weight,
            weight,
            P(),
            P("col", None),
            expert,
            expert,
            expert,
        ),
        out_specs=(
            tokens,
            tokens,
            P(),
            weight,
            weight,
            P(),
            P("col", None),
            expert,
            expert,
            expert,
        ),
        check_vma=False,
    )
```
